32 devices in a mesh: batch: 4 (over x, core), seq: 8 (over z, y).
Axes of the slice: x: 2, y: 2, z: 4, core: 2. Of those that a mesh axis runs over, the one named last changes fastest.
Arguments:
- inputs: bfloat16 [8, 2048, 512], P('batch', 'seq'), may hold values from -6 to 6
- lengths: int32 [8], P('batch'), may hold values from 1 to 2048, 10240 in all
- conv_taps: bfloat16 [512, 9], P(('batch', 'seq')), may hold values from -4 to 4
- gain_attn: bfloat16 [512], P(('batch', 'seq')), may hold values from 0.5 to 1.5
- w_proj: bfloat16 [512, 512], P(('batch', 'seq')), may hold values from -0.25 to 0.25
- w_query: bfloat16 [512, 512], P(('batch', 'seq')), may hold values from -0.03125 to 0.03125
- w_key: bfloat16 [512, 512], P(('batch', 'seq')), may hold values from -0.25 to 0.25
- w_value: bfloat16 [512, 512], P(('batch', 'seq')), may hold values from -0.25 to 0.25
- w_out: bfloat16 [512, 512], P(('batch', 'seq')), may hold values from -2 to 2
- gain_ffn: bfloat16 [512], P(('batch', 'seq')), may hold values from 0.5 to 1.5
- w_gate: bfloat16 [512, 2048], P(('batch', 'seq')), may hold values from -0.25 to 0.25
- w_up: bfloat16 [512, 2048], P(('batch', 'seq')), may hold values from -0.25 to 0.25
- w_down: bfloat16 [2048, 512], P(('batch', 'seq')), may hold values from -0.125 to 0.125
- rel_bias: bfloat16 [256], P(('batch', 'seq')), may hold values from -4 to 4
- cotangent: bfloat16 [8, 2048, 512], P('batch', 'seq'), may hold values from -6 to 6
Outputs:
- layer_out: bfloat16 [8, 2048, 512], P('batch', 'seq')
- input_grad: bfloat16 [8, 2048, 512], P('batch', 'seq')
- grad_taps: float32 [512, 9], P(('batch', 'seq'))
- grad_gain_attn: float32 [512], P(('batch', 'seq'))
- grad_proj: float32 [512, 512], P(('batch', 'seq'))
- grad_query: float32 [512, 512], P(('batch', 'seq'))
- grad_key: float32 [512, 512], P(('batch', 'seq'))
- grad_value: float32 [512, 512], P(('batch', 'seq'))
- grad_out: float32 [512, 512], P(('batch', 'seq'))
- grad_gain_ffn: float32 [512], P(('batch', 'seq'))
- grad_gate: float32 [512, 2048], P(('batch', 'seq'))
- grad_up: float32 [512, 2048], P(('batch', 'seq'))
- grad_down: float32 [2048, 512], P(('batch', 'seq'))
- grad_rel_bias: float32 [256], P(('batch', 'seq'))
The draws below stay inside these ranges and needn't reach their ends.
Inputs may be any that keep to these rules, and one draw needn't show every extreme that they name: Sequence s holds lengths[s] valid bytes at its start, the rest is padding; some sequence has all 2048 bytes valid.
All inputs are finite; a program needn't handle non-finite values. No bound on the sum of `lengths` on one device may be relied on, other than what follows from the above.
Results may differ from the reference program's by a relative error of at most 0.035.
Values may be sent and summed in bfloat16 or wider, within the bound.
A program may use at most 256 MiB of HBM per device.

```python
import math
import jax
import jax.numpy as jnp
import numpy as np
from jax import lax

D = 512
FF = 2048
H = 8
HD = 64
NB = 32
TAPS = 9
SEQ_LEN = 2048
SEQS = 8


def block_scale(rng, extent, pieces, smallest, largest):
    def one(dim, parts):
        draws = jax.random.uniform(jax.random.fold_in(jax.random.fold_in(rng, 6), dim), (parts,), jnp.float32, smallest / len(pieces), largest / len(pieces))
        return jnp.repeat(jnp.exp(draws), extent[dim] // parts).reshape((-1,) + (1,) * (len(extent) - dim - 1))

    gain = one(*pieces[0])
    for cut in pieces[1:]:
        gain = gain * one(*cut)
    return gain


def profile(number_of, total, reach, slope):
    loads = [(1 << 20) // math.isqrt(rank ** slope) + 1 for rank in range(2, number_of + 1)]
    surplus, given = total - reach - (number_of - 1), [1] * (number_of - 1)
    while surplus > 0:
        movable = [i for i in range(number_of - 1) if given[i] < reach]
        whole, remaining = sum([loads[i] for i in movable]), surplus
        for i in movable:
            more = min(reach - given[i], max(1, remaining * loads[i] // whole), surplus)
            given[i] = given[i] + more
            surplus = surplus - more
    return np.array([reach] + given)


def uneven_parts(stream_key, number_of, total, bound, slope):
    if number_of == 2:
        one = jax.random.randint(stream_key, (), max(1, total - bound), min(bound, total - 1) + 1)
        return jnp.stack([one, total - one])
    tallies = jnp.asarray(profile(number_of, total, bound, slope), jnp.int32)
    pairs = (number_of - 1) // 2
    donor, sink = tallies[1:1 + 2 * pairs:2], tallies[2:2 + 2 * pairs:2]
    slack = jnp.minimum(donor - 1, bound - sink)
    moved = jax.random.randint(jax.random.fold_in(stream_key, 1), (pairs,), 0, 1 << 20) % (slack + 1)
    tallies = tallies.at[1:1 + 2 * pairs:2].set(donor - moved).at[2:2 + 2 * pairs:2].set(sink + moved)
    return tallies[jax.random.permutation(jax.random.fold_in(stream_key, 2), number_of)]


def centred(stream_key, shape, width, bound, shards=(), held_as=jnp.bfloat16):
    loudness = block_scale(stream_key, shape, shards, -0.22, 0.18) if shards else 1.0
    result = jax.random.normal(stream_key, shape, jnp.float32) * width * loudness
    return jnp.minimum(jnp.maximum(result, -bound), bound).astype(held_as)


def setup_inputs(seed: int = 0) -> dict:
    key_of = jax.random.split(jax.random.key(seed), 16)
    inputs = centred(key_of[0], (SEQS, SEQ_LEN, D), 1.0, 6.0, ((0, 4), (1, 8)))
    lengths = uneven_parts(key_of[1], SEQS, SEQS * SEQ_LEN * 5 // 8, SEQ_LEN, 1).astype(jnp.int32)
    conv_taps = centred(key_of[2], (D, TAPS), 1.0, 4.0, ((0, 32),))
    gain_attn = jnp.clip(1.0 + 0.1 * jax.random.normal(key_of[3], (D,), jnp.float32), 0.5, 1.5).astype(jnp.bfloat16)
    w_proj = centred(key_of[4], (D, D), D ** -0.5, 0.25, ((0, 32),))
    w_query = centred(key_of[5], (D, D), (D * HD) ** -0.5, 0.03125, ((0, 32),))
    w_key = centred(key_of[6], (D, D), D ** -0.5, 0.25, ((0, 32),))
    w_value = centred(key_of[7], (D, D), D ** -0.5, 0.25, ((0, 32),))
    w_out = centred(key_of[8], (D, D), (D // 64) ** -0.5, 2.0, ((0, 32),))
    gain_ffn = jnp.clip(1.0 + 0.1 * jax.random.normal(key_of[9], (D,), jnp.float32), 0.5, 1.5).astype(jnp.bfloat16)
    w_gate = centred(key_of[10], (D, FF), D ** -0.5, 0.25, ((0, 32),))
    w_up = centred(key_of[11], (D, FF), D ** -0.5, 0.25, ((0, 32),))
    w_down = centred(key_of[12], (FF, D), FF ** -0.5, 0.125, ((0, 32),))
    rel_bias = centred(key_of[13], (H * NB,), 1.0, 4.0, ((0, 32),))
    cotangent = centred(key_of[14], (SEQS, SEQ_LEN, D), 1.0, 6.0, ((0, 4), (1, 8)))
    return dict(inputs=inputs, lengths=lengths, conv_taps=conv_taps, gain_attn=gain_attn, w_proj=w_proj, w_query=w_query, w_key=w_key, w_value=w_value, w_out=w_out, gain_ffn=gain_ffn, w_gate=w_gate, w_up=w_up, w_down=w_down, rel_bias=rel_bias, cotangent=cotangent)


@jax.custom_vjp
def low(v):
    return lax.optimization_barrier(v.astype(jnp.bfloat16)).astype(jnp.float32)

@jax.custom_vjp
def low_back(v):
    return v

def low_keep(v):
    return (low(v), None)

def low_pass(kept, grad):
    return (grad,)

def back_keep(v):
    return (v, None)

def back_low(kept, grad):
    return (low(grad),)
low.defvjp(low_keep, low_pass)
low_back.defvjp(back_keep, back_low)
EPSILON = 1e-06
LIMITS = (12, 16, 23, 32, 46, 64, 91)
WINDOWS = ((2, 0), (3, 2), (4, 5))

def mat_dot(lhs_array, rhs_array):
    return jnp.dot(lhs_array, rhs_array, precision=lax.Precision.HIGHEST, preferred_element_type=jnp.float32)

def bucket_of(relative):
    distance = jnp.abs(relative)
    larger = jnp.full(relative.shape, 8, jnp.int32)
    for threshold in LIMITS:
        larger = larger + (distance >= threshold).astype(jnp.int32)
    inside = jnp.where(distance < 8, distance, larger)
    return inside + 16 * (relative > 0).astype(jnp.int32)

def norm_rows(hidden, gain_row):
    return hidden * lax.rsqrt(lax.optimization_barrier(jnp.mean(hidden * hidden, axis=-1, keepdims=True)) + EPSILON) * gain_row

def conv_mix(padded, taps, row_count):
    summed = jnp.zeros(padded.shape[:-2] + (row_count, padded.shape[-1]), jnp.float32)
    for window_len, offset in WINDOWS:
        conv_sum = jnp.zeros_like(summed)
        for tap_index in range(window_len):
            shifted = lax.slice_in_dim(padded, 3 - tap_index, 3 - tap_index + row_count, axis=padded.ndim - 2)
            conv_sum = conv_sum + taps[:, offset + tap_index] * shifted
        summed = summed + jax.nn.gelu(conv_sum, approximate=True)
    return summed

def sequence_layer(seq_in, seq_len, params):
    taps, gain_one, proj_w, query_w, key_w, value_w, out_w, gain_two, gate_w, up_w, down_w, bias_table = params
    full_len = seq_in.shape[0]
    padded = jnp.concatenate([jnp.zeros((3, D), jnp.float32), seq_in], axis=0)
    mixed_conv = low(conv_mix(padded, taps, full_len))
    hidden_one = seq_in + low_back(mat_dot(mixed_conv, proj_w))
    normed_one = low(norm_rows(hidden_one, gain_one))
    queries = low(low_back(mat_dot(normed_one, query_w))).reshape(full_len, H, HD)
    key_vecs = low(low_back(mat_dot(normed_one, key_w))).reshape(full_len, H, HD)
    values = low(low_back(mat_dot(normed_one, value_w))).reshape(full_len, H, HD)
    key_pos = jnp.arange(full_len, dtype=jnp.int32)
    key_valid = key_pos < seq_len
    block_len = min(512, full_len)

    def attend(begin_at):
        query_block = lax.dynamic_slice_in_dim(queries, begin_at, block_len, 0)
        query_pos = begin_at + jnp.arange(block_len, dtype=jnp.int32)
        buckets = bucket_of(key_pos[None, :] - query_pos[:, None])
        pos_bias = bias_table[:, buckets]
        products = jnp.einsum('qhd,khd->hqk', query_block, key_vecs, precision=lax.Precision.HIGHEST)
        scores = low_back(products) + pos_bias
        scores = jnp.where(key_valid[None, None, :], scores, -1000000000.0)
        probs = low(jax.nn.softmax(scores, axis=-1))
        return jnp.einsum('hqk,khd->qhd', probs, values, precision=lax.Precision.HIGHEST)
    starts = jnp.arange(full_len // block_len, dtype=jnp.int32) * block_len
    attended = lax.map(jax.checkpoint(attend), starts).reshape(full_len, D)
    attended = low(low_back(attended))
    hidden_two = hidden_one + low_back(mat_dot(attended, out_w))
    normed_two = low(norm_rows(hidden_two, gain_two))
    gate_pre = low_back(mat_dot(normed_two, gate_w))
    up_pre = low_back(mat_dot(normed_two, up_w))
    inner_act = low(jax.nn.gelu(gate_pre, approximate=True) * up_pre)
    return hidden_two + low_back(mat_dot(inner_act, down_w))

def forward(all_in, params, lengths):
    layer_fn = jax.checkpoint(sequence_layer)

    def map_step(seq_item):
        seq_in, seq_len = seq_item
        return layer_fn(seq_in, seq_len, params)
    return lax.map(map_step, (all_in, lengths))

def reference(inputs, lengths, conv_taps, gain_attn, w_proj, w_query, w_key, w_value, w_out, gain_ffn, w_gate, w_up, w_down, rel_bias, cotangent):
    params = (conv_taps.astype(jnp.float32), gain_attn.astype(jnp.float32), w_proj.astype(jnp.float32), w_query.astype(jnp.float32), w_key.astype(jnp.float32), w_value.astype(jnp.float32), w_out.astype(jnp.float32), gain_ffn.astype(jnp.float32), w_gate.astype(jnp.float32), w_up.astype(jnp.float32), w_down.astype(jnp.float32), rel_bias.astype(jnp.float32).reshape(H, NB))
    all_in = inputs.astype(jnp.float32)
    seq_lengths = lengths.astype(jnp.int32)

    def whole(all_arg, param_arg):
        return forward(all_arg, param_arg, seq_lengths)
    layer_rows, back_fn = jax.vjp(whole, all_in, params)
    input_grad, param_grads = back_fn(cotangent.astype(jnp.float32))
    grads = list(param_grads)
    grads[11] = grads[11].reshape(H * NB)
    return (layer_rows.astype(jnp.bfloat16), input_grad.astype(jnp.bfloat16), grads[0], grads[1], grads[2], grads[3], grads[4], grads[5], grads[6], grads[7], grads[8], grads[9], grads[10], grads[11])
```

```python
import functools
from functools import partial

import jax
import jax.numpy as jnp
import numpy as np
from jax import lax
from jax.experimental import pallas as pl
from jax.experimental.pallas import tpu as pltpu
from jax.sharding import PartitionSpec as P

NB = 32
EPSILON = 1e-06
LIMITS = (12, 16, 23, 32, 46, 64, 91)
WINDOWS = ((2, 0), (3, 2), (4, 5))
TAPS = 9
PACK = 128

def from_behind(shard, axis, by):
    count = lax.axis_size(axis)
    pairs = [(i, i + by) for i in range(count) if 0 <= i + by < count]
    return lax.ppermute(shard, axis, pairs)


def mat_dot(lhs_array, rhs_array):
    return jnp.dot(lhs_array, rhs_array, preferred_element_type=jnp.float32)


def outer_sum(lhs_array, rhs_array):
    return lax.dot_general(
        lhs_array, rhs_array, (((0,), (0,)), ((), ())), preferred_element_type=jnp.float32
    )


def back_dot(grad_rows, weight):
    return lax.dot_general(
        grad_rows, weight, (((1,), (1,)), ((), ())), preferred_element_type=jnp.float32
    )


def bucket_of(relative):
    distance = jnp.abs(relative)
    larger = jnp.full(relative.shape, 8, jnp.int32)
    for threshold in LIMITS:
        larger = larger + (distance >= threshold).astype(jnp.int32)
    inside = jnp.where(distance < 8, distance, larger)
    return inside + 16 * (relative > 0).astype(jnp.int32)


def norm_rows(hidden, gain_row):
    return (
        hidden * lax.rsqrt(jnp.mean(hidden * hidden, axis=-1, keepdims=True) + EPSILON) * gain_row
    )


def gated(gate_pre, up_pre):
    return jax.nn.gelu(gate_pre, approximate=True) * up_pre


def conv_mix(padded, taps, row_count):
    summed = jnp.zeros(padded.shape[:-2] + (row_count, padded.shape[-1]), jnp.float32)
    for window_len, offset in WINDOWS:
        conv_sum = jnp.zeros_like(summed)
        for tap_index in range(window_len):
            shifted = lax.slice_in_dim(
                padded, 3 - tap_index, 3 - tap_index + row_count, axis=padded.ndim - 2
            )
            conv_sum = conv_sum + taps[:, offset + tap_index] * shifted
        summed = summed + jax.nn.gelu(conv_sum, approximate=True)
    return summed


def near_offsets(rows):
    lane = np.arange(2 * rows)
    lane = np.where(lane < rows, lane, lane - 2 * rows)
    return rows * (np.arange(3)[:, None, None] - 1) + np.arange(8)[None, :, None] - lane[None, None, :]


def bias_tables(table, rows):
    heads = table.shape[0]
    buckets = bucket_of(jnp.asarray(near_offsets(rows)[:, 0, :], jnp.int32)).reshape(-1)
    onehot = (buckets[None, :] == jnp.arange(NB, dtype=jnp.int32)[:, None]).astype(jnp.float32)
    diag = jnp.dot(table, onehot, precision=lax.Precision.HIGHEST)
    far = jnp.stack([table[:, NB // 2 - 1], table[:, NB - 1]], axis=1)
    return far, diag.reshape(heads // 2, 6, 2 * rows)


def bias_grad(near, rows):
    near = near.reshape(near.shape[0] * 2, 5, 8, 2 * rows)
    buckets = bucket_of(jnp.asarray(near_offsets(rows), jnp.int32))
    hit = buckets[None] == jnp.arange(NB, dtype=jnp.int32)[:, None, None, None]
    grad = jnp.sum(jnp.where(hit[None], near[:, None, 1:4], 0.0), axis=(2, 3, 4))
    left = jnp.sum(near[:, 0], axis=(1, 2))
    right = jnp.sum(near[:, 4], axis=(1, 2))
    return grad.at[:, NB // 2 - 1].add(left).at[:, NB - 1].add(right)


def nt_dot(a, b):
    return lax.dot_general(a, b, (((1,), (1,)), ((), ())), preferred_element_type=jnp.float32)


def tn_dot(a, b):
    return lax.dot_general(a, b, (((0,), (0,)), ((), ())), preferred_element_type=jnp.float32)


def nn_dot(a, b):
    return lax.dot_general(a, b, (((1,), (0,)), ((), ())), preferred_element_type=jnp.float32)


def fill_bias(rows, far_ref, diag_ref, bias_ref, pair):
    for a in range(2):
        bias_ref[a, 0] = jnp.full((rows, rows), far_ref[2 * pair + a, 0], jnp.float32)
        bias_ref[a, 4] = jnp.full((rows, rows), far_ref[2 * pair + a, 1], jnp.float32)
        for c in range(3):
            base = jnp.broadcast_to(diag_ref[0, 3 * a + c : 3 * a + c + 1, :], (rows, 2 * rows))
            bias_ref[a, 1 + c] = pltpu.roll(base, 0, 1, stride=1, stride_axis=0)[:, :rows]


def head_halves(block):
    lane = lax.broadcasted_iota(jnp.int32, block.shape, 1)
    zero = jnp.zeros_like(block)
    half = block.shape[1] // 2
    return jnp.where(lane < half, block, zero), jnp.where(lane < half, zero, block)


def attend_kernel(
    rows, info_ref, far_ref, diag_ref, q_ref, k_ref, v_ref, o_ref, full_ref, inv_ref, peak_ref, bias_ref, s_ref, acc_ref
):
    pair, b = pl.program_id(0), pl.program_id(1)

    @pl.when(b == 0)
    def _():
        fill_bias(rows, far_ref, diag_ref, bias_ref, pair)

    length, first = info_ref[b], info_ref[pl.num_programs(1)]
    count = lax.div(length + rows - 1, rows)
    halves = head_halves(q_ref[...])
    wide = q_ref.shape[1]
    half = wide // 2
    key_row = lax.broadcasted_iota(jnp.int32, (rows, rows), 0)

    def scores(kc, peaks):
        k = k_ref[0, pl.ds(kc * rows, rows), :]
        slot = jnp.clip(kc - first + 2, 0, 4)
        valid = key_row < length - kc * rows
        new = []
        for a in range(2):
            s = nt_dot(k, halves[a]) + bias_ref[a, slot]
            s = jnp.where(valid, s, -1e9)
            s_ref[a, pl.ds(kc * rows, rows), :] = s
            new.append(jnp.maximum(peaks[a], jnp.max(s.reshape(rows // 8, 8, rows), axis=0)))
        return tuple(new)

    low = jnp.full((8, rows), -jnp.inf, jnp.float32)
    peaks = lax.fori_loop(0, count, scores, (low, low))
    peaks = [jnp.max(p, axis=0, keepdims=True) for p in peaks]
    acc_ref[...] = jnp.zeros_like(acc_ref)
    lane = lax.broadcasted_iota(jnp.int32, (rows, wide), 1)

    def weigh(kc, carry):
        v = v_ref[0, pl.ds(kc * rows, rows), :]
        ones = jnp.ones_like(v)
        for a, v_one in enumerate((jnp.where(lane < half, v, ones), jnp.where(lane < half, ones, v))):
            e = jnp.exp(s_ref[a, pl.ds(kc * rows, rows), :] - peaks[a])
            acc_ref[a] += tn_dot(v_one, e.astype(jnp.bfloat16))
        return carry

    lax.fori_loop(0, count, weigh, 0)
    inv = jnp.concatenate([1.0 / acc_ref[0, half:], 1.0 / acc_ref[1, :half]], axis=0)
    out = jnp.concatenate([acc_ref[0, :half], acc_ref[1, half:]], axis=0) * inv
    out = out.T
    o_ref[...] = out.astype(o_ref.dtype)
    full_ref[...] = out
    inv_ref[...] = inv.T
    for a in range(2):
        peak_ref[0, 0, a : a + 1, :] = peaks[a]


def attention_cost(q, kv, products):
    flops = products * 8 * q.shape[0] * kv.shape[1] * q.shape[1]
    return pl.CostEstimate(
        flops=flops, bytes_accessed=2 * (q.size + kv.size) * products, transcendentals=8 * q.shape[0] * kv.shape[1]
    )


def attend(info, far, diag, q, kv, rows, length):
    heads = far.shape[0]
    seqs = kv.shape[0]
    wide = 2 * (q.shape[1] // heads)
    pairs = heads // 2
    smem = pl.BlockSpec(memory_space=pltpu.SMEM)
    return pl.pallas_call(
        functools.partial(attend_kernel, rows),
        grid=(pairs, seqs),
        in_specs=[
            smem, smem,
            pl.BlockSpec((1, 6, 2 * rows), lambda p, b: (p, 0, 0)),
            pl.BlockSpec((rows, wide), lambda p, b: (b, p)),
            pl.BlockSpec((1, length, wide), lambda p, b: (b, 0, 2 * p)),
            pl.BlockSpec((1, length, wide), lambda p, b: (b, 0, 2 * p + 1)),
        ],
        out_specs=[pl.BlockSpec((rows, wide), lambda p, b: (b, p))] * 3
        + [pl.BlockSpec((1, 1, 2, rows), lambda p, b: (b, p, 0, 0))],
        out_shape=[
            jax.ShapeDtypeStruct(q.shape, jnp.bfloat16),
            jax.ShapeDtypeStruct(q.shape, jnp.float32),
            jax.ShapeDtypeStruct(q.shape, jnp.float32),
            jax.ShapeDtypeStruct((seqs, pairs, 2, rows), jnp.float32),
        ],
        scratch_shapes=[
            pltpu.VMEM((2, 5, rows, rows), jnp.float32),
            pltpu.VMEM((2, length, rows), jnp.float32),
            pltpu.VMEM((2, wide, rows), jnp.float32),
        ],
        compiler_params=pltpu.CompilerParams(vmem_limit_bytes=48 << 20),
        cost_estimate=attention_cost(q, kv, 2),
        name="attend",
    )(info, far, diag, q, kv, kv)


def attend_back_kernel(rows, info_ref, far_ref, diag_ref, q_ref, g_ref, full_ref, k_ref, v_ref, peak_ref,
                       dq_ref, dkv_ref, near_ref, bias_ref, sum_ref, acc_ref):
    pair, b = pl.program_id(0), pl.program_id(1)

    @pl.when(b == 0)
    def _():
        fill_bias(rows, far_ref, diag_ref, bias_ref, pair)
        sum_ref[...] = jnp.zeros_like(sum_ref)

    seqs = pl.num_programs(1)
    length, first = info_ref[b], info_ref[seqs]
    count = lax.div(length + rows - 1, rows)
    total = k_ref.shape[1] // rows
    q_half = head_halves(q_ref[...])
    g_half = head_halves(g_ref[...])
    wide = q_ref.shape[1]
    half = wide // 2
    key_row = lax.broadcasted_iota(jnp.int32, (rows, rows), 0)
    acc_ref[...] = jnp.zeros_like(acc_ref)
    peak = [peak_ref[0, 0, a : a + 1, :] for a in range(2)]
    along = (g_ref[...].astype(jnp.float32) * full_ref[...]).T
    delta = [jnp.sum(along[a * half : (a + 1) * half], axis=0, keepdims=True) for a in range(2)]

    def step(kc, carry):
        here = pl.ds(kc * rows, rows)
        k = k_ref[0, here, :]
        v = v_ref[0, here, :]
        slot = jnp.clip(kc - first + 2, 0, 4)
        valid = key_row < length - kc * rows
        dk = dv = None
        for a in range(2):
            s = nt_dot(k, q_half[a]) + bias_ref[a, slot]
            e_low = jnp.where(valid, jnp.exp(s - peak[a]), 0.0).astype(jnp.bfloat16)
            ds = e_low.astype(jnp.float32) * (nt_dot(v, g_half[a]) - delta[a])
            sum_ref[a, slot] += ds
            ds_low = ds.astype(jnp.bfloat16)
            dv_a = nn_dot(e_low, g_half[a])
            dk_a = nn_dot(ds_low, q_half[a])
            dv = dv_a if dv is None else dv + dv_a
            dk = dk_a if dk is None else dk + dk_a
            acc_ref[a] += tn_dot(k, ds_low)
        dkv_ref[0, here, :wide] = dk.astype(dkv_ref.dtype)
        dkv_ref[0, here, wide:] = dv.astype(dkv_ref.dtype)
        return carry

    lax.fori_loop(0, count, step, 0)

    def blank(kc, carry):
        here = pl.ds(kc * rows, rows)
        dkv_ref[0, here, :] = jnp.zeros((rows, 2 * wide), dkv_ref.dtype)
        return carry

    lax.fori_loop(count, total, blank, 0)
    dq_ref[...] = jnp.concatenate([acc_ref[0, :half], acc_ref[1, half:]], axis=0).T.astype(dq_ref.dtype)

    @pl.when(b == seqs - 1)
    def _():
        for a in range(2):
            for slot in range(5):
                total_sum = jnp.zeros((8, 2 * rows), jnp.float32)
                for g in range(rows // 8):
                    part = jnp.concatenate(
                        [sum_ref[a, slot, 8 * g : 8 * g + 8, :], jnp.zeros((8, rows), jnp.float32)], axis=1
                    )
                    if g and 0 < slot < 4:
                        part = pltpu.roll(part, 2 * rows - 8 * g, 1)
                    total_sum = total_sum + part
                near_ref[0, a, slot] = total_sum


def attend_back(info, far, diag, q, g, full, kv, peak, rows, length):
    heads = far.shape[0]
    seqs = kv.shape[0]
    wide = 2 * (q.shape[1] // heads)
    pairs = heads // 2
    smem = pl.BlockSpec(memory_space=pltpu.SMEM)
    row_spec = pl.BlockSpec((rows, wide), lambda p, b: (b, p))
    return pl.pallas_call(
        functools.partial(attend_back_kernel, rows),
        grid=(pairs, seqs),
        in_specs=[
            smem,
            smem,
            pl.BlockSpec((1, 6, 2 * rows), lambda p, b: (p, 0, 0)),
            row_spec,
            row_spec,
            row_spec,
            pl.BlockSpec((1, length, wide), lambda p, b: (b, 0, 2 * p)),
            pl.BlockSpec((1, length, wide), lambda p, b: (b, 0, 2 * p + 1)),
            pl.BlockSpec((1, 1, 2, rows), lambda p, b: (b, p, 0, 0)),
        ],
        out_specs=[
            row_spec,
            pl.BlockSpec((1, length, 2 * wide), lambda p, b: (b, 0, p)),
            pl.BlockSpec((1, 2, 5, 8, 2 * rows), lambda p, b: (p, 0, 0, 0, 0)),
        ],
        out_shape=[
            jax.ShapeDtypeStruct(q.shape, jnp.bfloat16),
            jax.ShapeDtypeStruct(kv.shape, jnp.bfloat16),
            jax.ShapeDtypeStruct((pairs, 2, 5, 8, 2 * rows), jnp.float32),
        ],
        scratch_shapes=[
            pltpu.VMEM((2, 5, rows, rows), jnp.float32),
            pltpu.VMEM((2, 5, rows, rows), jnp.float32),
            pltpu.VMEM((2, wide, rows), jnp.float32),
        ],
        compiler_params=pltpu.CompilerParams(vmem_limit_bytes=48 << 20),
        cost_estimate=attention_cost(q, kv, 5),
        name="attend_back",
    )(info, far, diag, q, g, full, kv, kv, peak)


SLOTS = ("x", "c", "z", "y")
MESH = pl.DeviceIdType.MESH


def layout_of(batch, seq):
    fast = 1 << ((seq.bit_length() - 1) // 2)
    return {"x": batch // 2, "c": 2, "z": seq // fast, "y": fast}


def tile_block(rows, cols):
    return (rows, cols) if rows % 16 == 0 else (rows * cols // 128, 128)


def place(sizes):
    b, s = lax.axis_index("batch"), lax.axis_index("seq")
    return {
        "x": lax.div(b, 2),
        "c": lax.rem(b, 2),
        "z": lax.div(s, sizes["y"]),
        "y": lax.rem(s, sizes["y"]),
    }


def device_at(sizes, me, dim, at):
    spot = dict(me)
    spot[dim] = at
    return (spot["x"] * 2 + spot["c"], spot["z"] * sizes["y"] + spot["y"])


def seq_peer(sizes, me, k):
    n = sizes["z"] * sizes["y"]
    return (me["x"] * 2 + me["c"], lax.rem(me["z"] * sizes["y"] + me["y"] + k, n))


def greet(sizes, me, dims):
    barrier = pltpu.get_barrier_semaphore()
    total = 0
    if "s" in dims:
        total = sizes["z"] * sizes["y"] - 1
        for k in range(1, total + 1):
            pl.semaphore_signal(barrier, inc=1, device_id=seq_peer(sizes, me, k), device_id_type=MESH)
        dims = [d for d in dims if d not in "szy"]
    for dim in dims:
        for k in range(1, sizes[dim]):
            peer = device_at(sizes, me, dim, lax.rem(me[dim] + k, sizes[dim]))
            pl.semaphore_signal(barrier, inc=1, device_id=peer, device_id_type=MESH)
            total += 1
    pl.semaphore_wait(barrier, total)


class Sems:
    def __init__(self, send, recv):
        self.send, self.recv, self.used = send, recv, 0

    def take(self, count):
        first = self.used
        self.used += count
        return first

    def copy(self, src, dst, index, device):
        return pltpu.make_async_remote_copy(
            src_ref=src, dst_ref=dst, send_sem=self.send.at[index], recv_sem=self.recv.at[index],
            device_id=device, device_id_type=MESH,
        )


def run_together(tasks):
    tasks = list(tasks)
    while tasks:
        left = []
        for task in tasks:
            try:
                next(task)
                left.append(task)
            except StopIteration:
                pass
        tasks = left


def gather_task(sizes, me, src, out, local_sem, sems, order):
    dims = [d for d in SLOTS if d in order.lower()]
    own = pltpu.make_async_copy(src, out.at[tuple(me[d] for d in dims)], local_sem)
    own.start()
    own.wait()
    done = []
    sent = []
    for dim in order:
        direct, dim = dim.isupper(), dim.lower()
        n, at = sizes[dim], me[dim]

        def region(origin):
            spots = []
            for d in dims:
                spots.append(slice(None) if d in done else (origin if d == dim else me[d]))
            return out.at[tuple(spots)]

        if n == 2:
            base = sems.take(1)
            other = 1 - at
            send = sems.copy(region(at), region(at), base, device_at(sizes, me, dim, other))
            send.start()
            yield
            sems.copy(region(other), region(other), base, device_at(sizes, me, dim, other)).wait_recv()
            sent.append((None, send))
        elif direct:
            base = sems.take(n - 1)
            for k in range(1, n):
                peer = device_at(sizes, me, dim, lax.rem(at + k, n))
                send = sems.copy(region(at), region(at), base + k - 1, peer)
                send.start()
                sent.append((None, send))
            yield
            for k in range(1, n):
                origin = lax.rem(at + n - k, n)
                sems.copy(region(origin), region(origin), base + k - 1, device_at(sizes, me, dim, origin)).wait_recv()
        else:
            for t in range(n - 1):
                base = sems.take(2)
                to_right = (at + 1 < n) & (at - t >= 0)
                to_left = (at >= 1) & (at + t < n)
                from_left = (at >= 1) & (at - 1 - t >= 0)
                from_right = (at + 1 < n) & (at + 1 + t < n)
                right = sems.copy(region(at - t), region(at - t), base, device_at(sizes, me, dim, at + 1))
                left = sems.copy(region(at + t), region(at + t), base + 1, device_at(sizes, me, dim, at - 1))
                pl.when(to_right)(right.start)
                pl.when(to_left)(left.start)
                sent += [(to_right, right), (to_left, left)]
                yield
                got = sems.copy(region(at - 1 - t), region(at - 1 - t), base, device_at(sizes, me, dim, at - 1))
                pl.when(from_left)(got.wait_recv)
                got = sems.copy(region(at + 1 + t), region(at + 1 + t), base + 1, device_at(sizes, me, dim, at + 1))
                pl.when(from_right)(got.wait_recv)
        done.append(dim)
    for cond, send in sent:
        if cond is None:
            send.wait_send()
        else:
            pl.when(cond)(send.wait_send)


def spread_task(sizes, me, src, out, local_sem, sems):
    z, y, n, fast = me["z"], me["y"], sizes["z"], sizes["y"]
    own = pltpu.make_async_copy(src, out.at[:, z, y], local_sem)
    own.start()
    own.wait()
    fan = sems.take((fast - 1) * n)

    def fan_copy(k, origin, owner):
        peer = device_at(sizes, me, "y", lax.rem(y + k, fast))
        spot = out.at[:, origin, owner]
        return sems.copy(spot, spot, fan + (k - 1) * n + origin, peer)

    def fan_out(origin):
        for k in range(1, fast):
            fan_copy(k, origin, y).start()

    fan_out(z)
    sent = []
    for t in range(n - 1):
        base = sems.take(2)
        to_right = (z + 1 < n) & (z - t >= 0)
        to_left = (z >= 1) & (z + t < n)
        from_left = (z >= 1) & (z - 1 - t >= 0)
        from_right = (z + 1 < n) & (z + 1 + t < n)
        right = sems.copy(out.at[:, z - t, y], out.at[:, z - t, y], base, device_at(sizes, me, "z", z + 1))
        left = sems.copy(out.at[:, z + t, y], out.at[:, z + t, y], base + 1, device_at(sizes, me, "z", z - 1))
        pl.when(to_right)(right.start)
        pl.when(to_left)(left.start)
        sent += [(to_right, right), (to_left, left)]
        yield

        @pl.when(from_left)
        def _():
            spot = out.at[:, z - 1 - t, y]
            sems.copy(spot, spot, base, device_at(sizes, me, "z", z - 1)).wait_recv()
            fan_out(z - 1 - t)

        @pl.when(from_right)
        def _():
            spot = out.at[:, z + 1 + t, y]
            sems.copy(spot, spot, base + 1, device_at(sizes, me, "z", z + 1)).wait_recv()
            fan_out(z + 1 + t)

    yield
    for k in range(1, fast):
        for origin in range(n):
            fan_copy(k, origin, lax.rem(y + fast - k, fast)).wait_recv()
    for k in range(1, fast):
        for origin in range(n):
            fan_copy(k, origin, y).wait_send()
    for cond, send in sent:
        pl.when(cond)(send.wait_send)


def stage_count(sizes, order):
    return sum(1 if sizes[d] == 2 else 2 * (sizes[d] - 1) for d in order.lower())


def gather_kernel(sizes, orders, has_rows, *refs):
    count = len(orders)
    ins, outs = refs[: count + has_rows], refs[count + has_rows : 2 * (count + has_rows)]
    local_sem, send_sem, recv_sem = refs[2 * (count + has_rows) :]
    me = place(sizes)
    greet(sizes, me, [d for d in SLOTS if any(d in o.lower() for o in orders) or (has_rows and d in "zy")])
    sems = Sems(send_sem, recv_sem)
    tasks = []
    for i in range(count):
        tasks.append(gather_task(sizes, me, ins[i], outs[i], local_sem.at[i], sems, orders[i]))
    if has_rows:
        tasks.append(spread_task(sizes, me, ins[count], outs[count], local_sem.at[count], sems))
    run_together(tasks)


def gather_all(shards, orders, sizes, collective_id, rows=None, name="gather"):
    ins, shapes = [], []
    for shard, order in zip(shards, orders):
        ins.append(shard.reshape(tile_block(*shard.shape)))
        whole = tuple(sizes[d] for d in SLOTS if d in order.lower())
        shapes.append(jax.ShapeDtypeStruct(whole + ins[-1].shape, shard.dtype))
    total = sum(stage_count(sizes, o) for o in orders)
    if rows is not None:
        ins.append(rows)
        shapes.append(jax.ShapeDtypeStruct((rows.shape[0], sizes["z"], sizes["y"]) + rows.shape[1:], rows.dtype))
        total += (sizes["y"] - 1) * sizes["z"] + 2 * (sizes["z"] - 1)
    outs = pl.pallas_call(
        functools.partial(gather_kernel, sizes, orders, int(rows is not None)),
        in_specs=[pl.BlockSpec(memory_space=pltpu.VMEM)] * len(ins),
        out_specs=[pl.BlockSpec(memory_space=pl.ANY)] * len(ins),
        out_shape=shapes,
        scratch_shapes=[
            pltpu.SemaphoreType.DMA((len(ins),)),
            pltpu.SemaphoreType.DMA((total,)),
            pltpu.SemaphoreType.DMA((total,)),
        ],
        compiler_params=pltpu.CompilerParams(collective_id=collective_id, has_side_effects=True),
        name=name,
    )(*ins)
    full = [o if len(order) < 4 else o.reshape(-1, s.shape[1]) for o, s, order in zip(outs, shards, orders)]
    if rows is not None:
        full.append(outs[-1].reshape(rows.shape[0], -1, rows.shape[-1]))
    return full


def across(block, sizes, k):
    n = sizes["x"]
    pairs = [(((x + k) % n) * 2 + c, x * 2 + c) for x in range(n) for c in range(2)]
    return lax.ppermute(block, "batch", pairs)


def share_kernel(sizes, count, *refs):
    n = sizes["x"]
    ins, outs = refs[: count * n], refs[count * n : count * (n + 1)]
    local_sem, send_sem, recv_sem = refs[count * (n + 1) :]
    me = place(sizes)
    greet(sizes, me, ("c",))
    sems = Sems(send_sem, recv_sem)
    peer = device_at(sizes, me, "c", 1 - me["c"])
    sends, recvs, locals_ = [], [], []
    for i in range(count):
        for k in range(n):
            at = lax.rem(me["x"] + k, n)
            index = sems.take(1)
            send = sems.copy(ins[i * n + k], outs[i].at[at, me["c"]], index, peer)
            send.start()
            sends.append(send)
            recvs.append(sems.copy(ins[i * n + k], outs[i].at[at, 1 - me["c"]], index, peer))
            keep = pltpu.make_async_copy(ins[i * n + k], outs[i].at[at, me["c"]], local_sem.at[index])
            keep.start()
            locals_.append(keep)
    for keep, send, recv in zip(locals_, sends, recvs):
        keep.wait()
        recv.wait_recv()
        send.wait_send()


def share_cores(pieces, sizes, collective_id, columns, name="share"):
    n = sizes["x"]
    flat = [p for group in pieces for p in group]
    shapes = [jax.ShapeDtypeStruct((n, 2) + group[0].shape, group[0].dtype) for group in pieces]
    outs = pl.pallas_call(
        functools.partial(share_kernel, sizes, len(pieces)),
        in_specs=[pl.BlockSpec(memory_space=pltpu.VMEM)] * len(flat),
        out_specs=[pl.BlockSpec(memory_space=pl.ANY)] * len(pieces),
        out_shape=shapes,
        scratch_shapes=[pltpu.SemaphoreType.DMA((len(flat),))] * 3,
        compiler_params=pltpu.CompilerParams(collective_id=collective_id, has_side_effects=True),
        name=name,
    )(*flat)
    return [o.reshape(-1, c) for o, c in zip(outs, columns)]


def over(extents, body):
    total = 1
    for e in extents:
        total *= e
    if total == 1:
        body((0,) * len(extents))
        return

    def step(i, carry):
        spots = []
        for e in reversed(extents):
            spots.append(lax.rem(i, e))
            i = lax.div(i, e)
        body(tuple(reversed(spots)))
        return carry

    lax.fori_loop(0, total, step, 0)


def add_into(dst, src_of, extents):
    def body(spots):
        here = spots + (slice(None), slice(None))
        dst[here] = (dst[here].astype(jnp.float32) + src_of(spots).astype(jnp.float32)).astype(dst.dtype)

    over(extents, body)


def add_pair(out, first, second_of, extents):
    def body(spots):
        here = spots + (slice(None), slice(None))
        out[here] = (first[here].astype(jnp.float32) + second_of(spots).astype(jnp.float32)).astype(out.dtype)

    over(extents, body)


def reduce_task(sizes, me, src, out, bufs, sems, order, dims):
    remaining = list(dims)
    current = src
    sent = []
    for stage, dim in enumerate(order):
        if dim == "s":
            n = sizes["z"] * sizes["y"]
            base = sems.take(n)
            gathered = bufs[stage]
            s = me["z"] * sizes["y"] + me["y"]
            for k in range(1, n):
                to = lax.rem(s + k, n)
                send = sems.copy(
                    current.at[lax.div(to, sizes["y"]), lax.rem(to, sizes["y"])],
                    gathered.at[k],
                    base + k,
                    seq_peer(sizes, me, k),
                )
                send.start()
                sent.append((None, send))
            yield
            total = current[me["z"], me["y"]].astype(jnp.float32)
            for k in range(1, n):
                sems.copy(gathered.at[k], gathered.at[k], base + k, seq_peer(sizes, me, k)).wait_recv()
                total = total + gathered[k].astype(jnp.float32)
            out[...] = total
            continue
        n, at = sizes[dim], me[dim]
        spot = remaining.index(dim)
        after = remaining[:spot] + remaining[spot + 1 :]
        extents = [sizes[d] for d in after]
        last = stage == len(order) - 1
        source = current

        def block(j):
            return source.at[(slice(None),) * spot + (j,)]

        def values(j):
            return lambda spots: source[spots[:spot] + (j,) + spots[spot:] + (slice(None), slice(None))]

        if n == 2:
            buf = bufs[stage]
            base = sems.take(1)
            send = sems.copy(block(1 - at), buf, base, device_at(sizes, me, dim, 1 - at))
            send.start()
            sent.append((None, send))
            yield
            send.wait_recv()
            if last:
                add_pair(out, buf, values(at), extents)
            else:
                add_into(buf, values(at), extents)
            current = buf
        else:
            chains = bufs[stage][0]
            base = sems.take(2 * n)
            for slot in range(n - 1):
                for side in range(2):
                    lead = at if side == 0 else n - 1 - at
                    j = lax.rem((n - 1 - slot + at) if side == 0 else (slot + 1 + at + n), n)
                    buf = chains.at[side, j]
                    to = device_at(sizes, me, dim, at + 1 if side == 0 else at - 1)
                    index = base + side * n + j
                    plain = sems.copy(block(j), buf, index, to)
                    summed = sems.copy(buf, buf, index, to)
                    pl.when(lead == 0)(plain.start)

                    def pass_on(summed=summed, buf=buf, j=j):
                        summed.wait_recv()
                        add_into(buf, values(j), extents)
                        summed.start()

                    pl.when((lead > 0) & (lead <= slot))(pass_on)
                    sent.append((lead <= slot, summed))
                yield

            def arrived(side):
                buf = chains.at[side, at]
                sems.copy(buf, buf, base + side * n + at, device_at(sizes, me, dim, at)).wait_recv()

            result = out if last else bufs[stage][1]

            def start(spots):
                here = spots + (slice(None), slice(None))
                result[here] = values(at)(spots).astype(result.dtype)

            def add(side):
                add_into(result, lambda spots: chains[(side, at) + spots + (slice(None), slice(None))], extents)

            over(extents, start)

            @pl.when(at > 0)
            def _():
                arrived(0)
                add(0)

            @pl.when(at < n - 1)
            def _():
                arrived(1)
                add(1)

            current = result
        remaining = after
    for cond, send in sent:
        if cond is None:
            send.wait_send()
        else:
            pl.when(cond)(send.wait_send)


def total_task(sizes, me, src, out, bufs, sems):
    out[...] = src[...]
    taken = 0
    sent = []
    n = sizes["z"] * sizes["y"]
    stages = [[device_at(sizes, me, "c", 1 - me["c"])]]
    stages.append([device_at(sizes, me, "x", lax.rem(me["x"] + k, sizes["x"])) for k in range(1, sizes["x"])])
    stages.append([seq_peer(sizes, me, k) for k in range(1, n)])
    for stage, peers in enumerate(stages):
        first = taken
        stage_src = bufs.at[first]
        stage_src[...] = out[...]
        base = sems.take(len(peers) + 1)
        for k, peer in enumerate(peers):
            send = sems.copy(stage_src, bufs.at[first + 1 + k], base + k, peer)
            send.start()
            sent.append(send)
        taken += len(peers) + 1
        yield
        for k, peer in enumerate(peers):
            sems.copy(stage_src, bufs.at[first + 1 + k], base + k, peer).wait_recv()
            out[...] += bufs[first + 1 + k]
    for send in sent:
        send.wait_send()


def reduce_kernel(sizes, orders, dims, counts, collect, whole, *refs):
    count = len(orders)
    total = count + collect
    ports = total + whole
    ins, outs = refs[:ports], refs[ports : 2 * ports]
    send_sem, recv_sem = refs[-2:]
    bufs = list(refs[2 * ports : -2])
    me = place(sizes)
    used = [d for d in SLOTS if any(d in o for o in orders) or (collect and d in "zy")]
    greet(sizes, me, used + ["s"] * any("s" in o for o in orders))
    sems = Sems(send_sem, recv_sem)
    tasks = []
    if whole:
        tasks.append(total_task(sizes, me, ins[total], outs[total], bufs.pop(0), sems))
    if collect:
        ybuf, chain = bufs.pop(0), bufs.pop(0)
    for i in range(count):
        stages = []
        for size in counts[i]:
            taken = [bufs.pop(0) for _ in range(size)]
            dim = orders[i][len(stages)]
            stages.append(taken[0] if dim == "s" or sizes[dim] == 2 else taken)
        tasks.append(reduce_task(sizes, me, ins[i], outs[i], stages, sems, orders[i], dims[i]))
    if collect:
        tasks.append(collect_task(sizes, me, ins[count], outs[count], ybuf, chain, sems))
    run_together(tasks)


def reduce_all(grads, orders, sizes, collective_id, rows=None, summed=None, name="reduce"):
    ins, scratch, shapes, counts, all_dims = [], [], [], [], []
    total = 0
    if summed is not None:
        slots = sizes["x"] + sizes["z"] * sizes["y"] + 2
        scratch.append(pltpu.VMEM((slots,) + summed.shape, jnp.float32))
        total += slots
    if rows is not None:
        seqs, length, width = rows.shape
        n, fast = sizes["z"], sizes["y"]
        block = (seqs, length // (n * fast), width)
        scratch += [pltpu.VMEM((fast - 1, n) + block, rows.dtype), pltpu.VMEM((2, n) + block, rows.dtype)]
        total += seqs * ((fast - 1) * n + 2 * n)
    for grad, order in zip(grads, orders):
        dims = SLOTS[-(grad.ndim - 2) :] if grad.ndim > 2 else SLOTS
        if grad.ndim == 2:
            whole = tuple(sizes[d] for d in SLOTS)
            devices = whole[0] * whole[1] * whole[2] * whole[3]
            grad = grad.reshape(whole + tile_block(grad.shape[0] // devices, grad.shape[1]))
        block = grad.shape[-2:]
        ins.append(grad)
        all_dims.append(dims)
        left = [d for d in dims]
        taken = []
        for dim in order:
            taken.append(1)
            if dim == "s":
                left = []
                n = sizes["z"] * sizes["y"]
                scratch.append(pltpu.VMEM((n,) + block, grad.dtype))
                total += n
                continue
            left.remove(dim)
            shape = tuple(sizes[d] for d in left) + block
            n = sizes[dim]
            if n == 2:
                scratch.append(pltpu.VMEM(shape, grad.dtype))
                total += 1
            else:
                scratch.append(pltpu.VMEM((2, n) + shape, grad.dtype))
                total += 2 * n
                if dim != order[-1]:
                    scratch.append(pltpu.VMEM(shape, grad.dtype))
                    taken[-1] = 2
        counts.append(taken)
        shapes.append(jax.ShapeDtypeStruct(tuple(sizes[d] for d in left) + block, grad.dtype if left else jnp.float32))
    if rows is not None:
        ins.append(rows.reshape(seqs, sizes["z"], sizes["y"], -1, width))
        shapes.append(jax.ShapeDtypeStruct((seqs, length // (sizes["z"] * sizes["y"]), width), jnp.float32))
    if summed is not None:
        ins.append(summed)
        shapes.append(jax.ShapeDtypeStruct(summed.shape, jnp.float32))
    return pl.pallas_call(
        functools.partial(
            reduce_kernel, sizes, orders, all_dims, counts, int(rows is not None), int(summed is not None)
        ),
        in_specs=[pl.BlockSpec(memory_space=pltpu.VMEM)] * len(ins),
        out_specs=[pl.BlockSpec(memory_space=pltpu.VMEM)] * len(ins),
        out_shape=shapes,
        scratch_shapes=scratch + [pltpu.SemaphoreType.DMA((total,)), pltpu.SemaphoreType.DMA((total,))],
        compiler_params=pltpu.CompilerParams(
            collective_id=collective_id, has_side_effects=True, vmem_limit_bytes=56 << 20
        ),
        name=name,
    )(*ins)


def collect_task(sizes, me, src, out, ybuf, chain, sems):
    z, y, n, fast = me["z"], me["y"], sizes["z"], sizes["y"]
    pieces = out.shape[0]
    fan = sems.take(pieces * (fast - 1) * n)
    slots = []
    for slot in range(n - 1):
        for side in range(2):
            lead = z if side == 0 else n - 1 - z
            j = lax.rem((n - 1 - slot + z) if side == 0 else (slot + 1 + z + n), n)
            slots.append((lead, lead <= slot, side, j))

    def fan_copy(k, j, p):
        to = lax.rem(y + k, fast)
        index = fan + (p * (fast - 1) + k - 1) * n + j
        return sems.copy(src.at[p, j, to], ybuf.at[k - 1, j, p], index, device_at(sizes, me, "y", to))

    def fan_out(j, p):
        for k in range(1, fast):
            fan_copy(k, j, p).start()

    for slot in range(n - 1):
        for p in range(pieces):
            for lead, active, side, j in slots[2 * slot : 2 * slot + 2]:
                pl.when(active)(partial(fan_out, j, p))
    for p in range(pieces):
        fan_out(z, p)
    yield

    def merge(j, p):
        for k in range(1, fast):
            fan_copy(k, j, p).wait_recv()
        value = src[p, j, y].astype(jnp.float32)
        for k in range(1, fast):
            value = value + ybuf[k - 1, j, p].astype(jnp.float32)
        return value

    base = sems.take(2 * n * pieces)
    sent = []

    def chain_copy(side, j, p, to, plain=False):
        buf = chain.at[side, j, p]
        return sems.copy(
            ybuf.at[0, j, p] if plain else buf, buf, base + (p * 2 + side) * n + j, device_at(sizes, me, "z", to)
        )

    for slot in range(n - 1):
        for p in range(pieces):
            for lead, active, side, j in slots[2 * slot : 2 * slot + 2]:
                to = z + 1 if side == 0 else z - 1
                plain = chain_copy(side, j, p, to, True)
                summed = chain_copy(side, j, p, to)

                def begin(plain=plain, j=j, p=p):
                    ybuf[0, j, p] = merge(j, p).astype(ybuf.dtype)
                    plain.start()

                def pass_on(summed=summed, side=side, j=j, p=p):
                    value = merge(j, p)
                    summed.wait_recv()
                    chain[side, j, p] = (chain[side, j, p].astype(jnp.float32) + value).astype(chain.dtype)
                    summed.start()

                pl.when(lead == 0)(begin)
                pl.when((lead > 0) & active)(pass_on)
                sent.append((active, summed))
        yield
    for p in range(pieces):
        out[p] = merge(z, p)

        def finish(side, p=p):
            chain_copy(side, z, p, z).wait_recv()
            out[p] += chain[side, z, p].astype(jnp.float32)

        pl.when(z > 0)(partial(finish, 0))
        pl.when(z < n - 1)(partial(finish, 1))
    for j in range(n):
        for p in range(pieces):
            for k in range(1, fast):
                fan_copy(k, j, p).wait_send()
    for cond, send in sent:
        pl.when(cond)(send.wait_send)


def halve_kernel(sizes, count, *refs):
    n = sizes["x"]
    ins, outs = refs[:count], refs[count : count * (n + 1)]
    bufs = refs[count * (n + 1) : count * (n + 2)]
    send_sem, recv_sem = refs[-2:]
    me = place(sizes)
    greet(sizes, me, ("c",))
    sems = Sems(send_sem, recv_sem)
    c = me["c"]
    peer = device_at(sizes, me, "c", 1 - c)
    sends = {}
    for k in range(n - 1, -1, -1):
        at = lax.rem(me["x"] + k, n)
        for i in range(count):
            send = sems.copy(ins[i].at[at, 1 - c], bufs[i].at[k], sems.take(1), peer)
            send.start()
            sends[k, i] = send
    for k in range(n - 1, -1, -1):
        at = lax.rem(me["x"] + k, n)
        for i in range(count):
            sends[k, i].wait_recv()
            buf, src = bufs[i].at[k], ins[i]

            def own(spots, src=src, at=at):
                return src[(at, c) + spots + (slice(None), slice(None))]

            add_pair(outs[i * n + k], buf, own, src.shape[2:-2])
    for send in sends.values():
        send.wait_send()


def halve_cores(grads, sizes, collective_id, name="halve"):
    n = sizes["x"]
    whole = tuple(sizes[d] for d in SLOTS)
    devices = whole[0] * whole[1] * whole[2] * whole[3]
    ins = [g.reshape(whole + tile_block(g.shape[0] // devices, g.shape[1])) for g in grads]
    shapes = [jax.ShapeDtypeStruct(g.shape[2:], g.dtype) for g in ins for _ in range(n)]
    total = n * len(ins)
    outs = pl.pallas_call(
        functools.partial(halve_kernel, sizes, len(ins)),
        in_specs=[pl.BlockSpec(memory_space=pltpu.VMEM)] * len(ins),
        out_specs=[pl.BlockSpec(memory_space=pltpu.VMEM)] * len(shapes),
        out_shape=shapes,
        scratch_shapes=[pltpu.VMEM((n,) + g.shape[2:], g.dtype) for g in ins]
        + [pltpu.SemaphoreType.DMA((total,)), pltpu.SemaphoreType.DMA((total,))],
        compiler_params=pltpu.CompilerParams(
            collective_id=collective_id, has_side_effects=True, vmem_limit_bytes=56 << 20
        ),
        name=name,
    )(*ins)
    return [outs[i * n : (i + 1) * n] for i in range(len(ins))]


def from_others(pieces, sizes):
    return [across(pieces[sizes["x"] - k], sizes, k) for k in range(1, sizes["x"])]


def sum_blocks(blocks):
    total = blocks[0].astype(jnp.float32)
    for block in blocks[1:]:
        total = total + block.astype(jnp.float32)
    return total.astype(blocks[0].dtype)


def on_device(
    inputs,
    lengths,
    conv_taps,
    gain_attn,
    w_proj,
    w_query,
    w_key,
    w_value,
    w_out,
    gain_ffn,
    w_gate,
    w_up,
    w_down,
    rel_bias,
    cotangent,
):
    batch, seq = lax.axis_size("batch"), lax.axis_size("seq")
    sizes = layout_of(batch, seq)
    devices = batch * seq
    seqs, rows, width = inputs.shape
    length = rows * seq
    count = seqs * rows
    own = w_proj.shape[0]
    own_bias = rel_bias.shape[0]
    heads = own_bias * devices // NB
    hidden = w_gate.shape[1]

    small = jnp.concatenate(
        [
            conv_taps,
            gain_attn[:, None],
            gain_ffn[:, None],
            jnp.pad(rel_bias, (0, own - own_bias))[:, None],
            jnp.zeros((own, PACK - TAPS - 3), jnp.bfloat16),
        ],
        axis=1,
    )
    left_rim = from_behind(inputs[:, rows - 3 :, :], "seq", 1)
    pairs = heads // 2
    key_value_w = jnp.stack([w_key.reshape(own, pairs, -1), w_value.reshape(own, pairs, -1)], axis=2)
    first, second = gather_all(
        [jnp.concatenate([small, w_proj, w_query], axis=1), key_value_w.reshape(own, -1)],
        ["Zyxc", "Zxyc"],
        sizes,
        1,
        name="gather_first",
    )
    taps = first[:, :TAPS].astype(jnp.float32)
    gain_first = first[:, TAPS].astype(jnp.float32)
    gain_second = first[:, TAPS + 1].astype(jnp.float32)
    table = first[:, TAPS + 2].reshape(devices, own)[:, :own_bias].reshape(heads, NB).astype(jnp.float32)
    proj_w = first[:, PACK : PACK + width]
    query_w = first[:, PACK + width :]

    padded = jnp.concatenate([left_rim, inputs], axis=1).astype(jnp.float32)
    mixed_conv, conv_back = jax.vjp(partial(conv_mix, row_count=rows), padded, taps)
    mixed_low = mixed_conv.astype(jnp.bfloat16).reshape(count, width)
    resid_in = inputs.astype(jnp.float32).reshape(count, width)
    hidden_one = resid_in + mat_dot(mixed_low, proj_w)
    normed_one, norm_one_back = jax.vjp(norm_rows, hidden_one, gain_first)
    normed_low = normed_one.astype(jnp.bfloat16)

    outer_plane, down_plane, normed_all = gather_all(
        [jnp.concatenate([w_out, w_gate, w_up], axis=1), w_down],
        ["zy", "yz"],
        sizes,
        2,
        rows=normed_low.reshape(seqs, rows, width),
        name="gather_rows",
    )
    outer_pieces = [outer_plane] + [across(outer_plane, sizes, k) for k in range(1, sizes["x"])]
    down_pieces = [down_plane] + [across(down_plane, sizes, k) for k in range(1, sizes["x"])]
    normed_all = normed_all.reshape(seqs * length, width)
    queries = mat_dot(normed_low, query_w).astype(jnp.bfloat16)
    key_value = mat_dot(normed_all, second).astype(jnp.bfloat16).reshape(seqs, length, 2 * width)

    far, diag = bias_tables(table, rows)
    info = jnp.concatenate([lengths, lax.axis_index("seq")[None].astype(jnp.int32)])
    attended, attended_full, inverse, peak = attend(info, far, diag, queries, key_value, rows, length)
    outer_w, down_w = share_cores([outer_pieces, down_pieces], sizes, 3, [width + 2 * hidden, width])
    out_w = outer_w[:, :width]
    wide_w = outer_w[:, width:]

    hidden_two = hidden_one + mat_dot(attended, out_w)
    normed_two, norm_two_back = jax.vjp(norm_rows, hidden_two, gain_second)
    normed_two_low = normed_two.astype(jnp.bfloat16)
    both_pre = mat_dot(normed_two_low, wide_w)
    inner_act, inner_back = jax.vjp(gated, both_pre[:, :hidden], both_pre[:, hidden:])
    inner_low = inner_act.astype(jnp.bfloat16)
    layer_out = (hidden_two + mat_dot(inner_low, down_w)).astype(jnp.bfloat16).reshape(seqs, rows, width)

    grad_low = cotangent.reshape(count, width)
    d_down_w = outer_sum(inner_low, grad_low).astype(jnp.bfloat16)
    d_gate, d_up = inner_back(back_dot(grad_low, down_w))
    d_both = jnp.concatenate([d_gate.astype(jnp.bfloat16), d_up.astype(jnp.bfloat16)], axis=1)
    d_wide_w = outer_sum(normed_two_low, d_both).astype(jnp.bfloat16)
    d_hidden_part, d_gain_two = norm_two_back(back_dot(d_both, wide_w))
    d_hidden_two = grad_low.astype(jnp.float32) + d_hidden_part
    d_attn_low = d_hidden_two.astype(jnp.bfloat16)
    d_out_w = outer_sum(attended, d_attn_low).astype(jnp.bfloat16)
    d_attended = back_dot(d_attn_low, out_w).astype(jnp.bfloat16)
    scaled = (d_attended.astype(jnp.float32) * inverse).astype(jnp.bfloat16)
    wide_pieces, down_grads = halve_cores([d_wide_w, d_down_w], sizes, 4)
    scaled, wide_pieces, down_grads, d_out_w, layer_out = lax.optimization_barrier(
        (scaled, wide_pieces, down_grads, d_out_w, layer_out)
    )
    wide_others = from_others(wide_pieces, sizes)
    down_others = from_others(down_grads, sizes)
    d_queries, d_key_value, near = attend_back(
        info, far, diag, queries, scaled, attended_full, key_value, peak, rows, length
    )
    d_queries, d_key_value, near, wide_others, down_others = lax.optimization_barrier(
        (d_queries, d_key_value, near, wide_others, down_others)
    )
    wide_part = sum_blocks([wide_pieces[0]] + wide_others)
    down_part = sum_blocks([down_grads[0]] + down_others)
    d_table = bias_grad(near, rows).reshape(heads * NB)
    d_key_value = d_key_value.reshape(seqs * length, 2 * width)
    d_second_w = outer_sum(normed_all, d_key_value).astype(jnp.bfloat16)
    d_query_w = outer_sum(normed_low, d_queries).astype(jnp.bfloat16)
    d_rows = back_dot(d_key_value, second).astype(jnp.bfloat16)
    d_inner_w = jnp.concatenate([d_query_w, d_out_w, d_second_w], axis=1)
    g_wide, g_down, inner_part, d_normed_one = reduce_all(
        [wide_part, down_part, d_inner_w],
        ["zy", "zy", "cx"],
        sizes,
        5,
        rows=d_rows.reshape(seqs, length, width),
        name="collect",
    )
    d_normed_one = d_normed_one.reshape(count, width)
    d_normed_one = d_normed_one + back_dot(d_queries, query_w)
    d_first_part, d_gain_one = norm_one_back(d_normed_one)
    d_hidden_one = d_hidden_two + d_first_part
    d_mix_low = d_hidden_one.astype(jnp.bfloat16)
    d_proj_w = outer_sum(mixed_low, d_mix_low).astype(jnp.bfloat16)
    d_mixed = back_dot(d_mix_low, proj_w).reshape(seqs, rows, width)
    d_padded, d_taps = conv_back(d_mixed)
    spill_rows = from_behind(d_padded[:, :3, :], "seq", -1)
    d_inputs = d_hidden_one.reshape(seqs, rows, width) + d_padded[:, 3:, :]
    input_grad = d_inputs.at[:, rows - 3 :, :].add(spill_rows).astype(jnp.bfloat16)

    d_small = jnp.concatenate(
        [
            d_taps.T,
            d_gain_one[None],
            d_gain_two[None],
            jnp.pad(d_table, (0, width - heads * NB))[None],
            jnp.zeros((16 - TAPS - 3, width), jnp.float32),
        ],
        axis=0,
    )
    g_proj, g_inner, g_small = reduce_all([d_proj_w, inner_part], ["cxs", "s"], sizes, 6, summed=d_small)
    device = lax.axis_index("batch") * seq + lax.axis_index("seq")
    g_own = lax.dynamic_slice(g_small, (0, device * own), (16, own))
    g_table = lax.dynamic_slice(g_small[TAPS + 2], (device * own_bias,), (own_bias,))
    g_inner = g_inner.reshape(own, 4 * width)
    g_wide = g_wide.reshape(own, 2 * hidden)
    g_second = g_inner[:, 2 * width :].reshape(own, pairs, 2, -1)
    return (
        layer_out,
        input_grad,
        g_own[:TAPS].T,
        g_own[TAPS],
        g_proj.reshape(own, width),
        g_inner[:, :width],
        g_second[:, :, 0].reshape(own, width),
        g_second[:, :, 1].reshape(own, width),
        g_inner[:, width : 2 * width],
        g_own[TAPS + 1],
        g_wide[:, :hidden],
        g_wide[:, hidden:],
        g_down.reshape(w_down.shape),
        g_table,
    )


def solution(mesh):
    in_specs = (
        P("batch", "seq", None),
        P("batch"),
        P(("batch", "seq"), None),
        P(("batch", "seq")),
        P(("batch", "seq"), None),
        P(("batch", "seq"), None),
        P(("batch", "seq"), None),
        P(("batch", "seq"), None),
        P(("batch", "seq"), None),
        P(("batch", "seq")),
        P(("batch", "seq"), None),
        P(("batch", "seq"), None),
        P(("batch", "seq"), None),
        P(("batch", "seq")),
        P("batch", "seq", None),
    )
    out_specs = (
        P("batch", "seq", None),
        P("batch", "seq", None),
        P(("batch", "seq"), None),
        P(("batch", "seq")),
        P(("batch", "seq"), None),
        P(("batch", "seq"), None),
        P(("batch", "seq"), None),
        P(("batch", "seq"), None),
        P(("batch", "seq"), None),
        P(("batch", "seq")),
        P(("batch", "seq"), None),
        P(("batch", "seq"), None),
        P(("batch", "seq"), None),
        P(("batch", "seq")),
    )
    return jax.shard_map(
        on_device, mesh=mesh, in_specs=in_specs, out_specs=out_specs, check_vma=False
    )
```

```python
import functools
from functools import partial

import jax
import jax.numpy as jnp
import numpy as np
from jax import lax
from jax.experimental import pallas as pl
from jax.experimental.pallas import tpu as pltpu
from jax.sharding import PartitionSpec as P

NB = 32
EPSILON = 1e-06
LIMITS = (12, 16, 23, 32, 46, 64, 91)
WINDOWS = ((2, 0), (3, 2), (4, 5))
TAPS = 9
PACK = 128
SPAN = 8
SPANB = 8

def mat_dot(lhs_array, rhs_array):
    return jnp.dot(lhs_array, rhs_array, preferred_element_type=jnp.float32)


def outer_sum(lhs_array, rhs_array):
    return lax.dot_general(
        lhs_array, rhs_array, (((0,), (0,)), ((), ())), preferred_element_type=jnp.float32
    )


def back_dot(grad_rows, weight):
    return lax.dot_general(
        grad_rows, weight, (((1,), (1,)), ((), ())), preferred_element_type=jnp.float32
    )


def bucket_of(relative):
    distance = jnp.abs(relative)
    larger = jnp.full(relative.shape, 8, jnp.int32)
    for threshold in LIMITS:
        larger = larger + (distance >= threshold).astype(jnp.int32)
    inside = jnp.where(distance < 8, distance, larger)
    return inside + 16 * (relative > 0).astype(jnp.int32)


def norm_rows(hidden, gain_row):
    return (
        hidden * lax.rsqrt(jnp.mean(hidden * hidden, axis=-1, keepdims=True) + EPSILON) * gain_row
    )


def gated(gate_pre, up_pre):
    return jax.nn.gelu(gate_pre, approximate=True) * up_pre


def conv_mix(padded, taps, row_count):
    summed = jnp.zeros(padded.shape[:-2] + (row_count, padded.shape[-1]), jnp.float32)
    for window_len, offset in WINDOWS:
        conv_sum = jnp.zeros_like(summed)
        for tap_index in range(window_len):
            shifted = lax.slice_in_dim(
                padded, 3 - tap_index, 3 - tap_index + row_count, axis=padded.ndim - 2
            )
            conv_sum = conv_sum + taps[:, offset + tap_index] * shifted
        summed = summed + jax.nn.gelu(conv_sum, approximate=True)
    return summed


def near_offsets(rows):
    lane = np.arange(2 * rows)
    lane = np.where(lane < rows, lane, lane - 2 * rows)
    return rows * (np.arange(3)[:, None, None] - 1) + np.arange(8)[None, :, None] - lane[None, None, :]


def bias_tables(table, rows):
    heads = table.shape[0]
    buckets = bucket_of(jnp.asarray(near_offsets(rows)[:, 0, :], jnp.int32)).reshape(-1)
    onehot = (buckets[None, :] == jnp.arange(NB, dtype=jnp.int32)[:, None]).astype(jnp.float32)
    diag = jnp.dot(table, onehot, precision=lax.Precision.HIGHEST)
    far = jnp.stack([table[:, NB // 2 - 1], table[:, NB - 1]], axis=1)
    return far, diag.reshape(heads // 2, 6, 2 * rows)


def bias_grad(near, rows):
    near = near.reshape(near.shape[0] * 2, 5, 8, 2 * rows)
    buckets = bucket_of(jnp.asarray(near_offsets(rows), jnp.int32))
    hit = buckets[None] == jnp.arange(NB, dtype=jnp.int32)[:, None, None, None]
    grad = jnp.sum(jnp.where(hit[None], near[:, None, 1:4], 0.0), axis=(2, 3, 4))
    left = jnp.sum(near[:, 0], axis=(1, 2))
    right = jnp.sum(near[:, 4], axis=(1, 2))
    return grad.at[:, NB // 2 - 1].add(left).at[:, NB - 1].add(right)


def nt_dot(a, b):
    return lax.dot_general(a, b, (((1,), (1,)), ((), ())), preferred_element_type=jnp.float32)


def tn_dot(a, b):
    return lax.dot_general(a, b, (((0,), (0,)), ((), ())), preferred_element_type=jnp.float32)


def nn_dot(a, b):
    return lax.dot_general(a, b, (((1,), (0,)), ((), ())), preferred_element_type=jnp.float32)


def fill_bias(rows, far_ref, diag_ref, bias_ref, pair):
    for a in range(2):
        bias_ref[a, 0] = jnp.full((rows, rows), far_ref[2 * pair + a, 0], jnp.float32)
        bias_ref[a, 4] = jnp.full((rows, rows), far_ref[2 * pair + a, 1], jnp.float32)
        for c in range(3):
            base = jnp.broadcast_to(diag_ref[0, 3 * a + c : 3 * a + c + 1, :], (rows, 2 * rows))
            bias_ref[a, 1 + c] = pltpu.roll(base, 0, 1, stride=1, stride_axis=0)[:, :rows]


def head_halves(block):
    lane = lax.broadcasted_iota(jnp.int32, block.shape, 1)
    zero = jnp.zeros_like(block)
    half = block.shape[1] // 2
    return jnp.where(lane < half, block, zero), jnp.where(lane < half, zero, block)


def attend_kernel(
    rows, info_ref, far_ref, diag_ref, q_ref, k_ref, v_ref, o_ref, full_ref, inv_ref, peak_ref, bias_ref, s_ref, acc_ref
):
    pair, b = pl.program_id(0), pl.program_id(1)

    @pl.when(b == 0)
    def _():
        fill_bias(rows, far_ref, diag_ref, bias_ref, pair)

    length, first = info_ref[b], info_ref[pl.num_programs(1)]
    count = lax.div(length + rows - 1, rows)
    halves = head_halves(q_ref[...])
    wide = q_ref.shape[1]
    half = wide // 2
    key_row = lax.broadcasted_iota(jnp.int32, (rows, rows), 0)

    def scores(kc, peaks):
        k = k_ref[0, pl.ds(kc * rows, SPAN * rows), :]
        new = list(peaks)
        for a in range(2):
            full = nt_dot(k, halves[a])
            for u in range(SPAN):
                slot = jnp.clip(kc + u - first + 2, 0, 4)
                valid = key_row < length - (kc + u) * rows
                s = full[u * rows : (u + 1) * rows] + bias_ref[a, slot]
                s = jnp.where(valid, s, -1e9)
                s_ref[a, pl.ds((kc + u) * rows, rows), :] = s
                new[a] = jnp.maximum(new[a], jnp.max(s.reshape(rows // 8, 8, rows), axis=0))
        return tuple(new)

    low = jnp.full((8, rows), -jnp.inf, jnp.float32)
    spans = lax.div(count + SPAN - 1, SPAN)
    peaks = lax.fori_loop(0, spans, lambda i, p: scores(i * SPAN, p), (low, low))
    peaks = [jnp.max(p, axis=0, keepdims=True) for p in peaks]
    acc_ref[...] = jnp.zeros_like(acc_ref)
    lane = lax.broadcasted_iota(jnp.int32, (SPAN * rows, wide), 1)

    def weigh(i, carry):
        here = pl.ds(i * SPAN * rows, SPAN * rows)
        v = v_ref[0, here, :]
        ones = jnp.ones_like(v)
        for a, v_one in enumerate((jnp.where(lane < half, v, ones), jnp.where(lane < half, ones, v))):
            e = jnp.exp(s_ref[a, here, :] - peaks[a])
            acc_ref[a] += tn_dot(v_one, e.astype(jnp.bfloat16))
        return carry

    lax.fori_loop(0, spans, weigh, 0)
    inv = jnp.concatenate([1.0 / acc_ref[0, half:], 1.0 / acc_ref[1, :half]], axis=0)
    out = jnp.concatenate([acc_ref[0, :half], acc_ref[1, half:]], axis=0) * inv
    out = out.T
    o_ref[...] = out.astype(o_ref.dtype)
    full_ref[...] = out
    inv_ref[...] = inv.T
    for a in range(2):
        peak_ref[0, 0, a : a + 1, :] = peaks[a]


def attention_cost(q, kv, products):
    flops = products * 8 * q.shape[0] * kv.shape[1] * q.shape[1]
    return pl.CostEstimate(
        flops=flops, bytes_accessed=2 * (q.size + kv.size) * products, transcendentals=8 * q.shape[0] * kv.shape[1]
    )


def attend(info, far, diag, q, kv, rows, length):
    heads = far.shape[0]
    seqs = kv.shape[0]
    wide = 2 * (q.shape[1] // heads)
    pairs = heads // 2
    smem = pl.BlockSpec(memory_space=pltpu.SMEM)
    return pl.pallas_call(
        functools.partial(attend_kernel, rows),
        grid=(pairs, seqs),
        in_specs=[
            smem, smem,
            pl.BlockSpec((1, 6, 2 * rows), lambda p, b: (p, 0, 0)),
            pl.BlockSpec((rows, wide), lambda p, b: (b, p)),
            pl.BlockSpec((1, length, wide), lambda p, b: (b, 0, 2 * p)),
            pl.BlockSpec((1, length, wide), lambda p, b: (b, 0, 2 * p + 1)),
        ],
        out_specs=[pl.BlockSpec((rows, wide), lambda p, b: (b, p))] * 3
        + [pl.BlockSpec((1, 1, 2, rows), lambda p, b: (b, p, 0, 0))],
        out_shape=[
            jax.ShapeDtypeStruct(q.shape, jnp.bfloat16),
            jax.ShapeDtypeStruct(q.shape, jnp.float32),
            jax.ShapeDtypeStruct(q.shape, jnp.float32),
            jax.ShapeDtypeStruct((seqs, pairs, 2, rows), jnp.float32),
        ],
        scratch_shapes=[
            pltpu.VMEM((2, 5, rows, rows), jnp.float32),
            pltpu.VMEM((2, length, rows), jnp.float32),
            pltpu.VMEM((2, wide, rows), jnp.float32),
        ],
        compiler_params=pltpu.CompilerParams(vmem_limit_bytes=48 << 20),
        cost_estimate=attention_cost(q, kv, 2),
        name="attend",
    )(info, far, diag, q, kv, kv)


def attend_back_kernel(rows, info_ref, far_ref, diag_ref, q_ref, g_ref, full_ref, k_ref, v_ref, peak_ref,
                       dq_ref, dkv_ref, near_ref, bias_ref, sum_ref, acc_ref):
    pair, b = pl.program_id(0), pl.program_id(1)

    @pl.when(b == 0)
    def _():
        fill_bias(rows, far_ref, diag_ref, bias_ref, pair)
        sum_ref[...] = jnp.zeros_like(sum_ref)

    seqs = pl.num_programs(1)
    length, first = info_ref[b], info_ref[seqs]
    count = lax.div(length + rows - 1, rows)
    total = k_ref.shape[1] // rows
    q_half = head_halves(q_ref[...])
    g_half = head_halves(g_ref[...])
    wide = q_ref.shape[1]
    half = wide // 2
    key_row = lax.broadcasted_iota(jnp.int32, (rows, rows), 0)
    acc_ref[...] = jnp.zeros_like(acc_ref)
    peak = [peak_ref[0, 0, a : a + 1, :] for a in range(2)]
    along = (g_ref[...].astype(jnp.float32) * full_ref[...]).T
    delta = [jnp.sum(along[a * half : (a + 1) * half], axis=0, keepdims=True) for a in range(2)]

    def step(i, carry):
        kc = i * SPANB
        here = pl.ds(kc * rows, SPANB * rows)
        k = k_ref[0, here, :]
        v = v_ref[0, here, :]
        dk = dv = None
        for a in range(2):
            s = nt_dot(k, q_half[a])
            dp = nt_dot(v, g_half[a])
            es, dss = [], []
            for u in range(SPANB):
                part = slice(u * rows, (u + 1) * rows)
                slot = jnp.clip(kc + u - first + 2, 0, 4)
                valid = key_row < length - (kc + u) * rows
                e = jnp.exp(s[part] + bias_ref[a, slot] - peak[a])
                e_low = jnp.where(valid, e, 0.0).astype(jnp.bfloat16)
                ds = e_low.astype(jnp.float32) * (dp[part] - delta[a])
                sum_ref[a, slot] += ds
                es.append(e_low)
                dss.append(ds.astype(jnp.bfloat16))
            e_low, ds_low = jnp.concatenate(es, axis=0), jnp.concatenate(dss, axis=0)
            dv_a = nn_dot(e_low, g_half[a])
            dk_a = nn_dot(ds_low, q_half[a])
            dv = dv_a if dv is None else dv + dv_a
            dk = dk_a if dk is None else dk + dk_a
            acc_ref[a] += tn_dot(k, ds_low)
        dkv_ref[0, here, :wide] = dk.astype(dkv_ref.dtype)
        dkv_ref[0, here, wide:] = dv.astype(dkv_ref.dtype)
        return carry

    spans = lax.div(count + SPANB - 1, SPANB)
    lax.fori_loop(0, spans, step, 0)

    def blank(kc, carry):
        here = pl.ds(kc * rows, rows)
        dkv_ref[0, here, :] = jnp.zeros((rows, 2 * wide), dkv_ref.dtype)
        return carry

    lax.fori_loop(SPANB * spans, total, blank, 0)
    dq_ref[...] = jnp.concatenate([acc_ref[0, :half], acc_ref[1, half:]], axis=0).T.astype(dq_ref.dtype)

    @pl.when(b == seqs - 1)
    def _():
        for a in range(2):
            for slot in range(5):
                total_sum = jnp.zeros((8, 2 * rows), jnp.float32)
                for g in range(rows // 8):
                    part = jnp.concatenate(
                        [sum_ref[a, slot, 8 * g : 8 * g + 8, :], jnp.zeros((8, rows), jnp.float32)], axis=1
                    )
                    if g and 0 < slot < 4:
                        part = pltpu.roll(part, 2 * rows - 8 * g, 1)
                    total_sum = total_sum + part
                near_ref[0, a, slot] = total_sum


def attend_back(info, far, diag, q, g, full, kv, peak, rows, length):
    heads = far.shape[0]
    seqs = kv.shape[0]
    wide = 2 * (q.shape[1] // heads)
    pairs = heads // 2
    smem = pl.BlockSpec(memory_space=pltpu.SMEM)
    row_spec = pl.BlockSpec((rows, wide), lambda p, b: (b, p))
    return pl.pallas_call(
        functools.partial(attend_back_kernel, rows),
        grid=(pairs, seqs),
        in_specs=[
            smem,
            smem,
            pl.BlockSpec((1, 6, 2 * rows), lambda p, b: (p, 0, 0)),
            row_spec,
            row_spec,
            row_spec,
            pl.BlockSpec((1, length, wide), lambda p, b: (b, 0, 2 * p)),
            pl.BlockSpec((1, length, wide), lambda p, b: (b, 0, 2 * p + 1)),
            pl.BlockSpec((1, 1, 2, rows), lambda p, b: (b, p, 0, 0)),
        ],
        out_specs=[
            row_spec,
            pl.BlockSpec((1, length, 2 * wide), lambda p, b: (b, 0, p)),
            pl.BlockSpec((1, 2, 5, 8, 2 * rows), lambda p, b: (p, 0, 0, 0, 0)),
        ],
        out_shape=[
            jax.ShapeDtypeStruct(q.shape, jnp.bfloat16),
            jax.ShapeDtypeStruct(kv.shape, jnp.bfloat16),
            jax.ShapeDtypeStruct((pairs, 2, 5, 8, 2 * rows), jnp.float32),
        ],
        scratch_shapes=[
            pltpu.VMEM((2, 5, rows, rows), jnp.float32),
            pltpu.VMEM((2, 5, rows, rows), jnp.float32),
            pltpu.VMEM((2, wide, rows), jnp.float32),
        ],
        compiler_params=pltpu.CompilerParams(vmem_limit_bytes=48 << 20),
        cost_estimate=attention_cost(q, kv, 5),
        name="attend_back",
    )(info, far, diag, q, g, full, kv, kv, peak)


SLOTS = ("x", "c", "z", "y")
MESH = pl.DeviceIdType.MESH


def layout_of(batch, seq):
    fast = 1 << ((seq.bit_length() - 1) // 2)
    return {"x": batch // 2, "c": 2, "z": seq // fast, "y": fast}


def tile_block(rows, cols):
    return (rows, cols) if rows % 16 == 0 else (rows * cols // 128, 128)


def place(sizes):
    b, s = lax.axis_index("batch"), lax.axis_index("seq")
    return {
        "x": lax.div(b, 2),
        "c": lax.rem(b, 2),
        "z": lax.div(s, sizes["y"]),
        "y": lax.rem(s, sizes["y"]),
    }


def device_at(sizes, me, dim, at):
    spot = dict(me)
    spot[dim] = at
    return (spot["x"] * 2 + spot["c"], spot["z"] * sizes["y"] + spot["y"])


def seq_peer(sizes, me, k):
    n = sizes["z"] * sizes["y"]
    return (me["x"] * 2 + me["c"], lax.rem(me["z"] * sizes["y"] + me["y"] + k, n))


def greet(sizes, me, dims):
    barrier = pltpu.get_barrier_semaphore()
    total = 0
    if "s" in dims:
        total = sizes["z"] * sizes["y"] - 1
        for k in range(1, total + 1):
            pl.semaphore_signal(barrier, inc=1, device_id=seq_peer(sizes, me, k), device_id_type=MESH)
        dims = [d for d in dims if d not in "szy"]
    for dim in dims:
        for k in range(1, sizes[dim]):
            peer = device_at(sizes, me, dim, lax.rem(me[dim] + k, sizes[dim]))
            pl.semaphore_signal(barrier, inc=1, device_id=peer, device_id_type=MESH)
            total += 1
    pl.semaphore_wait(barrier, total)


class Sems:
    def __init__(self, send, recv):
        self.send, self.recv, self.used = send, recv, 0

    def take(self, count):
        first = self.used
        self.used += count
        assert self.used <= self.send.shape[0]
        return first

    def copy(self, src, dst, index, device):
        return pltpu.make_async_remote_copy(
            src_ref=src, dst_ref=dst, send_sem=self.send.at[index], recv_sem=self.recv.at[index],
            device_id=device, device_id_type=MESH,
        )


def run_together(tasks, plan=()):
    tasks = list(tasks)
    over_already = set()
    for i in plan:
        if i not in over_already:
            try:
                next(tasks[i])
            except StopIteration:
                over_already.add(i)
    tasks = [t for i, t in enumerate(tasks) if i not in over_already]
    while tasks:
        left = []
        for task in tasks:
            try:
                next(task)
                left.append(task)
            except StopIteration:
                pass
        tasks = left


def gather_task(sizes, me, src, out, local_sem, sems, order):
    before = list(SLOTS[len(SLOTS) - (len(src.shape) - 2) :])
    dims = [d for d in SLOTS if d in order.lower() or d in before]
    own = pltpu.make_async_copy(src, out.at[tuple(me[d] for d in dims if d not in before)], local_sem)
    own.start()
    own.wait()
    done = before
    sent = []
    for dim in order:
        direct, dim = dim.isupper(), dim.lower()
        n, at = sizes[dim], me[dim]

        def region(origin):
            spots = []
            for d in dims:
                spots.append(slice(None) if d in done else (origin if d == dim else me[d]))
            return out.at[tuple(spots)]

        if n == 2:
            base = sems.take(1)
            other = 1 - at
            send = sems.copy(region(at), region(at), base, device_at(sizes, me, dim, other))
            send.start()
            yield
            sems.copy(region(other), region(other), base, device_at(sizes, me, dim, other)).wait_recv()
            sent.append((None, send))
        elif direct:
            base = sems.take(n - 1)
            for k in range(1, n):
                peer = device_at(sizes, me, dim, lax.rem(at + k, n))
                send = sems.copy(region(at), region(at), base + k - 1, peer)
                send.start()
                sent.append((None, send))
            yield
            for k in range(1, n):
                origin = lax.rem(at + n - k, n)
                sems.copy(region(origin), region(origin), base + k - 1, device_at(sizes, me, dim, origin)).wait_recv()
        else:
            for t in range(n - 1):
                base = sems.take(2)
                to_right = (at + 1 < n) & (at - t >= 0)
                to_left = (at >= 1) & (at + t < n)
                from_left = (at >= 1) & (at - 1 - t >= 0)
                from_right = (at + 1 < n) & (at + 1 + t < n)
                right = sems.copy(region(at - t), region(at - t), base, device_at(sizes, me, dim, at + 1))
                left = sems.copy(region(at + t), region(at + t), base + 1, device_at(sizes, me, dim, at - 1))
                pl.when(to_right)(right.start)
                pl.when(to_left)(left.start)
                sent += [(to_right, right), (to_left, left)]
                yield
                got = sems.copy(region(at - 1 - t), region(at - 1 - t), base, device_at(sizes, me, dim, at - 1))
                pl.when(from_left)(got.wait_recv)
                got = sems.copy(region(at + 1 + t), region(at + 1 + t), base + 1, device_at(sizes, me, dim, at + 1))
                pl.when(from_right)(got.wait_recv)
        done.append(dim)
    for cond, send in sent:
        if cond is None:
            send.wait_send()
        else:
            pl.when(cond)(send.wait_send)


def spread_task(sizes, me, src, out, local_sem, sems):
    z, y, n, fast = me["z"], me["y"], sizes["z"], sizes["y"]
    own = pltpu.make_async_copy(src, out.at[:, z, y], local_sem)
    own.start()
    own.wait()
    fan = sems.take((fast - 1) * n)

    def fan_copy(k, origin, owner):
        peer = device_at(sizes, me, "y", lax.rem(y + k, fast))
        spot = out.at[:, origin, owner]
        return sems.copy(spot, spot, fan + (k - 1) * n + origin, peer)

    def fan_out(origin):
        for k in range(1, fast):
            fan_copy(k, origin, y).start()

    fan_out(z)
    sent = []
    for t in range(n - 1):
        base = sems.take(2)
        to_right = (z + 1 < n) & (z - t >= 0)
        to_left = (z >= 1) & (z + t < n)
        from_left = (z >= 1) & (z - 1 - t >= 0)
        from_right = (z + 1 < n) & (z + 1 + t < n)
        right = sems.copy(out.at[:, z - t, y], out.at[:, z - t, y], base, device_at(sizes, me, "z", z + 1))
        left = sems.copy(out.at[:, z + t, y], out.at[:, z + t, y], base + 1, device_at(sizes, me, "z", z - 1))
        pl.when(to_right)(right.start)
        pl.when(to_left)(left.start)
        sent += [(to_right, right), (to_left, left)]
        yield

        @pl.when(from_left)
        def _():
            spot = out.at[:, z - 1 - t, y]
            sems.copy(spot, spot, base, device_at(sizes, me, "z", z - 1)).wait_recv()
            fan_out(z - 1 - t)

        @pl.when(from_right)
        def _():
            spot = out.at[:, z + 1 + t, y]
            sems.copy(spot, spot, base + 1, device_at(sizes, me, "z", z + 1)).wait_recv()
            fan_out(z + 1 + t)

    yield
    for k in range(1, fast):
        for origin in range(n):
            fan_copy(k, origin, lax.rem(y + fast - k, fast)).wait_recv()
    for k in range(1, fast):
        for origin in range(n):
            fan_copy(k, origin, y).wait_send()
    for cond, send in sent:
        pl.when(cond)(send.wait_send)


def shift_task(sizes, me, src, out, sems, step):
    n = sizes["z"] * sizes["y"]
    s = me["z"] * sizes["y"] + me["y"]
    base = sems.take(1)
    send = sems.copy(src, out, base, seq_peer(sizes, me, step % n))
    has_to = (s < n - 1) if step > 0 else (s > 0)
    has_from = (s > 0) if step > 0 else (s < n - 1)
    pl.when(has_to)(send.start)
    yield
    pl.when(has_from)(send.wait_recv)

    @pl.when(jnp.logical_not(has_from))
    def _():
        out[...] = jnp.zeros_like(out)

    yield
    pl.when(has_to)(send.wait_send)


def stage_count(sizes, order):
    return sum(1 if sizes[d] == 2 else 2 * (sizes[d] - 1) for d in order.lower())


def gather_kernel(sizes, orders, has_rows, has_rim, plan, *refs):
    count = len(orders)
    total = count + has_rows + has_rim
    ins, outs = refs[:total], refs[total : 2 * total]
    local_sem, send_sem, recv_sem = refs[2 * total :]
    me = place(sizes)
    used = [d for d in SLOTS if any(d in o.lower() for o in orders) or (has_rows and d in "zy")]
    greet(sizes, me, used + ["s"] * has_rim)
    sems = Sems(send_sem, recv_sem)
    tasks = []
    for i in range(count):
        tasks.append(gather_task(sizes, me, ins[i], outs[i], local_sem.at[i], sems, orders[i]))
    if has_rows:
        tasks.append(spread_task(sizes, me, ins[count], outs[count], local_sem.at[count], sems))
    if has_rim:
        tasks.append(shift_task(sizes, me, ins[-1], outs[-1], sems, 1))
    run_together(tasks, plan)


def gather_all(shards, orders, sizes, collective_id, rows=None, rim=None, plan=(), name="gather"):
    ins, shapes, out_specs = [], [], []
    for shard, order in zip(shards, orders):
        ins.append(shard if shard.ndim > 2 else shard.reshape(tile_block(*shard.shape)))
        before = SLOTS[len(SLOTS) - (ins[-1].ndim - 2) :]
        whole = tuple(sizes[d] for d in SLOTS if d in order.lower() or d in before)
        shapes.append(jax.ShapeDtypeStruct(whole + ins[-1].shape[-2:], shard.dtype))
    total = sum(stage_count(sizes, o) for o in orders)
    out_specs = [pl.BlockSpec(memory_space=pl.ANY)] * len(ins)
    if rows is not None:
        ins.append(rows)
        shapes.append(jax.ShapeDtypeStruct((rows.shape[0], sizes["z"], sizes["y"]) + rows.shape[1:], rows.dtype))
        out_specs.append(pl.BlockSpec(memory_space=pl.ANY))
        total += (sizes["y"] - 1) * sizes["z"] + 2 * (sizes["z"] - 1)
    if rim is not None:
        ins.append(rim)
        shapes.append(jax.ShapeDtypeStruct(rim.shape, rim.dtype))
        out_specs.append(pl.BlockSpec(memory_space=pltpu.VMEM))
        total += 1
    return pl.pallas_call(
        functools.partial(gather_kernel, sizes, orders, int(rows is not None), int(rim is not None), plan),
        in_specs=[pl.BlockSpec(memory_space=pltpu.VMEM)] * len(ins),
        out_specs=out_specs,
        out_shape=shapes,
        scratch_shapes=[
            pltpu.SemaphoreType.DMA((len(ins),)),
            pltpu.SemaphoreType.DMA((total,)),
            pltpu.SemaphoreType.DMA((total,)),
        ],
        compiler_params=pltpu.CompilerParams(collective_id=collective_id, has_side_effects=True),
        name=name,
    )(*ins)


def across(block, sizes, k):
    n = sizes["x"]
    pairs = [(((x + k) % n) * 2 + c, x * 2 + c) for x in range(n) for c in range(2)]
    return lax.ppermute(block, "batch", pairs)


def over(extents, body):
    total = 1
    for e in extents:
        total *= e
    if total == 1:
        body((0,) * len(extents))
        return

    def step(i, carry):
        spots = []
        for e in reversed(extents):
            spots.append(lax.rem(i, e))
            i = lax.div(i, e)
        body(tuple(reversed(spots)))
        return carry

    lax.fori_loop(0, total, step, 0)


def add_into(dst, src_of, extents):
    def body(spots):
        here = spots + (slice(None), slice(None))
        dst[here] = (dst[here].astype(jnp.float32) + src_of(spots).astype(jnp.float32)).astype(dst.dtype)

    over(extents, body)


def add_pair(out, first, second_of, extents):
    def body(spots):
        here = spots + (slice(None), slice(None))
        out[here] = (first[here].astype(jnp.float32) + second_of(spots).astype(jnp.float32)).astype(out.dtype)

    over(extents, body)


def reduce_task(sizes, me, src, out, bufs, sems, order, dims):
    remaining = list(dims)
    current = src
    sent = []
    for stage, dim in enumerate(order):
        if dim == "s":
            n = sizes["z"] * sizes["y"]
            base = sems.take(n)
            gathered = bufs[stage]
            s = me["z"] * sizes["y"] + me["y"]
            for k in range(1, n):
                to = lax.rem(s + k, n)
                send = sems.copy(
                    current.at[lax.div(to, sizes["y"]), lax.rem(to, sizes["y"])],
                    gathered.at[k],
                    base + k,
                    seq_peer(sizes, me, k),
                )
                send.start()
                sent.append((None, send))
            yield
            total = current[me["z"], me["y"]].astype(jnp.float32)
            for k in range(1, n):
                sems.copy(gathered.at[k], gathered.at[k], base + k, seq_peer(sizes, me, k)).wait_recv()
                total = total + gathered[k].astype(jnp.float32)
            out[...] = total
            continue
        n, at = sizes[dim], me[dim]
        spot = remaining.index(dim)
        after = remaining[:spot] + remaining[spot + 1 :]
        extents = [sizes[d] for d in after]
        last = stage == len(order) - 1
        source = current

        def block(j):
            return source.at[(slice(None),) * spot + (j,)]

        def values(j):
            return lambda spots: source[spots[:spot] + (j,) + spots[spot:] + (slice(None), slice(None))]

        if n == 2:
            buf = bufs[stage]
            base = sems.take(1)
            send = sems.copy(block(1 - at), buf, base, device_at(sizes, me, dim, 1 - at))
            send.start()
            sent.append((None, send))
            yield
            send.wait_recv()
            if last:
                add_pair(out, buf, values(at), extents)
            else:
                add_into(buf, values(at), extents)
            current = buf
        else:
            chains = bufs[stage][0]
            base = sems.take(2 * n)
            for slot in range(n - 1):
                for side in range(2):
                    lead = at if side == 0 else n - 1 - at
                    j = lax.rem((n - 1 - slot + at) if side == 0 else (slot + 1 + at + n), n)
                    buf = chains.at[side, j]
                    to = device_at(sizes, me, dim, at + 1 if side == 0 else at - 1)
                    index = base + side * n + j
                    plain = sems.copy(block(j), buf, index, to)
                    summed = sems.copy(buf, buf, index, to)
                    pl.when(lead == 0)(plain.start)

                    def pass_on(summed=summed, buf=buf, j=j):
                        summed.wait_recv()
                        add_into(buf, values(j), extents)
                        summed.start()

                    pl.when((lead > 0) & (lead <= slot))(pass_on)
                    sent.append((lead <= slot, summed))
                yield

            def arrived(side):
                buf = chains.at[side, at]
                sems.copy(buf, buf, base + side * n + at, device_at(sizes, me, dim, at)).wait_recv()

            result = out if last else bufs[stage][1]

            def start(spots):
                here = spots + (slice(None), slice(None))
                result[here] = values(at)(spots).astype(result.dtype)

            def add(side):
                add_into(result, lambda spots: chains[(side, at) + spots + (slice(None), slice(None))], extents)

            over(extents, start)

            @pl.when(at > 0)
            def _():
                arrived(0)
                add(0)

            @pl.when(at < n - 1)
            def _():
                arrived(1)
                add(1)

            current = result
        remaining = after
    for cond, send in sent:
        if cond is None:
            send.wait_send()
        else:
            pl.when(cond)(send.wait_send)


class Split:
    def __init__(self, parts):
        self.parts = parts
        self.dtype = parts[0].dtype

    def __setitem__(self, here, value):
        first = 0
        for part in self.parts:
            last = first + part.shape[-1]
            part[here] = value[:, first:last]
            first = last

    def __getitem__(self, here):
        return jnp.concatenate([part[here] for part in self.parts], axis=1)


def reduce_kernel(sizes, orders, dims, counts, splits, collect, spill, *refs):
    count = len(orders)
    total = count + collect + spill
    ends = sum(splits) + collect + spill
    ins, outs = refs[:total], list(refs[total : total + ends])
    send_sem, recv_sem = refs[-2:]
    bufs = list(refs[total + ends : -2])
    me = place(sizes)
    used = [d for d in SLOTS if any(d in o for o in orders) or (collect and d in "zy")]
    greet(sizes, me, used + ["s"] * (spill or any("s" in o for o in orders)))
    sems = Sems(send_sem, recv_sem)
    tasks = []
    if collect:
        ybuf, chain = bufs.pop(0), bufs.pop(0)
    for i in range(count):
        stages = []
        for size in counts[i]:
            taken = [bufs.pop(0) for _ in range(size)]
            dim = orders[i][len(stages)]
            stages.append(taken[0] if dim == "s" or sizes[dim] == 2 else taken)
        parts = [outs.pop(0) for _ in range(splits[i])]
        out = parts[0] if len(parts) == 1 else Split(parts)
        tasks.append(reduce_task(sizes, me, ins[i], out, stages, sems, orders[i], dims[i]))
    if collect:
        tasks.append(collect_task(sizes, me, ins[count], outs.pop(0), ybuf, chain, sems))
    if spill:
        tasks.insert(0, shift_task(sizes, me, ins[-1], outs.pop(0), sems, -1))
    run_together(tasks)


def reduce_all(grads, orders, sizes, collective_id, rows=None, spill=None, splits=None, name="reduce"):
    ins, scratch, shapes, counts, all_dims, cuts, later = [], [], [], [], [], [], []
    splits = splits or [None] * len(grads)
    total = 0
    if rows is not None:
        seqs, length, width = rows.shape
        n, fast = sizes["z"], sizes["y"]
        block = (seqs, length // (n * fast), width)
        scratch += [pltpu.VMEM((fast - 1, n) + block, rows.dtype), pltpu.VMEM((2, n) + block, rows.dtype)]
        total += seqs * ((fast - 1) * n + 2 * n)
    devices = sizes["x"] * sizes["c"] * sizes["z"] * sizes["y"]
    for grad, order, widths in zip(grads, orders, splits):
        dims = SLOTS[-(grad.ndim - 2) :] if grad.ndim > 2 else SLOTS
        plain = True
        if grad.ndim == 2:
            whole = tuple(sizes[d] for d in SLOTS)
            final = (grad.shape[0] // devices, grad.shape[1])
            grad = grad.reshape(whole + tile_block(*final))
        block = grad.shape[-2:]
        ins.append(grad)
        all_dims.append(dims)
        left = [d for d in dims]
        taken = []
        for dim in order:
            taken.append(1)
            if dim == "s":
                left = []
                n = sizes["z"] * sizes["y"]
                scratch.append(pltpu.VMEM((n,) + block, grad.dtype))
                total += n
                continue
            left.remove(dim)
            shape = tuple(sizes[d] for d in left) + block
            n = sizes[dim]
            if n == 2:
                scratch.append(pltpu.VMEM(shape, grad.dtype))
                total += 1
            else:
                scratch.append(pltpu.VMEM((2, n) + shape, grad.dtype))
                total += 2 * n
                if dim != order[-1]:
                    scratch.append(pltpu.VMEM(shape, grad.dtype))
                    taken[-1] = 2
        counts.append(taken)
        if left or widths is None or sum(widths) != block[1]:
            shapes.append(
                jax.ShapeDtypeStruct(tuple(sizes[d] for d in left) + block, grad.dtype if left else jnp.float32)
            )
            cuts.append(1)
            later.append(widths)
        else:
            shapes += [jax.ShapeDtypeStruct((block[0], w), jnp.float32) for w in widths]
            cuts.append(len(widths))
            later.append(None)
    if rows is not None:
        ins.append(rows.reshape(seqs, sizes["z"], sizes["y"], -1, width))
        shapes.append(jax.ShapeDtypeStruct((seqs, length // (sizes["z"] * sizes["y"]), width), jnp.float32))
    if spill is not None:
        ins.append(spill)
        shapes.append(jax.ShapeDtypeStruct(spill.shape, spill.dtype))
        total += 1
    outs = pl.pallas_call(
        functools.partial(
            reduce_kernel, sizes, orders, all_dims, counts, cuts, int(rows is not None), int(spill is not None)
        ),
        in_specs=[pl.BlockSpec(memory_space=pltpu.VMEM)] * len(ins),
        out_specs=[pl.BlockSpec(memory_space=pltpu.VMEM)] * len(shapes),
        out_shape=shapes,
        scratch_shapes=scratch + [pltpu.SemaphoreType.DMA((total,)), pltpu.SemaphoreType.DMA((total,))],
        compiler_params=pltpu.CompilerParams(
            collective_id=collective_id, has_side_effects=True, vmem_limit_bytes=56 << 20
        ),
        name=name,
    )(*ins)
    outs = list(outs)
    results = []
    for cut, widths in zip(cuts, later):
        parts = [outs.pop(0) for _ in range(cut)]
        if widths is not None:
            full = parts[0].reshape(-1, sum(widths))
            edges = np.cumsum([0] + list(widths))
            parts = [full[:, int(lo) : int(hi)] for lo, hi in zip(edges[:-1], edges[1:])]
        results.append(parts)
    return results + outs


def collect_task(sizes, me, src, out, ybuf, chain, sems):
    z, y, n, fast = me["z"], me["y"], sizes["z"], sizes["y"]
    pieces = out.shape[0]
    fan = sems.take(pieces * (fast - 1) * n)
    slots = []
    for slot in range(n - 1):
        for side in range(2):
            lead = z if side == 0 else n - 1 - z
            j = lax.rem((n - 1 - slot + z) if side == 0 else (slot + 1 + z + n), n)
            slots.append((lead, lead <= slot, side, j))

    def fan_copy(k, j, p):
        to = lax.rem(y + k, fast)
        index = fan + (p * (fast - 1) + k - 1) * n + j
        return sems.copy(src.at[p, j, to], ybuf.at[k - 1, j, p], index, device_at(sizes, me, "y", to))

    def fan_out(j, p):
        for k in range(1, fast):
            fan_copy(k, j, p).start()

    for slot in range(n - 1):
        for p in range(pieces):
            for lead, active, side, j in slots[2 * slot : 2 * slot + 2]:
                pl.when(active)(partial(fan_out, j, p))
    for p in range(pieces):
        fan_out(z, p)
    yield

    def merge(j, p):
        for k in range(1, fast):
            fan_copy(k, j, p).wait_recv()
        value = src[p, j, y].astype(jnp.float32)
        for k in range(1, fast):
            value = value + ybuf[k - 1, j, p].astype(jnp.float32)
        return value

    base = sems.take(2 * n * pieces)
    sent = []

    def chain_copy(side, j, p, to, plain=False):
        buf = chain.at[side, j, p]
        return sems.copy(
            ybuf.at[0, j, p] if plain else buf, buf, base + (p * 2 + side) * n + j, device_at(sizes, me, "z", to)
        )

    for slot in range(n - 1):
        for p in range(pieces):
            for lead, active, side, j in slots[2 * slot : 2 * slot + 2]:
                to = z + 1 if side == 0 else z - 1
                plain = chain_copy(side, j, p, to, True)
                summed = chain_copy(side, j, p, to)

                def begin(plain=plain, j=j, p=p):
                    ybuf[0, j, p] = merge(j, p).astype(ybuf.dtype)
                    plain.start()

                def pass_on(summed=summed, side=side, j=j, p=p):
                    value = merge(j, p)
                    summed.wait_recv()
                    chain[side, j, p] = (chain[side, j, p].astype(jnp.float32) + value).astype(chain.dtype)
                    summed.start()

                pl.when(lead == 0)(begin)
                pl.when((lead > 0) & active)(pass_on)
                sent.append((active, summed))
        yield
    for p in range(pieces):
        out[p] = merge(z, p)

        def finish(side, p=p):
            chain_copy(side, z, p, z).wait_recv()
            out[p] += chain[side, z, p].astype(jnp.float32)

        pl.when(z > 0)(partial(finish, 0))
        pl.when(z < n - 1)(partial(finish, 1))
    for j in range(n):
        for p in range(pieces):
            for k in range(1, fast):
                fan_copy(k, j, p).wait_send()
    for cond, send in sent:
        pl.when(cond)(send.wait_send)


def halve_kernel(sizes, count, *refs):
    n = sizes["x"]
    ins, outs = refs[:count], refs[count : count * (n + 1)]
    bufs = refs[count * (n + 1) : count * (n + 2)]
    send_sem, recv_sem = refs[-2:]
    me = place(sizes)
    greet(sizes, me, ("c",))
    sems = Sems(send_sem, recv_sem)
    c = me["c"]
    peer = device_at(sizes, me, "c", 1 - c)
    sends = {}
    for k in range(n - 1, -1, -1):
        at = lax.rem(me["x"] + k, n)
        for i in range(count):
            send = sems.copy(ins[i].at[at, 1 - c], bufs[i].at[k], sems.take(1), peer)
            send.start()
            sends[k, i] = send
    for k in range(n - 1, -1, -1):
        at = lax.rem(me["x"] + k, n)
        for i in range(count):
            sends[k, i].wait_recv()
            buf, src = bufs[i].at[k], ins[i]

            def own(spots, src=src, at=at):
                return src[(at, c) + spots + (slice(None), slice(None))]

            add_pair(outs[i * n + k], buf, own, src.shape[2:-2])
    for send in sends.values():
        send.wait_send()


def halve_cores(grads, sizes, collective_id, name="halve"):
    n = sizes["x"]
    whole = tuple(sizes[d] for d in SLOTS)
    devices = whole[0] * whole[1] * whole[2] * whole[3]
    ins = [g.reshape(whole + tile_block(g.shape[0] // devices, g.shape[1])) for g in grads]
    shapes = [jax.ShapeDtypeStruct(g.shape[2:], g.dtype) for g in ins for _ in range(n)]
    total = n * len(ins)
    outs = pl.pallas_call(
        functools.partial(halve_kernel, sizes, len(ins)),
        in_specs=[pl.BlockSpec(memory_space=pltpu.VMEM)] * len(ins),
        out_specs=[pl.BlockSpec(memory_space=pltpu.VMEM)] * len(shapes),
        out_shape=shapes,
        scratch_shapes=[pltpu.VMEM((n,) + g.shape[2:], g.dtype) for g in ins]
        + [pltpu.SemaphoreType.DMA((total,)), pltpu.SemaphoreType.DMA((total,))],
        compiler_params=pltpu.CompilerParams(
            collective_id=collective_id, has_side_effects=True, vmem_limit_bytes=56 << 20
        ),
        name=name,
    )(*ins)
    return [outs[i * n : (i + 1) * n] for i in range(len(ins))]


def from_others(pieces, sizes):
    return [across(pieces[sizes["x"] - k], sizes, k) for k in range(1, sizes["x"])]


def sum_blocks(blocks):
    total = blocks[0].astype(jnp.float32)
    for block in blocks[1:]:
        total = total + block.astype(jnp.float32)
    return total.astype(blocks[0].dtype)


def on_device(
    inputs,
    lengths,
    conv_taps,
    gain_attn,
    w_proj,
    w_query,
    w_key,
    w_value,
    w_out,
    gain_ffn,
    w_gate,
    w_up,
    w_down,
    rel_bias,
    cotangent,
):
    batch, seq = lax.axis_size("batch"), lax.axis_size("seq")
    sizes = layout_of(batch, seq)
    devices = batch * seq
    seqs, rows, width = inputs.shape
    length = rows * seq
    count = seqs * rows
    own = w_proj.shape[0]
    own_bias = rel_bias.shape[0]
    heads = own_bias * devices // NB
    hidden = w_gate.shape[1]

    small = jnp.concatenate(
        [
            conv_taps,
            gain_attn[:, None],
            gain_ffn[:, None],
            jnp.pad(rel_bias, (0, own - own_bias))[:, None],
            jnp.zeros((own, PACK - TAPS - 3), jnp.bfloat16),
        ],
        axis=1,
    )
    pairs = heads // 2
    key_value_w = jnp.stack([w_key.reshape(own, pairs, -1), w_value.reshape(own, pairs, -1)], axis=2)
    first, second, outer_plane, down_plane, left_rim = gather_all(
        [
            jnp.concatenate([small, w_proj, w_query], axis=1),
            key_value_w.reshape(own, -1),
            jnp.concatenate([w_out, w_gate, w_up], axis=1),
            w_down,
        ],
        ["Zyxc", "Zxyc", "zy", "yz"],
        sizes,
        1,
        rim=inputs[:, rows - 16 :, :],
        name="gather_first",
    )
    first = first.reshape(width, -1)
    second = second.reshape(width, -1)
    taps = first[:, :TAPS].astype(jnp.float32)
    gain_first = first[:, TAPS].astype(jnp.float32)
    gain_second = first[:, TAPS + 1].astype(jnp.float32)
    table = first[:, TAPS + 2].reshape(devices, own)[:, :own_bias].reshape(heads, NB).astype(jnp.float32)
    proj_w = first[:, PACK : PACK + width]
    query_w = first[:, PACK + width :]

    padded = jnp.concatenate([left_rim[:, 13:], inputs], axis=1).astype(jnp.float32)
    mixed_conv, conv_back = jax.vjp(partial(conv_mix, row_count=rows), padded, taps)
    mixed_low = mixed_conv.astype(jnp.bfloat16).reshape(count, width)
    resid_in = inputs.astype(jnp.float32).reshape(count, width)
    hidden_one = resid_in + mat_dot(mixed_low, proj_w)
    normed_one, norm_one_back = jax.vjp(norm_rows, hidden_one, gain_first)
    normed_low = normed_one.astype(jnp.bfloat16)

    outer_w, down_w, normed_all = gather_all(
        [outer_plane, down_plane],
        ["xc", "xc"],
        sizes,
        2,
        rows=normed_low.reshape(seqs, rows, width),
        plan=(0, 1, 2, 2, 2, 2),
        name="gather_rows",
    )
    outer_w = outer_w.reshape(width, -1)
    down_w = down_w.reshape(hidden, -1)
    out_w = outer_w[:, :width]
    wide_w = outer_w[:, width:]
    normed_all = normed_all.reshape(seqs * length, width)
    queries = mat_dot(normed_low, query_w).astype(jnp.bfloat16)
    key_value = mat_dot(normed_all, second).astype(jnp.bfloat16).reshape(seqs, length, 2 * width)

    far, diag = bias_tables(table, rows)
    info = jnp.concatenate([lengths, lax.axis_index("seq")[None].astype(jnp.int32)])
    attended, attended_full, inverse, peak = attend(info, far, diag, queries, key_value, rows, length)

    hidden_two = hidden_one + mat_dot(attended, out_w)
    normed_two, norm_two_back = jax.vjp(norm_rows, hidden_two, gain_second)
    normed_two_low = normed_two.astype(jnp.bfloat16)
    both_pre = mat_dot(normed_two_low, wide_w)
    inner_act, inner_back = jax.vjp(gated, both_pre[:, :hidden], both_pre[:, hidden:])
    inner_low = inner_act.astype(jnp.bfloat16)
    layer_out = (hidden_two + mat_dot(inner_low, down_w)).astype(jnp.bfloat16).reshape(seqs, rows, width)

    grad_low = cotangent.reshape(count, width)
    d_down_w = outer_sum(inner_low, grad_low).astype(jnp.bfloat16)
    d_gate, d_up = inner_back(back_dot(grad_low, down_w))
    d_both = jnp.concatenate([d_gate.astype(jnp.bfloat16), d_up.astype(jnp.bfloat16)], axis=1)
    d_wide_w = outer_sum(normed_two_low, d_both).astype(jnp.bfloat16)
    d_hidden_part, d_gain_two = norm_two_back(back_dot(d_both, wide_w))
    d_hidden_two = grad_low.astype(jnp.float32) + d_hidden_part
    d_attn_low = d_hidden_two.astype(jnp.bfloat16)
    d_out_w = outer_sum(attended, d_attn_low).astype(jnp.bfloat16)
    d_attended = back_dot(d_attn_low, out_w).astype(jnp.bfloat16)
    scaled = (d_attended.astype(jnp.float32) * inverse).astype(jnp.bfloat16)
    wide_pieces, down_grads = halve_cores([d_wide_w, d_down_w], sizes, 4)
    scaled, wide_pieces, down_grads, d_out_w, layer_out = lax.optimization_barrier(
        (scaled, wide_pieces, down_grads, d_out_w, layer_out)
    )
    wide_others = from_others(wide_pieces, sizes)
    down_others = from_others(down_grads, sizes)
    d_queries, d_key_value, near = attend_back(
        info, far, diag, queries, scaled, attended_full, key_value, peak, rows, length
    )
    d_queries, d_key_value, near, wide_others, down_others = lax.optimization_barrier(
        (d_queries, d_key_value, near, wide_others, down_others)
    )
    wide_part = sum_blocks([wide_pieces[0]] + wide_others)
    down_part = sum_blocks([down_grads[0]] + down_others)
    d_table = bias_grad(near, rows).reshape(heads * NB)
    d_key_value = d_key_value.reshape(seqs * length, 2 * width)
    d_second_w = outer_sum(normed_all, d_key_value).astype(jnp.bfloat16)
    d_query_w = outer_sum(normed_low, d_queries).astype(jnp.bfloat16)
    d_rows = back_dot(d_key_value, second).astype(jnp.bfloat16)
    d_inner_w = jnp.concatenate([d_query_w, d_out_w, d_second_w], axis=1)
    (g_gate, g_up), (g_down,), (inner_part,), d_normed_one = reduce_all(
        [wide_part, down_part, d_inner_w],
        ["zy", "zy", "cx"],
        sizes,
        5,
        rows=d_rows.reshape(seqs, length, width),
        splits=[(hidden, hidden), None, None],
        name="collect",
    )
    d_normed_one = d_normed_one.reshape(count, width)
    d_normed_one = d_normed_one + back_dot(d_queries, query_w)
    d_first_part, d_gain_one = norm_one_back(d_normed_one)
    d_hidden_one = d_hidden_two + d_first_part
    d_mix_low = d_hidden_one.astype(jnp.bfloat16)
    d_proj_w = outer_sum(mixed_low, d_mix_low).astype(jnp.bfloat16)
    d_mixed = back_dot(d_mix_low, proj_w).reshape(seqs, rows, width)
    d_padded, d_taps = conv_back(d_mixed)
    d_inputs = d_hidden_one.reshape(seqs, rows, width) + d_padded[:, 3:, :]
    d_small = jnp.concatenate(
        [
            d_taps.T,
            d_gain_one[None],
            d_gain_two[None],
            jnp.pad(d_table.reshape(devices, own_bias), ((0, 0), (0, own - own_bias))).reshape(1, width),
            jnp.zeros((16 - TAPS - 3, width), jnp.float32),
        ],
        axis=0,
    )
    d_last = jnp.concatenate([d_proj_w, jnp.pad(d_small.T, ((0, 0), (0, PACK - 16))).astype(jnp.bfloat16)], axis=1)
    (g_proj, g_small), (g_query, g_out, g_second), spill = reduce_all(
        [d_last, inner_part],
        ["cxs", "s"],
        sizes,
        6,
        spill=d_padded[:, :8, :],
        splits=[(width, PACK), (width, width, 2 * width)],
    )
    input_grad = d_inputs.at[:, rows - 3 :, :].add(spill[:, :3]).astype(jnp.bfloat16)
    g_second = g_second.reshape(own, pairs, 2, -1)
    return (
        layer_out,
        input_grad,
        g_small[:, :TAPS],
        g_small[:, TAPS],
        g_proj,
        g_query,
        g_second[:, :, 0].reshape(own, width),
        g_second[:, :, 1].reshape(own, width),
        g_out,
        g_small[:, TAPS + 1],
        g_gate,
        g_up,
        g_down.reshape(w_down.shape),
        g_small[:own_bias, TAPS + 2],
    )


def solution(mesh):
    in_specs = (
        P("batch", "seq", None),
        P("batch"),
        P(("batch", "seq"), None),
        P(("batch", "seq")),
        P(("batch", "seq"), None),
        P(("batch", "seq"), None),
        P(("batch", "seq"), None),
        P(("batch", "seq"), None),
        P(("batch", "seq"), None),
        P(("batch", "seq")),
        P(("batch", "seq"), None),
        P(("batch", "seq"), None),
        P(("batch", "seq"), None),
        P(("batch", "seq")),
        P("batch", "seq", None),
    )
    out_specs = (
        P("batch", "seq", None),
        P("batch", "seq", None),
        P(("batch", "seq"), None),
        P(("batch", "seq")),
        P(("batch", "seq"), None),
        P(("batch", "seq"), None),
        P(("batch", "seq"), None),
        P(("batch", "seq"), None),
        P(("batch", "seq"), None),
        P(("batch", "seq")),
        P(("batch", "seq"), None),
        P(("batch", "seq"), None),
        P(("batch", "seq"), None),
        P(("batch", "seq")),
    )
    return jax.shard_map(
        on_device, mesh=mesh, in_specs=in_specs, out_specs=out_specs, check_vma=False
    )
```

```python
import functools
from functools import partial

import jax
import jax.numpy as jnp
import numpy as np
from jax import lax
from jax.experimental import pallas as pl
from jax.experimental.pallas import tpu as pltpu
from jax.sharding import PartitionSpec as P

NB = 32
EPSILON = 1e-06
LIMITS = (12, 16, 23, 32, 46, 64, 91)
WINDOWS = ((2, 0), (3, 2), (4, 5))
TAPS = 9
PACK = 128
SPAN = 8

def mat_dot(lhs_array, rhs_array):
    return jnp.dot(lhs_array, rhs_array, preferred_element_type=jnp.float32)


def outer_sum(lhs_array, rhs_array):
    return lax.dot_general(
        lhs_array, rhs_array, (((0,), (0,)), ((), ())), preferred_element_type=jnp.float32
    )


def back_dot(grad_rows, weight):
    return lax.dot_general(
        grad_rows, weight, (((1,), (1,)), ((), ())), preferred_element_type=jnp.float32
    )


def bucket_of(relative):
    distance = jnp.abs(relative)
    larger = jnp.full(relative.shape, 8, jnp.int32)
    for threshold in LIMITS:
        larger = larger + (distance >= threshold).astype(jnp.int32)
    inside = jnp.where(distance < 8, distance, larger)
    return inside + 16 * (relative > 0).astype(jnp.int32)


def norm_rows(hidden, gain_row):
    return (
        hidden * lax.rsqrt(jnp.mean(hidden * hidden, axis=-1, keepdims=True) + EPSILON) * gain_row
    )


def gated(gate_pre, up_pre):
    return jax.nn.gelu(gate_pre, approximate=True) * up_pre


def conv_mix(padded, taps, row_count):
    summed = jnp.zeros(padded.shape[:-2] + (row_count, padded.shape[-1]), jnp.float32)
    for window_len, offset in WINDOWS:
        conv_sum = jnp.zeros_like(summed)
        for tap_index in range(window_len):
            shifted = lax.slice_in_dim(
                padded, 3 - tap_index, 3 - tap_index + row_count, axis=padded.ndim - 2
            )
            conv_sum = conv_sum + taps[:, offset + tap_index] * shifted
        summed = summed + jax.nn.gelu(conv_sum, approximate=True)
    return summed


def near_offsets(rows):
    lane = np.arange(2 * rows)
    lane = np.where(lane < rows, lane, lane - 2 * rows)
    return rows * (np.arange(3)[:, None, None] - 1) + np.arange(8)[None, :, None] - lane[None, None, :]


def bias_tables(table, rows):
    heads = table.shape[0]
    buckets = bucket_of(jnp.asarray(near_offsets(rows)[:, 0, :], jnp.int32)).reshape(-1)
    onehot = (buckets[None, :] == jnp.arange(NB, dtype=jnp.int32)[:, None]).astype(jnp.float32)
    diag = jnp.dot(table, onehot, precision=lax.Precision.HIGHEST)
    far = jnp.stack([table[:, NB // 2 - 1], table[:, NB - 1]], axis=1)
    return far, diag.reshape(heads // 2, 6, 2 * rows)


def bias_grad(near, rows):
    near = near.reshape(near.shape[0] * 2, 5, 8, 2 * rows)
    buckets = bucket_of(jnp.asarray(near_offsets(rows), jnp.int32))
    hit = buckets[None] == jnp.arange(NB, dtype=jnp.int32)[:, None, None, None]
    grad = jnp.sum(jnp.where(hit[None], near[:, None, 1:4], 0.0), axis=(2, 3, 4))
    left = jnp.sum(near[:, 0], axis=(1, 2))
    right = jnp.sum(near[:, 4], axis=(1, 2))
    return grad.at[:, NB // 2 - 1].add(left).at[:, NB - 1].add(right)


def nt_dot(a, b):
    return lax.dot_general(a, b, (((1,), (1,)), ((), ())), preferred_element_type=jnp.float32)


def tn_dot(a, b):
    return lax.dot_general(a, b, (((0,), (0,)), ((), ())), preferred_element_type=jnp.float32)


def nn_dot(a, b):
    return lax.dot_general(a, b, (((1,), (0,)), ((), ())), preferred_element_type=jnp.float32)


def fill_bias(rows, far_ref, diag_ref, bias_ref, pair):
    for a in range(2):
        bias_ref[a, 0] = jnp.full((rows, rows), far_ref[2 * pair + a, 0], jnp.float32)
        bias_ref[a, 4] = jnp.full((rows, rows), far_ref[2 * pair + a, 1], jnp.float32)
        for c in range(3):
            base = jnp.broadcast_to(diag_ref[0, 3 * a + c : 3 * a + c + 1, :], (rows, 2 * rows))
            bias_ref[a, 1 + c] = pltpu.roll(base, 0, 1, stride=1, stride_axis=0)[:, :rows]


def head_halves(block):
    lane = lax.broadcasted_iota(jnp.int32, block.shape, 1)
    zero = jnp.zeros_like(block)
    half = block.shape[1] // 2
    return jnp.where(lane < half, block, zero), jnp.where(lane < half, zero, block)


def attend_kernel(
    rows, info_ref, far_ref, diag_ref, q_ref, k_ref, v_ref, o_ref, full_ref, inv_ref, peak_ref, bias_ref, s_ref, acc_ref
):
    pair, b = pl.program_id(0), pl.program_id(1)

    @pl.when(b == 0)
    def _():
        fill_bias(rows, far_ref, diag_ref, bias_ref, pair)

    length, first = info_ref[b], info_ref[pl.num_programs(1)]
    count = lax.div(length + rows - 1, rows)
    halves = head_halves(q_ref[...])
    wide = q_ref.shape[1]
    half = wide // 2
    key_row = lax.broadcasted_iota(jnp.int32, (rows, rows), 0)

    def scores(kc, peaks):
        k = k_ref[0, pl.ds(kc * rows, SPAN * rows), :]
        new = list(peaks)
        for a in range(2):
            full = nt_dot(k, halves[a])
            for u in range(SPAN):
                slot = jnp.clip(kc + u - first + 2, 0, 4)
                valid = key_row < length - (kc + u) * rows
                s = full[u * rows : (u + 1) * rows] + bias_ref[a, slot]
                s = jnp.where(valid, s, -1e9)
                s_ref[a, pl.ds((kc + u) * rows, rows), :] = s
                new[a] = jnp.maximum(new[a], jnp.max(s.reshape(rows // 8, 8, rows), axis=0))
        return tuple(new)

    low = jnp.full((8, rows), -jnp.inf, jnp.float32)
    spans = lax.div(count + SPAN - 1, SPAN)
    peaks = lax.fori_loop(0, spans, lambda i, p: scores(i * SPAN, p), (low, low))
    peaks = [jnp.max(p, axis=0, keepdims=True) for p in peaks]
    acc_ref[...] = jnp.zeros_like(acc_ref)
    lane = lax.broadcasted_iota(jnp.int32, (SPAN * rows, wide), 1)

    def weigh(i, carry):
        here = pl.ds(i * SPAN * rows, SPAN * rows)
        v = v_ref[0, here, :]
        ones = jnp.ones_like(v)
        for a, v_one in enumerate((jnp.where(lane < half, v, ones), jnp.where(lane < half, ones, v))):
            e = jnp.exp(s_ref[a, here, :] - peaks[a])
            acc_ref[a] += tn_dot(v_one, e.astype(jnp.bfloat16))
        return carry

    lax.fori_loop(0, spans, weigh, 0)
    inv = jnp.concatenate([1.0 / acc_ref[0, half:], 1.0 / acc_ref[1, :half]], axis=0)
    out = jnp.concatenate([acc_ref[0, :half], acc_ref[1, half:]], axis=0) * inv
    out = out.T
    o_ref[...] = out.astype(o_ref.dtype)
    full_ref[...] = out
    inv_ref[...] = inv.T
    for a in range(2):
        peak_ref[0, 0, a : a + 1, :] = peaks[a]


def attention_cost(q, kv, products):
    flops = products * 8 * q.shape[0] * kv.shape[1] * q.shape[1]
    return pl.CostEstimate(
        flops=flops, bytes_accessed=2 * (q.size + kv.size) * products, transcendentals=8 * q.shape[0] * kv.shape[1]
    )


def attend(info, far, diag, q, kv, rows, length):
    heads = far.shape[0]
    seqs = kv.shape[0]
    wide = 2 * (q.shape[1] // heads)
    pairs = heads // 2
    smem = pl.BlockSpec(memory_space=pltpu.SMEM)
    return pl.pallas_call(
        functools.partial(attend_kernel, rows),
        grid=(pairs, seqs),
        in_specs=[
            smem, smem,
            pl.BlockSpec((1, 6, 2 * rows), lambda p, b: (p, 0, 0)),
            pl.BlockSpec((rows, wide), lambda p, b: (b, p)),
            pl.BlockSpec((1, length, wide), lambda p, b: (b, 0, 2 * p)),
            pl.BlockSpec((1, length, wide), lambda p, b: (b, 0, 2 * p + 1)),
        ],
        out_specs=[pl.BlockSpec((rows, wide), lambda p, b: (b, p))] * 3
        + [pl.BlockSpec((1, 1, 2, rows), lambda p, b: (b, p, 0, 0))],
        out_shape=[
            jax.ShapeDtypeStruct(q.shape, jnp.bfloat16),
            jax.ShapeDtypeStruct(q.shape, jnp.float32),
            jax.ShapeDtypeStruct(q.shape, jnp.float32),
            jax.ShapeDtypeStruct((seqs, pairs, 2, rows), jnp.float32),
        ],
        scratch_shapes=[
            pltpu.VMEM((2, 5, rows, rows), jnp.float32),
            pltpu.VMEM((2, length, rows), jnp.float32),
            pltpu.VMEM((2, wide, rows), jnp.float32),
        ],
        compiler_params=pltpu.CompilerParams(vmem_limit_bytes=48 << 20),
        cost_estimate=attention_cost(q, kv, 2),
        name="attend",
    )(info, far, diag, q, kv, kv)


def back_pair(rows, length, first, q, g, full, key_value, peak, bias_ref, sum_ref, acc_ref, write):
    q_half, g_half = head_halves(q), head_halves(g)
    wide = q.shape[1]
    half = wide // 2
    key_row = lax.broadcasted_iota(jnp.int32, (rows, rows), 0)
    acc_ref[...] = jnp.zeros_like(acc_ref)
    along = (g.astype(jnp.float32) * full).T
    delta = [jnp.sum(along[a * half : (a + 1) * half], axis=0, keepdims=True) for a in range(2)]
    keys, spans = key_value

    def step(i, carry):
        kc = i * SPAN
        here = pl.ds(kc * rows, SPAN * rows)
        k, v = keys(here)
        dk = dv = None
        for a in range(2):
            s = nt_dot(k, q_half[a])
            dp = nt_dot(v, g_half[a])
            es, dss = [], []
            for u in range(SPAN):
                part = slice(u * rows, (u + 1) * rows)
                slot = jnp.clip(kc + u - first + 2, 0, 4)
                valid = key_row < length - (kc + u) * rows
                e = jnp.exp(s[part] + bias_ref[a, slot] - peak[a])
                e_low = jnp.where(valid, e, 0.0).astype(jnp.bfloat16)
                ds = e_low.astype(jnp.float32) * (dp[part] - delta[a])
                sum_ref[a, slot] += ds
                es.append(e_low)
                dss.append(ds.astype(jnp.bfloat16))
            e_low, ds_low = jnp.concatenate(es, axis=0), jnp.concatenate(dss, axis=0)
            dv_a = nn_dot(e_low, g_half[a])
            dk_a = nn_dot(ds_low, q_half[a])
            dv = dv_a if dv is None else dv + dv_a
            dk = dk_a if dk is None else dk + dk_a
            acc_ref[a] += tn_dot(k, ds_low)
        write(here, dk.astype(jnp.bfloat16), dv.astype(jnp.bfloat16))
        return carry

    if spans == 1:
        step(0, 0)
    else:
        lax.fori_loop(0, spans, step, 0)
    return jnp.concatenate([acc_ref[0, :half], acc_ref[1, half:]], axis=0).T.astype(jnp.bfloat16)


def near_sums(rows, sum_ref, write):
    for a in range(2):
        for slot in range(5):
            total_sum = jnp.zeros((8, 2 * rows), jnp.float32)
            for g in range(rows // 8):
                part = jnp.concatenate(
                    [sum_ref[a, slot, 8 * g : 8 * g + 8, :], jnp.zeros((8, rows), jnp.float32)], axis=1
                )
                if g and 0 < slot < 4:
                    part = pltpu.roll(part, 2 * rows - 8 * g, 1)
                total_sum = total_sum + part
            write(a, slot, total_sum)


def attend_back_kernel(rows, info_ref, far_ref, diag_ref, q_ref, g_ref, full_ref, k_ref, v_ref, peak_ref,
                       dq_ref, dkv_ref, near_ref, bias_ref, sum_ref, acc_ref):
    pair, b = pl.program_id(0), pl.program_id(1)

    @pl.when(b == 0)
    def _():
        fill_bias(rows, far_ref, diag_ref, bias_ref, pair)
        sum_ref[...] = jnp.zeros_like(sum_ref)

    wide = q_ref.shape[1]

    def write(here, dk, dv):
        dkv_ref[0, here, :wide] = dk
        dkv_ref[0, here, wide:] = dv

    dq_ref[...] = back_pair(
        rows,
        info_ref[b],
        info_ref[info_ref.shape[0] - 1],
        q_ref[...],
        g_ref[...],
        full_ref[...],
        (lambda here: (k_ref[0, here, :], v_ref[0, here, :]), k_ref.shape[1] // (SPAN * rows)),
        [peak_ref[0, 0, a : a + 1, :] for a in range(2)],
        bias_ref,
        sum_ref,
        acc_ref,
        write,
    )

    @pl.when(b == pl.num_programs(1) - 1)
    def _():
        def keep(a, slot, value):
            near_ref[0, a, slot] = value

        near_sums(rows, sum_ref, keep)


def attend_back(info, far, diag, q, g, full, kv, peak, rows, length, seqs):
    heads = far.shape[0]
    wide = 2 * (q.shape[1] // heads)
    pairs = heads // 2
    smem = pl.BlockSpec(memory_space=pltpu.SMEM)
    row_spec = pl.BlockSpec((rows, wide), lambda p, b: (b, p))
    return pl.pallas_call(
        functools.partial(attend_back_kernel, rows),
        grid=(pairs, seqs),
        in_specs=[
            smem,
            smem,
            pl.BlockSpec((1, 6, 2 * rows), lambda p, b: (p, 0, 0)),
            row_spec,
            row_spec,
            row_spec,
            pl.BlockSpec((1, length, wide), lambda p, b: (b, 0, 2 * p)),
            pl.BlockSpec((1, length, wide), lambda p, b: (b, 0, 2 * p + 1)),
            pl.BlockSpec((1, 1, 2, rows), lambda p, b: (b, p, 0, 0)),
        ],
        out_specs=[
            row_spec,
            pl.BlockSpec((1, length, 2 * wide), lambda p, b: (b, 0, p)),
            pl.BlockSpec((1, 2, 5, 8, 2 * rows), lambda p, b: (p, 0, 0, 0, 0)),
        ],
        out_shape=[
            jax.ShapeDtypeStruct((seqs * rows, q.shape[1]), jnp.bfloat16),
            jax.ShapeDtypeStruct((seqs,) + kv.shape[1:], jnp.bfloat16),
            jax.ShapeDtypeStruct((pairs, 2, 5, 8, 2 * rows), jnp.float32),
        ],
        scratch_shapes=[
            pltpu.VMEM((2, 5, rows, rows), jnp.float32),
            pltpu.VMEM((2, 5, rows, rows), jnp.float32),
            pltpu.VMEM((2, wide, rows), jnp.float32),
        ],
        compiler_params=pltpu.CompilerParams(vmem_limit_bytes=48 << 20),
        cost_estimate=attention_cost(q, kv, 3),
        name="attend_back",
    )(info, far, diag, q, g, full, kv, kv, peak)


SLOTS = ("x", "c", "z", "y")
MESH = pl.DeviceIdType.MESH


def layout_of(batch, seq):
    fast = 1 << ((seq.bit_length() - 1) // 2)
    return {"x": batch // 2, "c": 2, "z": seq // fast, "y": fast}


def tile_block(rows, cols):
    return (rows, cols) if rows % 16 == 0 else (rows * cols // 128, 128)


def place(sizes):
    b, s = lax.axis_index("batch"), lax.axis_index("seq")
    return {
        "x": lax.div(b, 2),
        "c": lax.rem(b, 2),
        "z": lax.div(s, sizes["y"]),
        "y": lax.rem(s, sizes["y"]),
    }


def device_at(sizes, me, dim, at):
    spot = dict(me)
    spot[dim] = at
    return (spot["x"] * 2 + spot["c"], spot["z"] * sizes["y"] + spot["y"])


def seq_peer(sizes, me, k):
    n = sizes["z"] * sizes["y"]
    return (me["x"] * 2 + me["c"], lax.rem(me["z"] * sizes["y"] + me["y"] + k, n))


def greet(sizes, me, dims):
    barrier = pltpu.get_barrier_semaphore()
    total = 0
    if "s" in dims:
        total = sizes["z"] * sizes["y"] - 1
        for k in range(1, total + 1):
            pl.semaphore_signal(barrier, inc=1, device_id=seq_peer(sizes, me, k), device_id_type=MESH)
        dims = [d for d in dims if d not in "szy"]
    for dim in dims:
        for k in range(1, sizes[dim]):
            peer = device_at(sizes, me, dim, lax.rem(me[dim] + k, sizes[dim]))
            pl.semaphore_signal(barrier, inc=1, device_id=peer, device_id_type=MESH)
            total += 1
    pl.semaphore_wait(barrier, total)


class Sems:
    def __init__(self, send, recv):
        self.send, self.recv, self.used = send, recv, 0

    def take(self, count):
        first = self.used
        self.used += count
        assert self.used <= self.send.shape[0]
        return first

    def copy(self, src, dst, index, device):
        return pltpu.make_async_remote_copy(
            src_ref=src, dst_ref=dst, send_sem=self.send.at[index], recv_sem=self.recv.at[index],
            device_id=device, device_id_type=MESH,
        )


def run_together(tasks, plan=()):
    tasks = list(tasks)
    over_already = set()
    for i in plan:
        if i not in over_already:
            try:
                next(tasks[i])
            except StopIteration:
                over_already.add(i)
    tasks = [t for i, t in enumerate(tasks) if i not in over_already]
    while tasks:
        left = []
        for task in tasks:
            try:
                next(task)
                left.append(task)
            except StopIteration:
                pass
        tasks = left


def gather_task(sizes, me, src, out, local_sem, sems, order):
    before = list(SLOTS[len(SLOTS) - (len(src.shape) - 2) :])
    dims = [d for d in SLOTS if d in order.lower() or d in before]
    own = pltpu.make_async_copy(src, out.at[tuple(me[d] for d in dims if d not in before)], local_sem)
    own.start()
    own.wait()
    done = before
    sent = []
    for dim in order:
        direct, dim = dim.isupper(), dim.lower()
        n, at = sizes[dim], me[dim]

        def region(origin):
            spots = []
            for d in dims:
                spots.append(slice(None) if d in done else (origin if d == dim else me[d]))
            return out.at[tuple(spots)]

        if n == 2:
            base = sems.take(1)
            other = 1 - at
            send = sems.copy(region(at), region(at), base, device_at(sizes, me, dim, other))
            send.start()
            yield
            sems.copy(region(other), region(other), base, device_at(sizes, me, dim, other)).wait_recv()
            sent.append((None, send))
        elif direct:
            base = sems.take(n - 1)
            for k in range(1, n):
                peer = device_at(sizes, me, dim, lax.rem(at + k, n))
                send = sems.copy(region(at), region(at), base + k - 1, peer)
                send.start()
                sent.append((None, send))
            yield
            for k in range(1, n):
                origin = lax.rem(at + n - k, n)
                sems.copy(region(origin), region(origin), base + k - 1, device_at(sizes, me, dim, origin)).wait_recv()
        else:
            for t in range(n - 1):
                base = sems.take(2)
                to_right = (at + 1 < n) & (at - t >= 0)
                to_left = (at >= 1) & (at + t < n)
                from_left = (at >= 1) & (at - 1 - t >= 0)
                from_right = (at + 1 < n) & (at + 1 + t < n)
                right = sems.copy(region(at - t), region(at - t), base, device_at(sizes, me, dim, at + 1))
                left = sems.copy(region(at + t), region(at + t), base + 1, device_at(sizes, me, dim, at - 1))
                pl.when(to_right)(right.start)
                pl.when(to_left)(left.start)
                sent += [(to_right, right), (to_left, left)]
                yield
                got = sems.copy(region(at - 1 - t), region(at - 1 - t), base, device_at(sizes, me, dim, at - 1))
                pl.when(from_left)(got.wait_recv)
                got = sems.copy(region(at + 1 + t), region(at + 1 + t), base + 1, device_at(sizes, me, dim, at + 1))
                pl.when(from_right)(got.wait_recv)
        done.append(dim)
    for cond, send in sent:
        if cond is None:
            send.wait_send()
        else:
            pl.when(cond)(send.wait_send)


def spread_task(sizes, me, src, out, local_sem, sems):
    z, y, n, fast = me["z"], me["y"], sizes["z"], sizes["y"]
    own = pltpu.make_async_copy(src, out.at[:, z, y], local_sem)
    own.start()
    own.wait()
    fan = sems.take((fast - 1) * n)

    def fan_copy(k, origin, owner):
        peer = device_at(sizes, me, "y", lax.rem(y + k, fast))
        spot = out.at[:, origin, owner]
        return sems.copy(spot, spot, fan + (k - 1) * n + origin, peer)

    def fan_out(origin):
        for k in range(1, fast):
            fan_copy(k, origin, y).start()

    fan_out(z)
    sent = []
    for t in range(n - 1):
        base = sems.take(2)
        to_right = (z + 1 < n) & (z - t >= 0)
        to_left = (z >= 1) & (z + t < n)
        from_left = (z >= 1) & (z - 1 - t >= 0)
        from_right = (z + 1 < n) & (z + 1 + t < n)
        right = sems.copy(out.at[:, z - t, y], out.at[:, z - t, y], base, device_at(sizes, me, "z", z + 1))
        left = sems.copy(out.at[:, z + t, y], out.at[:, z + t, y], base + 1, device_at(sizes, me, "z", z - 1))
        pl.when(to_right)(right.start)
        pl.when(to_left)(left.start)
        sent += [(to_right, right), (to_left, left)]
        yield

        @pl.when(from_left)
        def _():
            spot = out.at[:, z - 1 - t, y]
            sems.copy(spot, spot, base, device_at(sizes, me, "z", z - 1)).wait_recv()
            fan_out(z - 1 - t)

        @pl.when(from_right)
        def _():
            spot = out.at[:, z + 1 + t, y]
            sems.copy(spot, spot, base + 1, device_at(sizes, me, "z", z + 1)).wait_recv()
            fan_out(z + 1 + t)

    yield
    for k in range(1, fast):
        for origin in range(n):
            fan_copy(k, origin, lax.rem(y + fast - k, fast)).wait_recv()
    for k in range(1, fast):
        for origin in range(n):
            fan_copy(k, origin, y).wait_send()
    for cond, send in sent:
        pl.when(cond)(send.wait_send)


def shift_task(sizes, me, src, out, sems, step):
    n = sizes["z"] * sizes["y"]
    s = me["z"] * sizes["y"] + me["y"]
    base = sems.take(1)
    send = sems.copy(src, out, base, seq_peer(sizes, me, step % n))
    has_to = (s < n - 1) if step > 0 else (s > 0)
    has_from = (s > 0) if step > 0 else (s < n - 1)
    pl.when(has_to)(send.start)
    yield
    pl.when(has_from)(send.wait_recv)

    @pl.when(jnp.logical_not(has_from))
    def _():
        out[...] = jnp.zeros_like(out)

    yield
    pl.when(has_to)(send.wait_send)


def stage_count(sizes, order):
    return sum(1 if sizes[d] == 2 else 2 * (sizes[d] - 1) for d in order.lower())


def gather_kernel(sizes, orders, has_rows, has_rim, plan, *refs):
    count = len(orders)
    total = count + has_rows + has_rim
    ins, outs = refs[:total], refs[total : 2 * total]
    local_sem, send_sem, recv_sem = refs[2 * total :]
    me = place(sizes)
    used = [d for d in SLOTS if any(d in o.lower() for o in orders) or (has_rows and d in "zy")]
    greet(sizes, me, used + ["s"] * has_rim)
    sems = Sems(send_sem, recv_sem)
    tasks = []
    for i in range(count):
        tasks.append(gather_task(sizes, me, ins[i], outs[i], local_sem.at[i], sems, orders[i]))
    if has_rows:
        tasks.append(spread_task(sizes, me, ins[count], outs[count], local_sem.at[count], sems))
    if has_rim:
        tasks.append(shift_task(sizes, me, ins[-1], outs[-1], sems, 1))
    run_together(tasks, plan)


def gather_all(shards, orders, sizes, collective_id, rows=None, rim=None, plan=(), name="gather"):
    ins, shapes, out_specs = [], [], []
    for shard, order in zip(shards, orders):
        ins.append(shard if shard.ndim > 2 else shard.reshape(tile_block(*shard.shape)))
        before = SLOTS[len(SLOTS) - (ins[-1].ndim - 2) :]
        whole = tuple(sizes[d] for d in SLOTS if d in order.lower() or d in before)
        shapes.append(jax.ShapeDtypeStruct(whole + ins[-1].shape[-2:], shard.dtype))
    total = sum(stage_count(sizes, o) for o in orders)
    out_specs = [pl.BlockSpec(memory_space=pl.ANY)] * len(ins)
    if rows is not None:
        ins.append(rows)
        shapes.append(jax.ShapeDtypeStruct((rows.shape[0], sizes["z"], sizes["y"]) + rows.shape[1:], rows.dtype))
        out_specs.append(pl.BlockSpec(memory_space=pl.ANY))
        total += (sizes["y"] - 1) * sizes["z"] + 2 * (sizes["z"] - 1)
    if rim is not None:
        ins.append(rim)
        shapes.append(jax.ShapeDtypeStruct(rim.shape, rim.dtype))
        out_specs.append(pl.BlockSpec(memory_space=pltpu.VMEM))
        total += 1
    return pl.pallas_call(
        functools.partial(gather_kernel, sizes, orders, int(rows is not None), int(rim is not None), plan),
        in_specs=[pl.BlockSpec(memory_space=pltpu.VMEM)] * len(ins),
        out_specs=out_specs,
        out_shape=shapes,
        scratch_shapes=[
            pltpu.SemaphoreType.DMA((len(ins),)),
            pltpu.SemaphoreType.DMA((total,)),
            pltpu.SemaphoreType.DMA((total,)),
        ],
        compiler_params=pltpu.CompilerParams(collective_id=collective_id, has_side_effects=True),
        name=name,
    )(*ins)


def over(extents, body):
    total = 1
    for e in extents:
        total *= e
    if total == 1:
        body((0,) * len(extents))
        return

    def step(i, carry):
        spots = []
        for e in reversed(extents):
            spots.append(lax.rem(i, e))
            i = lax.div(i, e)
        body(tuple(reversed(spots)))
        return carry

    lax.fori_loop(0, total, step, 0)


def add_into(dst, src_of, extents):
    def body(spots):
        here = spots + (slice(None), slice(None))
        dst[here] = (dst[here].astype(jnp.float32) + src_of(spots).astype(jnp.float32)).astype(dst.dtype)

    over(extents, body)


def add_pair(out, first, second_of, extents):
    def body(spots):
        here = spots + (slice(None), slice(None))
        out[here] = (first[here].astype(jnp.float32) + second_of(spots).astype(jnp.float32)).astype(out.dtype)

    over(extents, body)


def reduce_task(sizes, me, src, out, bufs, sems, order, dims):
    remaining = list(dims)
    current = src
    sent = []
    for stage, dim in enumerate(order):
        if dim == "s":
            n = sizes["z"] * sizes["y"]
            base = sems.take(n)
            gathered = bufs[stage]
            s = me["z"] * sizes["y"] + me["y"]
            for k in range(1, n):
                to = lax.rem(s + k, n)
                send = sems.copy(
                    current.at[lax.div(to, sizes["y"]), lax.rem(to, sizes["y"])],
                    gathered.at[k],
                    base + k,
                    seq_peer(sizes, me, k),
                )
                send.start()
                sent.append((None, send))
            yield
            total = current[me["z"], me["y"]].astype(jnp.float32)
            for k in range(1, n):
                sems.copy(gathered.at[k], gathered.at[k], base + k, seq_peer(sizes, me, k)).wait_recv()
                total = total + gathered[k].astype(jnp.float32)
            out[...] = total
            continue
        n, at = sizes[dim], me[dim]
        spot = remaining.index(dim)
        after = remaining[:spot] + remaining[spot + 1 :]
        extents = [sizes[d] for d in after]
        last = stage == len(order) - 1
        source = current

        def block(j):
            return source.at[(slice(None),) * spot + (j,)]

        def values(j):
            return lambda spots: source[spots[:spot] + (j,) + spots[spot:] + (slice(None), slice(None))]

        if n == 2:
            buf = bufs[stage]
            base = sems.take(1)
            send = sems.copy(block(1 - at), buf, base, device_at(sizes, me, dim, 1 - at))
            send.start()
            sent.append((None, send))
            yield
            send.wait_recv()
            if last:
                add_pair(out, buf, values(at), extents)
            else:
                add_into(buf, values(at), extents)
            current = buf
        else:
            chains = bufs[stage][0]
            base = sems.take(2 * n)
            for slot in range(n - 1):
                for side in range(2):
                    lead = at if side == 0 else n - 1 - at
                    j = lax.rem((n - 1 - slot + at) if side == 0 else (slot + 1 + at + n), n)
                    buf = chains.at[side, j]
                    to = device_at(sizes, me, dim, at + 1 if side == 0 else at - 1)
                    index = base + side * n + j
                    plain = sems.copy(block(j), buf, index, to)
                    summed = sems.copy(buf, buf, index, to)
                    pl.when(lead == 0)(plain.start)

                    def pass_on(summed=summed, buf=buf, j=j):
                        summed.wait_recv()
                        add_into(buf, values(j), extents)
                        summed.start()

                    pl.when((lead > 0) & (lead <= slot))(pass_on)
                    sent.append((lead <= slot, summed))
                yield

            def arrived(side):
                buf = chains.at[side, at]
                sems.copy(buf, buf, base + side * n + at, device_at(sizes, me, dim, at)).wait_recv()

            result = out if last else bufs[stage][1]

            def start(spots):
                here = spots + (slice(None), slice(None))
                result[here] = values(at)(spots).astype(result.dtype)

            def add(side):
                add_into(result, lambda spots: chains[(side, at) + spots + (slice(None), slice(None))], extents)

            over(extents, start)

            @pl.when(at > 0)
            def _():
                arrived(0)
                add(0)

            @pl.when(at < n - 1)
            def _():
                arrived(1)
                add(1)

            current = result
        remaining = after
    for cond, send in sent:
        if cond is None:
            send.wait_send()
        else:
            pl.when(cond)(send.wait_send)


class Split:
    def __init__(self, parts):
        self.parts = parts
        self.dtype = parts[0].dtype

    def __setitem__(self, here, value):
        first = 0
        for part in self.parts:
            last = first + part.shape[-1]
            part[here] = value[:, first:last]
            first = last

    def __getitem__(self, here):
        return jnp.concatenate([part[here] for part in self.parts], axis=1)


def stage_buffers(sizes, block, dtype, dims, order):
    scratch, counts, left, total = [], [], list(dims), 0
    for dim in order:
        counts.append(1)
        if dim == "s":
            left = []
            n = sizes["z"] * sizes["y"]
            scratch.append(pltpu.VMEM((n,) + block, dtype))
            total += n
            continue
        left.remove(dim)
        shape = tuple(sizes[d] for d in left) + block
        n = sizes[dim]
        if n == 2:
            scratch.append(pltpu.VMEM(shape, dtype))
            total += 1
        else:
            scratch.append(pltpu.VMEM((2, n) + shape, dtype))
            total += 2 * n
            if dim != order[-1]:
                scratch.append(pltpu.VMEM(shape, dtype))
                counts[-1] = 2
    return scratch, counts, total, left


def stage_refs(sizes, order, counts, bufs):
    stages = []
    for dim, size in zip(order, counts):
        taken = [bufs.pop(0) for _ in range(size)]
        stages.append(taken[0] if dim == "s" or sizes[dim] == 2 else taken)
    return stages


def reduce_kernel(sizes, orders, dims, counts, splits, spill, *refs):
    count = len(orders)
    total = count + spill
    ends = sum(splits) + spill
    ins, outs = refs[:total], list(refs[total : total + ends])
    send_sem, recv_sem = refs[-2:]
    bufs = list(refs[total + ends : -2])
    me = place(sizes)
    used = [d for d in SLOTS if any(d in o for o in orders)]
    greet(sizes, me, used + ["s"] * (spill or any("s" in o for o in orders)))
    sems = Sems(send_sem, recv_sem)
    tasks = []
    for i in range(count):
        stages = stage_refs(sizes, orders[i], counts[i], bufs)
        parts = [outs.pop(0) for _ in range(splits[i])]
        out = parts[0] if len(parts) == 1 else Split(parts)
        tasks.append(reduce_task(sizes, me, ins[i], out, stages, sems, orders[i], dims[i]))
    if spill:
        tasks.insert(0, shift_task(sizes, me, ins[-1], outs.pop(0), sems, -1))
    run_together(tasks)


def cut_shapes(block, left, widths, sizes, dtype):
    if left or widths is None or sum(widths) != block[1]:
        shape = tuple(sizes[d] for d in left) + block
        return [jax.ShapeDtypeStruct(shape, dtype if left else jnp.float32)], widths
    return [jax.ShapeDtypeStruct((block[0], w), jnp.float32) for w in widths], None


def cut_columns(parts, widths):
    if widths is None:
        return parts
    full = parts[0].reshape(-1, sum(widths))
    edges = np.cumsum([0] + list(widths))
    return [full[:, int(lo) : int(hi)] for lo, hi in zip(edges[:-1], edges[1:])]


def reduce_all(grads, orders, sizes, collective_id, spill=None, splits=None, name="reduce"):
    ins, scratch, shapes, counts, all_dims, cuts, later = [], [], [], [], [], [], []
    splits = splits or [None] * len(grads)
    total = 0
    devices = sizes["x"] * sizes["c"] * sizes["z"] * sizes["y"]
    for grad, order, widths in zip(grads, orders, splits):
        dims = SLOTS[-(grad.ndim - 2) :] if grad.ndim > 2 else SLOTS
        if grad.ndim == 2:
            whole = tuple(sizes[d] for d in SLOTS)
            grad = grad.reshape(whole + tile_block(grad.shape[0] // devices, grad.shape[1]))
        block = grad.shape[-2:]
        ins.append(grad)
        all_dims.append(dims)
        more, taken, needed, left = stage_buffers(sizes, block, grad.dtype, dims, order)
        scratch += more
        total += needed
        counts.append(taken)
        ends, widths = cut_shapes(block, left, widths, sizes, grad.dtype)
        shapes += ends
        cuts.append(len(ends))
        later.append(widths)
    if spill is not None:
        ins.append(spill)
        shapes.append(jax.ShapeDtypeStruct(spill.shape, spill.dtype))
        total += 1
    outs = pl.pallas_call(
        functools.partial(reduce_kernel, sizes, orders, all_dims, counts, cuts, int(spill is not None)),
        in_specs=[pl.BlockSpec(memory_space=pltpu.VMEM)] * len(ins),
        out_specs=[pl.BlockSpec(memory_space=pltpu.VMEM)] * len(shapes),
        out_shape=shapes,
        scratch_shapes=scratch + [pltpu.SemaphoreType.DMA((total,)), pltpu.SemaphoreType.DMA((total,))],
        compiler_params=pltpu.CompilerParams(
            collective_id=collective_id, has_side_effects=True, vmem_limit_bytes=56 << 20
        ),
        name=name,
    )(*ins)
    outs = list(outs)
    results = []
    for cut, widths in zip(cuts, later):
        results.append(cut_columns([outs.pop(0) for _ in range(cut)], widths))
    return results + outs


def collect_task(sizes, me, src, out, ybuf, chain, sems, produce):
    z, y, n, fast = me["z"], me["y"], sizes["z"], sizes["y"]
    fan = sems.take((fast - 1) * n)
    base = sems.take(2 * n)

    def fan_copy(k, j):
        to = lax.rem(y + k, fast)
        index = fan + (k - 1) * n + j
        return sems.copy(src.at[j, to], ybuf.at[k - 1, j], index, device_at(sizes, me, "y", to))

    def spread(i, carry):
        far = n - 1 - lax.div(i, 2)
        j = jnp.where(lax.rem(i, 2) == 0, z + far, z - far)

        @pl.when((j >= 0) & (j < n))
        def _():
            produce(j)
            for k in range(1, fast):
                fan_copy(k, j).start()

        return carry

    def chain_copy(side, j, to, plain=False):
        buf = chain.at[side, j]
        return sems.copy(ybuf.at[0, j] if plain else buf, buf, base + side * n + j, device_at(sizes, me, "z", to))

    slots = []
    for slot in range(n - 1):
        for side in range(2):
            lead = z if side == 0 else n - 1 - z
            j = lax.rem((n - 1 - slot + z) if side == 0 else (slot + 1 + z + n), n)
            to = z + 1 if side == 0 else z - 1
            ends = (chain_copy(side, j, to, True), chain_copy(side, j, to))
            slots.append((side, j, ends, lead == 0, (lead > 0) & (lead <= slot), lead <= slot))
    fans = [fan_copy(k, j) for j in range(n) for k in range(1, fast)]
    lax.fori_loop(0, 2 * n - 1, spread, 0)
    yield

    def merge(j):
        for k in range(1, fast):
            fan_copy(k, j).wait_recv()
        value = src[j, y].astype(jnp.float32)
        for k in range(1, fast):
            value = value + ybuf[k - 1, j].astype(jnp.float32)
        return value

    for slot in range(n - 1):
        for side, j, (plain, summed), is_first, is_later, _ in slots[2 * slot : 2 * slot + 2]:

            def begin(plain=plain, j=j):
                ybuf[0, j] = merge(j).astype(ybuf.dtype)
                plain.start()

            def pass_on(summed=summed, side=side, j=j):
                value = merge(j)
                summed.wait_recv()
                chain[side, j] = (chain[side, j].astype(jnp.float32) + value).astype(chain.dtype)
                summed.start()

            pl.when(is_first)(begin)
            pl.when(is_later)(pass_on)
        yield
    out[...] = merge(z)

    def finish(side):
        chain_copy(side, z, z).wait_recv()
        out[...] += chain[side, z].astype(jnp.float32)

    pl.when(z > 0)(partial(finish, 0))
    pl.when(z < n - 1)(partial(finish, 1))
    for fan_end in fans:
        fan_end.wait_send()
    for _, _, (_, summed), _, _, active in slots:
        pl.when(active)(summed.wait_send)


def halve_kernel(sizes, count, *refs):
    n = sizes["x"]
    ins, outs, bufs = refs[:count], refs[count : 2 * count], refs[2 * count : 3 * count]
    send_sem, recv_sem = refs[-2:]
    me = place(sizes)
    greet(sizes, me, ("c",))
    sems = Sems(send_sem, recv_sem)
    c = me["c"]
    peer = device_at(sizes, me, "c", 1 - c)
    sends = {}
    for x in range(n):
        for i in range(count):
            sends[x, i] = sems.copy(ins[i].at[x, 1 - c], bufs[i].at[x], sems.take(1), peer)
            sends[x, i].start()
    for x in range(n):
        for i in range(count):
            sends[x, i].wait_recv()
            src = ins[i]

            def own(spots, src=src, x=x):
                return src[(x, c) + spots + (slice(None), slice(None))]

            add_pair(outs[i].at[x], bufs[i].at[x], own, src.shape[2:-2])
    for send in sends.values():
        send.wait_send()


def halve_cores(grads, sizes, collective_id, name="halve"):
    n = sizes["x"]
    whole = tuple(sizes[d] for d in SLOTS)
    devices = whole[0] * whole[1] * whole[2] * whole[3]
    ins = [g.reshape(whole + tile_block(g.shape[0] // devices, g.shape[1])) for g in grads]
    halves = [g.shape[:1] + g.shape[2:] for g in ins]
    total = n * len(ins)
    return pl.pallas_call(
        functools.partial(halve_kernel, sizes, len(ins)),
        in_specs=[pl.BlockSpec(memory_space=pltpu.VMEM)] * len(ins),
        out_specs=[pl.BlockSpec(memory_space=pltpu.VMEM)] * len(ins),
        out_shape=[jax.ShapeDtypeStruct(h, g.dtype) for h, g in zip(halves, ins)],
        scratch_shapes=[pltpu.VMEM(h, g.dtype) for h, g in zip(halves, ins)]
        + [pltpu.SemaphoreType.DMA((total,)), pltpu.SemaphoreType.DMA((total,))],
        compiler_params=pltpu.CompilerParams(
            collective_id=collective_id, has_side_effects=True, vmem_limit_bytes=56 << 20
        ),
        name=name,
    )(*ins)


def back_rows_kernel(sizes, rows, tasks_info, inner, *refs):
    refs = list(refs)

    def take(count):
        taken = refs[:count]
        del refs[:count]
        return taken

    info_ref, far_ref, diag_ref, q_ref, g_ref, full_ref, peak_ref, kv_ref, dkv_ref, normed_ref, second_ref = take(11)
    if inner:
        own_ref, dq_before_ref, d_out_ref = take(3)
    grads = take(len(tasks_info))
    d_normed_ref, dq_ref, near_ref = take(3)
    outs = [take(cut) for _, _, _, cut in tasks_info]
    last_ref = take(1)[0]
    if inner:
        inner_ref = take(1)[0]
        inner_counts = inner
        d_last_ref = take(1)[0]
    else:
        d_last_ref = last_ref
    kv_buf, chunk_ref, normed_buf, d_rows_ref, ybuf, chain, bias_ref, sum_ref, acc_ref, total_ref = take(10)
    kv_sem, chunk_sem, normed_sem, send_sem, recv_sem = refs[-5:]
    bufs = refs[:-5]
    me = place(sizes)
    first = me["z"] * sizes["y"] + me["y"]
    seqs, length, _ = kv_ref.shape
    n = sizes["z"]
    step = length // n
    last = seqs - 1
    width = q_ref.shape[1]
    pairs = diag_ref.shape[0]
    wide = width // pairs
    fetch = pltpu.make_async_copy(kv_ref.at[last], kv_buf, kv_sem)
    fetch.start()
    greet(sizes, me, SLOTS)
    sems = Sems(send_sem, recv_sem)
    ffn = []
    for (order, dims, counts, _), grad, out in zip(tasks_info, grads, outs):
        stages = stage_refs(sizes, order, counts, bufs)
        ffn.append(reduce_task(sizes, me, grad, out[0] if len(out) == 1 else Split(out), stages, sems, order, dims))
    for task in ffn:
        next(task)

    def rows_of(p):
        def produce(j):
            here = pl.ds(pl.multiple_of(j * step, step), step)
            if p < last:
                copy = pltpu.make_async_copy(dkv_ref.at[p, here], chunk_ref.at[0], chunk_sem.at[0])
                copy.start()
                copy.wait()
                block = chunk_ref[0]
            else:
                block = d_last_ref[here, :]
            block = nt_dot(block, second_ref[...]).astype(jnp.bfloat16)
            d_rows_ref[p, j] = block.reshape(d_rows_ref.shape[2:])

        return collect_task(
            sizes, me, d_rows_ref.at[p], d_normed_ref.at[p], ybuf.at[p], chain.at[p], sems, produce
        )

    before = [rows_of(p) for p in range(last)]
    for task in before:
        next(task)
    fetch.wait()
    size = info_ref[last]

    def one_pair(p, carry):
        fill_bias(rows, far_ref, diag_ref.at[pl.ds(p, 1)], bias_ref, p)
        sum_ref[...] = jnp.zeros_like(sum_ref)
        lanes = pl.ds(pl.multiple_of(p * wide, wide), wide)
        k_lanes = pl.ds(pl.multiple_of(2 * p * wide, wide), wide)
        v_lanes = pl.ds(pl.multiple_of((2 * p + 1) * wide, wide), wide)

        def write(here, dk, dv):
            d_last_ref[here, k_lanes] = dk
            d_last_ref[here, v_lanes] = dv

        dq_ref[:, lanes] = back_pair(
            rows,
            size,
            first,
            q_ref[:, lanes],
            g_ref[:, lanes],
            full_ref[:, lanes],
            (lambda here: (kv_buf[here, k_lanes], kv_buf[here, v_lanes]), length // (SPAN * rows)),
            [peak_ref[p, a : a + 1, :] for a in range(2)],
            bias_ref,
            sum_ref,
            acc_ref,
            write,
        )

        def keep(a, slot, value):
            near_ref[p, a, slot] = value

        near_sums(rows, sum_ref, keep)
        for i in range(pairs):
            for task in before:
                pl.when(p == i)(lambda task=task: next(task, None))
        return carry

    lax.fori_loop(0, pairs, one_pair, 0)
    run_together(before)
    after = rows_of(last)
    next(after)
    tasks = ffn + [after]
    if inner:
        steps = seqs * n
        early = last * n

        def at_step(i):
            return pl.ds(pl.multiple_of(i * step, step), step)

        def normed_copy(i):
            slot = lax.rem(i, 2)
            return pltpu.make_async_copy(normed_ref.at[at_step(i)], normed_buf.at[slot], normed_sem.at[slot])

        def early_copy(i):
            slot = lax.rem(i, 2)
            src = dkv_ref.at[lax.div(i, n), at_step(lax.rem(i, n))]
            return pltpu.make_async_copy(src, chunk_ref.at[slot], chunk_sem.at[slot])

        normed_copy(0).start()
        early_copy(0).start()
        total_ref[...] = jnp.zeros_like(total_ref)

        def weigh(i, carry):
            pl.when(i + 1 < steps)(lambda: normed_copy(i + 1).start())
            pl.when(i + 1 < early)(lambda: early_copy(i + 1).start())
            normed_copy(i).wait()
            slot = lax.rem(i, 2)

            @pl.when(i < early)
            def _():
                early_copy(i).wait()
                total_ref[...] += tn_dot(normed_buf[slot], chunk_ref[slot])

            @pl.when(i >= early)
            def _():
                total_ref[...] += tn_dot(normed_buf[slot], d_last_ref[at_step(i - early), :])

            for k in range(1, n):
                pl.when(i == 2 * k)(lambda: next(after, None))
            return carry

        lax.fori_loop(0, steps, weigh, 0)
        block = inner_ref.shape[:-1]
        d_query = tn_dot(own_ref[last * rows :], dq_ref[...])
        if last:
            d_query = d_query + tn_dot(own_ref[: last * rows], dq_before_ref[...])
        inner_ref[..., :width] = d_query.astype(jnp.bfloat16).reshape(block + (width,))
        inner_ref[..., width : 2 * width] = d_out_ref[...]
        inner_ref[..., 2 * width :] = total_ref[...].astype(jnp.bfloat16).reshape(block + (2 * width,))
        stages = stage_refs(sizes, "cx", inner_counts, bufs)
        tasks.insert(0, reduce_task(sizes, me, inner_ref, last_ref, stages, sems, "cx", SLOTS))
    run_together(tasks)


def back_rows(info, far, diag, q, g, full, kv, peak, dkv, normed_all, normed_own, second, dq_before, d_out, grads,
              orders, splits, sizes, rows, collective_id, name="back_rows"):
    seqs, length, double = kv.shape
    width = q.shape[1]
    last = seqs - 1
    pairs = far.shape[0] // 2
    n, fast = sizes["z"], sizes["y"]
    step = length // n
    smem, vmem = pl.BlockSpec(memory_space=pltpu.SMEM), pl.BlockSpec(memory_space=pltpu.VMEM)
    anywhere = pl.BlockSpec(memory_space=pl.ANY)
    bf16, f32 = jnp.bfloat16, jnp.float32
    tail = slice(last * rows, seqs * rows)
    ins = [info, far, diag, q[tail], g[tail], full[tail], peak[last], kv, dkv, normed_all, second]
    in_specs = [smem, smem] + [vmem] * 5 + [anywhere] * 3 + [vmem]
    devices = sizes["x"] * sizes["c"] * n * fast
    own_block = (width // devices, 4 * width)
    inner = None
    scratch, total = [], 0
    if own_block[0] % 16 == 0:
        whole = tuple(sizes[d] for d in SLOTS)
        more, inner, needed, left = stage_buffers(sizes, own_block, bf16, SLOTS, "cx")
        inner_more = more
        total += needed
        ins += [normed_own, dq_before, d_out.reshape(whole + (own_block[0], width))]
        in_specs += [vmem] * 3
        last_shape = jax.ShapeDtypeStruct(tuple(sizes[d] for d in left) + own_block, bf16)
    else:
        last_shape = jax.ShapeDtypeStruct((length, double), bf16)
    tasks_info, shapes, later = [], [], []
    for grad, order, widths in zip(grads, orders, splits):
        block = grad.shape[-2:]
        dims = ("x", "z", "y")
        more, counts, needed, left = stage_buffers(sizes, block, grad.dtype, dims, order)
        scratch += more
        total += needed
        ends, widths = cut_shapes(block, left, widths, sizes, grad.dtype)
        shapes += ends
        later.append(widths)
        tasks_info.append((order, dims, counts, len(ends)))
        ins.append(grad)
        in_specs.append(vmem)
    head_shapes = [
        jax.ShapeDtypeStruct((seqs, rows, width), f32),
        jax.ShapeDtypeStruct((rows, width), bf16),
        jax.ShapeDtypeStruct((pairs, 2, 5, 8, 2 * rows), f32),
    ]
    own_scratch = []
    if inner:
        own_scratch = [pltpu.VMEM(whole + own_block, bf16), pltpu.VMEM((length, double), bf16)]
        scratch = scratch + inner_more
    block = (seqs, n, fast, rows, width)
    own_scratch += [
        pltpu.VMEM((length, double), bf16),
        pltpu.VMEM((2, step, double), bf16),
        pltpu.VMEM((2, step, width), bf16),
        pltpu.VMEM(block, bf16),
        pltpu.VMEM((seqs, fast - 1, n, rows, width), bf16),
        pltpu.VMEM((seqs, 2, n, rows, width), bf16),
        pltpu.VMEM((2, 5, rows, rows), f32),
        pltpu.VMEM((2, 5, rows, rows), f32),
        pltpu.VMEM((2, width // pairs, rows), f32),
        pltpu.VMEM((width, double), f32) if inner else pltpu.VMEM((8, 128), f32),
    ]
    total += seqs * ((fast - 1) * n + 2 * n)
    outs = pl.pallas_call(
        functools.partial(back_rows_kernel, sizes, rows, tasks_info, inner),
        in_specs=in_specs,
        out_specs=[vmem] * (len(shapes) + 4),
        out_shape=head_shapes + shapes + [last_shape],
        scratch_shapes=own_scratch
        + scratch
        + [
            pltpu.SemaphoreType.DMA,
            pltpu.SemaphoreType.DMA((2,)),
            pltpu.SemaphoreType.DMA((2,)),
            pltpu.SemaphoreType.DMA((total,)),
            pltpu.SemaphoreType.DMA((total,)),
        ],
        compiler_params=pltpu.CompilerParams(
            collective_id=collective_id, has_side_effects=True, vmem_limit_bytes=62 << 20
        ),
        name=name,
    )(*ins)
    outs = list(outs)
    heads = [outs.pop(0) for _ in range(3)]
    results = []
    for (_, _, _, cut), widths in zip(tasks_info, later):
        results.append(cut_columns([outs.pop(0) for _ in range(cut)], widths))
    return heads + results + [outs[0], inner is not None]


def on_device(
    inputs,
    lengths,
    conv_taps,
    gain_attn,
    w_proj,
    w_query,
    w_key,
    w_value,
    w_out,
    gain_ffn,
    w_gate,
    w_up,
    w_down,
    rel_bias,
    cotangent,
):
    batch, seq = lax.axis_size("batch"), lax.axis_size("seq")
    sizes = layout_of(batch, seq)
    devices = batch * seq
    seqs, rows, width = inputs.shape
    length = rows * seq
    count = seqs * rows
    own = w_proj.shape[0]
    own_bias = rel_bias.shape[0]
    heads = own_bias * devices // NB
    hidden = w_gate.shape[1]

    small = jnp.concatenate(
        [
            conv_taps,
            gain_attn[:, None],
            gain_ffn[:, None],
            jnp.pad(rel_bias, (0, own - own_bias))[:, None],
            jnp.zeros((own, PACK - TAPS - 3), jnp.bfloat16),
        ],
        axis=1,
    )
    pairs = heads // 2
    key_value_w = jnp.stack([w_key.reshape(own, pairs, -1), w_value.reshape(own, pairs, -1)], axis=2)
    first, second, outer_plane, down_plane, left_rim = gather_all(
        [
            jnp.concatenate([small, w_proj, w_query], axis=1),
            key_value_w.reshape(own, -1),
            jnp.concatenate([w_out, w_gate, w_up], axis=1),
            w_down,
        ],
        ["Zyxc", "Zxyc", "zy", "yz"],
        sizes,
        1,
        rim=inputs[:, rows - 16 :, :],
        name="gather_first",
    )
    first = first.reshape(width, -1)
    second = second.reshape(width, -1)
    taps = first[:, :TAPS].astype(jnp.float32)
    gain_first = first[:, TAPS].astype(jnp.float32)
    gain_second = first[:, TAPS + 1].astype(jnp.float32)
    table = first[:, TAPS + 2].reshape(devices, own)[:, :own_bias].reshape(heads, NB).astype(jnp.float32)
    proj_w = first[:, PACK : PACK + width]
    query_w = first[:, PACK + width :]

    padded = jnp.concatenate([left_rim[:, 13:], inputs], axis=1).astype(jnp.float32)
    mixed_conv, conv_back = jax.vjp(partial(conv_mix, row_count=rows), padded, taps)
    mixed_low = mixed_conv.astype(jnp.bfloat16).reshape(count, width)
    resid_in = inputs.astype(jnp.float32).reshape(count, width)
    hidden_one = resid_in + mat_dot(mixed_low, proj_w)
    normed_one, norm_one_back = jax.vjp(norm_rows, hidden_one, gain_first)
    normed_low = normed_one.astype(jnp.bfloat16)

    outer_w, down_w, normed_all = gather_all(
        [outer_plane, down_plane],
        ["xc", "xc"],
        sizes,
        2,
        rows=normed_low.reshape(seqs, rows, width),
        plan=(0, 1, 2, 2, 2, 2),
        name="gather_rows",
    )
    outer_w = outer_w.reshape(width, -1)
    down_w = down_w.reshape(hidden, -1)
    out_w = outer_w[:, :width]
    wide_w = outer_w[:, width:]
    normed_all = normed_all.reshape(seqs * length, width)
    queries = mat_dot(normed_low, query_w).astype(jnp.bfloat16)
    key_value = mat_dot(normed_all, second).astype(jnp.bfloat16).reshape(seqs, length, 2 * width)

    far, diag = bias_tables(table, rows)
    info = jnp.concatenate([lengths, lax.axis_index("seq")[None].astype(jnp.int32)])
    attended, attended_full, inverse, peak = attend(info, far, diag, queries, key_value, rows, length)

    hidden_two = hidden_one + mat_dot(attended, out_w)
    normed_two, norm_two_back = jax.vjp(norm_rows, hidden_two, gain_second)
    normed_two_low = normed_two.astype(jnp.bfloat16)
    both_pre = mat_dot(normed_two_low, wide_w)
    inner_act, inner_back = jax.vjp(gated, both_pre[:, :hidden], both_pre[:, hidden:])
    inner_low = inner_act.astype(jnp.bfloat16)
    layer_out = (hidden_two + mat_dot(inner_low, down_w)).astype(jnp.bfloat16).reshape(seqs, rows, width)

    grad_low = cotangent.reshape(count, width)
    d_down_w = outer_sum(inner_low, grad_low).astype(jnp.bfloat16)
    d_gate, d_up = inner_back(back_dot(grad_low, down_w))
    d_both = jnp.concatenate([d_gate.astype(jnp.bfloat16), d_up.astype(jnp.bfloat16)], axis=1)
    d_wide_w = outer_sum(normed_two_low, d_both).astype(jnp.bfloat16)
    d_hidden_part, d_gain_two = norm_two_back(back_dot(d_both, wide_w))
    d_hidden_two = grad_low.astype(jnp.float32) + d_hidden_part
    d_attn_low = d_hidden_two.astype(jnp.bfloat16)
    d_out_w = outer_sum(attended, d_attn_low).astype(jnp.bfloat16)
    d_attended = back_dot(d_attn_low, out_w).astype(jnp.bfloat16)
    scaled = (d_attended.astype(jnp.float32) * inverse).astype(jnp.bfloat16)
    wide_half, down_half = halve_cores([d_wide_w, d_down_w], sizes, 4)
    early = seqs - 1
    dq_before, dkv_before, near_before = attend_back(
        info, far, diag, queries, scaled, attended_full, key_value, peak, rows, length, early
    )
    d_normed_one, dq_last, near, (g_gate, g_up), (g_down,), last, joined = back_rows(
        info,
        far,
        diag,
        queries,
        scaled,
        attended_full,
        key_value,
        peak,
        dkv_before,
        normed_all,
        normed_low,
        second,
        dq_before,
        d_out_w,
        [wide_half, down_half],
        ["xzy", "xzy"],
        [(hidden, hidden), None],
        sizes,
        rows,
        5,
    )
    d_table = bias_grad(near_before + near, rows).reshape(heads * NB)
    d_queries = jnp.concatenate([dq_before, dq_last], axis=0)
    if joined:
        inner, inner_order = last, "s"
    else:
        d_key_value = jnp.concatenate([dkv_before, last[None]], axis=0).reshape(seqs * length, 2 * width)
        d_second_w = outer_sum(normed_all, d_key_value).astype(jnp.bfloat16)
        d_query_w = outer_sum(normed_low, d_queries).astype(jnp.bfloat16)
        inner, inner_order = jnp.concatenate([d_query_w, d_out_w, d_second_w], axis=1), "cxs"
    d_normed_one = d_normed_one.reshape(count, width)
    d_normed_one = d_normed_one + back_dot(d_queries, query_w)
    d_first_part, d_gain_one = norm_one_back(d_normed_one)
    d_hidden_one = d_hidden_two + d_first_part
    d_mix_low = d_hidden_one.astype(jnp.bfloat16)
    d_proj_w = outer_sum(mixed_low, d_mix_low).astype(jnp.bfloat16)
    d_mixed = back_dot(d_mix_low, proj_w).reshape(seqs, rows, width)
    d_padded, d_taps = conv_back(d_mixed)
    d_inputs = d_hidden_one.reshape(seqs, rows, width) + d_padded[:, 3:, :]
    d_small = jnp.concatenate(
        [
            d_taps.T,
            d_gain_one[None],
            d_gain_two[None],
            jnp.pad(d_table.reshape(devices, own_bias), ((0, 0), (0, own - own_bias))).reshape(1, width),
            jnp.zeros((16 - TAPS - 3, width), jnp.float32),
        ],
        axis=0,
    )
    d_last = jnp.concatenate([d_proj_w, jnp.pad(d_small.T, ((0, 0), (0, PACK - 16))).astype(jnp.bfloat16)], axis=1)
    (g_proj, g_small), (g_query, g_out, g_second), spill = reduce_all(
        [d_last, inner],
        ["cxs", inner_order],
        sizes,
        6,
        spill=d_padded[:, :8, :],
        splits=[(width, PACK), (width, width, 2 * width)],
    )
    input_grad = d_inputs.at[:, rows - 3 :, :].add(spill[:, :3]).astype(jnp.bfloat16)
    g_second = g_second.reshape(own, pairs, 2, -1)
    return (
        layer_out,
        input_grad,
        g_small[:, :TAPS],
        g_small[:, TAPS],
        g_proj,
        g_query,
        g_second[:, :, 0].reshape(own, width),
        g_second[:, :, 1].reshape(own, width),
        g_out,
        g_small[:, TAPS + 1],
        g_gate,
        g_up,
        g_down.reshape(w_down.shape),
        g_small[:own_bias, TAPS + 2],
    )


def solution(mesh):
    in_specs = (
        P("batch", "seq", None),
        P("batch"),
        P(("batch", "seq"), None),
        P(("batch", "seq")),
        P(("batch", "seq"), None),
        P(("batch", "seq"), None),
        P(("batch", "seq"), None),
        P(("batch", "seq"), None),
        P(("batch", "seq"), None),
        P(("batch", "seq")),
        P(("batch", "seq"), None),
        P(("batch", "seq"), None),
        P(("batch", "seq"), None),
        P(("batch", "seq")),
        P("batch", "seq", None),
    )
    out_specs = (
        P("batch", "seq", None),
        P("batch", "seq", None),
        P(("batch", "seq"), None),
        P(("batch", "seq")),
        P(("batch", "seq"), None),
        P(("batch", "seq"), None),
        P(("batch", "seq"), None),
        P(("batch", "seq"), None),
        P(("batch", "seq"), None),
        P(("batch", "seq")),
        P(("batch", "seq"), None),
        P(("batch", "seq"), None),
        P(("batch", "seq"), None),
        P(("batch", "seq")),
    )
    return jax.shard_map(
        on_device, mesh=mesh, in_specs=in_specs, out_specs=out_specs, check_vma=False
    )
```

```python
import functools
from functools import partial

import jax
import jax.numpy as jnp
import numpy as np
from jax import lax
from jax.experimental import pallas as pl
from jax.experimental.pallas import tpu as pltpu
from jax.sharding import PartitionSpec as P

NB = 32
EPSILON = 1e-06
LIMITS = (12, 16, 23, 32, 46, 64, 91)
WINDOWS = ((2, 0), (3, 2), (4, 5))
TAPS = 9
PACK = 128
SPAN = 8

def mat_dot(lhs_array, rhs_array):
    return jnp.dot(lhs_array, rhs_array, preferred_element_type=jnp.float32)


def outer_sum(lhs_array, rhs_array):
    return lax.dot_general(
        lhs_array, rhs_array, (((0,), (0,)), ((), ())), preferred_element_type=jnp.float32
    )


def back_dot(grad_rows, weight):
    return lax.dot_general(
        grad_rows, weight, (((1,), (1,)), ((), ())), preferred_element_type=jnp.float32
    )


def bucket_of(relative):
    distance = jnp.abs(relative)
    larger = jnp.full(relative.shape, 8, jnp.int32)
    for threshold in LIMITS:
        larger = larger + (distance >= threshold).astype(jnp.int32)
    inside = jnp.where(distance < 8, distance, larger)
    return inside + 16 * (relative > 0).astype(jnp.int32)


def norm_rows(hidden, gain_row):
    return (
        hidden * lax.rsqrt(jnp.mean(hidden * hidden, axis=-1, keepdims=True) + EPSILON) * gain_row
    )


def gated(gate_pre, up_pre):
    return jax.nn.gelu(gate_pre, approximate=True) * up_pre


def conv_mix(padded, taps, row_count):
    summed = jnp.zeros(padded.shape[:-2] + (row_count, padded.shape[-1]), jnp.float32)
    for window_len, offset in WINDOWS:
        conv_sum = jnp.zeros_like(summed)
        for tap_index in range(window_len):
            shifted = lax.slice_in_dim(
                padded, 3 - tap_index, 3 - tap_index + row_count, axis=padded.ndim - 2
            )
            conv_sum = conv_sum + taps[:, offset + tap_index] * shifted
        summed = summed + jax.nn.gelu(conv_sum, approximate=True)
    return summed


def near_offsets(rows):
    lane = np.arange(2 * rows)
    lane = np.where(lane < rows, lane, lane - 2 * rows)
    return rows * (np.arange(3)[:, None, None] - 1) + np.arange(8)[None, :, None] - lane[None, None, :]


def bias_tables(table, rows):
    heads = table.shape[0]
    buckets = bucket_of(jnp.asarray(near_offsets(rows)[:, 0, :], jnp.int32)).reshape(-1)
    onehot = (buckets[None, :] == jnp.arange(NB, dtype=jnp.int32)[:, None]).astype(jnp.float32)
    diag = jnp.dot(table, onehot, precision=lax.Precision.HIGHEST)
    far = jnp.stack([table[:, NB // 2 - 1], table[:, NB - 1]], axis=1)
    return far, diag.reshape(heads // 2, 6, 2 * rows)


def bias_grad(near, rows):
    near = near.reshape(near.shape[0] * 2, 5, 8, 2 * rows)
    buckets = bucket_of(jnp.asarray(near_offsets(rows), jnp.int32))
    hit = buckets[None] == jnp.arange(NB, dtype=jnp.int32)[:, None, None, None]
    grad = jnp.sum(jnp.where(hit[None], near[:, None, 1:4], 0.0), axis=(2, 3, 4))
    left = jnp.sum(near[:, 0], axis=(1, 2))
    right = jnp.sum(near[:, 4], axis=(1, 2))
    return grad.at[:, NB // 2 - 1].add(left).at[:, NB - 1].add(right)


def nt_dot(a, b):
    return lax.dot_general(a, b, (((1,), (1,)), ((), ())), preferred_element_type=jnp.float32)


def tn_dot(a, b):
    return lax.dot_general(a, b, (((0,), (0,)), ((), ())), preferred_element_type=jnp.float32)


def nn_dot(a, b):
    return lax.dot_general(a, b, (((1,), (0,)), ((), ())), preferred_element_type=jnp.float32)


def fill_bias(rows, far_ref, diag_ref, bias_ref, pair):
    for a in range(2):
        bias_ref[a, 0] = jnp.full((rows, rows), far_ref[2 * pair + a, 0], jnp.float32)
        bias_ref[a, 4] = jnp.full((rows, rows), far_ref[2 * pair + a, 1], jnp.float32)
        for c in range(3):
            base = jnp.broadcast_to(diag_ref[0, 3 * a + c : 3 * a + c + 1, :], (rows, 2 * rows))
            bias_ref[a, 1 + c] = pltpu.roll(base, 0, 1, stride=1, stride_axis=0)[:, :rows]


def head_halves(block):
    lane = lax.broadcasted_iota(jnp.int32, block.shape, 1)
    zero = jnp.zeros_like(block)
    half = block.shape[1] // 2
    return jnp.where(lane < half, block, zero), jnp.where(lane < half, zero, block)


def attend_kernel(
    rows, info_ref, far_ref, diag_ref, q_ref, k_ref, v_ref, o_ref, full_ref, inv_ref, peak_ref, bias_ref, s_ref, acc_ref
):
    pair, b = pl.program_id(0), pl.program_id(1)

    @pl.when(b == 0)
    def _():
        fill_bias(rows, far_ref, diag_ref, bias_ref, pair)

    length, first = info_ref[b], info_ref[pl.num_programs(1)]
    count = lax.div(length + rows - 1, rows)
    halves = head_halves(q_ref[...])
    wide = q_ref.shape[1]
    half = wide // 2
    key_row = lax.broadcasted_iota(jnp.int32, (rows, rows), 0)

    def scores(kc, peaks):
        k = k_ref[0, pl.ds(kc * rows, SPAN * rows), :]
        new = list(peaks)
        for a in range(2):
            full = nt_dot(k, halves[a])
            for u in range(SPAN):
                slot = jnp.clip(kc + u - first + 2, 0, 4)
                valid = key_row < length - (kc + u) * rows
                s = full[u * rows : (u + 1) * rows] + bias_ref[a, slot]
                s = jnp.where(valid, s, -1e9)
                s_ref[a, pl.ds((kc + u) * rows, rows), :] = s
                new[a] = jnp.maximum(new[a], jnp.max(s.reshape(rows // 8, 8, rows), axis=0))
        return tuple(new)

    low = jnp.full((8, rows), -jnp.inf, jnp.float32)
    spans = lax.div(count + SPAN - 1, SPAN)
    peaks = lax.fori_loop(0, spans, lambda i, p: scores(i * SPAN, p), (low, low))
    peaks = [jnp.max(p, axis=0, keepdims=True) for p in peaks]
    acc_ref[...] = jnp.zeros_like(acc_ref)
    lane = lax.broadcasted_iota(jnp.int32, (SPAN * rows, wide), 1)

    def weigh(i, carry):
        here = pl.ds(i * SPAN * rows, SPAN * rows)
        v = v_ref[0, here, :]
        ones = jnp.ones_like(v)
        for a, v_one in enumerate((jnp.where(lane < half, v, ones), jnp.where(lane < half, ones, v))):
            e = jnp.exp(s_ref[a, here, :] - peaks[a])
            acc_ref[a] += tn_dot(v_one, e.astype(jnp.bfloat16))
        return carry

    lax.fori_loop(0, spans, weigh, 0)
    inv = jnp.concatenate([1.0 / acc_ref[0, half:], 1.0 / acc_ref[1, :half]], axis=0)
    out = jnp.concatenate([acc_ref[0, :half], acc_ref[1, half:]], axis=0) * inv
    out = out.T
    o_ref[...] = out.astype(o_ref.dtype)
    full_ref[...] = out
    inv_ref[...] = inv.T
    for a in range(2):
        peak_ref[0, 0, a : a + 1, :] = peaks[a]


def attention_cost(q, kv, products):
    flops = products * 8 * q.shape[0] * kv.shape[1] * q.shape[1]
    return pl.CostEstimate(
        flops=flops, bytes_accessed=2 * (q.size + kv.size) * products, transcendentals=8 * q.shape[0] * kv.shape[1]
    )


def attend(info, far, diag, q, kv, rows, length):
    heads = far.shape[0]
    seqs = kv.shape[0]
    wide = 2 * (q.shape[1] // heads)
    pairs = heads // 2
    smem = pl.BlockSpec(memory_space=pltpu.SMEM)
    return pl.pallas_call(
        functools.partial(attend_kernel, rows),
        grid=(pairs, seqs),
        in_specs=[
            smem, smem,
            pl.BlockSpec((1, 6, 2 * rows), lambda p, b: (p, 0, 0)),
            pl.BlockSpec((rows, wide), lambda p, b: (b, p)),
            pl.BlockSpec((1, length, wide), lambda p, b: (b, 0, 2 * p)),
            pl.BlockSpec((1, length, wide), lambda p, b: (b, 0, 2 * p + 1)),
        ],
        out_specs=[pl.BlockSpec((rows, wide), lambda p, b: (b, p))] * 3
        + [pl.BlockSpec((1, 1, 2, rows), lambda p, b: (b, p, 0, 0))],
        out_shape=[
            jax.ShapeDtypeStruct(q.shape, jnp.bfloat16),
            jax.ShapeDtypeStruct(q.shape, jnp.float32),
            jax.ShapeDtypeStruct(q.shape, jnp.float32),
            jax.ShapeDtypeStruct((seqs, pairs, 2, rows), jnp.float32),
        ],
        scratch_shapes=[
            pltpu.VMEM((2, 5, rows, rows), jnp.float32),
            pltpu.VMEM((2, length, rows), jnp.float32),
            pltpu.VMEM((2, wide, rows), jnp.float32),
        ],
        compiler_params=pltpu.CompilerParams(vmem_limit_bytes=48 << 20),
        cost_estimate=attention_cost(q, kv, 2),
        name="attend",
    )(info, far, diag, q, kv, kv)


def back_pair(rows, length, first, q, g, full, key_value, peak, bias_ref, sum_ref, acc_ref, write):
    q_half, g_half = head_halves(q), head_halves(g)
    wide = q.shape[1]
    half = wide // 2
    key_row = lax.broadcasted_iota(jnp.int32, (rows, rows), 0)
    acc_ref[...] = jnp.zeros_like(acc_ref)
    along = (g.astype(jnp.float32) * full).T
    delta = [jnp.sum(along[a * half : (a + 1) * half], axis=0, keepdims=True) for a in range(2)]
    keys, spans = key_value

    def step(i, carry):
        kc = i * SPAN
        here = pl.ds(kc * rows, SPAN * rows)
        k, v = keys(here)
        dk = dv = None
        for a in range(2):
            s = nt_dot(k, q_half[a])
            dp = nt_dot(v, g_half[a])
            es, dss = [], []
            for u in range(SPAN):
                part = slice(u * rows, (u + 1) * rows)
                slot = jnp.clip(kc + u - first + 2, 0, 4)
                valid = key_row < length - (kc + u) * rows
                e = jnp.exp(s[part] + bias_ref[a, slot] - peak[a])
                e_low = jnp.where(valid, e, 0.0).astype(jnp.bfloat16)
                ds = e_low.astype(jnp.float32) * (dp[part] - delta[a])
                sum_ref[a, slot] += ds
                es.append(e_low)
                dss.append(ds.astype(jnp.bfloat16))
            e_low, ds_low = jnp.concatenate(es, axis=0), jnp.concatenate(dss, axis=0)
            dv_a = nn_dot(e_low, g_half[a])
            dk_a = nn_dot(ds_low, q_half[a])
            dv = dv_a if dv is None else dv + dv_a
            dk = dk_a if dk is None else dk + dk_a
            acc_ref[a] += tn_dot(k, ds_low)
        write(here, dk.astype(jnp.bfloat16), dv.astype(jnp.bfloat16))
        return carry

    if spans == 1:
        step(0, 0)
    else:
        lax.fori_loop(0, spans, step, 0)
    return jnp.concatenate([acc_ref[0, :half], acc_ref[1, half:]], axis=0).T.astype(jnp.bfloat16)


def near_sums(rows, sum_ref, write):
    for a in range(2):
        for slot in range(5):
            total_sum = jnp.zeros((8, 2 * rows), jnp.float32)
            for g in range(rows // 8):
                part = jnp.concatenate(
                    [sum_ref[a, slot, 8 * g : 8 * g + 8, :], jnp.zeros((8, rows), jnp.float32)], axis=1
                )
                if g and 0 < slot < 4:
                    part = pltpu.roll(part, 2 * rows - 8 * g, 1)
                total_sum = total_sum + part
            write(a, slot, total_sum)


def attend_back_kernel(rows, info_ref, far_ref, diag_ref, q_ref, g_ref, full_ref, k_ref, v_ref, peak_ref,
                       dq_ref, dkv_ref, near_ref, bias_ref, sum_ref, acc_ref):
    pair, b = pl.program_id(0), pl.program_id(1)

    @pl.when(b == 0)
    def _():
        fill_bias(rows, far_ref, diag_ref, bias_ref, pair)
        sum_ref[...] = jnp.zeros_like(sum_ref)

    wide = q_ref.shape[1]

    def write(here, dk, dv):
        dkv_ref[0, here, :wide] = dk
        dkv_ref[0, here, wide:] = dv

    dq_ref[...] = back_pair(
        rows,
        info_ref[b],
        info_ref[info_ref.shape[0] - 1],
        q_ref[...],
        g_ref[...],
        full_ref[...],
        (lambda here: (k_ref[0, here, :], v_ref[0, here, :]), k_ref.shape[1] // (SPAN * rows)),
        [peak_ref[0, 0, a : a + 1, :] for a in range(2)],
        bias_ref,
        sum_ref,
        acc_ref,
        write,
    )

    @pl.when(b == pl.num_programs(1) - 1)
    def _():
        def keep(a, slot, value):
            near_ref[0, a, slot] = value

        near_sums(rows, sum_ref, keep)


def attend_back(info, far, diag, q, g, full, kv, peak, rows, length, seqs):
    heads = far.shape[0]
    wide = 2 * (q.shape[1] // heads)
    pairs = heads // 2
    smem = pl.BlockSpec(memory_space=pltpu.SMEM)
    row_spec = pl.BlockSpec((rows, wide), lambda p, b: (b, p))
    return pl.pallas_call(
        functools.partial(attend_back_kernel, rows),
        grid=(pairs, seqs),
        in_specs=[
            smem,
            smem,
            pl.BlockSpec((1, 6, 2 * rows), lambda p, b: (p, 0, 0)),
            row_spec,
            row_spec,
            row_spec,
            pl.BlockSpec((1, length, wide), lambda p, b: (b, 0, 2 * p)),
            pl.BlockSpec((1, length, wide), lambda p, b: (b, 0, 2 * p + 1)),
            pl.BlockSpec((1, 1, 2, rows), lambda p, b: (b, p, 0, 0)),
        ],
        out_specs=[
            row_spec,
            pl.BlockSpec((1, length, 2 * wide), lambda p, b: (b, 0, p)),
            pl.BlockSpec((1, 2, 5, 8, 2 * rows), lambda p, b: (p, 0, 0, 0, 0)),
        ],
        out_shape=[
            jax.ShapeDtypeStruct((seqs * rows, q.shape[1]), jnp.bfloat16),
            jax.ShapeDtypeStruct((seqs,) + kv.shape[1:], jnp.bfloat16),
            jax.ShapeDtypeStruct((pairs, 2, 5, 8, 2 * rows), jnp.float32),
        ],
        scratch_shapes=[
            pltpu.VMEM((2, 5, rows, rows), jnp.float32),
            pltpu.VMEM((2, 5, rows, rows), jnp.float32),
            pltpu.VMEM((2, wide, rows), jnp.float32),
        ],
        compiler_params=pltpu.CompilerParams(vmem_limit_bytes=48 << 20),
        cost_estimate=attention_cost(q, kv, 3),
        name="attend_back",
    )(info, far, diag, q, g, full, kv, kv, peak)


SLOTS = ("x", "c", "z", "y")
MESH = pl.DeviceIdType.MESH


def layout_of(batch, seq):
    fast = 1 << ((seq.bit_length() - 1) // 2)
    return {"x": batch // 2, "c": 2, "z": seq // fast, "y": fast}


def tile_block(rows, cols):
    return (rows, cols) if rows % 16 == 0 else (rows * cols // 128, 128)


def place(sizes):
    b, s = lax.axis_index("batch"), lax.axis_index("seq")
    return {
        "x": lax.div(b, 2),
        "c": lax.rem(b, 2),
        "z": lax.div(s, sizes["y"]),
        "y": lax.rem(s, sizes["y"]),
    }


def device_at(sizes, me, dim, at):
    spot = dict(me)
    spot[dim] = at
    return (spot["x"] * 2 + spot["c"], spot["z"] * sizes["y"] + spot["y"])


def seq_peer(sizes, me, k):
    n = sizes["z"] * sizes["y"]
    return (me["x"] * 2 + me["c"], lax.rem(me["z"] * sizes["y"] + me["y"] + k, n))


def greet(sizes, me, dims):
    barrier = pltpu.get_barrier_semaphore()
    total = 0
    if "s" in dims:
        total = sizes["z"] * sizes["y"] - 1
        for k in range(1, total + 1):
            pl.semaphore_signal(barrier, inc=1, device_id=seq_peer(sizes, me, k), device_id_type=MESH)
        dims = [d for d in dims if d not in "szy"]
    for dim in dims:
        for k in range(1, sizes[dim]):
            peer = device_at(sizes, me, dim, lax.rem(me[dim] + k, sizes[dim]))
            pl.semaphore_signal(barrier, inc=1, device_id=peer, device_id_type=MESH)
            total += 1
    pl.semaphore_wait(barrier, total)


class Sems:
    def __init__(self, send, recv):
        self.send, self.recv, self.used = send, recv, 0

    def take(self, count):
        first = self.used
        self.used += count
        assert self.used <= self.send.shape[0]
        return first

    def copy(self, src, dst, index, device):
        return pltpu.make_async_remote_copy(
            src_ref=src, dst_ref=dst, send_sem=self.send.at[index], recv_sem=self.recv.at[index],
            device_id=device, device_id_type=MESH,
        )


def run_together(tasks, plan=()):
    tasks = list(tasks)
    over_already = set()
    for i in plan:
        if i not in over_already:
            try:
                next(tasks[i])
            except StopIteration:
                over_already.add(i)
    tasks = [t for i, t in enumerate(tasks) if i not in over_already]
    while tasks:
        left = []
        for task in tasks:
            try:
                next(task)
                left.append(task)
            except StopIteration:
                pass
        tasks = left


def gather_task(sizes, me, src, out, local_sem, sems, order):
    before = list(SLOTS[len(SLOTS) - (len(src.shape) - 2) :])
    dims = [d for d in SLOTS if d in order.lower() or d in before]
    own = pltpu.make_async_copy(src, out.at[tuple(me[d] for d in dims if d not in before)], local_sem)
    own.start()
    own.wait()
    done = before
    sent = []
    for dim in order:
        direct, dim = dim.isupper(), dim.lower()
        n, at = sizes[dim], me[dim]

        def region(origin):
            spots = []
            for d in dims:
                spots.append(slice(None) if d in done else (origin if d == dim else me[d]))
            return out.at[tuple(spots)]

        if n == 2:
            base = sems.take(1)
            other = 1 - at
            send = sems.copy(region(at), region(at), base, device_at(sizes, me, dim, other))
            send.start()
            yield
            sems.copy(region(other), region(other), base, device_at(sizes, me, dim, other)).wait_recv()
            sent.append((None, send))
        elif direct:
            base = sems.take(n - 1)
            for k in range(1, n):
                peer = device_at(sizes, me, dim, lax.rem(at + k, n))
                send = sems.copy(region(at), region(at), base + k - 1, peer)
                send.start()
                sent.append((None, send))
            yield
            for k in range(1, n):
                origin = lax.rem(at + n - k, n)
                sems.copy(region(origin), region(origin), base + k - 1, device_at(sizes, me, dim, origin)).wait_recv()
        else:
            for t in range(n - 1):
                base = sems.take(2)
                to_right = (at + 1 < n) & (at - t >= 0)
                to_left = (at >= 1) & (at + t < n)
                from_left = (at >= 1) & (at - 1 - t >= 0)
                from_right = (at + 1 < n) & (at + 1 + t < n)
                right = sems.copy(region(at - t), region(at - t), base, device_at(sizes, me, dim, at + 1))
                left = sems.copy(region(at + t), region(at + t), base + 1, device_at(sizes, me, dim, at - 1))
                pl.when(to_right)(right.start)
                pl.when(to_left)(left.start)
                sent += [(to_right, right), (to_left, left)]
                yield
                got = sems.copy(region(at - 1 - t), region(at - 1 - t), base, device_at(sizes, me, dim, at - 1))
                pl.when(from_left)(got.wait_recv)
                got = sems.copy(region(at + 1 + t), region(at + 1 + t), base + 1, device_at(sizes, me, dim, at + 1))
                pl.when(from_right)(got.wait_recv)
        done.append(dim)
    for cond, send in sent:
        if cond is None:
            send.wait_send()
        else:
            pl.when(cond)(send.wait_send)


def spread_task(sizes, me, src, out, local_sem, sems):
    z, y, n, fast = me["z"], me["y"], sizes["z"], sizes["y"]
    own = pltpu.make_async_copy(src, out.at[:, z, y], local_sem)
    own.start()
    own.wait()
    fan = sems.take((fast - 1) * n)

    def fan_copy(k, origin, owner):
        peer = device_at(sizes, me, "y", lax.rem(y + k, fast))
        spot = out.at[:, origin, owner]
        return sems.copy(spot, spot, fan + (k - 1) * n + origin, peer)

    def fan_out(origin):
        for k in range(1, fast):
            fan_copy(k, origin, y).start()

    fan_out(z)
    sent = []
    for t in range(n - 1):
        base = sems.take(2)
        to_right = (z + 1 < n) & (z - t >= 0)
        to_left = (z >= 1) & (z + t < n)
        from_left = (z >= 1) & (z - 1 - t >= 0)
        from_right = (z + 1 < n) & (z + 1 + t < n)
        right = sems.copy(out.at[:, z - t, y], out.at[:, z - t, y], base, device_at(sizes, me, "z", z + 1))
        left = sems.copy(out.at[:, z + t, y], out.at[:, z + t, y], base + 1, device_at(sizes, me, "z", z - 1))
        pl.when(to_right)(right.start)
        pl.when(to_left)(left.start)
        sent += [(to_right, right), (to_left, left)]
        yield

        @pl.when(from_left)
        def _():
            spot = out.at[:, z - 1 - t, y]
            sems.copy(spot, spot, base, device_at(sizes, me, "z", z - 1)).wait_recv()
            fan_out(z - 1 - t)

        @pl.when(from_right)
        def _():
            spot = out.at[:, z + 1 + t, y]
            sems.copy(spot, spot, base + 1, device_at(sizes, me, "z", z + 1)).wait_recv()
            fan_out(z + 1 + t)

    yield
    for k in range(1, fast):
        for origin in range(n):
            fan_copy(k, origin, lax.rem(y + fast - k, fast)).wait_recv()
    for k in range(1, fast):
        for origin in range(n):
            fan_copy(k, origin, y).wait_send()
    for cond, send in sent:
        pl.when(cond)(send.wait_send)


def shift_task(sizes, me, src, out, sems, step):
    n = sizes["z"] * sizes["y"]
    s = me["z"] * sizes["y"] + me["y"]
    base = sems.take(1)
    send = sems.copy(src, out, base, seq_peer(sizes, me, step % n))
    has_to = (s < n - 1) if step > 0 else (s > 0)
    has_from = (s > 0) if step > 0 else (s < n - 1)
    pl.when(has_to)(send.start)
    yield
    pl.when(has_from)(send.wait_recv)

    @pl.when(jnp.logical_not(has_from))
    def _():
        out[...] = jnp.zeros_like(out)

    yield
    pl.when(has_to)(send.wait_send)


def stage_count(sizes, order):
    return sum(1 if sizes[d] == 2 else 2 * (sizes[d] - 1) for d in order.lower())


def gather_kernel(sizes, orders, has_rows, has_rim, plan, *refs):
    count = len(orders)
    total = count + has_rows + has_rim
    ins, outs = refs[:total], refs[total : 2 * total]
    local_sem, send_sem, recv_sem = refs[2 * total :]
    me = place(sizes)
    used = [d for d in SLOTS if any(d in o.lower() for o in orders) or (has_rows and d in "zy")]
    greet(sizes, me, used + ["s"] * has_rim)
    sems = Sems(send_sem, recv_sem)
    tasks = []
    for i in range(count):
        tasks.append(gather_task(sizes, me, ins[i], outs[i], local_sem.at[i], sems, orders[i]))
    if has_rows:
        tasks.append(spread_task(sizes, me, ins[count], outs[count], local_sem.at[count], sems))
    if has_rim:
        tasks.append(shift_task(sizes, me, ins[-1], outs[-1], sems, 1))
    run_together(tasks, plan)


def gather_all(shards, orders, sizes, collective_id, rows=None, rim=None, plan=(), name="gather"):
    ins, shapes, out_specs = [], [], []
    for shard, order in zip(shards, orders):
        ins.append(shard if shard.ndim > 2 else shard.reshape(tile_block(*shard.shape)))
        before = SLOTS[len(SLOTS) - (ins[-1].ndim - 2) :]
        whole = tuple(sizes[d] for d in SLOTS if d in order.lower() or d in before)
        shapes.append(jax.ShapeDtypeStruct(whole + ins[-1].shape[-2:], shard.dtype))
    total = sum(stage_count(sizes, o) for o in orders)
    out_specs = [pl.BlockSpec(memory_space=pl.ANY)] * len(ins)
    if rows is not None:
        ins.append(rows)
        shapes.append(jax.ShapeDtypeStruct((rows.shape[0], sizes["z"], sizes["y"]) + rows.shape[1:], rows.dtype))
        out_specs.append(pl.BlockSpec(memory_space=pl.ANY))
        total += (sizes["y"] - 1) * sizes["z"] + 2 * (sizes["z"] - 1)
    if rim is not None:
        ins.append(rim)
        shapes.append(jax.ShapeDtypeStruct(rim.shape, rim.dtype))
        out_specs.append(pl.BlockSpec(memory_space=pltpu.VMEM))
        total += 1
    return pl.pallas_call(
        functools.partial(gather_kernel, sizes, orders, int(rows is not None), int(rim is not None), plan),
        in_specs=[pl.BlockSpec(memory_space=pltpu.VMEM)] * len(ins),
        out_specs=out_specs,
        out_shape=shapes,
        scratch_shapes=[
            pltpu.SemaphoreType.DMA((len(ins),)),
            pltpu.SemaphoreType.DMA((total,)),
            pltpu.SemaphoreType.DMA((total,)),
        ],
        compiler_params=pltpu.CompilerParams(collective_id=collective_id, has_side_effects=True),
        name=name,
    )(*ins)


def over(extents, body):
    total = 1
    for e in extents:
        total *= e
    if total == 1:
        body((0,) * len(extents))
        return

    def step(i, carry):
        spots = []
        for e in reversed(extents):
            spots.append(lax.rem(i, e))
            i = lax.div(i, e)
        body(tuple(reversed(spots)))
        return carry

    lax.fori_loop(0, total, step, 0)


def add_into(dst, src_of, extents):
    def body(spots):
        here = spots + (slice(None), slice(None))
        dst[here] = (dst[here].astype(jnp.float32) + src_of(spots).astype(jnp.float32)).astype(dst.dtype)

    over(extents, body)


def add_pair(out, first, second_of, extents):
    def body(spots):
        here = spots + (slice(None), slice(None))
        out[here] = (first[here].astype(jnp.float32) + second_of(spots).astype(jnp.float32)).astype(out.dtype)

    over(extents, body)


def reduce_task(sizes, me, src, out, bufs, sems, order, dims):
    remaining = list(dims)
    current = src
    stages = []
    for stage, dim in enumerate(order):
        last = stage == len(order) - 1
        if dim == "s":
            n, s = sizes["z"] * sizes["y"], me["z"] * sizes["y"] + me["y"]
            base = sems.take(n)
            sends, recvs = [], []
            for k in range(1, n):
                to = lax.rem(s + k, n)
                spot = current.at[lax.div(to, sizes["y"]), lax.rem(to, sizes["y"])]
                sends.append(sems.copy(spot, bufs[stage].at[k], base + k, seq_peer(sizes, me, k)))
                recvs.append(sems.copy(bufs[stage].at[k], bufs[stage].at[k], base + k, seq_peer(sizes, me, k)))
            stages.append((dim, n, current, bufs[stage], sends, recvs, None, None, None))
            continue
        direct, dim = dim.isupper(), dim.lower()
        n, at = sizes[dim], me[dim]
        spot = remaining.index(dim)
        remaining.remove(dim)
        extents = [sizes[d] for d in remaining]

        def block(j, source=current, spot=spot):
            return source.at[(slice(None),) * spot + (j,)]

        def values(j, source=current, spot=spot):
            return lambda spots: source[spots[:spot] + (j,) + spots[spot:] + (slice(None), slice(None))]

        if direct:
            base = sems.take(n)
            moves = []
            for k in range(1, n):
                to, origin = lax.rem(at + k, n), lax.rem(at + n - k, n)
                buf = bufs[stage].at[k]
                send = sems.copy(block(to), buf, base + k, device_at(sizes, me, dim, to))
                moves.append((send, sems.copy(buf, buf, base + k, device_at(sizes, me, dim, origin))))
            result = out if last else bufs[stage].at[0]
            stages.append(("direct", n, result, bufs[stage], moves, at, values, extents, last))
            current = result
        elif n == 2:
            send = sems.copy(block(1 - at), bufs[stage], sems.take(1), device_at(sizes, me, dim, 1 - at))
            stages.append((dim, n, None, bufs[stage], [send], at, values, extents, last))
            current = bufs[stage]
        else:
            chains = bufs[stage][0]
            result = out if last else bufs[stage][1]
            base = sems.take(2 * n)
            moves = []
            for slot in range(n - 1):
                for side in range(2):
                    lead = at if side == 0 else n - 1 - at
                    j = lax.rem((n - 1 - slot + at) if side == 0 else (slot + 1 + at + n), n)
                    buf = chains.at[side, j]
                    to = device_at(sizes, me, dim, at + 1 if side == 0 else at - 1)
                    index = base + side * n + j
                    plain, summed = sems.copy(block(j), buf, index, to), sems.copy(buf, buf, index, to)
                    moves.append((plain, summed, buf, j, lead == 0, (lead > 0) & (lead <= slot), lead <= slot))
            ends = []
            for side in range(2):
                buf = chains.at[side, at]
                ends.append(sems.copy(buf, buf, base + side * n + at, device_at(sizes, me, dim, at)))
            conds = (at > 0, at < n - 1)
            stages.append((dim, n, result, chains, moves, at, values, extents, (ends, conds)))
            current = result

    for dim, n, source, buf, moves, at, values, extents, last in stages:
        if dim == "s":
            for send in moves:
                send.start()
            yield
            total = source[me["z"], me["y"]].astype(jnp.float32)
            for k in range(1, n):
                at[k - 1].wait_recv()
                total = total + buf[k].astype(jnp.float32)
            out[...] = total
        elif dim == "direct":
            for send, _ in moves:
                send.start()
            yield
            for _, got in moves:
                got.wait_recv()

            def add_all(spots):
                here = spots + (slice(None), slice(None))
                total = values(at)(spots).astype(jnp.float32)
                for k in range(1, n):
                    total = total + buf[(k,) + here].astype(jnp.float32)
                source[here] = total.astype(source.dtype)

            over(extents, add_all)
        elif n == 2:
            moves[0].start()
            yield
            moves[0].wait_recv()
            if last:
                add_pair(out, buf, values(at), extents)
            else:
                add_into(buf, values(at), extents)
        else:
            for slot in range(n - 1):
                for plain, summed, target, j, is_first, is_later, _ in moves[2 * slot : 2 * slot + 2]:

                    def pass_on(summed=summed, target=target, j=j):
                        summed.wait_recv()
                        add_into(target, values(j), extents)
                        summed.start()

                    pl.when(is_first)(plain.start)
                    pl.when(is_later)(pass_on)
                yield

            def start(spots):
                here = spots + (slice(None), slice(None))
                source[here] = values(at)(spots).astype(source.dtype)

            over(extents, start)
            ends, conds = last
            for side in range(2):

                def finish(side=side):
                    ends[side].wait_recv()
                    add_into(source, lambda spots: buf[(side, at) + spots + (slice(None), slice(None))], extents)

                pl.when(conds[side])(finish)
    for dim, n, _, _, moves, _, _, _, _ in stages:
        for move in moves:
            if dim == "direct":
                move[0].wait_send()
            elif dim == "s" or n == 2:
                move.wait_send()
            else:
                pl.when(move[-1])(move[1].wait_send)


class Split:
    def __init__(self, parts):
        self.parts = parts
        self.dtype = parts[0].dtype

    def __setitem__(self, here, value):
        first = 0
        for part in self.parts:
            last = first + part.shape[-1]
            part[here] = value[:, first:last]
            first = last

    def __getitem__(self, here):
        return jnp.concatenate([part[here] for part in self.parts], axis=1)


def stage_buffers(sizes, block, dtype, dims, order):
    scratch, counts, left, total = [], [], list(dims), 0
    for dim in order:
        counts.append(1)
        if dim == "s":
            left = []
            n = sizes["z"] * sizes["y"]
            scratch.append(pltpu.VMEM((n,) + block, dtype))
            total += n
            continue
        left.remove(dim.lower())
        shape = tuple(sizes[d] for d in left) + block
        n = sizes[dim.lower()]
        if dim.isupper():
            scratch.append(pltpu.VMEM((n,) + shape, dtype))
            total += n
        elif n == 2:
            scratch.append(pltpu.VMEM(shape, dtype))
            total += 1
        else:
            scratch.append(pltpu.VMEM((2, n) + shape, dtype))
            total += 2 * n
            if dim != order[-1]:
                scratch.append(pltpu.VMEM(shape, dtype))
                counts[-1] = 2
    return scratch, counts, total, left


def stage_refs(sizes, order, counts, bufs):
    stages = []
    for dim, size in zip(order, counts):
        taken = [bufs.pop(0) for _ in range(size)]
        stages.append(taken[0] if dim == "s" or dim.isupper() or sizes[dim] == 2 else taken)
    return stages


def reduce_kernel(sizes, orders, dims, counts, splits, spill, *refs):
    count = len(orders)
    total = count + spill
    ends = sum(splits) + spill
    ins, outs = refs[:total], list(refs[total : total + ends])
    send_sem, recv_sem = refs[-2:]
    bufs = list(refs[total + ends : -2])
    me = place(sizes)
    used = [d for d in SLOTS if any(d in o.lower() for o in orders)]
    greet(sizes, me, used + ["s"] * (spill or any("s" in o for o in orders)))
    sems = Sems(send_sem, recv_sem)
    tasks = []
    for i in range(count):
        stages = stage_refs(sizes, orders[i], counts[i], bufs)
        parts = [outs.pop(0) for _ in range(splits[i])]
        out = parts[0] if len(parts) == 1 else Split(parts)
        tasks.append(reduce_task(sizes, me, ins[i], out, stages, sems, orders[i], dims[i]))
    if spill:
        tasks.insert(0, shift_task(sizes, me, ins[-1], outs.pop(0), sems, -1))
    run_together(tasks)


def cut_shapes(block, left, widths, sizes, dtype):
    if left or widths is None or sum(widths) != block[1]:
        shape = tuple(sizes[d] for d in left) + block
        return [jax.ShapeDtypeStruct(shape, dtype if left else jnp.float32)], widths
    return [jax.ShapeDtypeStruct((block[0], w), jnp.float32) for w in widths], None


def cut_columns(parts, widths):
    if widths is None:
        return parts
    full = parts[0].reshape(-1, sum(widths))
    edges = np.cumsum([0] + list(widths))
    return [full[:, int(lo) : int(hi)] for lo, hi in zip(edges[:-1], edges[1:])]


def reduce_all(grads, orders, sizes, collective_id, spill=None, splits=None, name="reduce"):
    ins, scratch, shapes, counts, all_dims, cuts, later = [], [], [], [], [], [], []
    splits = splits or [None] * len(grads)
    total = 0
    devices = sizes["x"] * sizes["c"] * sizes["z"] * sizes["y"]
    for grad, order, widths in zip(grads, orders, splits):
        dims = SLOTS[-(grad.ndim - 2) :] if grad.ndim > 2 else SLOTS
        if grad.ndim == 2:
            whole = tuple(sizes[d] for d in SLOTS)
            grad = grad.reshape(whole + tile_block(grad.shape[0] // devices, grad.shape[1]))
        block = grad.shape[-2:]
        ins.append(grad)
        all_dims.append(dims)
        more, taken, needed, left = stage_buffers(sizes, block, grad.dtype, dims, order)
        scratch += more
        total += needed
        counts.append(taken)
        ends, widths = cut_shapes(block, left, widths, sizes, grad.dtype)
        shapes += ends
        cuts.append(len(ends))
        later.append(widths)
    if spill is not None:
        ins.append(spill)
        shapes.append(jax.ShapeDtypeStruct(spill.shape, spill.dtype))
        total += 1
    outs = pl.pallas_call(
        functools.partial(reduce_kernel, sizes, orders, all_dims, counts, cuts, int(spill is not None)),
        in_specs=[pl.BlockSpec(memory_space=pltpu.VMEM)] * len(ins),
        out_specs=[pl.BlockSpec(memory_space=pltpu.VMEM)] * len(shapes),
        out_shape=shapes,
        scratch_shapes=scratch + [pltpu.SemaphoreType.DMA((total,)), pltpu.SemaphoreType.DMA((total,))],
        compiler_params=pltpu.CompilerParams(
            collective_id=collective_id, has_side_effects=True, vmem_limit_bytes=56 << 20
        ),
        name=name,
    )(*ins)
    outs = list(outs)
    results = []
    for cut, widths in zip(cuts, later):
        results.append(cut_columns([outs.pop(0) for _ in range(cut)], widths))
    return results + outs


def collect_task(sizes, me, src, out, ybuf, chain, sems, produce):
    z, y, n, fast = me["z"], me["y"], sizes["z"], sizes["y"]
    fan = sems.take((fast - 1) * n)
    base = sems.take(2 * n)

    def fan_copy(k, j):
        to = lax.rem(y + k, fast)
        index = fan + (k - 1) * n + j
        return sems.copy(src.at[j, to], ybuf.at[k - 1, j], index, device_at(sizes, me, "y", to))

    def spread(i, carry):
        far = n - 1 - lax.div(i, 2)
        j = jnp.where(lax.rem(i, 2) == 0, z + far, z - far)

        @pl.when((j >= 0) & (j < n))
        def _():
            produce(j)
            for k in range(1, fast):
                fan_copy(k, j).start()

        return carry

    def chain_copy(side, j, to, plain=False):
        buf = chain.at[side, j]
        return sems.copy(ybuf.at[0, j] if plain else buf, buf, base + side * n + j, device_at(sizes, me, "z", to))

    slots = []
    for slot in range(n - 1):
        for side in range(2):
            lead = z if side == 0 else n - 1 - z
            j = lax.rem((n - 1 - slot + z) if side == 0 else (slot + 1 + z + n), n)
            to = z + 1 if side == 0 else z - 1
            ends = (chain_copy(side, j, to, True), chain_copy(side, j, to))
            slots.append((side, j, ends, lead == 0, (lead > 0) & (lead <= slot), lead <= slot))
    fans = [fan_copy(k, j) for j in range(n) for k in range(1, fast)]
    lax.fori_loop(0, 2 * n - 1, spread, 0)
    yield

    def merge(j):
        for k in range(1, fast):
            fan_copy(k, j).wait_recv()
        value = src[j, y].astype(jnp.float32)
        for k in range(1, fast):
            value = value + ybuf[k - 1, j].astype(jnp.float32)
        return value

    for slot in range(n - 1):
        for side, j, (plain, summed), is_first, is_later, _ in slots[2 * slot : 2 * slot + 2]:

            def begin(plain=plain, j=j):
                ybuf[0, j] = merge(j).astype(ybuf.dtype)
                plain.start()

            def pass_on(summed=summed, side=side, j=j):
                value = merge(j)
                summed.wait_recv()
                chain[side, j] = (chain[side, j].astype(jnp.float32) + value).astype(chain.dtype)
                summed.start()

            pl.when(is_first)(begin)
            pl.when(is_later)(pass_on)
        yield
    out[...] = merge(z)

    def finish(side):
        chain_copy(side, z, z).wait_recv()
        out[...] += chain[side, z].astype(jnp.float32)

    pl.when(z > 0)(partial(finish, 0))
    pl.when(z < n - 1)(partial(finish, 1))
    for fan_end in fans:
        fan_end.wait_send()
    for _, _, (_, summed), _, _, active in slots:
        pl.when(active)(summed.wait_send)


def halve_kernel(sizes, apart, *refs):
    n, count = sizes["x"], len(apart)
    refs = list(refs)
    ins = [refs.pop(0) for _ in range(count)]
    outs = [[refs.pop(0) for _ in range(n)] if alone else refs.pop(0) for alone in apart]
    bufs = [refs.pop(0) for _ in range(count)]
    send_sem, recv_sem = refs
    me = place(sizes)
    greet(sizes, me, ("c",))
    sems = Sems(send_sem, recv_sem)
    c = me["c"]
    peer = device_at(sizes, me, "c", 1 - c)
    sends = {}
    for k in range(n - 1, -1, -1):
        for i, alone in enumerate(apart):
            at = lax.rem(me["x"] + k, n) if alone else k
            sends[k, i] = sems.copy(ins[i].at[at, 1 - c], bufs[i].at[k], sems.take(1), peer)
            sends[k, i].start()
    for k in range(n - 1, -1, -1):
        for i, alone in enumerate(apart):
            at = lax.rem(me["x"] + k, n) if alone else k
            sends[k, i].wait_recv()
            src = ins[i]

            def own(spots, src=src, at=at):
                return src[(at, c) + spots + (slice(None), slice(None))]

            add_pair(outs[i][k] if alone else outs[i].at[k], bufs[i].at[k], own, src.shape[2:-2])
    for send in sends.values():
        send.wait_send()


def halve_cores(grads, apart, sizes, collective_id, name="halve"):
    n = sizes["x"]
    whole = tuple(sizes[d] for d in SLOTS)
    devices = whole[0] * whole[1] * whole[2] * whole[3]
    ins = [g.reshape(whole + tile_block(g.shape[0] // devices, g.shape[1])) for g in grads]
    halves = [g.shape[:1] + g.shape[2:] for g in ins]
    shapes = []
    for h, g, alone in zip(halves, ins, apart):
        shapes += [jax.ShapeDtypeStruct(h[1:], g.dtype)] * n if alone else [jax.ShapeDtypeStruct(h, g.dtype)]
    total = n * len(ins)
    outs = pl.pallas_call(
        functools.partial(halve_kernel, sizes, apart),
        in_specs=[pl.BlockSpec(memory_space=pltpu.VMEM)] * len(ins),
        out_specs=[pl.BlockSpec(memory_space=pltpu.VMEM)] * len(shapes),
        out_shape=shapes,
        scratch_shapes=[pltpu.VMEM(h, g.dtype) for h, g in zip(halves, ins)]
        + [pltpu.SemaphoreType.DMA((total,)), pltpu.SemaphoreType.DMA((total,))],
        compiler_params=pltpu.CompilerParams(
            collective_id=collective_id, has_side_effects=True, vmem_limit_bytes=56 << 20
        ),
        name=name,
    )(*ins)
    outs = list(outs)
    return [[outs.pop(0) for _ in range(n)] if alone else outs.pop(0) for alone in apart]


def from_others(pieces, sizes):
    n = sizes["x"]
    got = []
    for k in range(1, n):
        pairs = [(((x + k) % n) * 2 + c, x * 2 + c) for x in range(n) for c in range(2)]
        got.append(lax.ppermute(pieces[n - k], "batch", pairs))
    return got


def back_rows_kernel(sizes, rows, tasks_info, inner, *refs):
    refs = list(refs)

    def take(count):
        taken = refs[:count]
        del refs[:count]
        return taken

    info_ref, far_ref, diag_ref, q_ref, g_ref, full_ref, peak_ref, kv_ref, dkv_ref, normed_ref, second_ref = take(11)
    if inner:
        own_ref, dq_before_ref, d_out_ref = take(3)
    grads = [take(info[4]) for info in tasks_info]
    d_normed_ref, dq_ref, near_ref = take(3)
    outs = [take(info[3]) for info in tasks_info]
    last_ref = take(1)[0]
    if inner:
        inner_ref = take(1)[0]
        inner_counts = inner
        d_last_ref = take(1)[0]
    else:
        d_last_ref = last_ref
    kv_buf, chunk_ref, normed_buf, d_rows_ref, ybuf, chain, bias_ref, sum_ref, acc_ref, total_ref = take(10)
    kv_sem, chunk_sem, normed_sem, send_sem, recv_sem = refs[-5:]
    bufs = refs[:-5]
    me = place(sizes)
    first = me["z"] * sizes["y"] + me["y"]
    seqs, length, _ = kv_ref.shape
    n = sizes["z"]
    step = length // n
    last = seqs - 1
    width = q_ref.shape[1]
    pairs = diag_ref.shape[0]
    wide = width // pairs
    fetch = pltpu.make_async_copy(kv_ref.at[last], kv_buf, kv_sem)
    fetch.start()
    greet(sizes, me, SLOTS + ("s",))
    sems = Sems(send_sem, recv_sem)
    ffn = []
    for (order, dims, counts, _, many), grad, out in zip(tasks_info, grads, outs):
        src = grad[0]
        if many > 1:
            src = bufs.pop(0)

            def total(spots, src=src, grad=grad):
                here = spots + (slice(None), slice(None))
                value = grad[0][here].astype(jnp.float32)
                for more in grad[1:]:
                    value = value + more[here].astype(jnp.float32)
                src[here] = value.astype(src.dtype)

            over(src.shape[:-2], total)
        stages = stage_refs(sizes, order, counts, bufs)
        ffn.append(reduce_task(sizes, me, src, out[0] if len(out) == 1 else Split(out), stages, sems, order, dims))
        next(ffn[-1])
    wide_task, down_task = ffn

    def rows_of(p):
        def produce(j):
            here = pl.ds(pl.multiple_of(j * step, step), step)
            if p < last:
                copy = pltpu.make_async_copy(dkv_ref.at[p, here], chunk_ref.at[0], chunk_sem.at[0])
                copy.start()
                copy.wait()
                block = chunk_ref[0]
            else:
                block = d_last_ref[here, :]
            block = nt_dot(block, second_ref[...]).astype(jnp.bfloat16)
            d_rows_ref[p, j] = block.reshape(d_rows_ref.shape[2:])

        return collect_task(
            sizes, me, d_rows_ref.at[p], d_normed_ref.at[p], ybuf.at[p], chain.at[p], sems, produce
        )

    before = [rows_of(p) for p in range(last)]
    for task in before:
        next(task)
    fetch.wait()
    size = info_ref[last]

    def one_pair(p, carry):
        fill_bias(rows, far_ref, diag_ref.at[pl.ds(p, 1)], bias_ref, p)
        sum_ref[...] = jnp.zeros_like(sum_ref)
        lanes = pl.ds(pl.multiple_of(p * wide, wide), wide)
        tail = slice(last * rows, seqs * rows)
        k_lanes = pl.ds(pl.multiple_of(2 * p * wide, wide), wide)
        v_lanes = pl.ds(pl.multiple_of((2 * p + 1) * wide, wide), wide)

        def write(here, dk, dv):
            d_last_ref[here, k_lanes] = dk
            d_last_ref[here, v_lanes] = dv

        dq_ref[:, lanes] = back_pair(
            rows,
            size,
            first,
            q_ref[tail, lanes],
            g_ref[tail, lanes],
            full_ref[tail, lanes],
            (lambda here: (kv_buf[here, k_lanes], kv_buf[here, v_lanes]), length // (SPAN * rows)),
            [peak_ref[last, p, a : a + 1, :] for a in range(2)],
            bias_ref,
            sum_ref,
            acc_ref,
            write,
        )

        def keep(a, slot, value):
            near_ref[p, a, slot] = value

        near_sums(rows, sum_ref, keep)
        for i in range(min(pairs, n - 1)):

            @pl.when(p == i)
            def _():
                for task in before:
                    next(task, None)

        @pl.when(p == pairs - 1)
        def _():
            next(wide_task)
            next(down_task)

        return carry

    lax.fori_loop(0, pairs, one_pair, 0)
    after = rows_of(last)
    next(after)
    tasks = ffn + before + [after]
    if inner:
        steps = seqs * n
        early = last * n

        def at_step(i):
            return pl.ds(pl.multiple_of(i * step, step), step)

        def normed_copy(i):
            slot = lax.rem(i, 2)
            return pltpu.make_async_copy(normed_ref.at[at_step(i)], normed_buf.at[slot], normed_sem.at[slot])

        def early_copy(i):
            slot = lax.rem(i, 2)
            src = dkv_ref.at[lax.div(i, n), at_step(lax.rem(i, n))]
            return pltpu.make_async_copy(src, chunk_ref.at[slot], chunk_sem.at[slot])

        normed_copy(0).start()
        early_copy(0).start()
        total_ref[...] = jnp.zeros_like(total_ref)

        plan = [[], before, [], [wide_task], [after], [], [after]]

        def weigh(i, carry):
            pl.when(i + 1 < steps)(lambda: normed_copy(i + 1).start())
            pl.when(i + 1 < early)(lambda: early_copy(i + 1).start())
            normed_copy(i).wait()
            slot = lax.rem(i, 2)

            @pl.when(i < early)
            def _():
                early_copy(i).wait()
                total_ref[...] += tn_dot(normed_buf[slot], chunk_ref[slot])

            @pl.when(i >= early)
            def _():
                total_ref[...] += tn_dot(normed_buf[slot], d_last_ref[at_step(i - early), :])

            for k, tasks_now in enumerate(plan):

                @pl.when(i == k)
                def _():
                    for task in tasks_now:
                        next(task, None)

            return carry

        lax.fori_loop(0, steps, weigh, 0)
        block = inner_ref.shape[:-1]
        d_query = tn_dot(own_ref[last * rows :], dq_ref[...])
        if last:
            d_query = d_query + tn_dot(own_ref[: last * rows], dq_before_ref[...])
        inner_ref[..., :width] = d_query.astype(jnp.bfloat16).reshape(block + (width,))
        inner_ref[..., width : 2 * width] = d_out_ref[...]
        inner_ref[..., 2 * width :] = total_ref[...].astype(jnp.bfloat16).reshape(block + (2 * width,))
        stages = stage_refs(sizes, "cx", inner_counts, bufs)
        tasks.insert(0, reduce_task(sizes, me, inner_ref, last_ref, stages, sems, "cx", SLOTS))
    run_together(tasks)


def back_rows(info, far, diag, q, g, full, kv, peak, dkv, normed_all, normed_own, second, dq_before, d_out, grads,
              orders, splits, sizes, rows, collective_id, name="back_rows"):
    seqs, length, double = kv.shape
    width = q.shape[1]
    last = seqs - 1
    pairs = far.shape[0] // 2
    n, fast = sizes["z"], sizes["y"]
    step = length // n
    smem, vmem = pl.BlockSpec(memory_space=pltpu.SMEM), pl.BlockSpec(memory_space=pltpu.VMEM)
    anywhere = pl.BlockSpec(memory_space=pl.ANY)
    bf16, f32 = jnp.bfloat16, jnp.float32
    ins = [info, far, diag, q, g, full, peak, kv, dkv, normed_all, second]
    in_specs = [smem, smem] + [vmem] * 5 + [anywhere] * 3 + [vmem]
    devices = sizes["x"] * sizes["c"] * n * fast
    own_block = (width // devices, 4 * width)
    inner = None
    scratch, total = [], 0
    if own_block[0] % 16 == 0:
        whole = tuple(sizes[d] for d in SLOTS)
        more, inner, needed, left = stage_buffers(sizes, own_block, bf16, SLOTS, "cx")
        inner_more = more
        total += needed
        ins += [normed_own, dq_before, d_out.reshape(whole + (own_block[0], width))]
        in_specs += [vmem] * 3
        last_shape = jax.ShapeDtypeStruct(tuple(sizes[d] for d in left) + own_block, bf16)
    else:
        last_shape = jax.ShapeDtypeStruct((length, double), bf16)
    tasks_info, shapes, later = [], [], []
    for grad, order, widths in zip(grads, orders, splits):
        many = isinstance(grad, list)
        given = grad if many else [grad]
        block = given[0].shape[-2:]
        dims = ("z", "y") if many else ("x", "z", "y")
        more, counts, needed, left = stage_buffers(sizes, block, given[0].dtype, dims, order)
        if len(given) > 1:
            more = [pltpu.VMEM(given[0].shape, given[0].dtype)] + more
        scratch += more
        total += needed
        ends, widths = cut_shapes(block, left, widths, sizes, given[0].dtype)
        shapes += ends
        later.append(widths)
        tasks_info.append((order, dims, counts, len(ends), len(given)))
        ins += given
        in_specs += [vmem] * len(given)
    head_shapes = [
        jax.ShapeDtypeStruct((seqs, rows, width), f32),
        jax.ShapeDtypeStruct((rows, width), bf16),
        jax.ShapeDtypeStruct((pairs, 2, 5, 8, 2 * rows), f32),
    ]
    own_scratch = []
    if inner:
        own_scratch = [pltpu.VMEM(whole + own_block, bf16), pltpu.VMEM((length, double), bf16)]
        scratch = scratch + inner_more
    block = (seqs, n, fast, rows, width)
    own_scratch += [
        pltpu.VMEM((length, double), bf16),
        pltpu.VMEM((2, step, double), bf16),
        pltpu.VMEM((2, step, width), bf16),
        pltpu.VMEM(block, bf16),
        pltpu.VMEM((seqs, fast - 1, n, rows, width), bf16),
        pltpu.VMEM((seqs, 2, n, rows, width), bf16),
        pltpu.VMEM((2, 5, rows, rows), f32),
        pltpu.VMEM((2, 5, rows, rows), f32),
        pltpu.VMEM((2, width // pairs, rows), f32),
        pltpu.VMEM((width, double), f32) if inner else pltpu.VMEM((8, 128), f32),
    ]
    total += seqs * ((fast - 1) * n + 2 * n)
    outs = pl.pallas_call(
        functools.partial(back_rows_kernel, sizes, rows, tasks_info, inner),
        in_specs=in_specs,
        out_specs=[vmem] * (len(shapes) + 4),
        out_shape=head_shapes + shapes + [last_shape],
        scratch_shapes=own_scratch
        + scratch
        + [
            pltpu.SemaphoreType.DMA,
            pltpu.SemaphoreType.DMA((2,)),
            pltpu.SemaphoreType.DMA((2,)),
            pltpu.SemaphoreType.DMA((total,)),
            pltpu.SemaphoreType.DMA((total,)),
        ],
        compiler_params=pltpu.CompilerParams(
            collective_id=collective_id, has_side_effects=True, vmem_limit_bytes=62 << 20
        ),
        name=name,
    )(*ins)
    outs = list(outs)
    heads = [outs.pop(0) for _ in range(3)]
    results = []
    for (_, _, _, cut, _), widths in zip(tasks_info, later):
        results.append(cut_columns([outs.pop(0) for _ in range(cut)], widths))
    return heads + results + [outs[0], inner is not None]


def on_device(
    inputs,
    lengths,
    conv_taps,
    gain_attn,
    w_proj,
    w_query,
    w_key,
    w_value,
    w_out,
    gain_ffn,
    w_gate,
    w_up,
    w_down,
    rel_bias,
    cotangent,
):
    batch, seq = lax.axis_size("batch"), lax.axis_size("seq")
    sizes = layout_of(batch, seq)
    devices = batch * seq
    seqs, rows, width = inputs.shape
    length = rows * seq
    count = seqs * rows
    own = w_proj.shape[0]
    own_bias = rel_bias.shape[0]
    heads = own_bias * devices // NB
    hidden = w_gate.shape[1]

    small = jnp.concatenate(
        [
            conv_taps,
            gain_attn[:, None],
            gain_ffn[:, None],
            jnp.pad(rel_bias, (0, own - own_bias))[:, None],
            jnp.zeros((own, PACK - TAPS - 3), jnp.bfloat16),
        ],
        axis=1,
    )
    pairs = heads // 2
    key_value_w = jnp.stack([w_key.reshape(own, pairs, -1), w_value.reshape(own, pairs, -1)], axis=2)
    first, second, outer_plane, down_plane, left_rim = gather_all(
        [
            jnp.concatenate([small, w_proj, w_query], axis=1),
            key_value_w.reshape(own, -1),
            jnp.concatenate([w_out, w_gate, w_up], axis=1),
            w_down,
        ],
        ["Zyxc", "Zxyc", "zy", "yz"],
        sizes,
        1,
        rim=inputs[:, rows - 16 :, :],
        name="gather_first",
    )
    first = first.reshape(width, -1)
    second = second.reshape(width, -1)
    taps = first[:, :TAPS].astype(jnp.float32)
    gain_first = first[:, TAPS].astype(jnp.float32)
    gain_second = first[:, TAPS + 1].astype(jnp.float32)
    table = first[:, TAPS + 2].reshape(devices, own)[:, :own_bias].reshape(heads, NB).astype(jnp.float32)
    proj_w = first[:, PACK : PACK + width]
    query_w = first[:, PACK + width :]

    padded = jnp.concatenate([left_rim[:, 13:], inputs], axis=1).astype(jnp.float32)
    mixed_conv, conv_back = jax.vjp(partial(conv_mix, row_count=rows), padded, taps)
    mixed_low = mixed_conv.astype(jnp.bfloat16).reshape(count, width)
    resid_in = inputs.astype(jnp.float32).reshape(count, width)
    hidden_one = resid_in + mat_dot(mixed_low, proj_w)
    normed_one, norm_one_back = jax.vjp(norm_rows, hidden_one, gain_first)
    normed_low = normed_one.astype(jnp.bfloat16)

    outer_w, down_w, normed_all = gather_all(
        [outer_plane, down_plane],
        ["xc", "xc"],
        sizes,
        2,
        rows=normed_low.reshape(seqs, rows, width),
        plan=(0, 1, 2, 2, 2, 2),
        name="gather_rows",
    )
    outer_w = outer_w.reshape(width, -1)
    down_w = down_w.reshape(hidden, -1)
    out_w = outer_w[:, :width]
    wide_w = outer_w[:, width:]
    normed_all = normed_all.reshape(seqs * length, width)
    queries = mat_dot(normed_low, query_w).astype(jnp.bfloat16)
    key_value = mat_dot(normed_all, second).astype(jnp.bfloat16).reshape(seqs, length, 2 * width)

    far, diag = bias_tables(table, rows)
    info = jnp.concatenate([lengths, lax.axis_index("seq")[None].astype(jnp.int32)])
    attended, attended_full, inverse, peak = attend(info, far, diag, queries, key_value, rows, length)

    hidden_two = hidden_one + mat_dot(attended, out_w)
    normed_two, norm_two_back = jax.vjp(norm_rows, hidden_two, gain_second)
    normed_two_low = normed_two.astype(jnp.bfloat16)
    both_pre = mat_dot(normed_two_low, wide_w)
    inner_act, inner_back = jax.vjp(gated, both_pre[:, :hidden], both_pre[:, hidden:])
    inner_low = inner_act.astype(jnp.bfloat16)
    layer_out = (hidden_two + mat_dot(inner_low, down_w)).astype(jnp.bfloat16).reshape(seqs, rows, width)

    grad_low = cotangent.reshape(count, width)
    d_down_w = outer_sum(inner_low, grad_low).astype(jnp.bfloat16)
    d_gate, d_up = inner_back(back_dot(grad_low, down_w))
    d_both = jnp.concatenate([d_gate.astype(jnp.bfloat16), d_up.astype(jnp.bfloat16)], axis=1)
    d_wide_w = outer_sum(normed_two_low, d_both).astype(jnp.bfloat16)
    d_hidden_part, d_gain_two = norm_two_back(back_dot(d_both, wide_w))
    d_hidden_two = grad_low.astype(jnp.float32) + d_hidden_part
    d_attn_low = d_hidden_two.astype(jnp.bfloat16)
    d_out_w = outer_sum(attended, d_attn_low).astype(jnp.bfloat16)
    d_attended = back_dot(d_attn_low, out_w).astype(jnp.bfloat16)
    scaled = (d_attended.astype(jnp.float32) * inverse).astype(jnp.bfloat16)
    wide_pieces, down_half = halve_cores([d_wide_w, d_down_w], [True, False], sizes, 4)
    scaled, wide_pieces, down_half, d_out_w, layer_out = lax.optimization_barrier(
        (scaled, wide_pieces, down_half, d_out_w, layer_out)
    )
    wide_others = from_others(wide_pieces, sizes)
    early = seqs - 1
    dq_before, dkv_before, near_before = attend_back(
        info, far, diag, queries, scaled, attended_full, key_value, peak, rows, length, early
    )
    dq_before, dkv_before, near_before, wide_others = lax.optimization_barrier(
        (dq_before, dkv_before, near_before, wide_others)
    )
    d_normed_one, dq_last, near, (g_gate, g_up), (g_down,), last, joined = back_rows(
        info,
        far,
        diag,
        queries,
        scaled,
        attended_full,
        key_value,
        peak,
        dkv_before,
        normed_all,
        normed_low,
        second,
        dq_before,
        d_out_w,
        [[wide_pieces[0]] + wide_others, down_half],
        ["Zy", "xs"],
        [(hidden, hidden), None],
        sizes,
        rows,
        5,
    )
    d_table = bias_grad(near_before + near, rows).reshape(heads * NB)
    d_queries = jnp.concatenate([dq_before, dq_last], axis=0)
    if joined:
        inner, inner_order = last, "s"
    else:
        d_key_value = jnp.concatenate([dkv_before, last[None]], axis=0).reshape(seqs * length, 2 * width)
        d_second_w = outer_sum(normed_all, d_key_value).astype(jnp.bfloat16)
        d_query_w = outer_sum(normed_low, d_queries).astype(jnp.bfloat16)
        inner, inner_order = jnp.concatenate([d_query_w, d_out_w, d_second_w], axis=1), "cxs"
    d_normed_one = d_normed_one.reshape(count, width)
    d_normed_one = d_normed_one + back_dot(d_queries, query_w)
    d_first_part, d_gain_one = norm_one_back(d_normed_one)
    d_hidden_one = d_hidden_two + d_first_part
    d_mix_low = d_hidden_one.astype(jnp.bfloat16)
    d_proj_w = outer_sum(mixed_low, d_mix_low).astype(jnp.bfloat16)
    d_mixed = back_dot(d_mix_low, proj_w).reshape(seqs, rows, width)
    d_padded, d_taps = conv_back(d_mixed)
    d_inputs = d_hidden_one.reshape(seqs, rows, width) + d_padded[:, 3:, :]
    d_small = jnp.concatenate(
        [
            d_taps.T,
            d_gain_one[None],
            d_gain_two[None],
            jnp.pad(d_table.reshape(devices, own_bias), ((0, 0), (0, own - own_bias))).reshape(1, width),
            jnp.zeros((16 - TAPS - 3, width), jnp.float32),
        ],
        axis=0,
    )
    d_last = jnp.concatenate([d_proj_w, jnp.pad(d_small.T, ((0, 0), (0, PACK - 16))).astype(jnp.bfloat16)], axis=1)
    (g_proj, g_small), (g_query, g_out, g_second), spill = reduce_all(
        [d_last, inner],
        ["cxs", inner_order],
        sizes,
        6,
        spill=d_padded[:, :8, :],
        splits=[(width, PACK), (width, width, 2 * width)],
    )
    input_grad = d_inputs.at[:, rows - 3 :, :].add(spill[:, :3]).astype(jnp.bfloat16)
    g_second = g_second.reshape(own, pairs, 2, -1)
    return (
        layer_out,
        input_grad,
        g_small[:, :TAPS],
        g_small[:, TAPS],
        g_proj,
        g_query,
        g_second[:, :, 0].reshape(own, width),
        g_second[:, :, 1].reshape(own, width),
        g_out,
        g_small[:, TAPS + 1],
        g_gate,
        g_up,
        g_down.reshape(w_down.shape),
        g_small[:own_bias, TAPS + 2],
    )


def solution(mesh):
    in_specs = (
        P("batch", "seq", None),
        P("batch"),
        P(("batch", "seq"), None),
        P(("batch", "seq")),
        P(("batch", "seq"), None),
        P(("batch", "seq"), None),
        P(("batch", "seq"), None),
        P(("batch", "seq"), None),
        P(("batch", "seq"), None),
        P(("batch", "seq")),
        P(("batch", "seq"), None),
        P(("batch", "seq"), None),
        P(("batch", "seq"), None),
        P(("batch", "seq")),
        P("batch", "seq", None),
    )
    out_specs = (
        P("batch", "seq", None),
        P("batch", "seq", None),
        P(("batch", "seq"), None),
        P(("batch", "seq")),
        P(("batch", "seq"), None),
        P(("batch", "seq"), None),
        P(("batch", "seq"), None),
        P(("batch", "seq"), None),
        P(("batch", "seq"), None),
        P(("batch", "seq")),
        P(("batch", "seq"), None),
        P(("batch", "seq"), None),
        P(("batch", "seq"), None),
        P(("batch", "seq")),
    )
    return jax.shard_map(
        on_device, mesh=mesh, in_specs=in_specs, out_specs=out_specs, check_vma=False
    )
```

```python
import functools
from functools import partial

import jax
import jax.numpy as jnp
import numpy as np
from jax import lax
from jax.experimental import pallas as pl
from jax.experimental.pallas import tpu as pltpu
from jax.sharding import PartitionSpec as P

NB = 32
EPSILON = 1e-06
LIMITS = (12, 16, 23, 32, 46, 64, 91)
WINDOWS = ((2, 0), (3, 2), (4, 5))
TAPS = 9
PACK = 128
SPAN = 8

def mat_dot(lhs_array, rhs_array):
    return jnp.dot(lhs_array, rhs_array, preferred_element_type=jnp.float32)


def outer_sum(lhs_array, rhs_array):
    return lax.dot_general(
        lhs_array, rhs_array, (((0,), (0,)), ((), ())), preferred_element_type=jnp.float32
    )


def back_dot(grad_rows, weight):
    return lax.dot_general(
        grad_rows, weight, (((1,), (1,)), ((), ())), preferred_element_type=jnp.float32
    )


def bucket_of(relative):
    distance = jnp.abs(relative)
    larger = jnp.full(relative.shape, 8, jnp.int32)
    for threshold in LIMITS:
        larger = larger + (distance >= threshold).astype(jnp.int32)
    inside = jnp.where(distance < 8, distance, larger)
    return inside + 16 * (relative > 0).astype(jnp.int32)


def norm_rows(hidden, gain_row):
    return (
        hidden * lax.rsqrt(jnp.mean(hidden * hidden, axis=-1, keepdims=True) + EPSILON) * gain_row
    )


def gated(gate_pre, up_pre):
    return jax.nn.gelu(gate_pre, approximate=True) * up_pre


def conv_mix(padded, taps, row_count):
    summed = jnp.zeros(padded.shape[:-2] + (row_count, padded.shape[-1]), jnp.float32)
    for window_len, offset in WINDOWS:
        conv_sum = jnp.zeros_like(summed)
        for tap_index in range(window_len):
            shifted = lax.slice_in_dim(
                padded, 3 - tap_index, 3 - tap_index + row_count, axis=padded.ndim - 2
            )
            conv_sum = conv_sum + taps[:, offset + tap_index] * shifted
        summed = summed + jax.nn.gelu(conv_sum, approximate=True)
    return summed


def near_offsets(rows):
    lane = np.arange(2 * rows)
    lane = np.where(lane < rows, lane, lane - 2 * rows)
    return rows * (np.arange(3)[:, None, None] - 1) + np.arange(8)[None, :, None] - lane[None, None, :]


def bias_tables(table, rows):
    heads = table.shape[0]
    buckets = bucket_of(jnp.asarray(near_offsets(rows)[:, 0, :], jnp.int32)).reshape(-1)
    onehot = (buckets[None, :] == jnp.arange(NB, dtype=jnp.int32)[:, None]).astype(jnp.float32)
    diag = jnp.dot(table, onehot, precision=lax.Precision.HIGHEST)
    far = jnp.stack([table[:, NB // 2 - 1], table[:, NB - 1]], axis=1)
    return far, diag.reshape(heads // 2, 6, 2 * rows)


def bias_grad(near, rows):
    near = near.reshape(near.shape[0] * 2, 5, 8, 2 * rows)
    buckets = bucket_of(jnp.asarray(near_offsets(rows), jnp.int32))
    hit = buckets[None] == jnp.arange(NB, dtype=jnp.int32)[:, None, None, None]
    grad = jnp.sum(jnp.where(hit[None], near[:, None, 1:4], 0.0), axis=(2, 3, 4))
    left = jnp.sum(near[:, 0], axis=(1, 2))
    right = jnp.sum(near[:, 4], axis=(1, 2))
    return grad.at[:, NB // 2 - 1].add(left).at[:, NB - 1].add(right)


def nt_dot(a, b):
    return lax.dot_general(a, b, (((1,), (1,)), ((), ())), preferred_element_type=jnp.float32)


def tn_dot(a, b):
    return lax.dot_general(a, b, (((0,), (0,)), ((), ())), preferred_element_type=jnp.float32)


def nn_dot(a, b):
    return lax.dot_general(a, b, (((1,), (0,)), ((), ())), preferred_element_type=jnp.float32)


def fill_bias(rows, far_ref, diag_ref, bias_ref, pair):
    for a in range(2):
        bias_ref[a, 0] = jnp.full((rows, rows), far_ref[2 * pair + a, 0], jnp.float32)
        bias_ref[a, 4] = jnp.full((rows, rows), far_ref[2 * pair + a, 1], jnp.float32)
        for c in range(3):
            base = jnp.broadcast_to(diag_ref[0, 3 * a + c : 3 * a + c + 1, :], (rows, 2 * rows))
            bias_ref[a, 1 + c] = pltpu.roll(base, 0, 1, stride=1, stride_axis=0)[:, :rows]


def head_halves(block):
    lane = lax.broadcasted_iota(jnp.int32, block.shape, 1)
    zero = jnp.zeros_like(block)
    half = block.shape[1] // 2
    return jnp.where(lane < half, block, zero), jnp.where(lane < half, zero, block)


def attend_kernel(
    rows, info_ref, far_ref, diag_ref, q_ref, k_ref, v_ref, o_ref, full_ref, inv_ref, peak_ref, bias_ref, s_ref, acc_ref
):
    pair, b = pl.program_id(0), pl.program_id(1)

    @pl.when(b == 0)
    def _():
        fill_bias(rows, far_ref, diag_ref, bias_ref, pair)

    length, first = info_ref[b], info_ref[pl.num_programs(1)]
    count = lax.div(length + rows - 1, rows)
    halves = head_halves(q_ref[...])
    wide = q_ref.shape[1]
    half = wide // 2
    key_row = lax.broadcasted_iota(jnp.int32, (rows, rows), 0)

    def scores(kc, peaks):
        k = k_ref[0, pl.ds(kc * rows, SPAN * rows), :]
        new = list(peaks)
        for a in range(2):
            full = nt_dot(k, halves[a])
            for u in range(SPAN):
                slot = jnp.clip(kc + u - first + 2, 0, 4)
                valid = key_row < length - (kc + u) * rows
                s = full[u * rows : (u + 1) * rows] + bias_ref[a, slot]
                s = jnp.where(valid, s, -1e9)
                s_ref[a, pl.ds((kc + u) * rows, rows), :] = s
                new[a] = jnp.maximum(new[a], jnp.max(s.reshape(rows // 8, 8, rows), axis=0))
        return tuple(new)

    low = jnp.full((8, rows), -jnp.inf, jnp.float32)
    spans = lax.div(count + SPAN - 1, SPAN)
    peaks = lax.fori_loop(0, spans, lambda i, p: scores(i * SPAN, p), (low, low))
    peaks = [jnp.max(p, axis=0, keepdims=True) for p in peaks]
    acc_ref[...] = jnp.zeros_like(acc_ref)
    lane = lax.broadcasted_iota(jnp.int32, (SPAN * rows, wide), 1)

    def weigh(i, carry):
        here = pl.ds(i * SPAN * rows, SPAN * rows)
        v = v_ref[0, here, :]
        ones = jnp.ones_like(v)
        for a, v_one in enumerate((jnp.where(lane < half, v, ones), jnp.where(lane < half, ones, v))):
            e = jnp.exp(s_ref[a, here, :] - peaks[a])
            acc_ref[a] += tn_dot(v_one, e.astype(jnp.bfloat16))
        return carry

    lax.fori_loop(0, spans, weigh, 0)
    inv = jnp.concatenate([1.0 / acc_ref[0, half:], 1.0 / acc_ref[1, :half]], axis=0)
    out = jnp.concatenate([acc_ref[0, :half], acc_ref[1, half:]], axis=0) * inv
    out = out.T
    o_ref[...] = out.astype(o_ref.dtype)
    full_ref[...] = out
    inv_ref[...] = inv.T
    for a in range(2):
        peak_ref[0, 0, a : a + 1, :] = peaks[a]


def attention_cost(q, kv, products):
    flops = products * 8 * q.shape[0] * kv.shape[1] * q.shape[1]
    return pl.CostEstimate(
        flops=flops, bytes_accessed=2 * (q.size + kv.size) * products, transcendentals=8 * q.shape[0] * kv.shape[1]
    )


def attend(info, far, diag, q, kv, rows, length):
    heads = far.shape[0]
    seqs = kv.shape[0]
    wide = 2 * (q.shape[1] // heads)
    pairs = heads // 2
    smem = pl.BlockSpec(memory_space=pltpu.SMEM)
    return pl.pallas_call(
        functools.partial(attend_kernel, rows),
        grid=(pairs, seqs),
        in_specs=[
            smem, smem,
            pl.BlockSpec((1, 6, 2 * rows), lambda p, b: (p, 0, 0)),
            pl.BlockSpec((rows, wide), lambda p, b: (b, p)),
            pl.BlockSpec((1, length, wide), lambda p, b: (b, 0, 2 * p)),
            pl.BlockSpec((1, length, wide), lambda p, b: (b, 0, 2 * p + 1)),
        ],
        out_specs=[pl.BlockSpec((rows, wide), lambda p, b: (b, p))] * 3
        + [pl.BlockSpec((1, 1, 2, rows), lambda p, b: (b, p, 0, 0))],
        out_shape=[
            jax.ShapeDtypeStruct(q.shape, jnp.bfloat16),
            jax.ShapeDtypeStruct(q.shape, jnp.float32),
            jax.ShapeDtypeStruct(q.shape, jnp.float32),
            jax.ShapeDtypeStruct((seqs, pairs, 2, rows), jnp.float32),
        ],
        scratch_shapes=[
            pltpu.VMEM((2, 5, rows, rows), jnp.float32),
            pltpu.VMEM((2, length, rows), jnp.float32),
            pltpu.VMEM((2, wide, rows), jnp.float32),
        ],
        compiler_params=pltpu.CompilerParams(vmem_limit_bytes=48 << 20),
        cost_estimate=attention_cost(q, kv, 2),
        name="attend",
    )(info, far, diag, q, kv, kv)


def back_pair(rows, length, first, q, g, full, key_value, peak, bias_ref, sum_ref, acc_ref, write):
    q_half, g_half = head_halves(q), head_halves(g)
    wide = q.shape[1]
    half = wide // 2
    key_row = lax.broadcasted_iota(jnp.int32, (rows, rows), 0)
    acc_ref[...] = jnp.zeros_like(acc_ref)
    along = (g.astype(jnp.float32) * full).T
    delta = [jnp.sum(along[a * half : (a + 1) * half], axis=0, keepdims=True) for a in range(2)]
    keys, spans = key_value

    def step(i, carry):
        kc = i * SPAN
        here = pl.ds(kc * rows, SPAN * rows)
        k, v = keys(here)
        dk = dv = None
        for a in range(2):
            s = nt_dot(k, q_half[a])
            dp = nt_dot(v, g_half[a])
            es, dss = [], []
            for u in range(SPAN):
                part = slice(u * rows, (u + 1) * rows)
                slot = jnp.clip(kc + u - first + 2, 0, 4)
                valid = key_row < length - (kc + u) * rows
                e = jnp.exp(s[part] + bias_ref[a, slot] - peak[a])
                e_low = jnp.where(valid, e, 0.0).astype(jnp.bfloat16)
                ds = e_low.astype(jnp.float32) * (dp[part] - delta[a])
                sum_ref[a, slot] += ds
                es.append(e_low)
                dss.append(ds.astype(jnp.bfloat16))
            e_low, ds_low = jnp.concatenate(es, axis=0), jnp.concatenate(dss, axis=0)
            dv_a = nn_dot(e_low, g_half[a])
            dk_a = nn_dot(ds_low, q_half[a])
            dv = dv_a if dv is None else dv + dv_a
            dk = dk_a if dk is None else dk + dk_a
            acc_ref[a] += tn_dot(k, ds_low)
        write(here, dk.astype(jnp.bfloat16), dv.astype(jnp.bfloat16))
        return carry

    if spans == 1:
        step(0, 0)
    else:
        lax.fori_loop(0, spans, step, 0)
    return jnp.concatenate([acc_ref[0, :half], acc_ref[1, half:]], axis=0).T.astype(jnp.bfloat16)


def near_sums(rows, sum_ref, write):
    for a in range(2):
        for slot in range(5):
            total_sum = jnp.zeros((8, 2 * rows), jnp.float32)
            for g in range(rows // 8):
                part = jnp.concatenate(
                    [sum_ref[a, slot, 8 * g : 8 * g + 8, :], jnp.zeros((8, rows), jnp.float32)], axis=1
                )
                if g and 0 < slot < 4:
                    part = pltpu.roll(part, 2 * rows - 8 * g, 1)
                total_sum = total_sum + part
            write(a, slot, total_sum)


def attend_back_kernel(rows, info_ref, far_ref, diag_ref, q_ref, g_ref, full_ref, k_ref, v_ref, peak_ref,
                       dq_ref, dkv_ref, near_ref, bias_ref, sum_ref, acc_ref):
    pair, b = pl.program_id(0), pl.program_id(1)

    @pl.when(b == 0)
    def _():
        fill_bias(rows, far_ref, diag_ref, bias_ref, pair)
        sum_ref[...] = jnp.zeros_like(sum_ref)

    wide = q_ref.shape[1]

    def write(here, dk, dv):
        dkv_ref[0, here, :wide] = dk
        dkv_ref[0, here, wide:] = dv

    dq_ref[...] = back_pair(
        rows,
        info_ref[b],
        info_ref[info_ref.shape[0] - 1],
        q_ref[...],
        g_ref[...],
        full_ref[...],
        (lambda here: (k_ref[0, here, :], v_ref[0, here, :]), k_ref.shape[1] // (SPAN * rows)),
        [peak_ref[0, 0, a : a + 1, :] for a in range(2)],
        bias_ref,
        sum_ref,
        acc_ref,
        write,
    )

    @pl.when(b == pl.num_programs(1) - 1)
    def _():
        def keep(a, slot, value):
            near_ref[0, a, slot] = value

        near_sums(rows, sum_ref, keep)


def attend_back(info, far, diag, q, g, full, kv, peak, rows, length, seqs):
    heads = far.shape[0]
    wide = 2 * (q.shape[1] // heads)
    pairs = heads // 2
    smem = pl.BlockSpec(memory_space=pltpu.SMEM)
    row_spec = pl.BlockSpec((rows, wide), lambda p, b: (b, p))
    return pl.pallas_call(
        functools.partial(attend_back_kernel, rows),
        grid=(pairs, seqs),
        in_specs=[
            smem,
            smem,
            pl.BlockSpec((1, 6, 2 * rows), lambda p, b: (p, 0, 0)),
            row_spec,
            row_spec,
            row_spec,
            pl.BlockSpec((1, length, wide), lambda p, b: (b, 0, 2 * p)),
            pl.BlockSpec((1, length, wide), lambda p, b: (b, 0, 2 * p + 1)),
            pl.BlockSpec((1, 1, 2, rows), lambda p, b: (b, p, 0, 0)),
        ],
        out_specs=[
            row_spec,
            pl.BlockSpec((1, length, 2 * wide), lambda p, b: (b, 0, p)),
            pl.BlockSpec((1, 2, 5, 8, 2 * rows), lambda p, b: (p, 0, 0, 0, 0)),
        ],
        out_shape=[
            jax.ShapeDtypeStruct((seqs * rows, q.shape[1]), jnp.bfloat16),
            jax.ShapeDtypeStruct((seqs,) + kv.shape[1:], jnp.bfloat16),
            jax.ShapeDtypeStruct((pairs, 2, 5, 8, 2 * rows), jnp.float32),
        ],
        scratch_shapes=[
            pltpu.VMEM((2, 5, rows, rows), jnp.float32),
            pltpu.VMEM((2, 5, rows, rows), jnp.float32),
            pltpu.VMEM((2, wide, rows), jnp.float32),
        ],
        compiler_params=pltpu.CompilerParams(vmem_limit_bytes=48 << 20),
        cost_estimate=attention_cost(q, kv, 3),
        name="attend_back",
    )(info, far, diag, q, g, full, kv, kv, peak)


SLOTS = ("x", "c", "z", "y")
MESH = pl.DeviceIdType.MESH


def layout_of(batch, seq):
    fast = 1 << ((seq.bit_length() - 1) // 2)
    return {"x": batch // 2, "c": 2, "z": seq // fast, "y": fast}


def tile_block(rows, cols):
    return (rows, cols) if rows % 16 == 0 else (rows * cols // 128, 128)


def place(sizes):
    b, s = lax.axis_index("batch"), lax.axis_index("seq")
    return {
        "x": lax.div(b, 2),
        "c": lax.rem(b, 2),
        "z": lax.div(s, sizes["y"]),
        "y": lax.rem(s, sizes["y"]),
    }


def device_at(sizes, me, dim, at):
    spot = dict(me)
    spot[dim] = at
    return (spot["x"] * 2 + spot["c"], spot["z"] * sizes["y"] + spot["y"])


def seq_peer(sizes, me, k):
    n = sizes["z"] * sizes["y"]
    return (me["x"] * 2 + me["c"], lax.rem(me["z"] * sizes["y"] + me["y"] + k, n))


def greet(sizes, me, dims):
    barrier = pltpu.get_barrier_semaphore()
    total = 0
    if "s" in dims:
        total = sizes["z"] * sizes["y"] - 1
        for k in range(1, total + 1):
            pl.semaphore_signal(barrier, inc=1, device_id=seq_peer(sizes, me, k), device_id_type=MESH)
        dims = [d for d in dims if d not in "szy"]
    for dim in dims:
        for k in range(1, sizes[dim]):
            peer = device_at(sizes, me, dim, lax.rem(me[dim] + k, sizes[dim]))
            pl.semaphore_signal(barrier, inc=1, device_id=peer, device_id_type=MESH)
            total += 1
    pl.semaphore_wait(barrier, total)


class Sems:
    def __init__(self, send, recv):
        self.send, self.recv, self.used = send, recv, 0

    def take(self, count):
        first = self.used
        self.used += count
        assert self.used <= self.send.shape[0]
        return first

    def copy(self, src, dst, index, device):
        return pltpu.make_async_remote_copy(
            src_ref=src, dst_ref=dst, send_sem=self.send.at[index], recv_sem=self.recv.at[index],
            device_id=device, device_id_type=MESH,
        )


def run_together(tasks, plan=()):
    tasks = list(tasks)
    over_already = set()
    for i in plan:
        if i not in over_already:
            try:
                next(tasks[i])
            except StopIteration:
                over_already.add(i)
    tasks = [t for i, t in enumerate(tasks) if i not in over_already]
    while tasks:
        left = []
        for task in tasks:
            try:
                next(task)
                left.append(task)
            except StopIteration:
                pass
        tasks = left


def gather_task(sizes, me, src, out, local_sem, sems, order):
    before = list(SLOTS[len(SLOTS) - (len(src.shape) - 2) :])
    dims = [d for d in SLOTS if d in order.lower() or d in before]
    own = pltpu.make_async_copy(src, out.at[tuple(me[d] for d in dims if d not in before)], local_sem)
    own.start()
    own.wait()
    done = before
    sent = []
    for dim in order:
        direct, dim = dim.isupper(), dim.lower()
        n, at = sizes[dim], me[dim]

        def region(origin):
            spots = []
            for d in dims:
                spots.append(slice(None) if d in done else (origin if d == dim else me[d]))
            return out.at[tuple(spots)]

        if n == 2:
            base = sems.take(1)
            other = 1 - at
            send = sems.copy(region(at), region(at), base, device_at(sizes, me, dim, other))
            send.start()
            yield
            sems.copy(region(other), region(other), base, device_at(sizes, me, dim, other)).wait_recv()
            sent.append((None, send))
        elif direct:
            base = sems.take(n - 1)
            for k in range(1, n):
                peer = device_at(sizes, me, dim, lax.rem(at + k, n))
                send = sems.copy(region(at), region(at), base + k - 1, peer)
                send.start()
                sent.append((None, send))
            yield
            for k in range(1, n):
                origin = lax.rem(at + n - k, n)
                sems.copy(region(origin), region(origin), base + k - 1, device_at(sizes, me, dim, origin)).wait_recv()
        else:
            for t in range(n - 1):
                base = sems.take(2)
                to_right = (at + 1 < n) & (at - t >= 0)
                to_left = (at >= 1) & (at + t < n)
                from_left = (at >= 1) & (at - 1 - t >= 0)
                from_right = (at + 1 < n) & (at + 1 + t < n)
                right = sems.copy(region(at - t), region(at - t), base, device_at(sizes, me, dim, at + 1))
                left = sems.copy(region(at + t), region(at + t), base + 1, device_at(sizes, me, dim, at - 1))
                pl.when(to_right)(right.start)
                pl.when(to_left)(left.start)
                sent += [(to_right, right), (to_left, left)]
                yield
                got = sems.copy(region(at - 1 - t), region(at - 1 - t), base, device_at(sizes, me, dim, at - 1))
                pl.when(from_left)(got.wait_recv)
                got = sems.copy(region(at + 1 + t), region(at + 1 + t), base + 1, device_at(sizes, me, dim, at + 1))
                pl.when(from_right)(got.wait_recv)
        done.append(dim)
    for cond, send in sent:
        if cond is None:
            send.wait_send()
        else:
            pl.when(cond)(send.wait_send)


def spread_task(sizes, me, src, out, local_sem, sems):
    z, y, n, fast = me["z"], me["y"], sizes["z"], sizes["y"]
    own = pltpu.make_async_copy(src, out.at[:, z, y], local_sem)
    own.start()
    own.wait()
    fan = sems.take((fast - 1) * n)

    def fan_copy(k, origin, owner):
        peer = device_at(sizes, me, "y", lax.rem(y + k, fast))
        spot = out.at[:, origin, owner]
        return sems.copy(spot, spot, fan + (k - 1) * n + origin, peer)

    def fan_out(origin):
        for k in range(1, fast):
            fan_copy(k, origin, y).start()

    fan_out(z)
    sent = []
    for t in range(n - 1):
        base = sems.take(2)
        to_right = (z + 1 < n) & (z - t >= 0)
        to_left = (z >= 1) & (z + t < n)
        from_left = (z >= 1) & (z - 1 - t >= 0)
        from_right = (z + 1 < n) & (z + 1 + t < n)
        right = sems.copy(out.at[:, z - t, y], out.at[:, z - t, y], base, device_at(sizes, me, "z", z + 1))
        left = sems.copy(out.at[:, z + t, y], out.at[:, z + t, y], base + 1, device_at(sizes, me, "z", z - 1))
        pl.when(to_right)(right.start)
        pl.when(to_left)(left.start)
        sent += [(to_right, right), (to_left, left)]
        yield

        @pl.when(from_left)
        def _():
            spot = out.at[:, z - 1 - t, y]
            sems.copy(spot, spot, base, device_at(sizes, me, "z", z - 1)).wait_recv()
            fan_out(z - 1 - t)

        @pl.when(from_right)
        def _():
            spot = out.at[:, z + 1 + t, y]
            sems.copy(spot, spot, base + 1, device_at(sizes, me, "z", z + 1)).wait_recv()
            fan_out(z + 1 + t)

    yield
    for k in range(1, fast):
        for origin in range(n):
            fan_copy(k, origin, lax.rem(y + fast - k, fast)).wait_recv()
    for k in range(1, fast):
        for origin in range(n):
            fan_copy(k, origin, y).wait_send()
    for cond, send in sent:
        pl.when(cond)(send.wait_send)


def shift_task(sizes, me, src, out, sems, step):
    n = sizes["z"] * sizes["y"]
    s = me["z"] * sizes["y"] + me["y"]
    base = sems.take(1)
    send = sems.copy(src, out, base, seq_peer(sizes, me, step % n))
    has_to = (s < n - 1) if step > 0 else (s > 0)
    has_from = (s > 0) if step > 0 else (s < n - 1)
    pl.when(has_to)(send.start)
    yield
    pl.when(has_from)(send.wait_recv)

    @pl.when(jnp.logical_not(has_from))
    def _():
        out[...] = jnp.zeros_like(out)

    yield
    pl.when(has_to)(send.wait_send)


def stage_count(sizes, order):
    return sum(1 if sizes[d] == 2 else 2 * (sizes[d] - 1) for d in order.lower())


def gather_kernel(sizes, orders, has_rows, has_rim, plan, *refs):
    count = len(orders)
    total = count + has_rows + has_rim
    ins, outs = refs[:total], refs[total : 2 * total]
    local_sem, send_sem, recv_sem = refs[2 * total :]
    me = place(sizes)
    used = [d for d in SLOTS if any(d in o.lower() for o in orders) or (has_rows and d in "zy")]
    greet(sizes, me, used + ["s"] * has_rim)
    sems = Sems(send_sem, recv_sem)
    tasks = []
    for i in range(count):
        tasks.append(gather_task(sizes, me, ins[i], outs[i], local_sem.at[i], sems, orders[i]))
    if has_rows:
        tasks.append(spread_task(sizes, me, ins[count], outs[count], local_sem.at[count], sems))
    if has_rim:
        tasks.append(shift_task(sizes, me, ins[-1], outs[-1], sems, 1))
    run_together(tasks, plan)


def gather_all(shards, orders, sizes, collective_id, rows=None, rim=None, plan=(), name="gather"):
    ins, shapes, out_specs = [], [], []
    for shard, order in zip(shards, orders):
        ins.append(shard if shard.ndim > 2 else shard.reshape(tile_block(*shard.shape)))
        before = SLOTS[len(SLOTS) - (ins[-1].ndim - 2) :]
        whole = tuple(sizes[d] for d in SLOTS if d in order.lower() or d in before)
        shapes.append(jax.ShapeDtypeStruct(whole + ins[-1].shape[-2:], shard.dtype))
    total = sum(stage_count(sizes, o) for o in orders)
    out_specs = [pl.BlockSpec(memory_space=pl.ANY)] * len(ins)
    if rows is not None:
        ins.append(rows)
        shapes.append(jax.ShapeDtypeStruct((rows.shape[0], sizes["z"], sizes["y"]) + rows.shape[1:], rows.dtype))
        out_specs.append(pl.BlockSpec(memory_space=pl.ANY))
        total += (sizes["y"] - 1) * sizes["z"] + 2 * (sizes["z"] - 1)
    if rim is not None:
        ins.append(rim)
        shapes.append(jax.ShapeDtypeStruct(rim.shape, rim.dtype))
        out_specs.append(pl.BlockSpec(memory_space=pltpu.VMEM))
        total += 1
    return pl.pallas_call(
        functools.partial(gather_kernel, sizes, orders, int(rows is not None), int(rim is not None), plan),
        in_specs=[pl.BlockSpec(memory_space=pltpu.VMEM)] * len(ins),
        out_specs=out_specs,
        out_shape=shapes,
        scratch_shapes=[
            pltpu.SemaphoreType.DMA((len(ins),)),
            pltpu.SemaphoreType.DMA((total,)),
            pltpu.SemaphoreType.DMA((total,)),
        ],
        compiler_params=pltpu.CompilerParams(collective_id=collective_id, has_side_effects=True),
        name=name,
    )(*ins)


def over(extents, body):
    total = 1
    for e in extents:
        total *= e
    if total == 1:
        body((0,) * len(extents))
        return

    def step(i, carry):
        spots = []
        for e in reversed(extents):
            spots.append(lax.rem(i, e))
            i = lax.div(i, e)
        body(tuple(reversed(spots)))
        return carry

    lax.fori_loop(0, total, step, 0)


def add_into(dst, src_of, extents):
    def body(spots):
        here = spots + (slice(None), slice(None))
        dst[here] = (dst[here].astype(jnp.float32) + src_of(spots).astype(jnp.float32)).astype(dst.dtype)

    over(extents, body)


def add_pair(out, first, second_of, extents):
    def body(spots):
        here = spots + (slice(None), slice(None))
        out[here] = (first[here].astype(jnp.float32) + second_of(spots).astype(jnp.float32)).astype(out.dtype)

    over(extents, body)


def reduce_task(sizes, me, src, out, bufs, sems, order, dims):
    remaining = list(dims)
    current = src
    stages = []
    for stage, dim in enumerate(order):
        last = stage == len(order) - 1
        if dim == "s":
            n, s = sizes["z"] * sizes["y"], me["z"] * sizes["y"] + me["y"]
            base = sems.take(n)
            sends, recvs = [], []
            for k in range(1, n):
                to = lax.rem(s + k, n)
                spot = current.at[lax.div(to, sizes["y"]), lax.rem(to, sizes["y"])]
                sends.append(sems.copy(spot, bufs[stage].at[k], base + k, seq_peer(sizes, me, k)))
                recvs.append(sems.copy(bufs[stage].at[k], bufs[stage].at[k], base + k, seq_peer(sizes, me, k)))
            stages.append((dim, n, current, bufs[stage], sends, recvs, None, None, None))
            continue
        direct, dim = dim.isupper(), dim.lower()
        n, at = sizes[dim], me[dim]
        spot = remaining.index(dim)
        remaining.remove(dim)
        extents = [sizes[d] for d in remaining]

        def block(j, source=current, spot=spot):
            return source.at[(slice(None),) * spot + (j,)]

        def values(j, source=current, spot=spot):
            return lambda spots: source[spots[:spot] + (j,) + spots[spot:] + (slice(None), slice(None))]

        if direct:
            base = sems.take(n)
            moves = []
            for k in range(1, n):
                to, origin = lax.rem(at + k, n), lax.rem(at + n - k, n)
                buf = bufs[stage].at[k]
                send = sems.copy(block(to), buf, base + k, device_at(sizes, me, dim, to))
                moves.append((send, sems.copy(buf, buf, base + k, device_at(sizes, me, dim, origin))))
            result = out if last else bufs[stage].at[0]
            stages.append(("direct", n, result, bufs[stage], moves, at, values, extents, last))
            current = result
        elif n == 2:
            send = sems.copy(block(1 - at), bufs[stage], sems.take(1), device_at(sizes, me, dim, 1 - at))
            stages.append((dim, n, None, bufs[stage], [send], at, values, extents, last))
            current = bufs[stage]
        else:
            chains = bufs[stage][0]
            result = out if last else bufs[stage][1]
            base = sems.take(2 * n)
            moves = []
            for slot in range(n - 1):
                for side in range(2):
                    lead = at if side == 0 else n - 1 - at
                    j = lax.rem((n - 1 - slot + at) if side == 0 else (slot + 1 + at + n), n)
                    buf = chains.at[side, j]
                    to = device_at(sizes, me, dim, at + 1 if side == 0 else at - 1)
                    index = base + side * n + j
                    plain, summed = sems.copy(block(j), buf, index, to), sems.copy(buf, buf, index, to)
                    moves.append((plain, summed, buf, j, lead == 0, (lead > 0) & (lead <= slot), lead <= slot))
            ends = []
            for side in range(2):
                buf = chains.at[side, at]
                ends.append(sems.copy(buf, buf, base + side * n + at, device_at(sizes, me, dim, at)))
            conds = (at > 0, at < n - 1)
            stages.append((dim, n, result, chains, moves, at, values, extents, (ends, conds)))
            current = result

    for dim, n, source, buf, moves, at, values, extents, last in stages:
        if dim == "s":
            for send in moves:
                send.start()
            yield
            total = source[me["z"], me["y"]].astype(jnp.float32)
            for k in range(1, n):
                at[k - 1].wait_recv()
                total = total + buf[k].astype(jnp.float32)
            out[...] = total
        elif dim == "direct":
            for send, _ in moves:
                send.start()
            yield
            for _, got in moves:
                got.wait_recv()

            def add_all(spots):
                here = spots + (slice(None), slice(None))
                total = values(at)(spots).astype(jnp.float32)
                for k in range(1, n):
                    total = total + buf[(k,) + here].astype(jnp.float32)
                source[here] = total.astype(source.dtype)

            over(extents, add_all)
        elif n == 2:
            moves[0].start()
            yield
            moves[0].wait_recv()
            if last:
                add_pair(out, buf, values(at), extents)
            else:
                add_into(buf, values(at), extents)
        else:
            for slot in range(n - 1):
                for plain, summed, target, j, is_first, is_later, _ in moves[2 * slot : 2 * slot + 2]:

                    def pass_on(summed=summed, target=target, j=j):
                        summed.wait_recv()
                        add_into(target, values(j), extents)
                        summed.start()

                    pl.when(is_first)(plain.start)
                    pl.when(is_later)(pass_on)
                yield

            def start(spots):
                here = spots + (slice(None), slice(None))
                source[here] = values(at)(spots).astype(source.dtype)

            over(extents, start)
            ends, conds = last
            for side in range(2):

                def finish(side=side):
                    ends[side].wait_recv()
                    add_into(source, lambda spots: buf[(side, at) + spots + (slice(None), slice(None))], extents)

                pl.when(conds[side])(finish)
    for dim, n, _, _, moves, _, _, _, _ in stages:
        for move in moves:
            if dim == "direct":
                move[0].wait_send()
            elif dim == "s" or n == 2:
                move.wait_send()
            else:
                pl.when(move[-1])(move[1].wait_send)


class Split:
    def __init__(self, parts):
        self.parts = parts
        self.dtype = parts[0].dtype

    def __setitem__(self, here, value):
        first = 0
        for part in self.parts:
            last = first + part.shape[-1]
            part[here] = value[:, first:last]
            first = last

    def __getitem__(self, here):
        return jnp.concatenate([part[here] for part in self.parts], axis=1)


def stage_buffers(sizes, block, dtype, dims, order):
    scratch, counts, left, total = [], [], list(dims), 0
    for dim in order:
        counts.append(1)
        if dim == "s":
            left = []
            n = sizes["z"] * sizes["y"]
            scratch.append(pltpu.VMEM((n,) + block, dtype))
            total += n
            continue
        left.remove(dim.lower())
        shape = tuple(sizes[d] for d in left) + block
        n = sizes[dim.lower()]
        if dim.isupper():
            scratch.append(pltpu.VMEM((n,) + shape, dtype))
            total += n
        elif n == 2:
            scratch.append(pltpu.VMEM(shape, dtype))
            total += 1
        else:
            scratch.append(pltpu.VMEM((2, n) + shape, dtype))
            total += 2 * n
            if dim != order[-1]:
                scratch.append(pltpu.VMEM(shape, dtype))
                counts[-1] = 2
    return scratch, counts, total, left


def stage_refs(sizes, order, counts, bufs):
    stages = []
    for dim, size in zip(order, counts):
        taken = [bufs.pop(0) for _ in range(size)]
        stages.append(taken[0] if dim == "s" or dim.isupper() or sizes[dim] == 2 else taken)
    return stages


def reduce_kernel(sizes, orders, dims, counts, splits, spill, *refs):
    count = len(orders)
    total = count + spill
    ends = sum(splits) + spill
    ins, outs = refs[:total], list(refs[total : total + ends])
    send_sem, recv_sem = refs[-2:]
    bufs = list(refs[total + ends : -2])
    me = place(sizes)
    used = [d for d in SLOTS if any(d in o.lower() for o in orders)]
    greet(sizes, me, used + ["s"] * (spill or any("s" in o for o in orders)))
    sems = Sems(send_sem, recv_sem)
    tasks = []
    for i in range(count):
        stages = stage_refs(sizes, orders[i], counts[i], bufs)
        parts = [outs.pop(0) for _ in range(splits[i])]
        out = parts[0] if len(parts) == 1 else Split(parts)
        tasks.append(reduce_task(sizes, me, ins[i], out, stages, sems, orders[i], dims[i]))
    if spill:
        tasks.insert(0, shift_task(sizes, me, ins[-1], outs.pop(0), sems, -1))
    run_together(tasks)


def cut_shapes(block, left, widths, sizes, dtype):
    if left or widths is None or sum(widths) != block[1]:
        shape = tuple(sizes[d] for d in left) + block
        return [jax.ShapeDtypeStruct(shape, dtype if left else jnp.float32)], widths
    return [jax.ShapeDtypeStruct((block[0], w), jnp.float32) for w in widths], None


def cut_columns(parts, widths):
    if widths is None:
        return parts
    full = parts[0].reshape(-1, sum(widths))
    edges = np.cumsum([0] + list(widths))
    return [full[:, int(lo) : int(hi)] for lo, hi in zip(edges[:-1], edges[1:])]


def reduce_all(grads, orders, sizes, collective_id, spill=None, splits=None, name="reduce"):
    ins, scratch, shapes, counts, all_dims, cuts, later = [], [], [], [], [], [], []
    splits = splits or [None] * len(grads)
    total = 0
    devices = sizes["x"] * sizes["c"] * sizes["z"] * sizes["y"]
    for grad, order, widths in zip(grads, orders, splits):
        dims = SLOTS[-(grad.ndim - 2) :] if grad.ndim > 2 else SLOTS
        if grad.ndim == 2:
            whole = tuple(sizes[d] for d in SLOTS)
            grad = grad.reshape(whole + tile_block(grad.shape[0] // devices, grad.shape[1]))
        block = grad.shape[-2:]
        ins.append(grad)
        all_dims.append(dims)
        more, taken, needed, left = stage_buffers(sizes, block, grad.dtype, dims, order)
        scratch += more
        total += needed
        counts.append(taken)
        ends, widths = cut_shapes(block, left, widths, sizes, grad.dtype)
        shapes += ends
        cuts.append(len(ends))
        later.append(widths)
    if spill is not None:
        ins.append(spill)
        shapes.append(jax.ShapeDtypeStruct(spill.shape, spill.dtype))
        total += 1
    outs = pl.pallas_call(
        functools.partial(reduce_kernel, sizes, orders, all_dims, counts, cuts, int(spill is not None)),
        in_specs=[pl.BlockSpec(memory_space=pltpu.VMEM)] * len(ins),
        out_specs=[pl.BlockSpec(memory_space=pltpu.VMEM)] * len(shapes),
        out_shape=shapes,
        scratch_shapes=scratch + [pltpu.SemaphoreType.DMA((total,)), pltpu.SemaphoreType.DMA((total,))],
        compiler_params=pltpu.CompilerParams(
            collective_id=collective_id, has_side_effects=True, vmem_limit_bytes=56 << 20
        ),
        name=name,
    )(*ins)
    outs = list(outs)
    results = []
    for cut, widths in zip(cuts, later):
        results.append(cut_columns([outs.pop(0) for _ in range(cut)], widths))
    return results + outs


def collect_task(sizes, me, src, out, ybuf, chain, sems, produce):
    z, y, n, fast = me["z"], me["y"], sizes["z"], sizes["y"]
    fan = sems.take((fast - 1) * n)
    base = sems.take(2 * n)

    def fan_copy(k, j):
        to = lax.rem(y + k, fast)
        index = fan + (k - 1) * n + j
        return sems.copy(src.at[j, to], ybuf.at[k - 1, j], index, device_at(sizes, me, "y", to))

    def spread(i, carry):
        far = n - 1 - lax.div(i, 2)
        j = jnp.where(lax.rem(i, 2) == 0, z + far, z - far)

        @pl.when((j >= 0) & (j < n))
        def _():
            produce(j)
            for k in range(1, fast):
                fan_copy(k, j).start()

        return carry

    def chain_copy(side, j, to, plain=False):
        buf = chain.at[side, j]
        return sems.copy(ybuf.at[0, j] if plain else buf, buf, base + side * n + j, device_at(sizes, me, "z", to))

    slots = []
    for slot in range(n - 1):
        for side in range(2):
            lead = z if side == 0 else n - 1 - z
            j = lax.rem((n - 1 - slot + z) if side == 0 else (slot + 1 + z + n), n)
            to = z + 1 if side == 0 else z - 1
            ends = (chain_copy(side, j, to, True), chain_copy(side, j, to))
            slots.append((side, j, ends, lead == 0, (lead > 0) & (lead <= slot), lead <= slot))
    fans = [fan_copy(k, j) for j in range(n) for k in range(1, fast)]
    lax.fori_loop(0, 2 * n - 1, spread, 0)
    yield

    def merge(j):
        for k in range(1, fast):
            fan_copy(k, j).wait_recv()
        value = src[j, y].astype(jnp.float32)
        for k in range(1, fast):
            value = value + ybuf[k - 1, j].astype(jnp.float32)
        return value

    for slot in range(n - 1):
        for side, j, (plain, summed), is_first, is_later, _ in slots[2 * slot : 2 * slot + 2]:

            def begin(plain=plain, j=j):
                ybuf[0, j] = merge(j).astype(ybuf.dtype)
                plain.start()

            def pass_on(summed=summed, side=side, j=j):
                value = merge(j)
                summed.wait_recv()
                chain[side, j] = (chain[side, j].astype(jnp.float32) + value).astype(chain.dtype)
                summed.start()

            pl.when(is_first)(begin)
            pl.when(is_later)(pass_on)
        yield
    out[...] = merge(z)

    def finish(side):
        chain_copy(side, z, z).wait_recv()
        out[...] += chain[side, z].astype(jnp.float32)

    pl.when(z > 0)(partial(finish, 0))
    pl.when(z < n - 1)(partial(finish, 1))
    for fan_end in fans:
        fan_end.wait_send()
    for _, _, (_, summed), _, _, active in slots:
        pl.when(active)(summed.wait_send)


def halve_kernel(sizes, apart, *refs):
    n, count = sizes["x"], len(apart)
    refs = list(refs)
    ins = [refs.pop(0) for _ in range(count)]
    outs = [[refs.pop(0) for _ in range(n)] if alone else refs.pop(0) for alone in apart]
    bufs = [refs.pop(0) for _ in range(count)]
    send_sem, recv_sem = refs
    me = place(sizes)
    greet(sizes, me, ("c",))
    sems = Sems(send_sem, recv_sem)
    c = me["c"]
    peer = device_at(sizes, me, "c", 1 - c)
    sends = {}
    for k in range(n - 1, -1, -1):
        for i, alone in enumerate(apart):
            at = lax.rem(me["x"] + k, n) if alone else k
            sends[k, i] = sems.copy(ins[i].at[at, 1 - c], bufs[i].at[k], sems.take(1), peer)
            sends[k, i].start()
    for k in range(n - 1, -1, -1):
        for i, alone in enumerate(apart):
            at = lax.rem(me["x"] + k, n) if alone else k
            sends[k, i].wait_recv()
            src = ins[i]

            def own(spots, src=src, at=at):
                return src[(at, c) + spots + (slice(None), slice(None))]

            add_pair(outs[i][k] if alone else outs[i].at[k], bufs[i].at[k], own, src.shape[2:-2])
    for send in sends.values():
        send.wait_send()


def halve_cores(grads, apart, sizes, collective_id, name="halve"):
    n = sizes["x"]
    whole = tuple(sizes[d] for d in SLOTS)
    devices = whole[0] * whole[1] * whole[2] * whole[3]
    ins = [g.reshape(whole + tile_block(g.shape[0] // devices, g.shape[1])) for g in grads]
    halves = [g.shape[:1] + g.shape[2:] for g in ins]
    shapes = []
    for h, g, alone in zip(halves, ins, apart):
        shapes += [jax.ShapeDtypeStruct(h[1:], g.dtype)] * n if alone else [jax.ShapeDtypeStruct(h, g.dtype)]
    total = n * len(ins)
    outs = pl.pallas_call(
        functools.partial(halve_kernel, sizes, apart),
        in_specs=[pl.BlockSpec(memory_space=pltpu.VMEM)] * len(ins),
        out_specs=[pl.BlockSpec(memory_space=pltpu.VMEM)] * len(shapes),
        out_shape=shapes,
        scratch_shapes=[pltpu.VMEM(h, g.dtype) for h, g in zip(halves, ins)]
        + [pltpu.SemaphoreType.DMA((total,)), pltpu.SemaphoreType.DMA((total,))],
        compiler_params=pltpu.CompilerParams(
            collective_id=collective_id, has_side_effects=True, vmem_limit_bytes=56 << 20
        ),
        name=name,
    )(*ins)
    outs = list(outs)
    return [[outs.pop(0) for _ in range(n)] if alone else outs.pop(0) for alone in apart]


def feed_forward_kernel(sizes, *refs):
    n = sizes["x"]
    hidden_ref, att_ref, cot_ref, outer_ref, down_ref, gain_ref, inv_ref = refs[:7]
    layer_ref, d_hidden_ref, d_out_ref, scaled_ref, d_gain_ref = refs[7:12]
    wide_outs, down_out = refs[12 : 12 + n], refs[12 + n]
    d_wide, d_down, wide_buf, down_buf, two_ref, low_ref, d_normed, send_sem, recv_sem = refs[13 + n :]
    me = place(sizes)
    greet(sizes, me, ("c",))
    sems = Sems(send_sem, recv_sem)
    c = me["c"]
    peer = device_at(sizes, me, "c", 1 - c)
    width = hidden_ref.shape[1]
    parts = 2 * n
    units = down_ref.shape[0] // parts
    two_ref[...] = hidden_ref[...] + nn_dot(att_ref[...], outer_ref[:, :width])
    gain = gain_ref[...]

    def scale():
        return lax.rsqrt(jnp.mean(two_ref[...] * two_ref[...], axis=1, keepdims=True) + EPSILON)

    low_ref[...] = (two_ref[...] * scale() * gain).astype(jnp.bfloat16)
    d_normed[...] = jnp.zeros_like(d_normed)
    d_hidden_ref[...] = two_ref[...]

    def down_copy(x):
        return sems.copy(d_down.at[x, 1 - c], down_buf.at[x], x, peer)

    def part(i, carry):
        gate_at = pl.ds(pl.multiple_of(i * units, units), units)
        up_at = pl.ds(pl.multiple_of((parts + i) * units, units), units)
        gate_w = outer_ref[:, pl.ds(pl.multiple_of(width + i * units, units), units)]
        up_w = outer_ref[:, pl.ds(pl.multiple_of(width + (parts + i) * units, units), units)]
        down_w = down_ref[gate_at, :]
        low, cot = low_ref[...], cot_ref[...]
        gate, up = nn_dot(low, gate_w), nn_dot(low, up_w)
        square = gate * gate
        bend = jnp.tanh(0.7978845608 * gate * (1.0 + 0.044715 * square))
        half = 0.5 * (1.0 + bend)
        act = gate * half
        slope = half + gate * (0.5 * (1.0 - bend * bend)) * (0.7978845608 * (1.0 + 3.0 * 0.044715 * square))
        inner = (act * up).astype(jnp.bfloat16)
        d_hidden_ref[...] += nn_dot(inner, down_w)
        d_inner = nt_dot(cot, down_w)
        d_gate = (d_inner * up * slope).astype(jnp.bfloat16)
        d_up = (d_inner * act).astype(jnp.bfloat16)
        d_down[lax.div(i, 2), lax.rem(i, 2)] = (
            tn_dot(inner, cot).astype(jnp.bfloat16).reshape(d_down.shape[2:])
        )
        pl.when(lax.rem(i, 2) != c)(lambda: down_copy(lax.div(i, 2)).start())
        block = d_wide.shape[:-1] + (units,)
        d_wide[..., gate_at] = tn_dot(low, d_gate).astype(jnp.bfloat16).reshape(block)
        d_wide[..., up_at] = tn_dot(low, d_up).astype(jnp.bfloat16).reshape(block)
        d_normed[...] += nt_dot(d_gate, gate_w) + nt_dot(d_up, up_w)
        return carry

    lax.fori_loop(0, parts, part, 0)
    sends = [down_copy(x) for x in range(n)]
    for x in range(n):
        send = sems.copy(d_wide.at[x, 1 - c], wide_buf.at[x], n + x, peer)
        send.start()
        sends.append(send)
    layer_ref[...] = d_hidden_ref[...].astype(jnp.bfloat16)
    two, s2 = two_ref[...], scale()
    pulled = gain * d_normed[...]
    d_gain_ref[...] = jnp.sum(d_normed[...] * two * s2, axis=0, keepdims=True)
    drift = jnp.mean(two * pulled, axis=1, keepdims=True)
    d_two = cot_ref[...].astype(jnp.float32) + s2 * pulled - two * (s2 * s2 * s2 * drift)
    d_hidden_ref[...] = d_two
    d_low = d_two.astype(jnp.bfloat16)
    d_out_ref[...] = tn_dot(att_ref[...], d_low).astype(jnp.bfloat16)
    d_att = nt_dot(d_low, outer_ref[:, :width]).astype(jnp.bfloat16)
    scaled_ref[...] = (d_att.astype(jnp.float32) * inv_ref[...]).astype(jnp.bfloat16)
    for send in sends:
        send.wait_recv()
    for x in range(n):
        add_pair(down_out.at[x], down_buf.at[x], lambda at, x=x: d_down[(x, c) + at], d_down.shape[2:-2])
        at_x = lax.rem(me["x"] + x, n)
        add_pair(wide_outs[x], wide_buf.at[at_x], lambda at, at_x=at_x: d_wide[(at_x, c) + at], d_wide.shape[2:-2])
    for send in sends:
        send.wait_send()


def feed_forward(hidden_one, attended, cotangent, outer_w, down_w, gain, inverse, sizes, collective_id):
    n = sizes["x"]
    whole = tuple(sizes[d] for d in SLOTS)
    devices = whole[0] * whole[1] * whole[2] * whole[3]
    count, width = hidden_one.shape
    hidden = down_w.shape[0]
    bf16, f32 = jnp.bfloat16, jnp.float32
    wide_block = (width // devices, 2 * hidden)
    down_block = (hidden // devices, width)
    plane = whole[2:]
    vmem = pl.BlockSpec(memory_space=pltpu.VMEM)
    outs = pl.pallas_call(
        functools.partial(feed_forward_kernel, sizes),
        in_specs=[vmem] * 7,
        out_specs=[vmem] * (6 + n),
        out_shape=[
            jax.ShapeDtypeStruct((count, width), bf16),
            jax.ShapeDtypeStruct((count, width), f32),
            jax.ShapeDtypeStruct((width, width), bf16),
            jax.ShapeDtypeStruct((count, width), bf16),
            jax.ShapeDtypeStruct((1, width), f32),
        ]
        + [jax.ShapeDtypeStruct(plane + wide_block, bf16)] * n
        + [jax.ShapeDtypeStruct((n,) + plane + down_block, bf16)],
        scratch_shapes=[
            pltpu.VMEM(whole + wide_block, bf16),
            pltpu.VMEM(whole + down_block, bf16),
            pltpu.VMEM((n,) + plane + wide_block, bf16),
            pltpu.VMEM((n,) + plane + down_block, bf16),
            pltpu.VMEM((count, width), f32),
            pltpu.VMEM((count, width), bf16),
            pltpu.VMEM((count, width), f32),
            pltpu.SemaphoreType.DMA((2 * n,)),
            pltpu.SemaphoreType.DMA((2 * n,)),
        ],
        compiler_params=pltpu.CompilerParams(
            collective_id=collective_id, has_side_effects=True, vmem_limit_bytes=60 << 20
        ),
        name="feed_forward",
    )(hidden_one, attended, cotangent, outer_w, down_w, gain, inverse)
    return list(outs[:5]) + [list(outs[5 : 5 + n]), outs[5 + n]]


def from_others(pieces, sizes):
    n = sizes["x"]
    got = []
    for k in range(1, n):
        pairs = [(((x + k) % n) * 2 + c, x * 2 + c) for x in range(n) for c in range(2)]
        got.append(lax.ppermute(pieces[n - k], "batch", pairs))
    return got


def back_rows_kernel(sizes, rows, tasks_info, inner, *refs):
    refs = list(refs)

    def take(count):
        taken = refs[:count]
        del refs[:count]
        return taken

    info_ref, far_ref, diag_ref, q_ref, g_ref, full_ref, peak_ref, kv_ref, dkv_ref, normed_ref, second_ref = take(11)
    if inner:
        own_ref, dq_before_ref, d_out_ref = take(3)
    grads = [take(info[4]) for info in tasks_info]
    d_normed_ref, dq_ref, near_ref = take(3)
    outs = [take(info[3]) for info in tasks_info]
    last_ref = take(1)[0]
    if inner:
        inner_ref = take(1)[0]
        inner_counts = inner
        d_last_ref = take(1)[0]
    else:
        d_last_ref = last_ref
    kv_buf, chunk_ref, normed_buf, d_rows_ref, ybuf, chain, bias_ref, sum_ref, acc_ref, total_ref = take(10)
    kv_sem, chunk_sem, normed_sem, send_sem, recv_sem = refs[-5:]
    bufs = refs[:-5]
    me = place(sizes)
    first = me["z"] * sizes["y"] + me["y"]
    seqs, length, _ = kv_ref.shape
    n = sizes["z"]
    step = length // n
    last = seqs - 1
    width = q_ref.shape[1]
    pairs = diag_ref.shape[0]
    wide = width // pairs
    fetch = pltpu.make_async_copy(kv_ref.at[last], kv_buf, kv_sem)
    fetch.start()
    greet(sizes, me, SLOTS + ("s",))
    sems = Sems(send_sem, recv_sem)
    ffn = []
    for (order, dims, counts, _, many), grad, out in zip(tasks_info, grads, outs):
        src = grad[0]
        if many > 1:
            src = bufs.pop(0)

            def total(spots, src=src, grad=grad):
                here = spots + (slice(None), slice(None))
                value = grad[0][here].astype(jnp.float32)
                for more in grad[1:]:
                    value = value + more[here].astype(jnp.float32)
                src[here] = value.astype(src.dtype)

            over(src.shape[:-2], total)
        stages = stage_refs(sizes, order, counts, bufs)
        ffn.append(reduce_task(sizes, me, src, out[0] if len(out) == 1 else Split(out), stages, sems, order, dims))
        next(ffn[-1])
    wide_task, down_task = ffn

    def rows_of(p):
        def produce(j):
            here = pl.ds(pl.multiple_of(j * step, step), step)
            if p < last:
                copy = pltpu.make_async_copy(dkv_ref.at[p, here], chunk_ref.at[0], chunk_sem.at[0])
                copy.start()
                copy.wait()
                block = chunk_ref[0]
            else:
                block = d_last_ref[here, :]
            block = nt_dot(block, second_ref[...]).astype(jnp.bfloat16)
            d_rows_ref[p, j] = block.reshape(d_rows_ref.shape[2:])

        return collect_task(
            sizes, me, d_rows_ref.at[p], d_normed_ref.at[p], ybuf.at[p], chain.at[p], sems, produce
        )

    before = [rows_of(p) for p in range(last)]
    for task in before:
        next(task)
    fetch.wait()
    size = info_ref[last]

    def one_pair(p, carry):
        fill_bias(rows, far_ref, diag_ref.at[pl.ds(p, 1)], bias_ref, p)
        sum_ref[...] = jnp.zeros_like(sum_ref)
        lanes = pl.ds(pl.multiple_of(p * wide, wide), wide)
        tail = slice(last * rows, seqs * rows)
        k_lanes = pl.ds(pl.multiple_of(2 * p * wide, wide), wide)
        v_lanes = pl.ds(pl.multiple_of((2 * p + 1) * wide, wide), wide)

        def write(here, dk, dv):
            d_last_ref[here, k_lanes] = dk
            d_last_ref[here, v_lanes] = dv

        dq_ref[:, lanes] = back_pair(
            rows,
            size,
            first,
            q_ref[tail, lanes],
            g_ref[tail, lanes],
            full_ref[tail, lanes],
            (lambda here: (kv_buf[here, k_lanes], kv_buf[here, v_lanes]), length // (SPAN * rows)),
            [peak_ref[last, p, a : a + 1, :] for a in range(2)],
            bias_ref,
            sum_ref,
            acc_ref,
            write,
        )

        def keep(a, slot, value):
            near_ref[p, a, slot] = value

        near_sums(rows, sum_ref, keep)
        for i in range(min(pairs, n - 1)):

            @pl.when(p == i)
            def _():
                for task in before:
                    next(task, None)

        @pl.when(p == pairs - 1)
        def _():
            next(wide_task)
            next(down_task)

        return carry

    lax.fori_loop(0, pairs, one_pair, 0)
    after = rows_of(last)
    next(after)
    tasks = ffn + before + [after]
    if inner:
        steps = seqs * n
        early = last * n

        def at_step(i):
            return pl.ds(pl.multiple_of(i * step, step), step)

        def normed_copy(i):
            slot = lax.rem(i, 2)
            return pltpu.make_async_copy(normed_ref.at[at_step(i)], normed_buf.at[slot], normed_sem.at[slot])

        def early_copy(i):
            slot = lax.rem(i, 2)
            src = dkv_ref.at[lax.div(i, n), at_step(lax.rem(i, n))]
            return pltpu.make_async_copy(src, chunk_ref.at[slot], chunk_sem.at[slot])

        normed_copy(0).start()
        early_copy(0).start()
        total_ref[...] = jnp.zeros_like(total_ref)

        plan = [[], before, [], [wide_task], [after], [], [after]]

        def weigh(i, carry):
            pl.when(i + 1 < steps)(lambda: normed_copy(i + 1).start())
            pl.when(i + 1 < early)(lambda: early_copy(i + 1).start())
            normed_copy(i).wait()
            slot = lax.rem(i, 2)

            @pl.when(i < early)
            def _():
                early_copy(i).wait()
                total_ref[...] += tn_dot(normed_buf[slot], chunk_ref[slot])

            @pl.when(i >= early)
            def _():
                total_ref[...] += tn_dot(normed_buf[slot], d_last_ref[at_step(i - early), :])

            for k, tasks_now in enumerate(plan):

                @pl.when(i == k)
                def _():
                    for task in tasks_now:
                        next(task, None)

            return carry

        lax.fori_loop(0, steps, weigh, 0)
        block = inner_ref.shape[:-1]
        d_query = tn_dot(own_ref[last * rows :], dq_ref[...])
        if last:
            d_query = d_query + tn_dot(own_ref[: last * rows], dq_before_ref[...])
        inner_ref[..., :width] = d_query.astype(jnp.bfloat16).reshape(block + (width,))
        inner_ref[..., width : 2 * width] = d_out_ref[...]
        inner_ref[..., 2 * width :] = total_ref[...].astype(jnp.bfloat16).reshape(block + (2 * width,))
        stages = stage_refs(sizes, "cx", inner_counts, bufs)
        tasks.insert(0, reduce_task(sizes, me, inner_ref, last_ref, stages, sems, "cx", SLOTS))
    run_together(tasks)


def back_rows(info, far, diag, q, g, full, kv, peak, dkv, normed_all, normed_own, second, dq_before, d_out, grads,
              orders, splits, sizes, rows, collective_id, name="back_rows"):
    seqs, length, double = kv.shape
    width = q.shape[1]
    last = seqs - 1
    pairs = far.shape[0] // 2
    n, fast = sizes["z"], sizes["y"]
    step = length // n
    smem, vmem = pl.BlockSpec(memory_space=pltpu.SMEM), pl.BlockSpec(memory_space=pltpu.VMEM)
    anywhere = pl.BlockSpec(memory_space=pl.ANY)
    bf16, f32 = jnp.bfloat16, jnp.float32
    ins = [info, far, diag, q, g, full, peak, kv, dkv, normed_all, second]
    in_specs = [smem, smem] + [vmem] * 5 + [anywhere] * 3 + [vmem]
    devices = sizes["x"] * sizes["c"] * n * fast
    own_block = (width // devices, 4 * width)
    inner = None
    scratch, total = [], 0
    if own_block[0] % 16 == 0:
        whole = tuple(sizes[d] for d in SLOTS)
        more, inner, needed, left = stage_buffers(sizes, own_block, bf16, SLOTS, "cx")
        inner_more = more
        total += needed
        ins += [normed_own, dq_before, d_out.reshape(whole + (own_block[0], width))]
        in_specs += [vmem] * 3
        last_shape = jax.ShapeDtypeStruct(tuple(sizes[d] for d in left) + own_block, bf16)
    else:
        last_shape = jax.ShapeDtypeStruct((length, double), bf16)
    tasks_info, shapes, later = [], [], []
    for grad, order, widths in zip(grads, orders, splits):
        many = isinstance(grad, list)
        given = grad if many else [grad]
        block = given[0].shape[-2:]
        dims = ("z", "y") if many else ("x", "z", "y")
        more, counts, needed, left = stage_buffers(sizes, block, given[0].dtype, dims, order)
        if len(given) > 1:
            more = [pltpu.VMEM(given[0].shape, given[0].dtype)] + more
        scratch += more
        total += needed
        ends, widths = cut_shapes(block, left, widths, sizes, given[0].dtype)
        shapes += ends
        later.append(widths)
        tasks_info.append((order, dims, counts, len(ends), len(given)))
        ins += given
        in_specs += [vmem] * len(given)
    head_shapes = [
        jax.ShapeDtypeStruct((seqs, rows, width), f32),
        jax.ShapeDtypeStruct((rows, width), bf16),
        jax.ShapeDtypeStruct((pairs, 2, 5, 8, 2 * rows), f32),
    ]
    own_scratch = []
    if inner:
        own_scratch = [pltpu.VMEM(whole + own_block, bf16), pltpu.VMEM((length, double), bf16)]
        scratch = scratch + inner_more
    block = (seqs, n, fast, rows, width)
    own_scratch += [
        pltpu.VMEM((length, double), bf16),
        pltpu.VMEM((2, step, double), bf16),
        pltpu.VMEM((2, step, width), bf16),
        pltpu.VMEM(block, bf16),
        pltpu.VMEM((seqs, fast - 1, n, rows, width), bf16),
        pltpu.VMEM((seqs, 2, n, rows, width), bf16),
        pltpu.VMEM((2, 5, rows, rows), f32),
        pltpu.VMEM((2, 5, rows, rows), f32),
        pltpu.VMEM((2, width // pairs, rows), f32),
        pltpu.VMEM((width, double), f32) if inner else pltpu.VMEM((8, 128), f32),
    ]
    total += seqs * ((fast - 1) * n + 2 * n)
    outs = pl.pallas_call(
        functools.partial(back_rows_kernel, sizes, rows, tasks_info, inner),
        in_specs=in_specs,
        out_specs=[vmem] * (len(shapes) + 4),
        out_shape=head_shapes + shapes + [last_shape],
        scratch_shapes=own_scratch
        + scratch
        + [
            pltpu.SemaphoreType.DMA,
            pltpu.SemaphoreType.DMA((2,)),
            pltpu.SemaphoreType.DMA((2,)),
            pltpu.SemaphoreType.DMA((total,)),
            pltpu.SemaphoreType.DMA((total,)),
        ],
        compiler_params=pltpu.CompilerParams(
            collective_id=collective_id, has_side_effects=True, vmem_limit_bytes=62 << 20
        ),
        name=name,
    )(*ins)
    outs = list(outs)
    heads = [outs.pop(0) for _ in range(3)]
    results = []
    for (_, _, _, cut, _), widths in zip(tasks_info, later):
        results.append(cut_columns([outs.pop(0) for _ in range(cut)], widths))
    return heads + results + [outs[0], inner is not None]


def on_device(
    inputs,
    lengths,
    conv_taps,
    gain_attn,
    w_proj,
    w_query,
    w_key,
    w_value,
    w_out,
    gain_ffn,
    w_gate,
    w_up,
    w_down,
    rel_bias,
    cotangent,
):
    batch, seq = lax.axis_size("batch"), lax.axis_size("seq")
    sizes = layout_of(batch, seq)
    devices = batch * seq
    seqs, rows, width = inputs.shape
    length = rows * seq
    count = seqs * rows
    own = w_proj.shape[0]
    own_bias = rel_bias.shape[0]
    heads = own_bias * devices // NB
    hidden = w_gate.shape[1]

    small = jnp.concatenate(
        [
            conv_taps,
            gain_attn[:, None],
            gain_ffn[:, None],
            jnp.pad(rel_bias, (0, own - own_bias))[:, None],
            jnp.zeros((own, PACK - TAPS - 3), jnp.bfloat16),
        ],
        axis=1,
    )
    pairs = heads // 2
    key_value_w = jnp.stack([w_key.reshape(own, pairs, -1), w_value.reshape(own, pairs, -1)], axis=2)
    first, second, outer_plane, down_plane, left_rim = gather_all(
        [
            jnp.concatenate([small, w_proj, w_query], axis=1),
            key_value_w.reshape(own, -1),
            jnp.concatenate([w_out, w_gate, w_up], axis=1),
            w_down,
        ],
        ["Zyxc", "Zxyc", "zy", "yz"],
        sizes,
        1,
        rim=inputs[:, rows - 16 :, :],
        name="gather_first",
    )
    first = first.reshape(width, -1)
    second = second.reshape(width, -1)
    taps = first[:, :TAPS].astype(jnp.float32)
    gain_first = first[:, TAPS].astype(jnp.float32)
    gain_second = first[:, TAPS + 1].astype(jnp.float32)
    table = first[:, TAPS + 2].reshape(devices, own)[:, :own_bias].reshape(heads, NB).astype(jnp.float32)
    proj_w = first[:, PACK : PACK + width]
    query_w = first[:, PACK + width :]

    padded = jnp.concatenate([left_rim[:, 13:], inputs], axis=1).astype(jnp.float32)
    mixed_conv, conv_back = jax.vjp(partial(conv_mix, row_count=rows), padded, taps)
    mixed_low = mixed_conv.astype(jnp.bfloat16).reshape(count, width)
    resid_in = inputs.astype(jnp.float32).reshape(count, width)
    hidden_one = resid_in + mat_dot(mixed_low, proj_w)
    normed_one, norm_one_back = jax.vjp(norm_rows, hidden_one, gain_first)
    normed_low = normed_one.astype(jnp.bfloat16)

    outer_w, down_w, normed_all = gather_all(
        [outer_plane, down_plane],
        ["xc", "xc"],
        sizes,
        2,
        rows=normed_low.reshape(seqs, rows, width),
        plan=(0, 1, 2, 2, 2, 2),
        name="gather_rows",
    )
    outer_w = outer_w.reshape(width, -1)
    down_w = down_w.reshape(hidden, -1)
    out_w = outer_w[:, :width]
    wide_w = outer_w[:, width:]
    normed_all = normed_all.reshape(seqs * length, width)
    queries = mat_dot(normed_low, query_w).astype(jnp.bfloat16)
    key_value = mat_dot(normed_all, second).astype(jnp.bfloat16).reshape(seqs, length, 2 * width)

    far, diag = bias_tables(table, rows)
    info = jnp.concatenate([lengths, lax.axis_index("seq")[None].astype(jnp.int32)])
    attended, attended_full, inverse, peak = attend(info, far, diag, queries, key_value, rows, length)

    grad_low = cotangent.reshape(count, width)
    if own % 16 == 0:
        layer_out, d_hidden_two, d_out_w, scaled, d_gain_two, wide_pieces, down_half = feed_forward(
            hidden_one, attended, grad_low, outer_w, down_w, gain_second[None], inverse, sizes, 4
        )
        d_gain_two = d_gain_two[0]
    else:
        hidden_two = hidden_one + mat_dot(attended, out_w)
        normed_two, norm_two_back = jax.vjp(norm_rows, hidden_two, gain_second)
        normed_two_low = normed_two.astype(jnp.bfloat16)
        both_pre = mat_dot(normed_two_low, wide_w)
        inner_act, inner_back = jax.vjp(gated, both_pre[:, :hidden], both_pre[:, hidden:])
        inner_low = inner_act.astype(jnp.bfloat16)
        layer_out = (hidden_two + mat_dot(inner_low, down_w)).astype(jnp.bfloat16)

        d_down_w = outer_sum(inner_low, grad_low).astype(jnp.bfloat16)
        d_gate, d_up = inner_back(back_dot(grad_low, down_w))
        d_both = jnp.concatenate([d_gate.astype(jnp.bfloat16), d_up.astype(jnp.bfloat16)], axis=1)
        d_wide_w = outer_sum(normed_two_low, d_both).astype(jnp.bfloat16)
        d_hidden_part, d_gain_two = norm_two_back(back_dot(d_both, wide_w))
        d_hidden_two = grad_low.astype(jnp.float32) + d_hidden_part
        d_attn_low = d_hidden_two.astype(jnp.bfloat16)
        d_out_w = outer_sum(attended, d_attn_low).astype(jnp.bfloat16)
        d_attended = back_dot(d_attn_low, out_w).astype(jnp.bfloat16)
        scaled = (d_attended.astype(jnp.float32) * inverse).astype(jnp.bfloat16)
        wide_pieces, down_half = halve_cores([d_wide_w, d_down_w], [True, False], sizes, 4)
    scaled, wide_pieces, down_half, d_out_w, layer_out = lax.optimization_barrier(
        (scaled, wide_pieces, down_half, d_out_w, layer_out)
    )
    wide_others = from_others(wide_pieces, sizes)
    early = seqs - 1
    dq_before, dkv_before, near_before = attend_back(
        info, far, diag, queries, scaled, attended_full, key_value, peak, rows, length, early
    )
    dq_before, dkv_before, near_before, wide_others = lax.optimization_barrier(
        (dq_before, dkv_before, near_before, wide_others)
    )
    d_normed_one, dq_last, near, (g_gate, g_up), (g_down,), last, joined = back_rows(
        info,
        far,
        diag,
        queries,
        scaled,
        attended_full,
        key_value,
        peak,
        dkv_before,
        normed_all,
        normed_low,
        second,
        dq_before,
        d_out_w,
        [[wide_pieces[0]] + wide_others, down_half],
        ["Zy", "xs"],
        [(hidden, hidden), None],
        sizes,
        rows,
        5,
    )
    d_table = bias_grad(near_before + near, rows).reshape(heads * NB)
    d_queries = jnp.concatenate([dq_before, dq_last], axis=0)
    if joined:
        inner, inner_order = last, "s"
    else:
        d_key_value = jnp.concatenate([dkv_before, last[None]], axis=0).reshape(seqs * length, 2 * width)
        d_second_w = outer_sum(normed_all, d_key_value).astype(jnp.bfloat16)
        d_query_w = outer_sum(normed_low, d_queries).astype(jnp.bfloat16)
        inner, inner_order = jnp.concatenate([d_query_w, d_out_w, d_second_w], axis=1), "cxs"
    d_normed_one = d_normed_one.reshape(count, width)
    d_normed_one = d_normed_one + back_dot(d_queries, query_w)
    d_first_part, d_gain_one = norm_one_back(d_normed_one)
    d_hidden_one = d_hidden_two + d_first_part
    d_mix_low = d_hidden_one.astype(jnp.bfloat16)
    d_proj_w = outer_sum(mixed_low, d_mix_low).astype(jnp.bfloat16)
    d_mixed = back_dot(d_mix_low, proj_w).reshape(seqs, rows, width)
    d_padded, d_taps = conv_back(d_mixed)
    d_inputs = d_hidden_one.reshape(seqs, rows, width) + d_padded[:, 3:, :]
    d_small = jnp.concatenate(
        [
            d_taps.T,
            d_gain_one[None],
            d_gain_two[None],
            jnp.pad(d_table.reshape(devices, own_bias), ((0, 0), (0, own - own_bias))).reshape(1, width),
            jnp.zeros((16 - TAPS - 3, width), jnp.float32),
        ],
        axis=0,
    )
    d_last = jnp.concatenate([d_proj_w, jnp.pad(d_small.T, ((0, 0), (0, PACK - 16))).astype(jnp.bfloat16)], axis=1)
    (g_proj, g_small), (g_query, g_out, g_second), spill = reduce_all(
        [d_last, inner],
        ["cxs", inner_order],
        sizes,
        6,
        spill=d_padded[:, :8, :],
        splits=[(width, PACK), (width, width, 2 * width)],
    )
    input_grad = d_inputs.at[:, rows - 3 :, :].add(spill[:, :3]).astype(jnp.bfloat16)
    g_second = g_second.reshape(own, pairs, 2, -1)
    return (
        layer_out.reshape(seqs, rows, width),
        input_grad,
        g_small[:, :TAPS],
        g_small[:, TAPS],
        g_proj,
        g_query,
        g_second[:, :, 0].reshape(own, width),
        g_second[:, :, 1].reshape(own, width),
        g_out,
        g_small[:, TAPS + 1],
        g_gate,
        g_up,
        g_down.reshape(w_down.shape),
        g_small[:own_bias, TAPS + 2],
    )


def solution(mesh):
    in_specs = (
        P("batch", "seq", None),
        P("batch"),
        P(("batch", "seq"), None),
        P(("batch", "seq")),
        P(("batch", "seq"), None),
        P(("batch", "seq"), None),
        P(("batch", "seq"), None),
        P(("batch", "seq"), None),
        P(("batch", "seq"), None),
        P(("batch", "seq")),
        P(("batch", "seq"), None),
        P(("batch", "seq"), None),
        P(("batch", "seq"), None),
        P(("batch", "seq")),
        P("batch", "seq", None),
    )
    out_specs = (
        P("batch", "seq", None),
        P("batch", "seq", None),
        P(("batch", "seq"), None),
        P(("batch", "seq")),
        P(("batch", "seq"), None),
        P(("batch", "seq"), None),
        P(("batch", "seq"), None),
        P(("batch", "seq"), None),
        P(("batch", "seq"), None),
        P(("batch", "seq")),
        P(("batch", "seq"), None),
        P(("batch", "seq"), None),
        P(("batch", "seq"), None),
        P(("batch", "seq")),
    )
    return jax.shard_map(
        on_device, mesh=mesh, in_specs=in_specs, out_specs=out_specs, check_vma=False
    )
```

```python
import functools
from functools import partial

import jax
import jax.numpy as jnp
import numpy as np
from jax import lax
from jax.experimental import pallas as pl
from jax.experimental.pallas import tpu as pltpu
from jax.sharding import PartitionSpec as P

NB = 32
EPSILON = 1e-06
LIMITS = (12, 16, 23, 32, 46, 64, 91)
WINDOWS = ((2, 0), (3, 2), (4, 5))
TAPS = 9
PACK = 128
SPAN = 8

def mat_dot(lhs_array, rhs_array):
    return jnp.dot(lhs_array, rhs_array, preferred_element_type=jnp.float32)


def outer_sum(lhs_array, rhs_array):
    return lax.dot_general(
        lhs_array, rhs_array, (((0,), (0,)), ((), ())), preferred_element_type=jnp.float32
    )


def back_dot(grad_rows, weight):
    return lax.dot_general(
        grad_rows, weight, (((1,), (1,)), ((), ())), preferred_element_type=jnp.float32
    )


def bucket_of(relative):
    distance = jnp.abs(relative)
    larger = jnp.full(relative.shape, 8, jnp.int32)
    for threshold in LIMITS:
        larger = larger + (distance >= threshold).astype(jnp.int32)
    inside = jnp.where(distance < 8, distance, larger)
    return inside + 16 * (relative > 0).astype(jnp.int32)


def norm_rows(hidden, gain_row):
    return (
        hidden * lax.rsqrt(jnp.mean(hidden * hidden, axis=-1, keepdims=True) + EPSILON) * gain_row
    )


def gated(gate_pre, up_pre):
    return jax.nn.gelu(gate_pre, approximate=True) * up_pre


def conv_mix(padded, taps, row_count):
    summed = jnp.zeros(padded.shape[:-2] + (row_count, padded.shape[-1]), jnp.float32)
    for window_len, offset in WINDOWS:
        conv_sum = jnp.zeros_like(summed)
        for tap_index in range(window_len):
            shifted = lax.slice_in_dim(
                padded, 3 - tap_index, 3 - tap_index + row_count, axis=padded.ndim - 2
            )
            conv_sum = conv_sum + taps[:, offset + tap_index] * shifted
        summed = summed + jax.nn.gelu(conv_sum, approximate=True)
    return summed


def near_offsets(rows):
    lane = np.arange(2 * rows)
    lane = np.where(lane < rows, lane, lane - 2 * rows)
    return rows * (np.arange(3)[:, None, None] - 1) + np.arange(8)[None, :, None] - lane[None, None, :]


def bias_tables(table, rows):
    heads = table.shape[0]
    buckets = bucket_of(jnp.asarray(near_offsets(rows)[:, 0, :], jnp.int32)).reshape(-1)
    onehot = (buckets[None, :] == jnp.arange(NB, dtype=jnp.int32)[:, None]).astype(jnp.float32)
    diag = jnp.dot(table, onehot, precision=lax.Precision.HIGHEST)
    far = jnp.stack([table[:, NB // 2 - 1], table[:, NB - 1]], axis=1)
    return far, diag.reshape(heads // 2, 6, 2 * rows)


def bias_grad(near, rows):
    near = near.reshape(near.shape[0] * 2, 5, 8, 2 * rows)
    buckets = bucket_of(jnp.asarray(near_offsets(rows), jnp.int32))
    hit = buckets[None] == jnp.arange(NB, dtype=jnp.int32)[:, None, None, None]
    grad = jnp.sum(jnp.where(hit[None], near[:, None, 1:4], 0.0), axis=(2, 3, 4))
    left = jnp.sum(near[:, 0], axis=(1, 2))
    right = jnp.sum(near[:, 4], axis=(1, 2))
    return grad.at[:, NB // 2 - 1].add(left).at[:, NB - 1].add(right)


def nt_dot(a, b):
    return lax.dot_general(a, b, (((1,), (1,)), ((), ())), preferred_element_type=jnp.float32)


def tn_dot(a, b):
    return lax.dot_general(a, b, (((0,), (0,)), ((), ())), preferred_element_type=jnp.float32)


def nn_dot(a, b):
    return lax.dot_general(a, b, (((1,), (0,)), ((), ())), preferred_element_type=jnp.float32)


def fill_bias(rows, far_ref, diag_ref, bias_ref, pair):
    for a in range(2):
        bias_ref[a, 0] = jnp.full((rows, rows), far_ref[2 * pair + a, 0], jnp.float32)
        bias_ref[a, 4] = jnp.full((rows, rows), far_ref[2 * pair + a, 1], jnp.float32)
        for c in range(3):
            base = jnp.broadcast_to(diag_ref[0, 3 * a + c : 3 * a + c + 1, :], (rows, 2 * rows))
            bias_ref[a, 1 + c] = pltpu.roll(base, 0, 1, stride=1, stride_axis=0)[:, :rows]


def head_halves(block):
    lane = lax.broadcasted_iota(jnp.int32, block.shape, 1)
    zero = jnp.zeros_like(block)
    half = block.shape[1] // 2
    return jnp.where(lane < half, block, zero), jnp.where(lane < half, zero, block)


def attend_pair(rows, length, first, q, keys, values, spans, bias_ref, s_ref, acc_ref):
    halves = head_halves(q)
    wide = q.shape[1]
    half = wide // 2
    key_row = lax.broadcasted_iota(jnp.int32, (rows, rows), 0)
    lane = lax.broadcasted_iota(jnp.int32, (SPAN * rows, wide), 1)

    def scores(i, peaks):
        kc = i * SPAN
        k = keys(pl.ds(kc * rows, SPAN * rows))
        new = list(peaks)
        for a in range(2):
            full = nt_dot(k, halves[a])
            for u in range(SPAN):
                slot = jnp.clip(kc + u - first + 2, 0, 4)
                valid = key_row < length - (kc + u) * rows
                s = full[u * rows : (u + 1) * rows] + bias_ref[a, slot]
                s = jnp.where(valid, s, -1e9)
                s_ref[a, pl.ds((kc + u) * rows, rows), :] = s
                new[a] = jnp.maximum(new[a], jnp.max(s.reshape(rows // 8, 8, rows), axis=0))
        return tuple(new)

    def weigh(i, carry):
        here = pl.ds(i * SPAN * rows, SPAN * rows)
        v = values(here)
        ones = jnp.ones_like(v)
        for a, v_one in enumerate((jnp.where(lane < half, v, ones), jnp.where(lane < half, ones, v))):
            e = jnp.exp(s_ref[a, here, :] - tops[a])
            acc_ref[a] += tn_dot(v_one, e.astype(jnp.bfloat16))
        return carry

    low = jnp.full((8, rows), -jnp.inf, jnp.float32)
    peaks = scores(0, (low, low)) if spans == 1 else lax.fori_loop(0, spans, scores, (low, low))
    tops = [jnp.max(p, axis=0, keepdims=True) for p in peaks]
    acc_ref[...] = jnp.zeros_like(acc_ref)
    if spans == 1:
        weigh(0, 0)
    else:
        lax.fori_loop(0, spans, weigh, 0)
    inv = jnp.concatenate([1.0 / acc_ref[0, half:], 1.0 / acc_ref[1, :half]], axis=0)
    out = jnp.concatenate([acc_ref[0, :half], acc_ref[1, half:]], axis=0) * inv
    return out.T, inv.T, tops


def attend_kernel(rows, skip, info_ref, far_ref, diag_ref, q_ref, k_ref, v_ref, *refs):
    o_ref, full_ref, inv_ref, peak_ref, bias_ref, s_ref, acc_ref = refs
    pair, b = pl.program_id(0), pl.program_id(1)

    @pl.when(b == 0)
    def _():
        fill_bias(rows, far_ref, diag_ref, bias_ref, pair)

    out, inv, tops = attend_pair(
        rows,
        info_ref[b + skip],
        info_ref[info_ref.shape[0] - 1],
        q_ref[...],
        lambda here: k_ref[0, here, :],
        lambda here: v_ref[0, here, :],
        k_ref.shape[1] // (SPAN * rows),
        bias_ref,
        s_ref,
        acc_ref,
    )
    o_ref[...] = out.astype(o_ref.dtype)
    full_ref[...] = out
    inv_ref[...] = inv
    for a in range(2):
        peak_ref[0, 0, a : a + 1, :] = tops[a]


def attention_cost(q, kv, products):
    flops = products * 8 * q.shape[0] * kv.shape[1] * q.shape[1]
    return pl.CostEstimate(
        flops=flops, bytes_accessed=2 * (q.size + kv.size) * products, transcendentals=8 * q.shape[0] * kv.shape[1]
    )


def attention_shapes(seqs, rows, width, pairs):
    shape = (seqs * rows, width)
    return [
        jax.ShapeDtypeStruct(shape, jnp.bfloat16),
        jax.ShapeDtypeStruct(shape, jnp.float32),
        jax.ShapeDtypeStruct(shape, jnp.float32),
        jax.ShapeDtypeStruct((seqs, pairs, 2, rows), jnp.float32),
    ]


def attend(info, far, diag, q, kv, rows, length, skip):
    heads = far.shape[0]
    seqs = kv.shape[0]
    wide = 2 * (q.shape[1] // heads)
    pairs = heads // 2
    smem = pl.BlockSpec(memory_space=pltpu.SMEM)
    return pl.pallas_call(
        functools.partial(attend_kernel, rows, skip),
        grid=(pairs, seqs - skip),
        in_specs=[
            smem,
            smem,
            pl.BlockSpec((1, 6, 2 * rows), lambda p, b: (p, 0, 0)),
            pl.BlockSpec((rows, wide), lambda p, b: (b + skip, p)),
            pl.BlockSpec((1, length, wide), lambda p, b: (b + skip, 0, 2 * p)),
            pl.BlockSpec((1, length, wide), lambda p, b: (b + skip, 0, 2 * p + 1)),
        ],
        out_specs=[pl.BlockSpec((rows, wide), lambda p, b: (b, p))] * 3
        + [pl.BlockSpec((1, 1, 2, rows), lambda p, b: (b, p, 0, 0))],
        out_shape=attention_shapes(seqs - skip, rows, q.shape[1], pairs),
        scratch_shapes=[
            pltpu.VMEM((2, 5, rows, rows), jnp.float32),
            pltpu.VMEM((2, length, rows), jnp.float32),
            pltpu.VMEM((2, wide, rows), jnp.float32),
        ],
        compiler_params=pltpu.CompilerParams(vmem_limit_bytes=48 << 20),
        cost_estimate=attention_cost(q, kv, 1),
        name="attend",
    )(info, far, diag, q, kv, kv)


def back_pair(rows, length, first, q, g, full, key_value, peak, bias_ref, sum_ref, acc_ref, write):
    q_half, g_half = head_halves(q), head_halves(g)
    wide = q.shape[1]
    half = wide // 2
    key_row = lax.broadcasted_iota(jnp.int32, (rows, rows), 0)
    acc_ref[...] = jnp.zeros_like(acc_ref)
    along = (g.astype(jnp.float32) * full).T
    delta = [jnp.sum(along[a * half : (a + 1) * half], axis=0, keepdims=True) for a in range(2)]
    keys, spans = key_value

    def step(i, carry):
        kc = i * SPAN
        here = pl.ds(kc * rows, SPAN * rows)
        k, v = keys(here)
        dk = dv = None
        for a in range(2):
            s = nt_dot(k, q_half[a])
            dp = nt_dot(v, g_half[a])
            es, dss = [], []
            for u in range(SPAN):
                part = slice(u * rows, (u + 1) * rows)
                slot = jnp.clip(kc + u - first + 2, 0, 4)
                valid = key_row < length - (kc + u) * rows
                e = jnp.exp(s[part] + bias_ref[a, slot] - peak[a])
                e_low = jnp.where(valid, e, 0.0).astype(jnp.bfloat16)
                ds = e_low.astype(jnp.float32) * (dp[part] - delta[a])
                sum_ref[a, slot] += ds
                es.append(e_low)
                dss.append(ds.astype(jnp.bfloat16))
            e_low, ds_low = jnp.concatenate(es, axis=0), jnp.concatenate(dss, axis=0)
            dv_a = nn_dot(e_low, g_half[a])
            dk_a = nn_dot(ds_low, q_half[a])
            dv = dv_a if dv is None else dv + dv_a
            dk = dk_a if dk is None else dk + dk_a
            acc_ref[a] += tn_dot(k, ds_low)
        write(here, dk.astype(jnp.bfloat16), dv.astype(jnp.bfloat16))
        return carry

    if spans == 1:
        step(0, 0)
    else:
        lax.fori_loop(0, spans, step, 0)
    return jnp.concatenate([acc_ref[0, :half], acc_ref[1, half:]], axis=0).T.astype(jnp.bfloat16)


def near_sums(rows, sum_ref, write):
    for a in range(2):
        for slot in range(5):
            total_sum = jnp.zeros((8, 2 * rows), jnp.float32)
            for g in range(rows // 8):
                part = jnp.concatenate(
                    [sum_ref[a, slot, 8 * g : 8 * g + 8, :], jnp.zeros((8, rows), jnp.float32)], axis=1
                )
                if g and 0 < slot < 4:
                    part = pltpu.roll(part, 2 * rows - 8 * g, 1)
                total_sum = total_sum + part
            write(a, slot, total_sum)


def attend_back_kernel(rows, info_ref, far_ref, diag_ref, q_ref, g_ref, full_ref, k_ref, v_ref, peak_ref,
                       dq_ref, dkv_ref, near_ref, bias_ref, sum_ref, acc_ref):
    pair, b = pl.program_id(0), pl.program_id(1)

    @pl.when(b == 0)
    def _():
        fill_bias(rows, far_ref, diag_ref, bias_ref, pair)
        sum_ref[...] = jnp.zeros_like(sum_ref)

    wide = q_ref.shape[1]

    def write(here, dk, dv):
        dkv_ref[0, here, :wide] = dk
        dkv_ref[0, here, wide:] = dv

    dq_ref[...] = back_pair(
        rows,
        info_ref[b],
        info_ref[info_ref.shape[0] - 1],
        q_ref[...],
        g_ref[...],
        full_ref[...],
        (lambda here: (k_ref[0, here, :], v_ref[0, here, :]), k_ref.shape[1] // (SPAN * rows)),
        [peak_ref[0, 0, a : a + 1, :] for a in range(2)],
        bias_ref,
        sum_ref,
        acc_ref,
        write,
    )

    @pl.when(b == pl.num_programs(1) - 1)
    def _():
        def keep(a, slot, value):
            near_ref[0, a, slot] = value

        near_sums(rows, sum_ref, keep)


def attend_back(info, far, diag, q, g, full, kv, peak, rows, length, seqs):
    heads = far.shape[0]
    wide = 2 * (q.shape[1] // heads)
    pairs = heads // 2
    smem = pl.BlockSpec(memory_space=pltpu.SMEM)
    row_spec = pl.BlockSpec((rows, wide), lambda p, b: (b, p))
    return pl.pallas_call(
        functools.partial(attend_back_kernel, rows),
        grid=(pairs, seqs),
        in_specs=[
            smem,
            smem,
            pl.BlockSpec((1, 6, 2 * rows), lambda p, b: (p, 0, 0)),
            row_spec,
            row_spec,
            row_spec,
            pl.BlockSpec((1, length, wide), lambda p, b: (b, 0, 2 * p)),
            pl.BlockSpec((1, length, wide), lambda p, b: (b, 0, 2 * p + 1)),
            pl.BlockSpec((1, 1, 2, rows), lambda p, b: (b, p, 0, 0)),
        ],
        out_specs=[
            row_spec,
            pl.BlockSpec((1, length, 2 * wide), lambda p, b: (b, 0, p)),
            pl.BlockSpec((1, 2, 5, 8, 2 * rows), lambda p, b: (p, 0, 0, 0, 0)),
        ],
        out_shape=[
            jax.ShapeDtypeStruct((seqs * rows, q.shape[1]), jnp.bfloat16),
            jax.ShapeDtypeStruct((seqs,) + kv.shape[1:], jnp.bfloat16),
            jax.ShapeDtypeStruct((pairs, 2, 5, 8, 2 * rows), jnp.float32),
        ],
        scratch_shapes=[
            pltpu.VMEM((2, 5, rows, rows), jnp.float32),
            pltpu.VMEM((2, 5, rows, rows), jnp.float32),
            pltpu.VMEM((2, wide, rows), jnp.float32),
        ],
        compiler_params=pltpu.CompilerParams(vmem_limit_bytes=48 << 20),
        cost_estimate=attention_cost(q, kv, 3),
        name="attend_back",
    )(info, far, diag, q, g, full, kv, kv, peak)


SLOTS = ("x", "c", "z", "y")
MESH = pl.DeviceIdType.MESH


def layout_of(batch, seq):
    fast = 1 << ((seq.bit_length() - 1) // 2)
    return {"x": batch // 2, "c": 2, "z": seq // fast, "y": fast}


def tile_block(rows, cols):
    return (rows, cols) if rows % 16 == 0 else (rows * cols // 128, 128)


def place(sizes):
    b, s = lax.axis_index("batch"), lax.axis_index("seq")
    return {
        "x": lax.div(b, 2),
        "c": lax.rem(b, 2),
        "z": lax.div(s, sizes["y"]),
        "y": lax.rem(s, sizes["y"]),
    }


def device_at(sizes, me, dim, at):
    spot = dict(me)
    spot[dim] = at
    return (spot["x"] * 2 + spot["c"], spot["z"] * sizes["y"] + spot["y"])


def seq_peer(sizes, me, k):
    n = sizes["z"] * sizes["y"]
    return (me["x"] * 2 + me["c"], lax.rem(me["z"] * sizes["y"] + me["y"] + k, n))


def greet(sizes, me, dims):
    barrier = pltpu.get_barrier_semaphore()
    total = 0
    if "s" in dims:
        total = sizes["z"] * sizes["y"] - 1
        for k in range(1, total + 1):
            pl.semaphore_signal(barrier, inc=1, device_id=seq_peer(sizes, me, k), device_id_type=MESH)
        dims = [d for d in dims if d not in "szy"]
    for dim in dims:
        for k in range(1, sizes[dim]):
            peer = device_at(sizes, me, dim, lax.rem(me[dim] + k, sizes[dim]))
            pl.semaphore_signal(barrier, inc=1, device_id=peer, device_id_type=MESH)
            total += 1
    pl.semaphore_wait(barrier, total)


class Sems:
    def __init__(self, send, recv):
        self.send, self.recv, self.used = send, recv, 0

    def take(self, count):
        first = self.used
        self.used += count
        assert self.used <= self.send.shape[0]
        return first

    def copy(self, src, dst, index, device):
        return pltpu.make_async_remote_copy(
            src_ref=src, dst_ref=dst, send_sem=self.send.at[index], recv_sem=self.recv.at[index],
            device_id=device, device_id_type=MESH,
        )


def run_together(tasks, plan=()):
    tasks = list(tasks)
    over_already = set()
    for i in plan:
        if i not in over_already:
            try:
                next(tasks[i])
            except StopIteration:
                over_already.add(i)
    tasks = [t for i, t in enumerate(tasks) if i not in over_already]
    while tasks:
        left = []
        for task in tasks:
            try:
                next(task)
                left.append(task)
            except StopIteration:
                pass
        tasks = left


def gather_task(sizes, me, src, out, local_sem, sems, order):
    before = list(SLOTS[len(SLOTS) - (len(src.shape) - 2) :])
    dims = [d for d in SLOTS if d in order.lower() or d in before]
    own = pltpu.make_async_copy(src, out.at[tuple(me[d] for d in dims if d not in before)], local_sem)
    own.start()
    own.wait()
    done = before
    sent = []
    for dim in order:
        direct, dim = dim.isupper(), dim.lower()
        n, at = sizes[dim], me[dim]

        def region(origin):
            spots = []
            for d in dims:
                spots.append(slice(None) if d in done else (origin if d == dim else me[d]))
            return out.at[tuple(spots)]

        if n == 2:
            base = sems.take(1)
            other = 1 - at
            send = sems.copy(region(at), region(at), base, device_at(sizes, me, dim, other))
            send.start()
            yield
            sems.copy(region(other), region(other), base, device_at(sizes, me, dim, other)).wait_recv()
            sent.append((None, send))
        elif direct:
            base = sems.take(n - 1)
            for k in range(1, n):
                peer = device_at(sizes, me, dim, lax.rem(at + k, n))
                send = sems.copy(region(at), region(at), base + k - 1, peer)
                send.start()
                sent.append((None, send))
            yield
            for k in range(1, n):
                origin = lax.rem(at + n - k, n)
                sems.copy(region(origin), region(origin), base + k - 1, device_at(sizes, me, dim, origin)).wait_recv()
        else:
            for t in range(n - 1):
                base = sems.take(2)
                to_right = (at + 1 < n) & (at - t >= 0)
                to_left = (at >= 1) & (at + t < n)
                from_left = (at >= 1) & (at - 1 - t >= 0)
                from_right = (at + 1 < n) & (at + 1 + t < n)
                right = sems.copy(region(at - t), region(at - t), base, device_at(sizes, me, dim, at + 1))
                left = sems.copy(region(at + t), region(at + t), base + 1, device_at(sizes, me, dim, at - 1))
                pl.when(to_right)(right.start)
                pl.when(to_left)(left.start)
                sent += [(to_right, right), (to_left, left)]
                yield
                got = sems.copy(region(at - 1 - t), region(at - 1 - t), base, device_at(sizes, me, dim, at - 1))
                pl.when(from_left)(got.wait_recv)
                got = sems.copy(region(at + 1 + t), region(at + 1 + t), base + 1, device_at(sizes, me, dim, at + 1))
                pl.when(from_right)(got.wait_recv)
        done.append(dim)
    for cond, send in sent:
        if cond is None:
            send.wait_send()
        else:
            pl.when(cond)(send.wait_send)


def spread_task(sizes, me, src, out, sems):
    z, y, n, fast = me["z"], me["y"], sizes["z"], sizes["y"]
    fan = sems.take((fast - 1) * n)
    base = sems.take(2 * (n - 1))

    def fan_copy(k, origin, owner, to):
        spot = out.at[origin, owner]
        return sems.copy(spot, spot, fan + (k - 1) * n + origin, device_at(sizes, me, "y", to))

    def fan_out(origin):
        for k in range(1, fast):
            fan_copy(k, origin, y, lax.rem(y + k, fast)).start()

    def along(origin, index, to):
        spot = out.at[origin, y]
        return sems.copy(spot, spot, base + index, device_at(sizes, me, "z", to))

    moves = []
    for t in range(n - 1):
        moves.append(
            (
                (along(z - t, 2 * t, z + 1), (z + 1 < n) & (z - t >= 0)),
                (along(z + t, 2 * t + 1, z - 1), (z >= 1) & (z + t < n)),
                (along(z - 1 - t, 2 * t, z - 1), (z >= 1) & (z - 1 - t >= 0), z - 1 - t),
                (along(z + 1 + t, 2 * t + 1, z + 1), (z + 1 < n) & (z + 1 + t < n), z + 1 + t),
            )
        )
    fans = [fan_copy(k, origin, y, lax.rem(y + k, fast)) for k in range(1, fast) for origin in range(n)]

    def begin(t):
        for send, cond in moves[t][:2]:
            pl.when(cond)(send.start)

    def chains():
        out[z, y] = src[...]
        begin(0)
        fan_out(z)
        yield
        for t in range(n - 1):
            for got, cond, origin in moves[t][2:]:
                pl.when(cond)(got.wait_recv)
            if t + 1 < n - 1:
                begin(t + 1)
            for got, cond, origin in moves[t][2:]:
                pl.when(cond)(partial(fan_out, origin))
            yield
        for send in fans:
            send.wait_send()
        for move in moves:
            for send, cond in move[:2]:
                pl.when(cond)(send.wait_send)

    def across_y(use):
        def step(i, carry):
            far = lax.div(i + 1, 2)
            origin = jnp.where(lax.rem(i, 2) == 1, z - far, z + far)

            @pl.when((origin >= 0) & (origin < n))
            def _():
                for k in range(1, fast):
                    owner = lax.rem(y + fast - k, fast)
                    fan_copy(k, origin, owner, owner).wait_recv()
                    use(origin, owner)

            return carry

        lax.fori_loop(0, 2 * n - 1, step, 0)

    return chains(), across_y


def shift_task(sizes, me, src, out, sems, step):
    n = sizes["z"] * sizes["y"]
    s = me["z"] * sizes["y"] + me["y"]
    base = sems.take(1)
    send = sems.copy(src, out, base, seq_peer(sizes, me, step % n))
    has_to = (s < n - 1) if step > 0 else (s > 0)
    has_from = (s > 0) if step > 0 else (s < n - 1)
    pl.when(has_to)(send.start)
    yield
    pl.when(has_from)(send.wait_recv)

    @pl.when(jnp.logical_not(has_from))
    def _():
        out[...] = jnp.zeros_like(out)

    yield
    pl.when(has_to)(send.wait_send)


def stage_count(sizes, order):
    return sum(1 if sizes[d] == 2 else 2 * (sizes[d] - 1) for d in order.lower())


def gather_kernel(sizes, orders, has_rim, *refs):
    count = len(orders)
    total = count + has_rim
    ins, outs = refs[:total], refs[total : 2 * total]
    local_sem, send_sem, recv_sem = refs[2 * total :]
    me = place(sizes)
    used = [d for d in SLOTS if any(d in o.lower() for o in orders)]
    greet(sizes, me, used + ["s"] * has_rim)
    sems = Sems(send_sem, recv_sem)
    tasks = []
    for i in range(count):
        tasks.append(gather_task(sizes, me, ins[i], outs[i], local_sem.at[i], sems, orders[i]))
    if has_rim:
        tasks.append(shift_task(sizes, me, ins[-1], outs[-1], sems, 1))
    run_together(tasks)


def gather_shapes(shards, orders, sizes):
    ins, shapes = [], []
    for shard, order in zip(shards, orders):
        ins.append(shard if shard.ndim > 2 else shard.reshape(tile_block(*shard.shape)))
        before = SLOTS[len(SLOTS) - (ins[-1].ndim - 2) :]
        whole = tuple(sizes[d] for d in SLOTS if d in order.lower() or d in before)
        shapes.append(jax.ShapeDtypeStruct(whole + ins[-1].shape[-2:], shard.dtype))
    return ins, shapes, sum(stage_count(sizes, o) for o in orders)


def gather_all(shards, orders, sizes, collective_id, rim=None, name="gather"):
    ins, shapes, total = gather_shapes(shards, orders, sizes)
    out_specs = [pl.BlockSpec(memory_space=pl.ANY)] * len(ins)
    if rim is not None:
        ins.append(rim)
        shapes.append(jax.ShapeDtypeStruct(rim.shape, rim.dtype))
        out_specs.append(pl.BlockSpec(memory_space=pltpu.VMEM))
        total += 1
    return pl.pallas_call(
        functools.partial(gather_kernel, sizes, orders, int(rim is not None)),
        in_specs=[pl.BlockSpec(memory_space=pltpu.VMEM)] * len(ins),
        out_specs=out_specs,
        out_shape=shapes,
        scratch_shapes=[
            pltpu.SemaphoreType.DMA((len(ins),)),
            pltpu.SemaphoreType.DMA((total,)),
            pltpu.SemaphoreType.DMA((total,)),
        ],
        compiler_params=pltpu.CompilerParams(collective_id=collective_id, has_side_effects=True),
        name=name,
    )(*ins)


def gather_rows_kernel(sizes, rows, orders, *refs):
    count = len(orders)
    info_ref, far_ref, diag_ref, rows_ref, q_ref, second_ref = refs[:6]
    planes, refs = refs[6 : 6 + count], refs[6 + count :]
    gathered, refs = refs[:count], refs[count:]
    normed_out, kv_out, o_ref, full_ref, inv_ref, peak_ref = refs[:6]
    rows_buf, kv_buf, bias_ref, s_ref, acc_ref, local_sem, out_sem, send_sem, recv_sem = refs[6:]
    me = place(sizes)
    greet(sizes, me, SLOTS)
    sems = Sems(send_sem, recv_sem)
    first = me["z"] * sizes["y"] + me["y"]
    seqs, n = rows_ref.shape[0], sizes["z"]
    length = kv_buf.shape[1]
    pairs = diag_ref.shape[0]
    wide = q_ref.shape[1] // pairs
    weights = []
    for i in range(count):
        weights.append(gather_task(sizes, me, planes[i], gathered[i], local_sem.at[i], sems, orders[i]))
        next(weights[-1])
    pieces = [spread_task(sizes, me, rows_ref.at[p], rows_buf.at[p], sems) for p in range(seqs)]
    begun, rest = pieces[0][0], [p[0] for p in pieces[1:]]
    for _ in range(n):
        next(begun)
    for task in rest:
        next(task)

    def project(p):
        def block(z, y):
            at = pl.ds(pl.multiple_of((z * sizes["y"] + y) * rows, rows), rows)
            kv_buf[p, at, :] = nn_dot(rows_buf[p, z, y], second_ref[...]).astype(jnp.bfloat16)

        def column(z, carry):
            block(z, me["y"])
            return carry

        lax.fori_loop(0, n, column, 0)
        pieces[p][1](block)
        copies = [
            pltpu.make_async_copy(rows_buf.at[p], normed_out.at[p], out_sem.at[p, 0]),
            pltpu.make_async_copy(kv_buf.at[p], kv_out.at[p], out_sem.at[p, 1]),
        ]
        for copy in copies:
            copy.start()
        return copies

    copies = project(0)
    size = info_ref[0]

    def one_pair(p, carry):
        fill_bias(rows, far_ref, diag_ref.at[pl.ds(p, 1)], bias_ref, p)
        lanes = pl.ds(pl.multiple_of(p * wide, wide), wide)
        k_lanes = pl.ds(pl.multiple_of(2 * p * wide, wide), wide)
        v_lanes = pl.ds(pl.multiple_of((2 * p + 1) * wide, wide), wide)
        out, inv, tops = attend_pair(
            rows,
            size,
            first,
            q_ref[:rows, lanes],
            lambda here: kv_buf[0, here, k_lanes],
            lambda here: kv_buf[0, here, v_lanes],
            length // (SPAN * rows),
            bias_ref,
            s_ref,
            acc_ref,
        )
        o_ref[:, lanes] = out.astype(o_ref.dtype)
        full_ref[:, lanes] = out
        inv_ref[:, lanes] = inv
        for a in range(2):
            peak_ref[0, p, a : a + 1, :] = tops[a]
        for i in range(min(pairs, n - 1)):

            @pl.when(p == i)
            def _():
                for task in rest:
                    next(task)

        return carry

    lax.fori_loop(0, pairs, one_pair, 0)
    for _ in range(n - 1 - min(pairs, n - 1)):
        for task in rest:
            next(task)
    for task in weights:
        next(task, None)
    for p in range(1, seqs):
        copies += project(p)
    run_together(weights + [begun] + rest)
    for copy in copies:
        copy.wait()


def gather_rows(info, far, diag, normed, queries, second, planes, orders, sizes, collective_id):
    seqs, rows, width = normed.shape
    n, fast = sizes["z"], sizes["y"]
    length = rows * n * fast
    pairs = far.shape[0] // 2
    ins, shapes, total = gather_shapes(planes, orders, sizes)
    total += seqs * ((fast - 1) * n + 2 * (n - 1))
    bf16, f32 = jnp.bfloat16, jnp.float32
    smem, vmem = pl.BlockSpec(memory_space=pltpu.SMEM), pl.BlockSpec(memory_space=pltpu.VMEM)
    anywhere = pl.BlockSpec(memory_space=pl.ANY)
    count = len(ins)
    outs = pl.pallas_call(
        functools.partial(gather_rows_kernel, sizes, rows, orders),
        in_specs=[smem, smem] + [vmem] * (4 + count),
        out_specs=[anywhere] * (count + 2) + [vmem] * 4,
        out_shape=shapes
        + [
            jax.ShapeDtypeStruct((seqs, n, fast, rows, width), bf16),
            jax.ShapeDtypeStruct((seqs, length, 2 * width), bf16),
        ]
        + attention_shapes(1, rows, width, pairs),
        scratch_shapes=[
            pltpu.VMEM((seqs, n, fast, rows, width), bf16),
            pltpu.VMEM((seqs, length, 2 * width), bf16),
            pltpu.VMEM((2, 5, rows, rows), f32),
            pltpu.VMEM((2, length, rows), f32),
            pltpu.VMEM((2, width // pairs, rows), f32),
            pltpu.SemaphoreType.DMA((count,)),
            pltpu.SemaphoreType.DMA((seqs, 2)),
            pltpu.SemaphoreType.DMA((total,)),
            pltpu.SemaphoreType.DMA((total,)),
        ],
        compiler_params=pltpu.CompilerParams(
            collective_id=collective_id, has_side_effects=True, vmem_limit_bytes=60 << 20
        ),
        name="gather_rows",
    )(info, far, diag, normed, queries, second, *ins)
    return outs[:count], outs[count], outs[count + 1], outs[count + 2 :]


def over(extents, body):
    total = 1
    for e in extents:
        total *= e
    if total == 1:
        body((0,) * len(extents))
        return

    def step(i, carry):
        spots = []
        for e in reversed(extents):
            spots.append(lax.rem(i, e))
            i = lax.div(i, e)
        body(tuple(reversed(spots)))
        return carry

    lax.fori_loop(0, total, step, 0)


def add_into(dst, src_of, extents):
    def body(spots):
        here = spots + (slice(None), slice(None))
        dst[here] = (dst[here].astype(jnp.float32) + src_of(spots).astype(jnp.float32)).astype(dst.dtype)

    over(extents, body)


def add_pair(out, first, second_of, extents):
    def body(spots):
        here = spots + (slice(None), slice(None))
        out[here] = (first[here].astype(jnp.float32) + second_of(spots).astype(jnp.float32)).astype(out.dtype)

    over(extents, body)


def reduce_task(sizes, me, src, out, bufs, sems, order, dims):
    remaining = list(dims)
    current = src
    stages = []
    for stage, dim in enumerate(order):
        last = stage == len(order) - 1
        if dim == "s":
            n, s = sizes["z"] * sizes["y"], me["z"] * sizes["y"] + me["y"]
            base = sems.take(n)
            sends, recvs = [], []
            for k in range(1, n):
                to = lax.rem(s + k, n)
                spot = current.at[lax.div(to, sizes["y"]), lax.rem(to, sizes["y"])]
                sends.append(sems.copy(spot, bufs[stage].at[k], base + k, seq_peer(sizes, me, k)))
                recvs.append(sems.copy(bufs[stage].at[k], bufs[stage].at[k], base + k, seq_peer(sizes, me, k)))
            stages.append((dim, n, current, bufs[stage], sends, recvs, None, None, None))
            continue
        direct, dim = dim.isupper(), dim.lower()
        n, at = sizes[dim], me[dim]
        spot = remaining.index(dim)
        remaining.remove(dim)
        extents = [sizes[d] for d in remaining]

        def block(j, source=current, spot=spot):
            return source.at[(slice(None),) * spot + (j,)]

        def values(j, source=current, spot=spot):
            return lambda spots: source[spots[:spot] + (j,) + spots[spot:] + (slice(None), slice(None))]

        if direct:
            base = sems.take(n)
            moves = []
            for k in range(1, n):
                to, origin = lax.rem(at + k, n), lax.rem(at + n - k, n)
                buf = bufs[stage].at[k]
                send = sems.copy(block(to), buf, base + k, device_at(sizes, me, dim, to))
                moves.append((send, sems.copy(buf, buf, base + k, device_at(sizes, me, dim, origin))))
            result = out if last else bufs[stage].at[0]
            stages.append(("direct", n, result, bufs[stage], moves, at, values, extents, last))
            current = result
        elif n == 2:
            send = sems.copy(block(1 - at), bufs[stage], sems.take(1), device_at(sizes, me, dim, 1 - at))
            stages.append((dim, n, None, bufs[stage], [send], at, values, extents, last))
            current = bufs[stage]
        else:
            chains = bufs[stage][0]
            result = out if last else bufs[stage][1]
            base = sems.take(2 * n)
            moves = []
            for slot in range(n - 1):
                for side in range(2):
                    lead = at if side == 0 else n - 1 - at
                    j = lax.rem((n - 1 - slot + at) if side == 0 else (slot + 1 + at + n), n)
                    buf = chains.at[side, j]
                    to = device_at(sizes, me, dim, at + 1 if side == 0 else at - 1)
                    index = base + side * n + j
                    plain, summed = sems.copy(block(j), buf, index, to), sems.copy(buf, buf, index, to)
                    moves.append((plain, summed, buf, j, lead == 0, (lead > 0) & (lead <= slot), lead <= slot))
            ends = []
            for side in range(2):
                buf = chains.at[side, at]
                ends.append(sems.copy(buf, buf, base + side * n + at, device_at(sizes, me, dim, at)))
            conds = (at > 0, at < n - 1)
            stages.append((dim, n, result, chains, moves, at, values, extents, (ends, conds)))
            current = result

    for dim, n, source, buf, moves, at, values, extents, last in stages:
        if dim == "s":
            for send in moves:
                send.start()
            yield
            total = source[me["z"], me["y"]].astype(jnp.float32)
            for k in range(1, n):
                at[k - 1].wait_recv()
                total = total + buf[k].astype(jnp.float32)
            out[...] = total
        elif dim == "direct":
            for send, _ in moves:
                send.start()
            yield
            for _, got in moves:
                got.wait_recv()

            def add_all(spots):
                here = spots + (slice(None), slice(None))
                total = values(at)(spots).astype(jnp.float32)
                for k in range(1, n):
                    total = total + buf[(k,) + here].astype(jnp.float32)
                source[here] = total.astype(source.dtype)

            over(extents, add_all)
        elif n == 2:
            moves[0].start()
            yield
            moves[0].wait_recv()
            if last:
                add_pair(out, buf, values(at), extents)
            else:
                add_into(buf, values(at), extents)
        else:
            for slot in range(n - 1):
                for plain, summed, target, j, is_first, is_later, _ in moves[2 * slot : 2 * slot + 2]:

                    def pass_on(summed=summed, target=target, j=j):
                        summed.wait_recv()
                        add_into(target, values(j), extents)
                        summed.start()

                    pl.when(is_first)(plain.start)
                    pl.when(is_later)(pass_on)
                yield

            def start(spots):
                here = spots + (slice(None), slice(None))
                source[here] = values(at)(spots).astype(source.dtype)

            over(extents, start)
            ends, conds = last
            for side in range(2):

                def finish(side=side):
                    ends[side].wait_recv()
                    add_into(source, lambda spots: buf[(side, at) + spots + (slice(None), slice(None))], extents)

                pl.when(conds[side])(finish)
    for dim, n, _, _, moves, _, _, _, _ in stages:
        for move in moves:
            if dim == "direct":
                move[0].wait_send()
            elif dim == "s" or n == 2:
                move.wait_send()
            else:
                pl.when(move[-1])(move[1].wait_send)


class Split:
    def __init__(self, parts):
        self.parts = parts
        self.dtype = parts[0].dtype

    def __setitem__(self, here, value):
        first = 0
        for part in self.parts:
            last = first + part.shape[-1]
            part[here] = value[:, first:last]
            first = last

    def __getitem__(self, here):
        return jnp.concatenate([part[here] for part in self.parts], axis=1)


def stage_buffers(sizes, block, dtype, dims, order):
    scratch, counts, left, total = [], [], list(dims), 0
    for dim in order:
        counts.append(1)
        if dim == "s":
            left = []
            n = sizes["z"] * sizes["y"]
            scratch.append(pltpu.VMEM((n,) + block, dtype))
            total += n
            continue
        left.remove(dim.lower())
        shape = tuple(sizes[d] for d in left) + block
        n = sizes[dim.lower()]
        if dim.isupper():
            scratch.append(pltpu.VMEM((n,) + shape, dtype))
            total += n
        elif n == 2:
            scratch.append(pltpu.VMEM(shape, dtype))
            total += 1
        else:
            scratch.append(pltpu.VMEM((2, n) + shape, dtype))
            total += 2 * n
            if dim != order[-1]:
                scratch.append(pltpu.VMEM(shape, dtype))
                counts[-1] = 2
    return scratch, counts, total, left


def stage_refs(sizes, order, counts, bufs):
    stages = []
    for dim, size in zip(order, counts):
        taken = [bufs.pop(0) for _ in range(size)]
        stages.append(taken[0] if dim == "s" or dim.isupper() or sizes[dim] == 2 else taken)
    return stages


def reduce_kernel(sizes, orders, dims, counts, splits, spill, *refs):
    count = len(orders)
    total = count + spill
    ends = sum(splits) + spill
    ins, outs = refs[:total], list(refs[total : total + ends])
    send_sem, recv_sem = refs[-2:]
    bufs = list(refs[total + ends : -2])
    me = place(sizes)
    used = [d for d in SLOTS if any(d in o.lower() for o in orders)]
    greet(sizes, me, used + ["s"] * (spill or any("s" in o for o in orders)))
    sems = Sems(send_sem, recv_sem)
    tasks = []
    for i in range(count):
        stages = stage_refs(sizes, orders[i], counts[i], bufs)
        parts = [outs.pop(0) for _ in range(splits[i])]
        out = parts[0] if len(parts) == 1 else Split(parts)
        tasks.append(reduce_task(sizes, me, ins[i], out, stages, sems, orders[i], dims[i]))
    if spill:
        tasks.insert(0, shift_task(sizes, me, ins[-1], outs.pop(0), sems, -1))
    run_together(tasks)


def cut_shapes(block, left, widths, sizes, dtype):
    if left or widths is None or sum(widths) != block[1]:
        shape = tuple(sizes[d] for d in left) + block
        return [jax.ShapeDtypeStruct(shape, dtype if left else jnp.float32)], widths
    return [jax.ShapeDtypeStruct((block[0], w), jnp.float32) for w in widths], None


def cut_columns(parts, widths):
    if widths is None:
        return parts
    full = parts[0].reshape(-1, sum(widths))
    edges = np.cumsum([0] + list(widths))
    return [full[:, int(lo) : int(hi)] for lo, hi in zip(edges[:-1], edges[1:])]


def reduce_all(grads, orders, sizes, collective_id, spill=None, splits=None, name="reduce"):
    ins, scratch, shapes, counts, all_dims, cuts, later = [], [], [], [], [], [], []
    splits = splits or [None] * len(grads)
    total = 0
    devices = sizes["x"] * sizes["c"] * sizes["z"] * sizes["y"]
    for grad, order, widths in zip(grads, orders, splits):
        dims = SLOTS[-(grad.ndim - 2) :] if grad.ndim > 2 else SLOTS
        if grad.ndim == 2:
            whole = tuple(sizes[d] for d in SLOTS)
            grad = grad.reshape(whole + tile_block(grad.shape[0] // devices, grad.shape[1]))
        block = grad.shape[-2:]
        ins.append(grad)
        all_dims.append(dims)
        more, taken, needed, left = stage_buffers(sizes, block, grad.dtype, dims, order)
        scratch += more
        total += needed
        counts.append(taken)
        ends, widths = cut_shapes(block, left, widths, sizes, grad.dtype)
        shapes += ends
        cuts.append(len(ends))
        later.append(widths)
    if spill is not None:
        ins.append(spill)
        shapes.append(jax.ShapeDtypeStruct(spill.shape, spill.dtype))
        total += 1
    outs = pl.pallas_call(
        functools.partial(reduce_kernel, sizes, orders, all_dims, counts, cuts, int(spill is not None)),
        in_specs=[pl.BlockSpec(memory_space=pltpu.VMEM)] * len(ins),
        out_specs=[pl.BlockSpec(memory_space=pltpu.VMEM)] * len(shapes),
        out_shape=shapes,
        scratch_shapes=scratch + [pltpu.SemaphoreType.DMA((total,)), pltpu.SemaphoreType.DMA((total,))],
        compiler_params=pltpu.CompilerParams(
            collective_id=collective_id, has_side_effects=True, vmem_limit_bytes=56 << 20
        ),
        name=name,
    )(*ins)
    outs = list(outs)
    results = []
    for cut, widths in zip(cuts, later):
        results.append(cut_columns([outs.pop(0) for _ in range(cut)], widths))
    return results + outs


def collect_task(sizes, me, src, out, ybuf, chain, sems, produce):
    z, y, n, fast = me["z"], me["y"], sizes["z"], sizes["y"]
    fan = sems.take((fast - 1) * n)
    base = sems.take(2 * n)

    def fan_copy(k, j):
        to = lax.rem(y + k, fast)
        index = fan + (k - 1) * n + j
        return sems.copy(src.at[j, to], ybuf.at[k - 1, j], index, device_at(sizes, me, "y", to))

    def spread(i, carry):
        far = n - 1 - lax.div(i, 2)
        j = jnp.where(lax.rem(i, 2) == 0, z + far, z - far)

        @pl.when((j >= 0) & (j < n))
        def _():
            produce(j)
            for k in range(1, fast):
                fan_copy(k, j).start()

        return carry

    def chain_copy(side, j, to, plain=False):
        buf = chain.at[side, j]
        return sems.copy(ybuf.at[0, j] if plain else buf, buf, base + side * n + j, device_at(sizes, me, "z", to))

    slots = []
    for slot in range(n - 1):
        for side in range(2):
            lead = z if side == 0 else n - 1 - z
            j = lax.rem((n - 1 - slot + z) if side == 0 else (slot + 1 + z + n), n)
            to = z + 1 if side == 0 else z - 1
            ends = (chain_copy(side, j, to, True), chain_copy(side, j, to))
            slots.append((side, j, ends, lead == 0, (lead > 0) & (lead <= slot), lead <= slot))
    fans = [fan_copy(k, j) for j in range(n) for k in range(1, fast)]
    lax.fori_loop(0, 2 * n - 1, spread, 0)
    yield

    def merge(j):
        for k in range(1, fast):
            fan_copy(k, j).wait_recv()
        value = src[j, y].astype(jnp.float32)
        for k in range(1, fast):
            value = value + ybuf[k - 1, j].astype(jnp.float32)
        return value

    for slot in range(n - 1):
        for side, j, (plain, summed), is_first, is_later, _ in slots[2 * slot : 2 * slot + 2]:

            def begin(plain=plain, j=j):
                ybuf[0, j] = merge(j).astype(ybuf.dtype)
                plain.start()

            def pass_on(summed=summed, side=side, j=j):
                value = merge(j)
                summed.wait_recv()
                chain[side, j] = (chain[side, j].astype(jnp.float32) + value).astype(chain.dtype)
                summed.start()

            pl.when(is_first)(begin)
            pl.when(is_later)(pass_on)
        yield
    out[...] = merge(z)

    def finish(side):
        chain_copy(side, z, z).wait_recv()
        out[...] += chain[side, z].astype(jnp.float32)

    pl.when(z > 0)(partial(finish, 0))
    pl.when(z < n - 1)(partial(finish, 1))
    for fan_end in fans:
        fan_end.wait_send()
    for _, _, (_, summed), _, _, active in slots:
        pl.when(active)(summed.wait_send)


def halve_kernel(sizes, apart, *refs):
    n, count = sizes["x"], len(apart)
    refs = list(refs)
    ins = [refs.pop(0) for _ in range(count)]
    outs = [[refs.pop(0) for _ in range(n)] if alone else refs.pop(0) for alone in apart]
    bufs = [refs.pop(0) for _ in range(count)]
    send_sem, recv_sem = refs
    me = place(sizes)
    greet(sizes, me, ("c",))
    sems = Sems(send_sem, recv_sem)
    c = me["c"]
    peer = device_at(sizes, me, "c", 1 - c)
    sends = {}
    for k in range(n - 1, -1, -1):
        for i, alone in enumerate(apart):
            at = lax.rem(me["x"] + k, n) if alone else k
            sends[k, i] = sems.copy(ins[i].at[at, 1 - c], bufs[i].at[k], sems.take(1), peer)
            sends[k, i].start()
    for k in range(n - 1, -1, -1):
        for i, alone in enumerate(apart):
            at = lax.rem(me["x"] + k, n) if alone else k
            sends[k, i].wait_recv()
            src = ins[i]

            def own(spots, src=src, at=at):
                return src[(at, c) + spots + (slice(None), slice(None))]

            add_pair(outs[i][k] if alone else outs[i].at[k], bufs[i].at[k], own, src.shape[2:-2])
    for send in sends.values():
        send.wait_send()


def halve_cores(grads, apart, sizes, collective_id, name="halve"):
    n = sizes["x"]
    whole = tuple(sizes[d] for d in SLOTS)
    devices = whole[0] * whole[1] * whole[2] * whole[3]
    ins = [g.reshape(whole + tile_block(g.shape[0] // devices, g.shape[1])) for g in grads]
    halves = [g.shape[:1] + g.shape[2:] for g in ins]
    shapes = []
    for h, g, alone in zip(halves, ins, apart):
        shapes += [jax.ShapeDtypeStruct(h[1:], g.dtype)] * n if alone else [jax.ShapeDtypeStruct(h, g.dtype)]
    total = n * len(ins)
    outs = pl.pallas_call(
        functools.partial(halve_kernel, sizes, apart),
        in_specs=[pl.BlockSpec(memory_space=pltpu.VMEM)] * len(ins),
        out_specs=[pl.BlockSpec(memory_space=pltpu.VMEM)] * len(shapes),
        out_shape=shapes,
        scratch_shapes=[pltpu.VMEM(h, g.dtype) for h, g in zip(halves, ins)]
        + [pltpu.SemaphoreType.DMA((total,)), pltpu.SemaphoreType.DMA((total,))],
        compiler_params=pltpu.CompilerParams(
            collective_id=collective_id, has_side_effects=True, vmem_limit_bytes=56 << 20
        ),
        name=name,
    )(*ins)
    outs = list(outs)
    return [[outs.pop(0) for _ in range(n)] if alone else outs.pop(0) for alone in apart]


def feed_forward_kernel(sizes, *refs):
    n = sizes["x"]
    hidden_ref, cot_ref, outer_ref, down_ref, gain_ref = refs[:5]
    att_parts, inv_parts, refs = refs[5:7], refs[7:9], refs[9:]
    layer_ref, d_hidden_ref, d_out_ref, scaled_ref, d_gain_ref = refs[:5]
    wide_outs, down_out = refs[5 : 5 + n], refs[5 + n]
    d_wide, d_down, wide_buf, down_buf, two_ref, low_ref, d_normed, att_ref, send_sem, recv_sem = refs[6 + n :]
    cut = att_parts[0].shape[0]
    att_ref[:cut] = att_parts[0][...]
    att_ref[cut:] = att_parts[1][...]
    me = place(sizes)
    greet(sizes, me, ("c",))
    sems = Sems(send_sem, recv_sem)
    c = me["c"]
    peer = device_at(sizes, me, "c", 1 - c)
    width = hidden_ref.shape[1]
    parts = 2 * n
    units = down_ref.shape[0] // parts
    two_ref[...] = hidden_ref[...] + nn_dot(att_ref[...], outer_ref[:, :width])
    gain = gain_ref[...]

    def scale():
        return lax.rsqrt(jnp.mean(two_ref[...] * two_ref[...], axis=1, keepdims=True) + EPSILON)

    low_ref[...] = (two_ref[...] * scale() * gain).astype(jnp.bfloat16)
    d_normed[...] = jnp.zeros_like(d_normed)
    d_hidden_ref[...] = two_ref[...]

    def down_copy(x):
        return sems.copy(d_down.at[x, 1 - c], down_buf.at[x], x, peer)

    def part(i, carry):
        gate_at = pl.ds(pl.multiple_of(i * units, units), units)
        up_at = pl.ds(pl.multiple_of((parts + i) * units, units), units)
        gate_w = outer_ref[:, pl.ds(pl.multiple_of(width + i * units, units), units)]
        up_w = outer_ref[:, pl.ds(pl.multiple_of(width + (parts + i) * units, units), units)]
        down_w = down_ref[gate_at, :]
        low, cot = low_ref[...], cot_ref[...]
        gate, up = nn_dot(low, gate_w), nn_dot(low, up_w)
        square = gate * gate
        bend = jnp.tanh(0.7978845608 * gate * (1.0 + 0.044715 * square))
        half = 0.5 * (1.0 + bend)
        act = gate * half
        slope = half + gate * (0.5 * (1.0 - bend * bend)) * (0.7978845608 * (1.0 + 3.0 * 0.044715 * square))
        inner = (act * up).astype(jnp.bfloat16)
        d_hidden_ref[...] += nn_dot(inner, down_w)
        d_inner = nt_dot(cot, down_w)
        d_gate = (d_inner * up * slope).astype(jnp.bfloat16)
        d_up = (d_inner * act).astype(jnp.bfloat16)
        d_down[lax.div(i, 2), lax.rem(i, 2)] = (
            tn_dot(inner, cot).astype(jnp.bfloat16).reshape(d_down.shape[2:])
        )
        pl.when(lax.rem(i, 2) != c)(lambda: down_copy(lax.div(i, 2)).start())
        block = d_wide.shape[:-1] + (units,)
        d_wide[..., gate_at] = tn_dot(low, d_gate).astype(jnp.bfloat16).reshape(block)
        d_wide[..., up_at] = tn_dot(low, d_up).astype(jnp.bfloat16).reshape(block)
        d_normed[...] += nt_dot(d_gate, gate_w) + nt_dot(d_up, up_w)
        return carry

    lax.fori_loop(0, parts, part, 0)
    sends = [down_copy(x) for x in range(n)]
    for x in range(n):
        send = sems.copy(d_wide.at[x, 1 - c], wide_buf.at[x], n + x, peer)
        send.start()
        sends.append(send)
    layer_ref[...] = d_hidden_ref[...].astype(jnp.bfloat16)
    two, s2 = two_ref[...], scale()
    pulled = gain * d_normed[...]
    d_gain_ref[...] = jnp.sum(d_normed[...] * two * s2, axis=0, keepdims=True)
    drift = jnp.mean(two * pulled, axis=1, keepdims=True)
    d_two = cot_ref[...].astype(jnp.float32) + s2 * pulled - two * (s2 * s2 * s2 * drift)
    d_hidden_ref[...] = d_two
    d_low = d_two.astype(jnp.bfloat16)
    d_out_ref[...] = tn_dot(att_ref[...], d_low).astype(jnp.bfloat16)
    d_att = nt_dot(d_low, outer_ref[:, :width]).astype(jnp.bfloat16)
    scaled_ref[:cut] = (d_att[:cut].astype(jnp.float32) * inv_parts[0][...]).astype(jnp.bfloat16)
    scaled_ref[cut:] = (d_att[cut:].astype(jnp.float32) * inv_parts[1][...]).astype(jnp.bfloat16)
    for send in sends:
        send.wait_recv()
    for x in range(n):
        add_pair(down_out.at[x], down_buf.at[x], lambda at, x=x: d_down[(x, c) + at], d_down.shape[2:-2])
        at_x = lax.rem(me["x"] + x, n)
        add_pair(wide_outs[x], wide_buf.at[at_x], lambda at, at_x=at_x: d_wide[(at_x, c) + at], d_wide.shape[2:-2])
    for send in sends:
        send.wait_send()


def feed_forward(hidden_one, cotangent, outer_w, down_w, gain, attended, inverse, sizes, collective_id):
    n = sizes["x"]
    whole = tuple(sizes[d] for d in SLOTS)
    devices = whole[0] * whole[1] * whole[2] * whole[3]
    count, width = hidden_one.shape
    hidden = down_w.shape[0]
    bf16, f32 = jnp.bfloat16, jnp.float32
    wide_block = (width // devices, 2 * hidden)
    down_block = (hidden // devices, width)
    plane = whole[2:]
    vmem = pl.BlockSpec(memory_space=pltpu.VMEM)
    outs = pl.pallas_call(
        functools.partial(feed_forward_kernel, sizes),
        in_specs=[vmem] * 9,
        out_specs=[vmem] * (6 + n),
        out_shape=[
            jax.ShapeDtypeStruct((count, width), bf16),
            jax.ShapeDtypeStruct((count, width), f32),
            jax.ShapeDtypeStruct((width, width), bf16),
            jax.ShapeDtypeStruct((count, width), bf16),
            jax.ShapeDtypeStruct((1, width), f32),
        ]
        + [jax.ShapeDtypeStruct(plane + wide_block, bf16)] * n
        + [jax.ShapeDtypeStruct((n,) + plane + down_block, bf16)],
        scratch_shapes=[
            pltpu.VMEM(whole + wide_block, bf16),
            pltpu.VMEM(whole + down_block, bf16),
            pltpu.VMEM((n,) + plane + wide_block, bf16),
            pltpu.VMEM((n,) + plane + down_block, bf16),
            pltpu.VMEM((count, width), f32),
            pltpu.VMEM((count, width), bf16),
            pltpu.VMEM((count, width), f32),
            pltpu.VMEM((count, width), bf16),
            pltpu.SemaphoreType.DMA((2 * n,)),
            pltpu.SemaphoreType.DMA((2 * n,)),
        ],
        compiler_params=pltpu.CompilerParams(
            collective_id=collective_id, has_side_effects=True, vmem_limit_bytes=60 << 20
        ),
        name="feed_forward",
    )(hidden_one, cotangent, outer_w, down_w, gain, *attended, *inverse)
    return list(outs[:5]) + [list(outs[5 : 5 + n]), outs[5 + n]]


def from_others(pieces, sizes):
    n = sizes["x"]
    got = []
    for k in range(1, n):
        pairs = [(((x + k) % n) * 2 + c, x * 2 + c) for x in range(n) for c in range(2)]
        got.append(lax.ppermute(pieces[n - k], "batch", pairs))
    return got


def back_rows_kernel(sizes, rows, tasks_info, inner, *refs):
    refs = list(refs)

    def take(count):
        taken = refs[:count]
        del refs[:count]
        return taken

    info_ref, far_ref, diag_ref, q_ref, g_ref, full_ref, peak_ref, kv_ref, dkv_ref, normed_ref, second_ref = take(11)
    if inner:
        own_ref, dq_before_ref, d_out_ref = take(3)
    grads = [take(info[4]) for info in tasks_info]
    d_normed_ref, dq_ref, near_ref = take(3)
    outs = [take(info[3]) for info in tasks_info]
    last_ref = take(1)[0]
    if inner:
        inner_ref = take(1)[0]
        inner_counts = inner
        d_last_ref = take(1)[0]
    else:
        d_last_ref = last_ref
    kv_buf, chunk_ref, normed_buf, d_rows_ref, ybuf, chain, bias_ref, sum_ref, acc_ref, total_ref = take(10)
    kv_sem, chunk_sem, normed_sem, send_sem, recv_sem = refs[-5:]
    bufs = refs[:-5]
    me = place(sizes)
    first = me["z"] * sizes["y"] + me["y"]
    seqs, length, _ = kv_ref.shape
    n = sizes["z"]
    step = length // n
    last = seqs - 1
    width = q_ref.shape[1]
    pairs = diag_ref.shape[0]
    wide = width // pairs
    fetch = pltpu.make_async_copy(kv_ref.at[last], kv_buf, kv_sem)
    fetch.start()
    greet(sizes, me, SLOTS + ("s",))
    sems = Sems(send_sem, recv_sem)
    ffn = []
    for (order, dims, counts, _, many), grad, out in zip(tasks_info, grads, outs):
        src = grad[0]
        if many > 1:
            src = bufs.pop(0)

            def total(spots, src=src, grad=grad):
                here = spots + (slice(None), slice(None))
                value = grad[0][here].astype(jnp.float32)
                for more in grad[1:]:
                    value = value + more[here].astype(jnp.float32)
                src[here] = value.astype(src.dtype)

            over(src.shape[:-2], total)
        stages = stage_refs(sizes, order, counts, bufs)
        ffn.append(reduce_task(sizes, me, src, out[0] if len(out) == 1 else Split(out), stages, sems, order, dims))
        next(ffn[-1])
    wide_task, down_task = ffn

    def rows_of(p):
        def produce(j):
            here = pl.ds(pl.multiple_of(j * step, step), step)
            if p < last:
                copy = pltpu.make_async_copy(dkv_ref.at[p, here], chunk_ref.at[0], chunk_sem.at[0])
                copy.start()
                copy.wait()
                block = chunk_ref[0]
            else:
                block = d_last_ref[here, :]
            block = nt_dot(block, second_ref[...]).astype(jnp.bfloat16)
            d_rows_ref[p, j] = block.reshape(d_rows_ref.shape[2:])

        return collect_task(
            sizes, me, d_rows_ref.at[p], d_normed_ref.at[p], ybuf.at[p], chain.at[p], sems, produce
        )

    before = [rows_of(p) for p in range(last)]
    for task in before:
        next(task)
    fetch.wait()
    size = info_ref[last]

    def one_pair(p, carry):
        fill_bias(rows, far_ref, diag_ref.at[pl.ds(p, 1)], bias_ref, p)
        sum_ref[...] = jnp.zeros_like(sum_ref)
        lanes = pl.ds(pl.multiple_of(p * wide, wide), wide)
        tail = slice(last * rows, seqs * rows)
        k_lanes = pl.ds(pl.multiple_of(2 * p * wide, wide), wide)
        v_lanes = pl.ds(pl.multiple_of((2 * p + 1) * wide, wide), wide)

        def write(here, dk, dv):
            d_last_ref[here, k_lanes] = dk
            d_last_ref[here, v_lanes] = dv

        dq_ref[:, lanes] = back_pair(
            rows,
            size,
            first,
            q_ref[tail, lanes],
            g_ref[tail, lanes],
            full_ref[:, lanes],
            (lambda here: (kv_buf[here, k_lanes], kv_buf[here, v_lanes]), length // (SPAN * rows)),
            [peak_ref[0, p, a : a + 1, :] for a in range(2)],
            bias_ref,
            sum_ref,
            acc_ref,
            write,
        )

        def keep(a, slot, value):
            near_ref[p, a, slot] = value

        near_sums(rows, sum_ref, keep)
        for i in range(min(pairs, n - 1)):

            @pl.when(p == i)
            def _():
                for task in before:
                    next(task, None)

        @pl.when(p == pairs - 1)
        def _():
            next(wide_task)
            next(down_task)

        return carry

    lax.fori_loop(0, pairs, one_pair, 0)
    after = rows_of(last)
    next(after)
    tasks = ffn + before + [after]
    if inner:
        steps = seqs * n
        early = last * n

        def at_step(i):
            return pl.ds(pl.multiple_of(i * step, step), step)

        def normed_copy(i):
            slot = lax.rem(i, 2)
            return pltpu.make_async_copy(normed_ref.at[at_step(i)], normed_buf.at[slot], normed_sem.at[slot])

        def early_copy(i):
            slot = lax.rem(i, 2)
            src = dkv_ref.at[lax.div(i, n), at_step(lax.rem(i, n))]
            return pltpu.make_async_copy(src, chunk_ref.at[slot], chunk_sem.at[slot])

        normed_copy(0).start()
        early_copy(0).start()
        total_ref[...] = jnp.zeros_like(total_ref)

        plan = [[], before, [], [wide_task], [after], [], [after]]

        def weigh(i, carry):
            pl.when(i + 1 < steps)(lambda: normed_copy(i + 1).start())
            pl.when(i + 1 < early)(lambda: early_copy(i + 1).start())
            normed_copy(i).wait()
            slot = lax.rem(i, 2)

            @pl.when(i < early)
            def _():
                early_copy(i).wait()
                total_ref[...] += tn_dot(normed_buf[slot], chunk_ref[slot])

            @pl.when(i >= early)
            def _():
                total_ref[...] += tn_dot(normed_buf[slot], d_last_ref[at_step(i - early), :])

            for k, tasks_now in enumerate(plan):

                @pl.when(i == k)
                def _():
                    for task in tasks_now:
                        next(task, None)

            return carry

        lax.fori_loop(0, steps, weigh, 0)
        block = inner_ref.shape[:-1]
        d_query = tn_dot(own_ref[last * rows :], dq_ref[...])
        if last:
            d_query = d_query + tn_dot(own_ref[: last * rows], dq_before_ref[...])
        inner_ref[..., :width] = d_query.astype(jnp.bfloat16).reshape(block + (width,))
        inner_ref[..., width : 2 * width] = d_out_ref[...]
        inner_ref[..., 2 * width :] = total_ref[...].astype(jnp.bfloat16).reshape(block + (2 * width,))
        stages = stage_refs(sizes, "cx", inner_counts, bufs)
        tasks.insert(0, reduce_task(sizes, me, inner_ref, last_ref, stages, sems, "cx", SLOTS))
    run_together(tasks)


def back_rows(info, far, diag, q, g, full, kv, peak, dkv, normed_all, normed_own, second, dq_before, d_out, grads,
              orders, splits, sizes, rows, collective_id, name="back_rows"):
    seqs, length, double = kv.shape
    width = q.shape[1]
    last = seqs - 1
    pairs = far.shape[0] // 2
    n, fast = sizes["z"], sizes["y"]
    step = length // n
    smem, vmem = pl.BlockSpec(memory_space=pltpu.SMEM), pl.BlockSpec(memory_space=pltpu.VMEM)
    anywhere = pl.BlockSpec(memory_space=pl.ANY)
    bf16, f32 = jnp.bfloat16, jnp.float32
    ins = [info, far, diag, q, g, full, peak, kv, dkv, normed_all, second]
    in_specs = [smem, smem] + [vmem] * 5 + [anywhere] * 3 + [vmem]
    devices = sizes["x"] * sizes["c"] * n * fast
    own_block = (width // devices, 4 * width)
    inner = None
    scratch, total = [], 0
    if own_block[0] % 16 == 0:
        whole = tuple(sizes[d] for d in SLOTS)
        more, inner, needed, left = stage_buffers(sizes, own_block, bf16, SLOTS, "cx")
        inner_more = more
        total += needed
        ins += [normed_own, dq_before, d_out.reshape(whole + (own_block[0], width))]
        in_specs += [vmem] * 3
        last_shape = jax.ShapeDtypeStruct(tuple(sizes[d] for d in left) + own_block, bf16)
    else:
        last_shape = jax.ShapeDtypeStruct((length, double), bf16)
    tasks_info, shapes, later = [], [], []
    for grad, order, widths in zip(grads, orders, splits):
        many = isinstance(grad, list)
        given = grad if many else [grad]
        block = given[0].shape[-2:]
        dims = ("z", "y") if many else ("x", "z", "y")
        more, counts, needed, left = stage_buffers(sizes, block, given[0].dtype, dims, order)
        if len(given) > 1:
            more = [pltpu.VMEM(given[0].shape, given[0].dtype)] + more
        scratch += more
        total += needed
        ends, widths = cut_shapes(block, left, widths, sizes, given[0].dtype)
        shapes += ends
        later.append(widths)
        tasks_info.append((order, dims, counts, len(ends), len(given)))
        ins += given
        in_specs += [vmem] * len(given)
    head_shapes = [
        jax.ShapeDtypeStruct((seqs, rows, width), f32),
        jax.ShapeDtypeStruct((rows, width), bf16),
        jax.ShapeDtypeStruct((pairs, 2, 5, 8, 2 * rows), f32),
    ]
    own_scratch = []
    if inner:
        own_scratch = [pltpu.VMEM(whole + own_block, bf16), pltpu.VMEM((length, double), bf16)]
        scratch = scratch + inner_more
    block = (seqs, n, fast, rows, width)
    own_scratch += [
        pltpu.VMEM((length, double), bf16),
        pltpu.VMEM((2, step, double), bf16),
        pltpu.VMEM((2, step, width), bf16),
        pltpu.VMEM(block, bf16),
        pltpu.VMEM((seqs, fast - 1, n, rows, width), bf16),
        pltpu.VMEM((seqs, 2, n, rows, width), bf16),
        pltpu.VMEM((2, 5, rows, rows), f32),
        pltpu.VMEM((2, 5, rows, rows), f32),
        pltpu.VMEM((2, width // pairs, rows), f32),
        pltpu.VMEM((width, double), f32) if inner else pltpu.VMEM((8, 128), f32),
    ]
    total += seqs * ((fast - 1) * n + 2 * n)
    outs = pl.pallas_call(
        functools.partial(back_rows_kernel, sizes, rows, tasks_info, inner),
        in_specs=in_specs,
        out_specs=[vmem] * (len(shapes) + 4),
        out_shape=head_shapes + shapes + [last_shape],
        scratch_shapes=own_scratch
        + scratch
        + [
            pltpu.SemaphoreType.DMA,
            pltpu.SemaphoreType.DMA((2,)),
            pltpu.SemaphoreType.DMA((2,)),
            pltpu.SemaphoreType.DMA((total,)),
            pltpu.SemaphoreType.DMA((total,)),
        ],
        compiler_params=pltpu.CompilerParams(
            collective_id=collective_id, has_side_effects=True, vmem_limit_bytes=62 << 20
        ),
        name=name,
    )(*ins)
    outs = list(outs)
    heads = [outs.pop(0) for _ in range(3)]
    results = []
    for (_, _, _, cut, _), widths in zip(tasks_info, later):
        results.append(cut_columns([outs.pop(0) for _ in range(cut)], widths))
    return heads + results + [outs[0], inner is not None]


def on_device(
    inputs,
    lengths,
    conv_taps,
    gain_attn,
    w_proj,
    w_query,
    w_key,
    w_value,
    w_out,
    gain_ffn,
    w_gate,
    w_up,
    w_down,
    rel_bias,
    cotangent,
):
    batch, seq = lax.axis_size("batch"), lax.axis_size("seq")
    sizes = layout_of(batch, seq)
    devices = batch * seq
    seqs, rows, width = inputs.shape
    length = rows * seq
    count = seqs * rows
    own = w_proj.shape[0]
    own_bias = rel_bias.shape[0]
    heads = own_bias * devices // NB
    hidden = w_gate.shape[1]

    small = jnp.concatenate(
        [
            conv_taps,
            gain_attn[:, None],
            gain_ffn[:, None],
            jnp.pad(rel_bias, (0, own - own_bias))[:, None],
            jnp.zeros((own, PACK - TAPS - 3), jnp.bfloat16),
        ],
        axis=1,
    )
    pairs = heads // 2
    key_value_w = jnp.stack([w_key.reshape(own, pairs, -1), w_value.reshape(own, pairs, -1)], axis=2)
    first, second, outer_plane, down_plane, left_rim = gather_all(
        [
            jnp.concatenate([small, w_proj, w_query], axis=1),
            key_value_w.reshape(own, -1),
            jnp.concatenate([w_out, w_gate, w_up], axis=1),
            w_down,
        ],
        ["Zyxc", "Zxyc", "zy", "yz"],
        sizes,
        1,
        rim=inputs[:, rows - 16 :, :],
        name="gather_first",
    )
    first = first.reshape(width, -1)
    second = second.reshape(width, -1)
    taps = first[:, :TAPS].astype(jnp.float32)
    gain_first = first[:, TAPS].astype(jnp.float32)
    gain_second = first[:, TAPS + 1].astype(jnp.float32)
    table = first[:, TAPS + 2].reshape(devices, own)[:, :own_bias].reshape(heads, NB).astype(jnp.float32)
    proj_w = first[:, PACK : PACK + width]
    query_w = first[:, PACK + width :]

    padded = jnp.concatenate([left_rim[:, 13:], inputs], axis=1).astype(jnp.float32)
    mixed_conv, conv_back = jax.vjp(partial(conv_mix, row_count=rows), padded, taps)
    mixed_low = mixed_conv.astype(jnp.bfloat16).reshape(count, width)
    resid_in = inputs.astype(jnp.float32).reshape(count, width)
    hidden_one = resid_in + mat_dot(mixed_low, proj_w)
    normed_one, norm_one_back = jax.vjp(norm_rows, hidden_one, gain_first)
    normed_low = normed_one.astype(jnp.bfloat16)

    queries = mat_dot(normed_low, query_w).astype(jnp.bfloat16)
    far, diag = bias_tables(table, rows)
    info = jnp.concatenate([lengths, lax.axis_index("seq")[None].astype(jnp.int32)])
    (outer_w, down_w), normed_all, key_value, begun = gather_rows(
        info,
        far,
        diag,
        normed_low.reshape(seqs, rows, width),
        queries,
        second,
        [outer_plane, down_plane],
        ["xc", "xc"],
        sizes,
        2,
    )
    outer_w = outer_w.reshape(width, -1)
    down_w = down_w.reshape(hidden, -1)
    out_w = outer_w[:, :width]
    wide_w = outer_w[:, width:]
    normed_all = normed_all.reshape(seqs * length, width)
    rest = attend(info, far, diag, queries, key_value, rows, length, 1)

    grad_low = cotangent.reshape(count, width)
    if own % 16 == 0:
        layer_out, d_hidden_two, d_out_w, scaled, d_gain_two, wide_pieces, down_half = feed_forward(
            hidden_one,
            grad_low,
            outer_w,
            down_w,
            gain_second[None],
            (begun[0], rest[0]),
            (begun[2], rest[2]),
            sizes,
            4,
        )
        d_gain_two = d_gain_two[0]
    else:
        attended = jnp.concatenate([begun[0], rest[0]], axis=0)
        inverse = jnp.concatenate([begun[2], rest[2]], axis=0)
        hidden_two = hidden_one + mat_dot(attended, out_w)
        normed_two, norm_two_back = jax.vjp(norm_rows, hidden_two, gain_second)
        normed_two_low = normed_two.astype(jnp.bfloat16)
        both_pre = mat_dot(normed_two_low, wide_w)
        inner_act, inner_back = jax.vjp(gated, both_pre[:, :hidden], both_pre[:, hidden:])
        inner_low = inner_act.astype(jnp.bfloat16)
        layer_out = (hidden_two + mat_dot(inner_low, down_w)).astype(jnp.bfloat16)

        d_down_w = outer_sum(inner_low, grad_low).astype(jnp.bfloat16)
        d_gate, d_up = inner_back(back_dot(grad_low, down_w))
        d_both = jnp.concatenate([d_gate.astype(jnp.bfloat16), d_up.astype(jnp.bfloat16)], axis=1)
        d_wide_w = outer_sum(normed_two_low, d_both).astype(jnp.bfloat16)
        d_hidden_part, d_gain_two = norm_two_back(back_dot(d_both, wide_w))
        d_hidden_two = grad_low.astype(jnp.float32) + d_hidden_part
        d_attn_low = d_hidden_two.astype(jnp.bfloat16)
        d_out_w = outer_sum(attended, d_attn_low).astype(jnp.bfloat16)
        d_attended = back_dot(d_attn_low, out_w).astype(jnp.bfloat16)
        scaled = (d_attended.astype(jnp.float32) * inverse).astype(jnp.bfloat16)
        wide_pieces, down_half = halve_cores([d_wide_w, d_down_w], [True, False], sizes, 4)
    scaled, wide_pieces, down_half, d_out_w, layer_out = lax.optimization_barrier(
        (scaled, wide_pieces, down_half, d_out_w, layer_out)
    )
    wide_others = from_others(wide_pieces, sizes)
    early = seqs - 1
    assert early == 1
    dq_before, dkv_before, near_before = attend_back(
        info, far, diag, queries, scaled, begun[1], key_value, begun[3], rows, length, early
    )
    dq_before, dkv_before, near_before, wide_others = lax.optimization_barrier(
        (dq_before, dkv_before, near_before, wide_others)
    )
    d_normed_one, dq_last, near, (g_gate, g_up), (g_down,), last, joined = back_rows(
        info,
        far,
        diag,
        queries,
        scaled,
        rest[1],
        key_value,
        rest[3],
        dkv_before,
        normed_all,
        normed_low,
        second,
        dq_before,
        d_out_w,
        [[wide_pieces[0]] + wide_others, down_half],
        ["Zy", "xs"],
        [(hidden, hidden), None],
        sizes,
        rows,
        5,
    )
    d_table = bias_grad(near_before + near, rows).reshape(heads * NB)
    d_queries = jnp.concatenate([dq_before, dq_last], axis=0)
    if joined:
        inner, inner_order = last, "s"
    else:
        d_key_value = jnp.concatenate([dkv_before, last[None]], axis=0).reshape(seqs * length, 2 * width)
        d_second_w = outer_sum(normed_all, d_key_value).astype(jnp.bfloat16)
        d_query_w = outer_sum(normed_low, d_queries).astype(jnp.bfloat16)
        inner, inner_order = jnp.concatenate([d_query_w, d_out_w, d_second_w], axis=1), "cxs"
    d_normed_one = d_normed_one.reshape(count, width)
    d_normed_one = d_normed_one + back_dot(d_queries, query_w)
    d_first_part, d_gain_one = norm_one_back(d_normed_one)
    d_hidden_one = d_hidden_two + d_first_part
    d_mix_low = d_hidden_one.astype(jnp.bfloat16)
    d_proj_w = outer_sum(mixed_low, d_mix_low).astype(jnp.bfloat16)
    d_mixed = back_dot(d_mix_low, proj_w).reshape(seqs, rows, width)
    d_padded, d_taps = conv_back(d_mixed)
    d_inputs = d_hidden_one.reshape(seqs, rows, width) + d_padded[:, 3:, :]
    d_small = jnp.concatenate(
        [
            d_taps.T,
            d_gain_one[None],
            d_gain_two[None],
            jnp.pad(d_table.reshape(devices, own_bias), ((0, 0), (0, own - own_bias))).reshape(1, width),
            jnp.zeros((16 - TAPS - 3, width), jnp.float32),
        ],
        axis=0,
    )
    d_last = jnp.concatenate([d_proj_w, jnp.pad(d_small.T, ((0, 0), (0, PACK - 16))).astype(jnp.bfloat16)], axis=1)
    (g_proj, g_small), (g_query, g_out, g_second), spill = reduce_all(
        [d_last, inner],
        ["cxs", inner_order],
        sizes,
        6,
        spill=d_padded[:, :8, :],
        splits=[(width, PACK), (width, width, 2 * width)],
    )
    input_grad = d_inputs.at[:, rows - 3 :, :].add(spill[:, :3]).astype(jnp.bfloat16)
    g_second = g_second.reshape(own, pairs, 2, -1)
    return (
        layer_out.reshape(seqs, rows, width),
        input_grad,
        g_small[:, :TAPS],
        g_small[:, TAPS],
        g_proj,
        g_query,
        g_second[:, :, 0].reshape(own, width),
        g_second[:, :, 1].reshape(own, width),
        g_out,
        g_small[:, TAPS + 1],
        g_gate,
        g_up,
        g_down.reshape(w_down.shape),
        g_small[:own_bias, TAPS + 2],
    )


def solution(mesh):
    in_specs = (
        P("batch", "seq", None),
        P("batch"),
        P(("batch", "seq"), None),
        P(("batch", "seq")),
        P(("batch", "seq"), None),
        P(("batch", "seq"), None),
        P(("batch", "seq"), None),
        P(("batch", "seq"), None),
        P(("batch", "seq"), None),
        P(("batch", "seq")),
        P(("batch", "seq"), None),
        P(("batch", "seq"), None),
        P(("batch", "seq"), None),
        P(("batch", "seq")),
        P("batch", "seq", None),
    )
    out_specs = (
        P("batch", "seq", None),
        P("batch", "seq", None),
        P(("batch", "seq"), None),
        P(("batch", "seq")),
        P(("batch", "seq"), None),
        P(("batch", "seq"), None),
        P(("batch", "seq"), None),
        P(("batch", "seq"), None),
        P(("batch", "seq"), None),
        P(("batch", "seq")),
        P(("batch", "seq"), None),
        P(("batch", "seq"), None),
        P(("batch", "seq"), None),
        P(("batch", "seq")),
    )
    return jax.shard_map(
        on_device, mesh=mesh, in_specs=in_specs, out_specs=out_specs, check_vma=False
    )
```

```python
import functools
from functools import partial

import jax
import jax.numpy as jnp
import numpy as np
from jax import lax
from jax.experimental import pallas as pl
from jax.experimental.pallas import tpu as pltpu
from jax.sharding import PartitionSpec as P

NB = 32
EPSILON = 1e-06
LIMITS = (12, 16, 23, 32, 46, 64, 91)
WINDOWS = ((2, 0), (3, 2), (4, 5))
TAPS = 9
PACK = 128
SPAN = 8

def mat_dot(lhs_array, rhs_array):
    return jnp.dot(lhs_array, rhs_array, preferred_element_type=jnp.float32)


def outer_sum(lhs_array, rhs_array):
    return lax.dot_general(
        lhs_array, rhs_array, (((0,), (0,)), ((), ())), preferred_element_type=jnp.float32
    )


def back_dot(grad_rows, weight):
    return lax.dot_general(
        grad_rows, weight, (((1,), (1,)), ((), ())), preferred_element_type=jnp.float32
    )


def bucket_of(relative):
    distance = jnp.abs(relative)
    larger = jnp.full(relative.shape, 8, jnp.int32)
    for threshold in LIMITS:
        larger = larger + (distance >= threshold).astype(jnp.int32)
    inside = jnp.where(distance < 8, distance, larger)
    return inside + 16 * (relative > 0).astype(jnp.int32)


def norm_rows(hidden, gain_row):
    return (
        hidden * lax.rsqrt(jnp.mean(hidden * hidden, axis=-1, keepdims=True) + EPSILON) * gain_row
    )


def gated(gate_pre, up_pre):
    return jax.nn.gelu(gate_pre, approximate=True) * up_pre


def conv_mix(padded, taps, row_count):
    summed = jnp.zeros(padded.shape[:-2] + (row_count, padded.shape[-1]), jnp.float32)
    for window_len, offset in WINDOWS:
        conv_sum = jnp.zeros_like(summed)
        for tap_index in range(window_len):
            shifted = lax.slice_in_dim(
                padded, 3 - tap_index, 3 - tap_index + row_count, axis=padded.ndim - 2
            )
            conv_sum = conv_sum + taps[:, offset + tap_index] * shifted
        summed = summed + jax.nn.gelu(conv_sum, approximate=True)
    return summed


def near_offsets(rows):
    lane = np.arange(2 * rows)
    lane = np.where(lane < rows, lane, lane - 2 * rows)
    return rows * (np.arange(3)[:, None, None] - 1) + np.arange(8)[None, :, None] - lane[None, None, :]


def bias_tables(table, rows):
    heads = table.shape[0]
    buckets = bucket_of(jnp.asarray(near_offsets(rows)[:, 0, :], jnp.int32)).reshape(-1)
    onehot = (buckets[None, :] == jnp.arange(NB, dtype=jnp.int32)[:, None]).astype(jnp.float32)
    diag = jnp.dot(table, onehot, precision=lax.Precision.HIGHEST)
    far = jnp.stack([table[:, NB // 2 - 1], table[:, NB - 1]], axis=1)
    return far, diag.reshape(heads // 2, 6, 2 * rows)


def bias_grad(near, rows):
    near = near.reshape(near.shape[0] * 2, 5, 8, 2 * rows)
    buckets = bucket_of(jnp.asarray(near_offsets(rows), jnp.int32))
    hit = buckets[None] == jnp.arange(NB, dtype=jnp.int32)[:, None, None, None]
    grad = jnp.sum(jnp.where(hit[None], near[:, None, 1:4], 0.0), axis=(2, 3, 4))
    left = jnp.sum(near[:, 0], axis=(1, 2))
    right = jnp.sum(near[:, 4], axis=(1, 2))
    return grad.at[:, NB // 2 - 1].add(left).at[:, NB - 1].add(right)


def nt_dot(a, b):
    return lax.dot_general(a, b, (((1,), (1,)), ((), ())), preferred_element_type=jnp.float32)


def tn_dot(a, b):
    return lax.dot_general(a, b, (((0,), (0,)), ((), ())), preferred_element_type=jnp.float32)


def nn_dot(a, b):
    return lax.dot_general(a, b, (((1,), (0,)), ((), ())), preferred_element_type=jnp.float32)


def fill_bias(rows, far_ref, diag_ref, bias_ref, pair):
    for a in range(2):
        bias_ref[a, 0] = jnp.full((rows, rows), far_ref[2 * pair + a, 0], jnp.float32)
        bias_ref[a, 4] = jnp.full((rows, rows), far_ref[2 * pair + a, 1], jnp.float32)
        for c in range(3):
            base = jnp.broadcast_to(diag_ref[0, 3 * a + c : 3 * a + c + 1, :], (rows, 2 * rows))
            bias_ref[a, 1 + c] = pltpu.roll(base, 0, 1, stride=1, stride_axis=0)[:, :rows]


def head_halves(block):
    lane = lax.broadcasted_iota(jnp.int32, block.shape, 1)
    zero = jnp.zeros_like(block)
    half = block.shape[1] // 2
    return jnp.where(lane < half, block, zero), jnp.where(lane < half, zero, block)


def attend_pair(rows, length, first, q, keys, values, spans, bias_ref, s_ref, acc_ref):
    halves = head_halves(q)
    wide = q.shape[1]
    half = wide // 2
    key_row = lax.broadcasted_iota(jnp.int32, (rows, rows), 0)
    lane = lax.broadcasted_iota(jnp.int32, (SPAN * rows, wide), 1)

    def scores(i, peaks):
        kc = i * SPAN
        k = keys(pl.ds(kc * rows, SPAN * rows))
        new = list(peaks)
        for a in range(2):
            full = nt_dot(k, halves[a])
            for u in range(SPAN):
                slot = jnp.clip(kc + u - first + 2, 0, 4)
                valid = key_row < length - (kc + u) * rows
                s = full[u * rows : (u + 1) * rows] + bias_ref[a, slot]
                s = jnp.where(valid, s, -1e9)
                s_ref[a, pl.ds((kc + u) * rows, rows), :] = s
                new[a] = jnp.maximum(new[a], jnp.max(s.reshape(rows // 8, 8, rows), axis=0))
        return tuple(new)

    def weigh(i, carry):
        here = pl.ds(i * SPAN * rows, SPAN * rows)
        v = values(here)
        ones = jnp.ones_like(v)
        for a, v_one in enumerate((jnp.where(lane < half, v, ones), jnp.where(lane < half, ones, v))):
            e = jnp.exp(s_ref[a, here, :] - tops[a])
            acc_ref[a] += tn_dot(v_one, e.astype(jnp.bfloat16))
        return carry

    low = jnp.full((8, rows), -jnp.inf, jnp.float32)
    peaks = scores(0, (low, low)) if spans == 1 else lax.fori_loop(0, spans, scores, (low, low))
    tops = [jnp.max(p, axis=0, keepdims=True) for p in peaks]
    acc_ref[...] = jnp.zeros_like(acc_ref)
    if spans == 1:
        weigh(0, 0)
    else:
        lax.fori_loop(0, spans, weigh, 0)
    inv = jnp.concatenate([1.0 / acc_ref[0, half:], 1.0 / acc_ref[1, :half]], axis=0)
    out = jnp.concatenate([acc_ref[0, :half], acc_ref[1, half:]], axis=0) * inv
    return out.T, inv.T, tops


def attend_kernel(rows, skip, info_ref, far_ref, diag_ref, q_ref, k_ref, v_ref, *refs):
    o_ref, full_ref, inv_ref, peak_ref, bias_ref, s_ref, acc_ref = refs
    pair, b = pl.program_id(0), pl.program_id(1)

    @pl.when(b == 0)
    def _():
        fill_bias(rows, far_ref, diag_ref, bias_ref, pair)

    out, inv, tops = attend_pair(
        rows,
        info_ref[b + skip],
        info_ref[info_ref.shape[0] - 1],
        q_ref[...],
        lambda here: k_ref[0, here, :],
        lambda here: v_ref[0, here, :],
        k_ref.shape[1] // (SPAN * rows),
        bias_ref,
        s_ref,
        acc_ref,
    )
    o_ref[...] = out.astype(o_ref.dtype)
    full_ref[...] = out
    inv_ref[...] = inv
    for a in range(2):
        peak_ref[0, 0, a : a + 1, :] = tops[a]


def attention_cost(q, kv, products):
    flops = products * 8 * q.shape[0] * kv.shape[1] * q.shape[1]
    return pl.CostEstimate(
        flops=flops, bytes_accessed=2 * (q.size + kv.size) * products, transcendentals=8 * q.shape[0] * kv.shape[1]
    )


def attention_shapes(seqs, rows, width, pairs):
    shape = (seqs * rows, width)
    return [
        jax.ShapeDtypeStruct(shape, jnp.bfloat16),
        jax.ShapeDtypeStruct(shape, jnp.float32),
        jax.ShapeDtypeStruct(shape, jnp.float32),
        jax.ShapeDtypeStruct((seqs, pairs, 2, rows), jnp.float32),
    ]


def attend(info, far, diag, q, kv, rows, length, skip):
    heads = far.shape[0]
    seqs = kv.shape[0]
    wide = 2 * (q.shape[1] // heads)
    pairs = heads // 2
    smem = pl.BlockSpec(memory_space=pltpu.SMEM)
    return pl.pallas_call(
        functools.partial(attend_kernel, rows, skip),
        grid=(pairs, seqs - skip),
        in_specs=[
            smem,
            smem,
            pl.BlockSpec((1, 6, 2 * rows), lambda p, b: (p, 0, 0)),
            pl.BlockSpec((rows, wide), lambda p, b: (b + skip, p)),
            pl.BlockSpec((1, length, wide), lambda p, b: (b + skip, 0, 2 * p)),
            pl.BlockSpec((1, length, wide), lambda p, b: (b + skip, 0, 2 * p + 1)),
        ],
        out_specs=[pl.BlockSpec((rows, wide), lambda p, b: (b, p))] * 3
        + [pl.BlockSpec((1, 1, 2, rows), lambda p, b: (b, p, 0, 0))],
        out_shape=attention_shapes(seqs - skip, rows, q.shape[1], pairs),
        scratch_shapes=[
            pltpu.VMEM((2, 5, rows, rows), jnp.float32),
            pltpu.VMEM((2, length, rows), jnp.float32),
            pltpu.VMEM((2, wide, rows), jnp.float32),
        ],
        compiler_params=pltpu.CompilerParams(vmem_limit_bytes=48 << 20),
        cost_estimate=attention_cost(q, kv, 1),
        name="attend",
    )(info, far, diag, q, kv, kv)


def back_pair(rows, length, first, q, g, full, key_value, peak, bias_ref, sum_ref, acc_ref, write):
    q_half, g_half = head_halves(q), head_halves(g)
    wide = q.shape[1]
    half = wide // 2
    key_row = lax.broadcasted_iota(jnp.int32, (rows, rows), 0)
    acc_ref[...] = jnp.zeros_like(acc_ref)
    along = (g.astype(jnp.float32) * full).T
    delta = [jnp.sum(along[a * half : (a + 1) * half], axis=0, keepdims=True) for a in range(2)]
    keys, spans = key_value

    def step(i, carry):
        kc = i * SPAN
        here = pl.ds(kc * rows, SPAN * rows)
        k, v = keys(here)
        dk = dv = None
        for a in range(2):
            s = nt_dot(k, q_half[a])
            dp = nt_dot(v, g_half[a])
            es, dss = [], []
            for u in range(SPAN):
                part = slice(u * rows, (u + 1) * rows)
                slot = jnp.clip(kc + u - first + 2, 0, 4)
                valid = key_row < length - (kc + u) * rows
                e = jnp.exp(s[part] + bias_ref[a, slot] - peak[a])
                e_low = jnp.where(valid, e, 0.0).astype(jnp.bfloat16)
                ds = e_low.astype(jnp.float32) * (dp[part] - delta[a])
                sum_ref[a, slot] += ds
                es.append(e_low)
                dss.append(ds.astype(jnp.bfloat16))
            e_low, ds_low = jnp.concatenate(es, axis=0), jnp.concatenate(dss, axis=0)
            dv_a = nn_dot(e_low, g_half[a])
            dk_a = nn_dot(ds_low, q_half[a])
            dv = dv_a if dv is None else dv + dv_a
            dk = dk_a if dk is None else dk + dk_a
            acc_ref[a] += tn_dot(k, ds_low)
        write(here, dk.astype(jnp.bfloat16), dv.astype(jnp.bfloat16))
        return carry

    if spans == 1:
        step(0, 0)
    else:
        lax.fori_loop(0, spans, step, 0)
    return jnp.concatenate([acc_ref[0, :half], acc_ref[1, half:]], axis=0).T.astype(jnp.bfloat16)


def near_sums(rows, sum_ref, write):
    for a in range(2):
        for slot in range(5):
            total_sum = jnp.zeros((8, 2 * rows), jnp.float32)
            for g in range(rows // 8):
                part = jnp.concatenate(
                    [sum_ref[a, slot, 8 * g : 8 * g + 8, :], jnp.zeros((8, rows), jnp.float32)], axis=1
                )
                if g and 0 < slot < 4:
                    part = pltpu.roll(part, 2 * rows - 8 * g, 1)
                total_sum = total_sum + part
            write(a, slot, total_sum)


def attend_back_kernel(rows, info_ref, far_ref, diag_ref, q_ref, g_ref, full_ref, k_ref, v_ref, peak_ref,
                       dq_ref, dkv_ref, near_ref, bias_ref, sum_ref, acc_ref):
    pair, b = pl.program_id(0), pl.program_id(1)

    @pl.when(b == 0)
    def _():
        fill_bias(rows, far_ref, diag_ref, bias_ref, pair)
        sum_ref[...] = jnp.zeros_like(sum_ref)

    wide = q_ref.shape[1]

    def write(here, dk, dv):
        dkv_ref[0, here, :wide] = dk
        dkv_ref[0, here, wide:] = dv

    dq_ref[...] = back_pair(
        rows,
        info_ref[b],
        info_ref[info_ref.shape[0] - 1],
        q_ref[...],
        g_ref[...],
        full_ref[...],
        (lambda here: (k_ref[0, here, :], v_ref[0, here, :]), k_ref.shape[1] // (SPAN * rows)),
        [peak_ref[0, 0, a : a + 1, :] for a in range(2)],
        bias_ref,
        sum_ref,
        acc_ref,
        write,
    )

    @pl.when(b == pl.num_programs(1) - 1)
    def _():
        def keep(a, slot, value):
            near_ref[0, a, slot] = value

        near_sums(rows, sum_ref, keep)


def attend_back(info, far, diag, q, g, full, kv, peak, rows, length, seqs):
    heads = far.shape[0]
    wide = 2 * (q.shape[1] // heads)
    pairs = heads // 2
    smem = pl.BlockSpec(memory_space=pltpu.SMEM)
    row_spec = pl.BlockSpec((rows, wide), lambda p, b: (b, p))
    return pl.pallas_call(
        functools.partial(attend_back_kernel, rows),
        grid=(pairs, seqs),
        in_specs=[
            smem,
            smem,
            pl.BlockSpec((1, 6, 2 * rows), lambda p, b: (p, 0, 0)),
            row_spec,
            row_spec,
            row_spec,
            pl.BlockSpec((1, length, wide), lambda p, b: (b, 0, 2 * p)),
            pl.BlockSpec((1, length, wide), lambda p, b: (b, 0, 2 * p + 1)),
            pl.BlockSpec((1, 1, 2, rows), lambda p, b: (b, p, 0, 0)),
        ],
        out_specs=[
            row_spec,
            pl.BlockSpec((1, length, 2 * wide), lambda p, b: (b, 0, p)),
            pl.BlockSpec((1, 2, 5, 8, 2 * rows), lambda p, b: (p, 0, 0, 0, 0)),
        ],
        out_shape=[
            jax.ShapeDtypeStruct((seqs * rows, q.shape[1]), jnp.bfloat16),
            jax.ShapeDtypeStruct((seqs,) + kv.shape[1:], jnp.bfloat16),
            jax.ShapeDtypeStruct((pairs, 2, 5, 8, 2 * rows), jnp.float32),
        ],
        scratch_shapes=[
            pltpu.VMEM((2, 5, rows, rows), jnp.float32),
            pltpu.VMEM((2, 5, rows, rows), jnp.float32),
            pltpu.VMEM((2, wide, rows), jnp.float32),
        ],
        compiler_params=pltpu.CompilerParams(vmem_limit_bytes=48 << 20),
        cost_estimate=attention_cost(q, kv, 3),
        name="attend_back",
    )(info, far, diag, q, g, full, kv, kv, peak)


SLOTS = ("x", "c", "z", "y")
MESH = pl.DeviceIdType.MESH


def layout_of(batch, seq):
    fast = 1 << ((seq.bit_length() - 1) // 2)
    return {"x": batch // 2, "c": 2, "z": seq // fast, "y": fast}


def tile_block(rows, cols):
    return (rows, cols) if rows % 16 == 0 else (rows * cols // 128, 128)


def place(sizes):
    b, s = lax.axis_index("batch"), lax.axis_index("seq")
    return {
        "x": lax.div(b, 2),
        "c": lax.rem(b, 2),
        "z": lax.div(s, sizes["y"]),
        "y": lax.rem(s, sizes["y"]),
    }


def device_at(sizes, me, dim, at):
    spot = dict(me)
    spot[dim] = at
    return (spot["x"] * 2 + spot["c"], spot["z"] * sizes["y"] + spot["y"])


def seq_peer(sizes, me, k):
    n = sizes["z"] * sizes["y"]
    return (me["x"] * 2 + me["c"], lax.rem(me["z"] * sizes["y"] + me["y"] + k, n))


def greet(sizes, me, dims):
    barrier = pltpu.get_barrier_semaphore()
    total = 0
    if "s" in dims:
        total = sizes["z"] * sizes["y"] - 1
        for k in range(1, total + 1):
            pl.semaphore_signal(barrier, inc=1, device_id=seq_peer(sizes, me, k), device_id_type=MESH)
        dims = [d for d in dims if d not in "szy"]
    for dim in dims:
        for k in range(1, sizes[dim]):
            peer = device_at(sizes, me, dim, lax.rem(me[dim] + k, sizes[dim]))
            pl.semaphore_signal(barrier, inc=1, device_id=peer, device_id_type=MESH)
            total += 1
    pl.semaphore_wait(barrier, total)


class Sems:
    def __init__(self, send, recv):
        self.send, self.recv, self.used = send, recv, 0

    def take(self, count):
        first = self.used
        self.used += count
        assert self.used <= self.send.shape[0]
        return first

    def copy(self, src, dst, index, device):
        return pltpu.make_async_remote_copy(
            src_ref=src, dst_ref=dst, send_sem=self.send.at[index], recv_sem=self.recv.at[index],
            device_id=device, device_id_type=MESH,
        )


def run_together(tasks, plan=()):
    tasks = list(tasks)
    over_already = set()
    for i in plan:
        if i not in over_already:
            try:
                next(tasks[i])
            except StopIteration:
                over_already.add(i)
    tasks = [t for i, t in enumerate(tasks) if i not in over_already]
    while tasks:
        left = []
        for task in tasks:
            try:
                next(task)
                left.append(task)
            except StopIteration:
                pass
        tasks = left


def gather_task(sizes, me, src, out, local_sem, sems, order):
    before = [] if isinstance(src, list) else list(SLOTS[len(SLOTS) - (len(src.shape) - 2) :])
    dims = [d for d in SLOTS if d in order.lower() or d in before]
    mine = out.at[tuple(me[d] for d in dims if d not in before)]
    if isinstance(src, list):
        first = 0
        owns = []
        for i, (ref, lo, hi) in enumerate(src):
            owns.append(
                pltpu.make_async_copy(ref.at[:, lo:hi], mine.at[:, first : first + hi - lo], local_sem.at[i])
            )
            first += hi - lo
    else:
        owns = [pltpu.make_async_copy(src, mine, local_sem.at[0])]
    for own in owns:
        own.start()
    for own in owns:
        own.wait()
    done = before
    sent = []
    for dim in order:
        direct, dim = dim.isupper(), dim.lower()
        n, at = sizes[dim], me[dim]

        def region(origin):
            spots = []
            for d in dims:
                spots.append(slice(None) if d in done else (origin if d == dim else me[d]))
            return out.at[tuple(spots)]

        if n == 2:
            base = sems.take(1)
            other = 1 - at
            send = sems.copy(region(at), region(at), base, device_at(sizes, me, dim, other))
            send.start()
            yield
            sems.copy(region(other), region(other), base, device_at(sizes, me, dim, other)).wait_recv()
            sent.append((None, send))
        elif direct:
            base = sems.take(n - 1)
            for k in range(1, n):
                peer = device_at(sizes, me, dim, lax.rem(at + k, n))
                send = sems.copy(region(at), region(at), base + k - 1, peer)
                send.start()
                sent.append((None, send))
            yield
            for k in range(1, n):
                origin = lax.rem(at + n - k, n)
                sems.copy(region(origin), region(origin), base + k - 1, device_at(sizes, me, dim, origin)).wait_recv()
        else:
            for t in range(n - 1):
                base = sems.take(2)
                to_right = (at + 1 < n) & (at - t >= 0)
                to_left = (at >= 1) & (at + t < n)
                from_left = (at >= 1) & (at - 1 - t >= 0)
                from_right = (at + 1 < n) & (at + 1 + t < n)
                right = sems.copy(region(at - t), region(at - t), base, device_at(sizes, me, dim, at + 1))
                left = sems.copy(region(at + t), region(at + t), base + 1, device_at(sizes, me, dim, at - 1))
                pl.when(to_right)(right.start)
                pl.when(to_left)(left.start)
                sent += [(to_right, right), (to_left, left)]
                yield
                got = sems.copy(region(at - 1 - t), region(at - 1 - t), base, device_at(sizes, me, dim, at - 1))
                pl.when(from_left)(got.wait_recv)
                got = sems.copy(region(at + 1 + t), region(at + 1 + t), base + 1, device_at(sizes, me, dim, at + 1))
                pl.when(from_right)(got.wait_recv)
        done.append(dim)
    for cond, send in sent:
        if cond is None:
            send.wait_send()
        else:
            pl.when(cond)(send.wait_send)


def spread_task(sizes, me, src, out, sems):
    z, y, n, fast = me["z"], me["y"], sizes["z"], sizes["y"]
    fan = sems.take((fast - 1) * n)
    base = sems.take(2 * (n - 1))

    def fan_copy(k, origin, owner, to):
        spot = out.at[origin, owner]
        return sems.copy(spot, spot, fan + (k - 1) * n + origin, device_at(sizes, me, "y", to))

    def fan_out(origin):
        for k in range(1, fast):
            fan_copy(k, origin, y, lax.rem(y + k, fast)).start()

    def along(origin, index, to):
        spot = out.at[origin, y]
        return sems.copy(spot, spot, base + index, device_at(sizes, me, "z", to))

    moves = []
    for t in range(n - 1):
        moves.append(
            (
                (along(z - t, 2 * t, z + 1), (z + 1 < n) & (z - t >= 0)),
                (along(z + t, 2 * t + 1, z - 1), (z >= 1) & (z + t < n)),
                (along(z - 1 - t, 2 * t, z - 1), (z >= 1) & (z - 1 - t >= 0), z - 1 - t),
                (along(z + 1 + t, 2 * t + 1, z + 1), (z + 1 < n) & (z + 1 + t < n), z + 1 + t),
            )
        )
    fans = [fan_copy(k, origin, y, lax.rem(y + k, fast)) for k in range(1, fast) for origin in range(n)]

    def begin(t):
        for send, cond in moves[t][:2]:
            pl.when(cond)(send.start)

    def chains():
        out[z, y] = src[...]
        begin(0)
        fan_out(z)
        yield
        for t in range(n - 1):
            for got, cond, origin in moves[t][2:]:
                pl.when(cond)(got.wait_recv)
            if t + 1 < n - 1:
                begin(t + 1)
            for got, cond, origin in moves[t][2:]:
                pl.when(cond)(partial(fan_out, origin))
            yield
        for send in fans:
            send.wait_send()
        for move in moves:
            for send, cond in move[:2]:
                pl.when(cond)(send.wait_send)

    def across_y(use):
        def step(i, carry):
            far = lax.div(i + 1, 2)
            origin = jnp.where(lax.rem(i, 2) == 1, z - far, z + far)

            @pl.when((origin >= 0) & (origin < n))
            def _():
                for k in range(1, fast):
                    owner = lax.rem(y + fast - k, fast)
                    fan_copy(k, origin, owner, owner).wait_recv()
                    use(origin, owner)

            return carry

        lax.fori_loop(0, 2 * n - 1, step, 0)

    return chains(), across_y


def shift_task(sizes, me, src, out, sems, step):
    n = sizes["z"] * sizes["y"]
    s = me["z"] * sizes["y"] + me["y"]
    base = sems.take(1)
    send = sems.copy(src, out, base, seq_peer(sizes, me, step % n))
    has_to = (s < n - 1) if step > 0 else (s > 0)
    has_from = (s > 0) if step > 0 else (s < n - 1)
    pl.when(has_to)(send.start)
    yield
    pl.when(has_from)(send.wait_recv)

    @pl.when(jnp.logical_not(has_from))
    def _():
        out[...] = jnp.zeros_like(out)

    yield
    pl.when(has_to)(send.wait_send)


def stage_count(sizes, order):
    return sum(1 if sizes[d] == 2 else 2 * (sizes[d] - 1) for d in order.lower())


def gather_kernel(sizes, orders, cuts, has_rim, *refs):
    count = len(orders)
    arrays = sum(1 if cut is None else len(cut) for cut in cuts)
    ins, outs = list(refs[: arrays + has_rim]), refs[arrays + has_rim : arrays + has_rim + count + has_rim]
    local_sem, send_sem, recv_sem = refs[arrays + count + 2 * has_rim :]
    me = place(sizes)
    used = [d for d in SLOTS if any(d in o.lower() for o in orders)]
    greet(sizes, me, used + ["s"] * has_rim)
    sems = Sems(send_sem, recv_sem)
    tasks = []
    for i in range(count):
        src = ins.pop(0) if cuts[i] is None else [(ins.pop(0), lo, hi) for lo, hi in cuts[i]]
        tasks.append(gather_task(sizes, me, src, outs[i], local_sem.at[i], sems, orders[i]))
    if has_rim:
        edge = ins[0].at[:, ins[0].shape[1] - outs[-1].shape[1] :, :]
        tasks.append(shift_task(sizes, me, edge, outs[-1], sems, 1))
    run_together(tasks)


def gather_shapes(shards, orders, sizes):
    ins, shapes = [], []
    cuts = []
    for shard, order in zip(shards, orders):
        if isinstance(shard, list) and shard[0][0].shape[0] % 16 == 0:
            whole = tuple(sizes[d] for d in SLOTS if d in order.lower())
            block = (shard[0][0].shape[0], sum(hi - lo for _, lo, hi in shard))
            shapes.append(jax.ShapeDtypeStruct(whole + block, shard[0][0].dtype))
            ins += [piece for piece, _, _ in shard]
            cuts.append([(lo, hi) for _, lo, hi in shard])
            continue
        if isinstance(shard, list):
            shard = jnp.concatenate([piece[:, lo:hi] for piece, lo, hi in shard], axis=1)
        ins.append(shard if shard.ndim > 2 else shard.reshape(tile_block(*shard.shape)))
        before = SLOTS[len(SLOTS) - (ins[-1].ndim - 2) :]
        whole = tuple(sizes[d] for d in SLOTS if d in order.lower() or d in before)
        shapes.append(jax.ShapeDtypeStruct(whole + ins[-1].shape[-2:], shard.dtype))
        cuts.append(None)
    return ins, shapes, sum(stage_count(sizes, o) for o in orders), cuts


def gather_all(shards, orders, sizes, collective_id, rim=None, name="gather"):
    ins, shapes, total, cuts = gather_shapes(shards, orders, sizes)
    out_specs = [pl.BlockSpec(memory_space=pl.ANY)] * len(shapes)
    in_specs = [pl.BlockSpec(memory_space=pltpu.VMEM)] * len(ins)
    if rim is not None:
        ins.append(rim)
        in_specs.append(pl.BlockSpec(memory_space=pl.ANY))
        shapes.append(jax.ShapeDtypeStruct((rim.shape[0], 16, rim.shape[2]), rim.dtype))
        out_specs.append(pl.BlockSpec(memory_space=pltpu.VMEM))
        total += 1
    return pl.pallas_call(
        functools.partial(gather_kernel, sizes, orders, cuts, int(rim is not None)),
        in_specs=in_specs,
        out_specs=out_specs,
        out_shape=shapes,
        scratch_shapes=[
            pltpu.SemaphoreType.DMA((len(orders), len(ins))),
            pltpu.SemaphoreType.DMA((total,)),
            pltpu.SemaphoreType.DMA((total,)),
        ],
        compiler_params=pltpu.CompilerParams(collective_id=collective_id, has_side_effects=True),
        name=name,
    )(*ins)


def gather_rows_kernel(sizes, rows, orders, *refs):
    count = len(orders)
    info_ref, far_ref, diag_ref, rows_ref, q_ref, second_ref = refs[:6]
    planes, refs = refs[6 : 6 + count], refs[6 + count :]
    gathered, refs = refs[:count], refs[count:]
    normed_out, kv_out, o_ref, full_ref, inv_ref, peak_ref = refs[:6]
    rows_buf, kv_buf, bias_ref, s_ref, acc_ref, local_sem, out_sem, send_sem, recv_sem = refs[6:]
    me = place(sizes)
    greet(sizes, me, SLOTS)
    sems = Sems(send_sem, recv_sem)
    first = me["z"] * sizes["y"] + me["y"]
    seqs, n = rows_ref.shape[0], sizes["z"]
    length = kv_buf.shape[1]
    pairs = diag_ref.shape[0]
    wide = q_ref.shape[1] // pairs
    weights = []
    for i in range(count):
        weights.append(gather_task(sizes, me, planes[i], gathered[i], local_sem.at[i], sems, orders[i]))
        next(weights[-1])
    pieces = [spread_task(sizes, me, rows_ref.at[p], rows_buf.at[p], sems) for p in range(seqs)]
    begun, rest = pieces[0][0], [p[0] for p in pieces[1:]]
    for _ in range(n):
        next(begun)
    for task in rest:
        next(task)

    def project(p):
        def block(z, y):
            at = pl.ds(pl.multiple_of((z * sizes["y"] + y) * rows, rows), rows)
            kv_buf[p, at, :] = nn_dot(rows_buf[p, z, y], second_ref[...]).astype(jnp.bfloat16)

        def column(z, carry):
            block(z, me["y"])
            return carry

        lax.fori_loop(0, n, column, 0)
        pieces[p][1](block)
        copies = [
            pltpu.make_async_copy(rows_buf.at[p], normed_out.at[p], out_sem.at[p, 0]),
            pltpu.make_async_copy(kv_buf.at[p], kv_out.at[p], out_sem.at[p, 1]),
        ]
        for copy in copies:
            copy.start()
        return copies

    copies = project(0)
    size = info_ref[0]

    def one_pair(p, carry):
        fill_bias(rows, far_ref, diag_ref.at[pl.ds(p, 1)], bias_ref, p)
        lanes = pl.ds(pl.multiple_of(p * wide, wide), wide)
        k_lanes = pl.ds(pl.multiple_of(2 * p * wide, wide), wide)
        v_lanes = pl.ds(pl.multiple_of((2 * p + 1) * wide, wide), wide)
        out, inv, tops = attend_pair(
            rows,
            size,
            first,
            q_ref[:rows, lanes],
            lambda here: kv_buf[0, here, k_lanes],
            lambda here: kv_buf[0, here, v_lanes],
            length // (SPAN * rows),
            bias_ref,
            s_ref,
            acc_ref,
        )
        o_ref[:, lanes] = out.astype(o_ref.dtype)
        full_ref[:, lanes] = out
        inv_ref[:, lanes] = inv
        for a in range(2):
            peak_ref[0, p, a : a + 1, :] = tops[a]
        for i in range(min(pairs, n - 1)):

            @pl.when(p == i)
            def _():
                for task in rest:
                    next(task)

        return carry

    lax.fori_loop(0, pairs, one_pair, 0)
    for _ in range(n - 1 - min(pairs, n - 1)):
        for task in rest:
            next(task)
    for task in weights:
        next(task, None)
    for p in range(1, seqs):
        copies += project(p)
    run_together(weights + [begun] + rest)
    for copy in copies:
        copy.wait()


def gather_rows(info, far, diag, normed, queries, second, planes, orders, sizes, collective_id):
    seqs, rows, width = normed.shape
    n, fast = sizes["z"], sizes["y"]
    length = rows * n * fast
    pairs = far.shape[0] // 2
    ins, shapes, total, _ = gather_shapes(planes, orders, sizes)
    total += seqs * ((fast - 1) * n + 2 * (n - 1))
    bf16, f32 = jnp.bfloat16, jnp.float32
    smem, vmem = pl.BlockSpec(memory_space=pltpu.SMEM), pl.BlockSpec(memory_space=pltpu.VMEM)
    anywhere = pl.BlockSpec(memory_space=pl.ANY)
    count = len(ins)
    outs = pl.pallas_call(
        functools.partial(gather_rows_kernel, sizes, rows, orders),
        in_specs=[smem, smem] + [vmem] * (4 + count),
        out_specs=[anywhere] * (count + 2) + [vmem] * 4,
        out_shape=shapes
        + [
            jax.ShapeDtypeStruct((seqs, n, fast, rows, width), bf16),
            jax.ShapeDtypeStruct((seqs, length, 2 * width), bf16),
        ]
        + attention_shapes(1, rows, width, pairs),
        scratch_shapes=[
            pltpu.VMEM((seqs, n, fast, rows, width), bf16),
            pltpu.VMEM((seqs, length, 2 * width), bf16),
            pltpu.VMEM((2, 5, rows, rows), f32),
            pltpu.VMEM((2, length, rows), f32),
            pltpu.VMEM((2, width // pairs, rows), f32),
            pltpu.SemaphoreType.DMA((count, 1)),
            pltpu.SemaphoreType.DMA((seqs, 2)),
            pltpu.SemaphoreType.DMA((total,)),
            pltpu.SemaphoreType.DMA((total,)),
        ],
        compiler_params=pltpu.CompilerParams(
            collective_id=collective_id, has_side_effects=True, vmem_limit_bytes=60 << 20
        ),
        name="gather_rows",
    )(info, far, diag, normed, queries, second, *ins)
    return outs[:count], outs[count], outs[count + 1], outs[count + 2 :]


def over(extents, body):
    total = 1
    for e in extents:
        total *= e
    if total == 1:
        body((0,) * len(extents))
        return

    def step(i, carry):
        spots = []
        for e in reversed(extents):
            spots.append(lax.rem(i, e))
            i = lax.div(i, e)
        body(tuple(reversed(spots)))
        return carry

    lax.fori_loop(0, total, step, 0)


def add_into(dst, src_of, extents):
    def body(spots):
        here = spots + (slice(None), slice(None))
        dst[here] = (dst[here].astype(jnp.float32) + src_of(spots).astype(jnp.float32)).astype(dst.dtype)

    over(extents, body)


def add_pair(out, first, second_of, extents):
    def body(spots):
        here = spots + (slice(None), slice(None))
        out[here] = (first[here].astype(jnp.float32) + second_of(spots).astype(jnp.float32)).astype(out.dtype)

    over(extents, body)


def reduce_task(sizes, me, src, out, bufs, sems, order, dims):
    remaining = list(dims)
    current = src
    stages = []
    for stage, dim in enumerate(order):
        last = stage == len(order) - 1
        if dim == "s":
            n, s = sizes["z"] * sizes["y"], me["z"] * sizes["y"] + me["y"]
            base = sems.take(n)
            sends, recvs = [], []
            for k in range(1, n):
                to = lax.rem(s + k, n)
                spot = current.at[lax.div(to, sizes["y"]), lax.rem(to, sizes["y"])]
                sends.append(sems.copy(spot, bufs[stage].at[k], base + k, seq_peer(sizes, me, k)))
                recvs.append(sems.copy(bufs[stage].at[k], bufs[stage].at[k], base + k, seq_peer(sizes, me, k)))
            stages.append((dim, n, current, bufs[stage], sends, recvs, None, None, None))
            continue
        direct, dim = dim.isupper(), dim.lower()
        n, at = sizes[dim], me[dim]
        spot = remaining.index(dim)
        remaining.remove(dim)
        extents = [sizes[d] for d in remaining]

        def block(j, source=current, spot=spot):
            return source.at[(slice(None),) * spot + (j,)]

        def values(j, source=current, spot=spot):
            return lambda spots: source[spots[:spot] + (j,) + spots[spot:] + (slice(None), slice(None))]

        if direct:
            base = sems.take(n)
            moves = []
            for k in range(1, n):
                to, origin = lax.rem(at + k, n), lax.rem(at + n - k, n)
                buf = bufs[stage].at[k]
                send = sems.copy(block(to), buf, base + k, device_at(sizes, me, dim, to))
                moves.append((send, sems.copy(buf, buf, base + k, device_at(sizes, me, dim, origin))))
            result = out if last else bufs[stage].at[0]
            stages.append(("direct", n, result, bufs[stage], moves, at, values, extents, last))
            current = result
        elif n == 2:
            send = sems.copy(block(1 - at), bufs[stage], sems.take(1), device_at(sizes, me, dim, 1 - at))
            stages.append((dim, n, None, bufs[stage], [send], at, values, extents, last))
            current = bufs[stage]
        else:
            chains = bufs[stage][0]
            result = out if last else bufs[stage][1]
            base = sems.take(2 * n)
            moves = []
            for slot in range(n - 1):
                for side in range(2):
                    lead = at if side == 0 else n - 1 - at
                    j = lax.rem((n - 1 - slot + at) if side == 0 else (slot + 1 + at + n), n)
                    buf = chains.at[side, j]
                    to = device_at(sizes, me, dim, at + 1 if side == 0 else at - 1)
                    index = base + side * n + j
                    plain, summed = sems.copy(block(j), buf, index, to), sems.copy(buf, buf, index, to)
                    moves.append((plain, summed, buf, j, lead == 0, (lead > 0) & (lead <= slot), lead <= slot))
            ends = []
            for side in range(2):
                buf = chains.at[side, at]
                ends.append(sems.copy(buf, buf, base + side * n + at, device_at(sizes, me, dim, at)))
            conds = (at > 0, at < n - 1)
            stages.append((dim, n, result, chains, moves, at, values, extents, (ends, conds)))
            current = result

    for dim, n, source, buf, moves, at, values, extents, last in stages:
        if dim == "s":
            for send in moves:
                send.start()
            yield
            total = source[me["z"], me["y"]].astype(jnp.float32)
            for k in range(1, n):
                at[k - 1].wait_recv()
                total = total + buf[k].astype(jnp.float32)
            out[...] = total
        elif dim == "direct":
            for send, _ in moves:
                send.start()
            yield
            for _, got in moves:
                got.wait_recv()

            def add_all(spots):
                here = spots + (slice(None), slice(None))
                total = values(at)(spots).astype(jnp.float32)
                for k in range(1, n):
                    total = total + buf[(k,) + here].astype(jnp.float32)
                source[here] = total.astype(source.dtype)

            over(extents, add_all)
        elif n == 2:
            moves[0].start()
            yield
            moves[0].wait_recv()
            if last:
                add_pair(out, buf, values(at), extents)
            else:
                add_into(buf, values(at), extents)
        else:
            for slot in range(n - 1):
                for plain, summed, target, j, is_first, is_later, _ in moves[2 * slot : 2 * slot + 2]:

                    def pass_on(summed=summed, target=target, j=j):
                        summed.wait_recv()
                        add_into(target, values(j), extents)
                        summed.start()

                    pl.when(is_first)(plain.start)
                    pl.when(is_later)(pass_on)
                yield

            def start(spots):
                here = spots + (slice(None), slice(None))
                source[here] = values(at)(spots).astype(source.dtype)

            over(extents, start)
            ends, conds = last
            for side in range(2):

                def finish(side=side):
                    ends[side].wait_recv()
                    add_into(source, lambda spots: buf[(side, at) + spots + (slice(None), slice(None))], extents)

                pl.when(conds[side])(finish)
    for dim, n, _, _, moves, _, _, _, _ in stages:
        for move in moves:
            if dim == "direct":
                move[0].wait_send()
            elif dim == "s" or n == 2:
                move.wait_send()
            else:
                pl.when(move[-1])(move[1].wait_send)


class Split:
    def __init__(self, parts):
        self.parts = parts
        self.dtype = parts[0].dtype

    def __setitem__(self, here, value):
        first = 0
        for part in self.parts:
            last = first + part.shape[-1]
            part[here] = value[:, first:last]
            first = last

    def __getitem__(self, here):
        return jnp.concatenate([part[here] for part in self.parts], axis=1)


def stage_buffers(sizes, block, dtype, dims, order):
    scratch, counts, left, total = [], [], list(dims), 0
    for dim in order:
        counts.append(1)
        if dim == "s":
            left = []
            n = sizes["z"] * sizes["y"]
            scratch.append(pltpu.VMEM((n,) + block, dtype))
            total += n
            continue
        left.remove(dim.lower())
        shape = tuple(sizes[d] for d in left) + block
        n = sizes[dim.lower()]
        if dim.isupper():
            scratch.append(pltpu.VMEM((n,) + shape, dtype))
            total += n
        elif n == 2:
            scratch.append(pltpu.VMEM(shape, dtype))
            total += 1
        else:
            scratch.append(pltpu.VMEM((2, n) + shape, dtype))
            total += 2 * n
            if dim != order[-1]:
                scratch.append(pltpu.VMEM(shape, dtype))
                counts[-1] = 2
    return scratch, counts, total, left


def stage_refs(sizes, order, counts, bufs):
    stages = []
    for dim, size in zip(order, counts):
        taken = [bufs.pop(0) for _ in range(size)]
        stages.append(taken[0] if dim == "s" or dim.isupper() or sizes[dim] == 2 else taken)
    return stages


def reduce_kernel(sizes, orders, dims, counts, splits, spill, *refs):
    count = len(orders)
    total = count + spill
    ends = sum(splits) + spill
    ins, outs = refs[:total], list(refs[total : total + ends])
    send_sem, recv_sem = refs[-2:]
    bufs = list(refs[total + ends : -2])
    me = place(sizes)
    used = [d for d in SLOTS if any(d in o.lower() for o in orders)]
    greet(sizes, me, used + ["s"] * (spill or any("s" in o for o in orders)))
    sems = Sems(send_sem, recv_sem)
    tasks = []
    for i in range(count):
        stages = stage_refs(sizes, orders[i], counts[i], bufs)
        parts = [outs.pop(0) for _ in range(splits[i])]
        out = parts[0] if len(parts) == 1 else Split(parts)
        tasks.append(reduce_task(sizes, me, ins[i], out, stages, sems, orders[i], dims[i]))
    if spill:
        tasks.insert(0, shift_task(sizes, me, ins[-1], outs.pop(0), sems, -1))
    run_together(tasks)


def cut_shapes(block, left, widths, sizes, dtype):
    if left or widths is None or sum(widths) != block[1]:
        shape = tuple(sizes[d] for d in left) + block
        return [jax.ShapeDtypeStruct(shape, dtype if left else jnp.float32)], widths
    return [jax.ShapeDtypeStruct((block[0], w), jnp.float32) for w in widths], None


def cut_columns(parts, widths):
    if widths is None:
        return parts
    full = parts[0].reshape(-1, sum(widths))
    edges = np.cumsum([0] + list(widths))
    return [full[:, int(lo) : int(hi)] for lo, hi in zip(edges[:-1], edges[1:])]


def reduce_all(grads, orders, sizes, collective_id, spill=None, splits=None, name="reduce"):
    ins, scratch, shapes, counts, all_dims, cuts, later = [], [], [], [], [], [], []
    splits = splits or [None] * len(grads)
    total = 0
    devices = sizes["x"] * sizes["c"] * sizes["z"] * sizes["y"]
    for grad, order, widths in zip(grads, orders, splits):
        dims = SLOTS[-(grad.ndim - 2) :] if grad.ndim > 2 else SLOTS
        if grad.ndim == 2:
            whole = tuple(sizes[d] for d in SLOTS)
            grad = grad.reshape(whole + tile_block(grad.shape[0] // devices, grad.shape[1]))
        block = grad.shape[-2:]
        ins.append(grad)
        all_dims.append(dims)
        more, taken, needed, left = stage_buffers(sizes, block, grad.dtype, dims, order)
        scratch += more
        total += needed
        counts.append(taken)
        ends, widths = cut_shapes(block, left, widths, sizes, grad.dtype)
        shapes += ends
        cuts.append(len(ends))
        later.append(widths)
    if spill is not None:
        ins.append(spill)
        shapes.append(jax.ShapeDtypeStruct(spill.shape, spill.dtype))
        total += 1
    outs = pl.pallas_call(
        functools.partial(reduce_kernel, sizes, orders, all_dims, counts, cuts, int(spill is not None)),
        in_specs=[pl.BlockSpec(memory_space=pltpu.VMEM)] * len(ins),
        out_specs=[pl.BlockSpec(memory_space=pltpu.VMEM)] * len(shapes),
        out_shape=shapes,
        scratch_shapes=scratch + [pltpu.SemaphoreType.DMA((total,)), pltpu.SemaphoreType.DMA((total,))],
        compiler_params=pltpu.CompilerParams(
            collective_id=collective_id, has_side_effects=True, vmem_limit_bytes=56 << 20
        ),
        name=name,
    )(*ins)
    outs = list(outs)
    results = []
    for cut, widths in zip(cuts, later):
        results.append(cut_columns([outs.pop(0) for _ in range(cut)], widths))
    return results + outs


def collect_task(sizes, me, src, out, ybuf, chain, sems, produce):
    z, y, n, fast = me["z"], me["y"], sizes["z"], sizes["y"]
    fan = sems.take((fast - 1) * n)
    base = sems.take(2 * n)

    def fan_copy(k, j):
        to = lax.rem(y + k, fast)
        index = fan + (k - 1) * n + j
        return sems.copy(src.at[j, to], ybuf.at[k - 1, j], index, device_at(sizes, me, "y", to))

    def spread(i, carry):
        far = n - 1 - lax.div(i, 2)
        j = jnp.where(lax.rem(i, 2) == 0, z + far, z - far)

        @pl.when((j >= 0) & (j < n))
        def _():
            produce(j)
            for k in range(1, fast):
                fan_copy(k, j).start()

        return carry

    def chain_copy(side, j, to, plain=False):
        buf = chain.at[side, j]
        return sems.copy(ybuf.at[0, j] if plain else buf, buf, base + side * n + j, device_at(sizes, me, "z", to))

    slots = []
    for slot in range(n - 1):
        for side in range(2):
            lead = z if side == 0 else n - 1 - z
            j = lax.rem((n - 1 - slot + z) if side == 0 else (slot + 1 + z + n), n)
            to = z + 1 if side == 0 else z - 1
            ends = (chain_copy(side, j, to, True), chain_copy(side, j, to))
            slots.append((side, j, ends, lead == 0, (lead > 0) & (lead <= slot), lead <= slot))
    fans = [fan_copy(k, j) for j in range(n) for k in range(1, fast)]
    lax.fori_loop(0, 2 * n - 1, spread, 0)
    yield

    def merge(j):
        for k in range(1, fast):
            fan_copy(k, j).wait_recv()
        value = src[j, y].astype(jnp.float32)
        for k in range(1, fast):
            value = value + ybuf[k - 1, j].astype(jnp.float32)
        return value

    for slot in range(n - 1):
        for side, j, (plain, summed), is_first, is_later, _ in slots[2 * slot : 2 * slot + 2]:

            def begin(plain=plain, j=j):
                ybuf[0, j] = merge(j).astype(ybuf.dtype)
                plain.start()

            def pass_on(summed=summed, side=side, j=j):
                value = merge(j)
                summed.wait_recv()
                chain[side, j] = (chain[side, j].astype(jnp.float32) + value).astype(chain.dtype)
                summed.start()

            pl.when(is_first)(begin)
            pl.when(is_later)(pass_on)
        yield
    out[...] = merge(z)

    def finish(side):
        chain_copy(side, z, z).wait_recv()
        out[...] += chain[side, z].astype(jnp.float32)

    pl.when(z > 0)(partial(finish, 0))
    pl.when(z < n - 1)(partial(finish, 1))
    for fan_end in fans:
        fan_end.wait_send()
    for _, _, (_, summed), _, _, active in slots:
        pl.when(active)(summed.wait_send)


def halve_kernel(sizes, apart, *refs):
    n, count = sizes["x"], len(apart)
    refs = list(refs)
    ins = [refs.pop(0) for _ in range(count)]
    outs = [[refs.pop(0) for _ in range(n)] if alone else refs.pop(0) for alone in apart]
    bufs = [refs.pop(0) for _ in range(count)]
    send_sem, recv_sem = refs
    me = place(sizes)
    greet(sizes, me, ("c",))
    sems = Sems(send_sem, recv_sem)
    c = me["c"]
    peer = device_at(sizes, me, "c", 1 - c)
    sends = {}
    for k in range(n - 1, -1, -1):
        for i, alone in enumerate(apart):
            at = lax.rem(me["x"] + k, n) if alone else k
            sends[k, i] = sems.copy(ins[i].at[at, 1 - c], bufs[i].at[k], sems.take(1), peer)
            sends[k, i].start()
    for k in range(n - 1, -1, -1):
        for i, alone in enumerate(apart):
            at = lax.rem(me["x"] + k, n) if alone else k
            sends[k, i].wait_recv()
            src = ins[i]

            def own(spots, src=src, at=at):
                return src[(at, c) + spots + (slice(None), slice(None))]

            add_pair(outs[i][k] if alone else outs[i].at[k], bufs[i].at[k], own, src.shape[2:-2])
    for send in sends.values():
        send.wait_send()


def halve_cores(grads, apart, sizes, collective_id, name="halve"):
    n = sizes["x"]
    whole = tuple(sizes[d] for d in SLOTS)
    devices = whole[0] * whole[1] * whole[2] * whole[3]
    ins = [g.reshape(whole + tile_block(g.shape[0] // devices, g.shape[1])) for g in grads]
    halves = [g.shape[:1] + g.shape[2:] for g in ins]
    shapes = []
    for h, g, alone in zip(halves, ins, apart):
        shapes += [jax.ShapeDtypeStruct(h[1:], g.dtype)] * n if alone else [jax.ShapeDtypeStruct(h, g.dtype)]
    total = n * len(ins)
    outs = pl.pallas_call(
        functools.partial(halve_kernel, sizes, apart),
        in_specs=[pl.BlockSpec(memory_space=pltpu.VMEM)] * len(ins),
        out_specs=[pl.BlockSpec(memory_space=pltpu.VMEM)] * len(shapes),
        out_shape=shapes,
        scratch_shapes=[pltpu.VMEM(h, g.dtype) for h, g in zip(halves, ins)]
        + [pltpu.SemaphoreType.DMA((total,)), pltpu.SemaphoreType.DMA((total,))],
        compiler_params=pltpu.CompilerParams(
            collective_id=collective_id, has_side_effects=True, vmem_limit_bytes=56 << 20
        ),
        name=name,
    )(*ins)
    outs = list(outs)
    return [[outs.pop(0) for _ in range(n)] if alone else outs.pop(0) for alone in apart]


def feed_forward_kernel(sizes, *refs):
    n = sizes["x"]
    hidden_ref, cot_ref, outer_ref, down_ref, gain_ref = refs[:5]
    att_parts, inv_parts, refs = refs[5:7], refs[7:9], refs[9:]
    layer_ref, d_hidden_ref, d_out_ref, scaled_ref, d_gain_ref = refs[:5]
    wide_outs, down_out = refs[5 : 5 + n], refs[5 + n]
    d_wide, d_down, wide_buf, down_buf, two_ref, low_ref, d_normed, att_ref, send_sem, recv_sem = refs[6 + n :]
    cut = att_parts[0].shape[0]
    att_ref[:cut] = att_parts[0][...]
    att_ref[cut:] = att_parts[1][...]
    me = place(sizes)
    greet(sizes, me, ("c",))
    sems = Sems(send_sem, recv_sem)
    c = me["c"]
    peer = device_at(sizes, me, "c", 1 - c)
    width = hidden_ref.shape[1]
    parts = 2 * n
    units = down_ref.shape[0] // parts
    two_ref[...] = hidden_ref[...] + nn_dot(att_ref[...], outer_ref[:, :width])
    gain = gain_ref[...]

    def scale():
        return lax.rsqrt(jnp.mean(two_ref[...] * two_ref[...], axis=1, keepdims=True) + EPSILON)

    low_ref[...] = (two_ref[...] * scale() * gain).astype(jnp.bfloat16)
    d_normed[...] = jnp.zeros_like(d_normed)
    d_hidden_ref[...] = two_ref[...]

    def down_copy(x):
        return sems.copy(d_down.at[x, 1 - c], down_buf.at[x], x, peer)

    def part(i, carry):
        gate_at = pl.ds(pl.multiple_of(i * units, units), units)
        up_at = pl.ds(pl.multiple_of((parts + i) * units, units), units)
        gate_w = outer_ref[:, pl.ds(pl.multiple_of(width + i * units, units), units)]
        up_w = outer_ref[:, pl.ds(pl.multiple_of(width + (parts + i) * units, units), units)]
        down_w = down_ref[gate_at, :]
        low, cot = low_ref[...], cot_ref[...]
        gate, up = nn_dot(low, gate_w), nn_dot(low, up_w)
        square = gate * gate
        bend = jnp.tanh(0.7978845608 * gate * (1.0 + 0.044715 * square))
        half = 0.5 * (1.0 + bend)
        act = gate * half
        slope = half + gate * (0.5 * (1.0 - bend * bend)) * (0.7978845608 * (1.0 + 3.0 * 0.044715 * square))
        inner = (act * up).astype(jnp.bfloat16)
        d_hidden_ref[...] += nn_dot(inner, down_w)
        d_inner = nt_dot(cot, down_w)
        d_gate = (d_inner * up * slope).astype(jnp.bfloat16)
        d_up = (d_inner * act).astype(jnp.bfloat16)
        d_down[lax.div(i, 2), lax.rem(i, 2)] = (
            tn_dot(inner, cot).astype(jnp.bfloat16).reshape(d_down.shape[2:])
        )
        pl.when(lax.rem(i, 2) != c)(lambda: down_copy(lax.div(i, 2)).start())
        block = d_wide.shape[:-1] + (units,)
        d_wide[..., gate_at] = tn_dot(low, d_gate).astype(jnp.bfloat16).reshape(block)
        d_wide[..., up_at] = tn_dot(low, d_up).astype(jnp.bfloat16).reshape(block)
        d_normed[...] += nt_dot(d_gate, gate_w) + nt_dot(d_up, up_w)
        return carry

    lax.fori_loop(0, parts, part, 0)
    sends = [down_copy(x) for x in range(n)]
    for x in range(n):
        send = sems.copy(d_wide.at[x, 1 - c], wide_buf.at[x], n + x, peer)
        send.start()
        sends.append(send)
    layer_ref[...] = d_hidden_ref[...].astype(jnp.bfloat16)
    two, s2 = two_ref[...], scale()
    pulled = gain * d_normed[...]
    d_gain_ref[...] = jnp.sum(d_normed[...] * two * s2, axis=0, keepdims=True)
    drift = jnp.mean(two * pulled, axis=1, keepdims=True)
    d_two = cot_ref[...].astype(jnp.float32) + s2 * pulled - two * (s2 * s2 * s2 * drift)
    d_hidden_ref[...] = d_two
    d_low = d_two.astype(jnp.bfloat16)
    d_out_ref[...] = tn_dot(att_ref[...], d_low).astype(jnp.bfloat16)
    d_att = nt_dot(d_low, outer_ref[:, :width]).astype(jnp.bfloat16)
    scaled_ref[:cut] = (d_att[:cut].astype(jnp.float32) * inv_parts[0][...]).astype(jnp.bfloat16)
    scaled_ref[cut:] = (d_att[cut:].astype(jnp.float32) * inv_parts[1][...]).astype(jnp.bfloat16)
    for send in sends:
        send.wait_recv()
    for x in range(n):
        add_pair(down_out.at[x], down_buf.at[x], lambda at, x=x: d_down[(x, c) + at], d_down.shape[2:-2])
        at_x = lax.rem(me["x"] + x, n)
        add_pair(wide_outs[x], wide_buf.at[at_x], lambda at, at_x=at_x: d_wide[(at_x, c) + at], d_wide.shape[2:-2])
    for send in sends:
        send.wait_send()


def feed_forward(hidden_one, cotangent, outer_w, down_w, gain, attended, inverse, sizes, collective_id):
    n = sizes["x"]
    whole = tuple(sizes[d] for d in SLOTS)
    devices = whole[0] * whole[1] * whole[2] * whole[3]
    count, width = hidden_one.shape
    hidden = down_w.shape[0]
    bf16, f32 = jnp.bfloat16, jnp.float32
    wide_block = (width // devices, 2 * hidden)
    down_block = (hidden // devices, width)
    plane = whole[2:]
    vmem = pl.BlockSpec(memory_space=pltpu.VMEM)
    outs = pl.pallas_call(
        functools.partial(feed_forward_kernel, sizes),
        in_specs=[vmem] * 9,
        out_specs=[vmem] * (6 + n),
        out_shape=[
            jax.ShapeDtypeStruct((count, width), bf16),
            jax.ShapeDtypeStruct((count, width), f32),
            jax.ShapeDtypeStruct((width, width), bf16),
            jax.ShapeDtypeStruct((count, width), bf16),
            jax.ShapeDtypeStruct((1, width), f32),
        ]
        + [jax.ShapeDtypeStruct(plane + wide_block, bf16)] * n
        + [jax.ShapeDtypeStruct((n,) + plane + down_block, bf16)],
        scratch_shapes=[
            pltpu.VMEM(whole + wide_block, bf16),
            pltpu.VMEM(whole + down_block, bf16),
            pltpu.VMEM((n,) + plane + wide_block, bf16),
            pltpu.VMEM((n,) + plane + down_block, bf16),
            pltpu.VMEM((count, width), f32),
            pltpu.VMEM((count, width), bf16),
            pltpu.VMEM((count, width), f32),
            pltpu.VMEM((count, width), bf16),
            pltpu.SemaphoreType.DMA((2 * n,)),
            pltpu.SemaphoreType.DMA((2 * n,)),
        ],
        compiler_params=pltpu.CompilerParams(
            collective_id=collective_id, has_side_effects=True, vmem_limit_bytes=60 << 20
        ),
        name="feed_forward",
    )(hidden_one, cotangent, outer_w, down_w, gain, *attended, *inverse)
    return list(outs[:5]) + [list(outs[5 : 5 + n]), outs[5 + n]]


def from_others(pieces, sizes):
    n = sizes["x"]
    got = []
    for k in range(1, n):
        pairs = [(((x + k) % n) * 2 + c, x * 2 + c) for x in range(n) for c in range(2)]
        got.append(lax.ppermute(pieces[n - k], "batch", pairs))
    return got


def back_rows_kernel(sizes, rows, tasks_info, inner, *refs):
    refs = list(refs)

    def take(count):
        taken = refs[:count]
        del refs[:count]
        return taken

    info_ref, far_ref, diag_ref, q_ref, g_ref, full_ref, peak_ref, kv_ref, dkv_ref, normed_ref, second_ref = take(11)
    if inner:
        own_ref, dq_before_ref, d_out_ref = take(3)
    grads = [take(info[4]) for info in tasks_info]
    d_normed_ref, dq_ref, near_ref = take(3)
    outs = [take(info[3]) for info in tasks_info]
    last_ref = take(1)[0]
    if inner:
        inner_ref = take(1)[0]
        inner_counts = inner
        d_last_ref = take(1)[0]
    else:
        d_last_ref = last_ref
    kv_buf, chunk_ref, normed_buf, d_rows_ref, ybuf, chain, bias_ref, sum_ref, acc_ref, total_ref = take(10)
    kv_sem, chunk_sem, normed_sem, send_sem, recv_sem = refs[-5:]
    bufs = refs[:-5]
    me = place(sizes)
    first = me["z"] * sizes["y"] + me["y"]
    seqs, length, _ = kv_ref.shape
    n = sizes["z"]
    step = length // n
    last = seqs - 1
    width = q_ref.shape[1]
    pairs = diag_ref.shape[0]
    wide = width // pairs
    fetch = pltpu.make_async_copy(kv_ref.at[last], kv_buf, kv_sem)
    fetch.start()
    greet(sizes, me, SLOTS + ("s",))
    sems = Sems(send_sem, recv_sem)
    ffn = []
    for (order, dims, counts, _, many), grad, out in zip(tasks_info, grads, outs):
        src = grad[0]
        if many > 1:
            src = bufs.pop(0)

            def total(spots, src=src, grad=grad):
                here = spots + (slice(None), slice(None))
                value = grad[0][here].astype(jnp.float32)
                for more in grad[1:]:
                    value = value + more[here].astype(jnp.float32)
                src[here] = value.astype(src.dtype)

            over(src.shape[:-2], total)
        stages = stage_refs(sizes, order, counts, bufs)
        ffn.append(reduce_task(sizes, me, src, out[0] if len(out) == 1 else Split(out), stages, sems, order, dims))
        next(ffn[-1])
    wide_task, down_task = ffn

    def rows_of(p):
        def produce(j):
            here = pl.ds(pl.multiple_of(j * step, step), step)
            if p < last:
                copy = pltpu.make_async_copy(dkv_ref.at[p, here], chunk_ref.at[0], chunk_sem.at[0])
                copy.start()
                copy.wait()
                block = chunk_ref[0]
            else:
                block = d_last_ref[here, :]
            block = nt_dot(block, second_ref[...]).astype(jnp.bfloat16)
            d_rows_ref[p, j] = block.reshape(d_rows_ref.shape[2:])

        return collect_task(
            sizes, me, d_rows_ref.at[p], d_normed_ref.at[p], ybuf.at[p], chain.at[p], sems, produce
        )

    before = [rows_of(p) for p in range(last)]
    for task in before:
        next(task)
    fetch.wait()
    size = info_ref[last]

    def one_pair(p, carry):
        fill_bias(rows, far_ref, diag_ref.at[pl.ds(p, 1)], bias_ref, p)
        sum_ref[...] = jnp.zeros_like(sum_ref)
        lanes = pl.ds(pl.multiple_of(p * wide, wide), wide)
        tail = slice(last * rows, seqs * rows)
        k_lanes = pl.ds(pl.multiple_of(2 * p * wide, wide), wide)
        v_lanes = pl.ds(pl.multiple_of((2 * p + 1) * wide, wide), wide)

        def write(here, dk, dv):
            d_last_ref[here, k_lanes] = dk
            d_last_ref[here, v_lanes] = dv

        dq_ref[:, lanes] = back_pair(
            rows,
            size,
            first,
            q_ref[tail, lanes],
            g_ref[tail, lanes],
            full_ref[:, lanes],
            (lambda here: (kv_buf[here, k_lanes], kv_buf[here, v_lanes]), length // (SPAN * rows)),
            [peak_ref[0, p, a : a + 1, :] for a in range(2)],
            bias_ref,
            sum_ref,
            acc_ref,
            write,
        )

        def keep(a, slot, value):
            near_ref[p, a, slot] = value

        near_sums(rows, sum_ref, keep)
        for i in range(min(pairs, n - 1)):

            @pl.when(p == i)
            def _():
                for task in before:
                    next(task, None)

        @pl.when(p == pairs - 1)
        def _():
            next(wide_task)
            next(down_task)

        return carry

    lax.fori_loop(0, pairs, one_pair, 0)
    after = rows_of(last)
    next(after)
    tasks = ffn + before + [after]
    if inner:
        steps = seqs * n
        early = last * n

        def at_step(i):
            return pl.ds(pl.multiple_of(i * step, step), step)

        def normed_copy(i):
            slot = lax.rem(i, 2)
            return pltpu.make_async_copy(normed_ref.at[at_step(i)], normed_buf.at[slot], normed_sem.at[slot])

        def early_copy(i):
            slot = lax.rem(i, 2)
            src = dkv_ref.at[lax.div(i, n), at_step(lax.rem(i, n))]
            return pltpu.make_async_copy(src, chunk_ref.at[slot], chunk_sem.at[slot])

        normed_copy(0).start()
        early_copy(0).start()
        total_ref[...] = jnp.zeros_like(total_ref)

        plan = [[], before, [], [wide_task], [after], [], [after]]

        def weigh(i, carry):
            pl.when(i + 1 < steps)(lambda: normed_copy(i + 1).start())
            pl.when(i + 1 < early)(lambda: early_copy(i + 1).start())
            normed_copy(i).wait()
            slot = lax.rem(i, 2)

            @pl.when(i < early)
            def _():
                early_copy(i).wait()
                total_ref[...] += tn_dot(normed_buf[slot], chunk_ref[slot])

            @pl.when(i >= early)
            def _():
                total_ref[...] += tn_dot(normed_buf[slot], d_last_ref[at_step(i - early), :])

            for k, tasks_now in enumerate(plan):

                @pl.when(i == k)
                def _():
                    for task in tasks_now:
                        next(task, None)

            return carry

        lax.fori_loop(0, steps, weigh, 0)
        block = inner_ref.shape[:-1]
        d_query = tn_dot(own_ref[last * rows :], dq_ref[...])
        if last:
            d_query = d_query + tn_dot(own_ref[: last * rows], dq_before_ref[...])
        inner_ref[..., :width] = d_query.astype(jnp.bfloat16).reshape(block + (width,))
        inner_ref[..., width : 2 * width] = d_out_ref[...]
        inner_ref[..., 2 * width :] = total_ref[...].astype(jnp.bfloat16).reshape(block + (2 * width,))
        stages = stage_refs(sizes, "cx", inner_counts, bufs)
        tasks.insert(0, reduce_task(sizes, me, inner_ref, last_ref, stages, sems, "cx", SLOTS))
    run_together(tasks)


def back_rows(info, far, diag, q, g, full, kv, peak, dkv, normed_all, normed_own, second, dq_before, d_out, grads,
              orders, splits, sizes, rows, collective_id, name="back_rows"):
    seqs, length, double = kv.shape
    width = q.shape[1]
    last = seqs - 1
    pairs = far.shape[0] // 2
    n, fast = sizes["z"], sizes["y"]
    step = length // n
    smem, vmem = pl.BlockSpec(memory_space=pltpu.SMEM), pl.BlockSpec(memory_space=pltpu.VMEM)
    anywhere = pl.BlockSpec(memory_space=pl.ANY)
    bf16, f32 = jnp.bfloat16, jnp.float32
    ins = [info, far, diag, q, g, full, peak, kv, dkv, normed_all, second]
    in_specs = [smem, smem] + [vmem] * 5 + [anywhere] * 3 + [vmem]
    devices = sizes["x"] * sizes["c"] * n * fast
    own_block = (width // devices, 4 * width)
    inner = None
    scratch, total = [], 0
    if own_block[0] % 16 == 0:
        whole = tuple(sizes[d] for d in SLOTS)
        more, inner, needed, left = stage_buffers(sizes, own_block, bf16, SLOTS, "cx")
        inner_more = more
        total += needed
        ins += [normed_own, dq_before, d_out.reshape(whole + (own_block[0], width))]
        in_specs += [vmem] * 3
        last_shape = jax.ShapeDtypeStruct(tuple(sizes[d] for d in left) + own_block, bf16)
    else:
        last_shape = jax.ShapeDtypeStruct((length, double), bf16)
    tasks_info, shapes, later = [], [], []
    for grad, order, widths in zip(grads, orders, splits):
        many = isinstance(grad, list)
        given = grad if many else [grad]
        block = given[0].shape[-2:]
        dims = ("z", "y") if many else ("x", "z", "y")
        more, counts, needed, left = stage_buffers(sizes, block, given[0].dtype, dims, order)
        if len(given) > 1:
            more = [pltpu.VMEM(given[0].shape, given[0].dtype)] + more
        scratch += more
        total += needed
        ends, widths = cut_shapes(block, left, widths, sizes, given[0].dtype)
        shapes += ends
        later.append(widths)
        tasks_info.append((order, dims, counts, len(ends), len(given)))
        ins += given
        in_specs += [vmem] * len(given)
    head_shapes = [
        jax.ShapeDtypeStruct((seqs, rows, width), f32),
        jax.ShapeDtypeStruct((rows, width), bf16),
        jax.ShapeDtypeStruct((pairs, 2, 5, 8, 2 * rows), f32),
    ]
    own_scratch = []
    if inner:
        own_scratch = [pltpu.VMEM(whole + own_block, bf16), pltpu.VMEM((length, double), bf16)]
        scratch = scratch + inner_more
    block = (seqs, n, fast, rows, width)
    own_scratch += [
        pltpu.VMEM((length, double), bf16),
        pltpu.VMEM((2, step, double), bf16),
        pltpu.VMEM((2, step, width), bf16),
        pltpu.VMEM(block, bf16),
        pltpu.VMEM((seqs, fast - 1, n, rows, width), bf16),
        pltpu.VMEM((seqs, 2, n, rows, width), bf16),
        pltpu.VMEM((2, 5, rows, rows), f32),
        pltpu.VMEM((2, 5, rows, rows), f32),
        pltpu.VMEM((2, width // pairs, rows), f32),
        pltpu.VMEM((width, double), f32) if inner else pltpu.VMEM((8, 128), f32),
    ]
    total += seqs * ((fast - 1) * n + 2 * n)
    outs = pl.pallas_call(
        functools.partial(back_rows_kernel, sizes, rows, tasks_info, inner),
        in_specs=in_specs,
        out_specs=[vmem] * (len(shapes) + 4),
        out_shape=head_shapes + shapes + [last_shape],
        scratch_shapes=own_scratch
        + scratch
        + [
            pltpu.SemaphoreType.DMA,
            pltpu.SemaphoreType.DMA((2,)),
            pltpu.SemaphoreType.DMA((2,)),
            pltpu.SemaphoreType.DMA((total,)),
            pltpu.SemaphoreType.DMA((total,)),
        ],
        compiler_params=pltpu.CompilerParams(
            collective_id=collective_id, has_side_effects=True, vmem_limit_bytes=62 << 20
        ),
        name=name,
    )(*ins)
    outs = list(outs)
    heads = [outs.pop(0) for _ in range(3)]
    results = []
    for (_, _, _, cut, _), widths in zip(tasks_info, later):
        results.append(cut_columns([outs.pop(0) for _ in range(cut)], widths))
    return heads + results + [outs[0], inner is not None]


def finish_kernel(refs_in, *refs):
    layer, d_inputs, spill, small, proj, query, out, second, gate, up, down = refs[:refs_in]
    (o_layer, o_input, o_taps, o_proj, o_query, o_key, o_value, o_out, o_gate, o_up, o_down) = refs[refs_in:]
    o_layer[...] = layer[...]
    rows = d_inputs.shape[1]
    edge = lax.broadcasted_iota(jnp.int32, spill.shape[1:], 0)
    for b in range(d_inputs.shape[0]):
        o_input[b] = d_inputs[b].astype(o_input.dtype)
        late = jnp.where(edge >= 5, pltpu.roll(spill[b], 5, 0), 0.0)
        tail = d_inputs[b, rows - 16 :, :]
        late = jnp.concatenate([jnp.zeros_like(late), late], axis=0)
        o_input[b, rows - 16 :, :] = (tail + late).astype(o_input.dtype)
    o_taps[...] = small[:, :TAPS]
    for source, target in ((proj, o_proj), (query, o_query), (out, o_out), (gate, o_gate), (up, o_up), (down, o_down)):
        target[...] = source[...]
    pair = PACK
    for p in range(second.shape[1] // (2 * pair)):
        o_key[:, p * pair : (p + 1) * pair] = second[:, 2 * p * pair : (2 * p + 1) * pair]
        o_value[:, p * pair : (p + 1) * pair] = second[:, (2 * p + 1) * pair : (2 * p + 2) * pair]


def finish(*ins):
    layer, d_inputs, _, small, proj, query, out, second, gate, up, down = ins
    like = lambda x: jax.ShapeDtypeStruct(x.shape, x.dtype)
    vmem = pl.BlockSpec(memory_space=pltpu.VMEM)
    return pl.pallas_call(
        functools.partial(finish_kernel, len(ins)),
        in_specs=[vmem] * len(ins),
        out_specs=[vmem] * 11,
        out_shape=[
            like(layer),
            jax.ShapeDtypeStruct(d_inputs.shape, jnp.bfloat16),
            jax.ShapeDtypeStruct((small.shape[0], TAPS), jnp.float32),
            like(proj),
            like(query),
            like(proj),
            like(proj),
            like(out),
            like(gate),
            like(up),
            like(down),
        ],
        compiler_params=pltpu.CompilerParams(vmem_limit_bytes=32 << 20),
        name="finish",
    )(*ins)


def on_device(
    inputs,
    lengths,
    conv_taps,
    gain_attn,
    w_proj,
    w_query,
    w_key,
    w_value,
    w_out,
    gain_ffn,
    w_gate,
    w_up,
    w_down,
    rel_bias,
    cotangent,
):
    batch, seq = lax.axis_size("batch"), lax.axis_size("seq")
    sizes = layout_of(batch, seq)
    devices = batch * seq
    seqs, rows, width = inputs.shape
    length = rows * seq
    count = seqs * rows
    own = w_proj.shape[0]
    own_bias = rel_bias.shape[0]
    heads = own_bias * devices // NB
    hidden = w_gate.shape[1]

    small = jnp.concatenate(
        [
            conv_taps,
            gain_attn[:, None],
            gain_ffn[:, None],
            jnp.pad(rel_bias, (0, own - own_bias))[:, None],
            jnp.zeros((own, PACK - TAPS - 3), jnp.bfloat16),
        ],
        axis=1,
    )
    pairs = heads // 2
    pair = width // pairs
    key_value_w = []
    for p in range(pairs):
        key_value_w += [(w_key, p * pair, (p + 1) * pair), (w_value, p * pair, (p + 1) * pair)]
    first, second, outer_plane, down_plane, left_rim = gather_all(
        [
            [(small, 0, PACK), (w_proj, 0, width), (w_query, 0, width)],
            key_value_w,
            [(w_out, 0, width), (w_gate, 0, hidden), (w_up, 0, hidden)],
            w_down,
        ],
        ["Zyxc", "Zxyc", "zy", "yz"],
        sizes,
        1,
        rim=inputs,
        name="gather_first",
    )
    first = first.reshape(width, -1)
    second = second.reshape(width, -1)
    taps = first[:, :TAPS].astype(jnp.float32)
    gain_first = first[:, TAPS].astype(jnp.float32)
    gain_second = first[:, TAPS + 1].astype(jnp.float32)
    table = first[:, TAPS + 2].reshape(devices, own)[:, :own_bias].reshape(heads, NB).astype(jnp.float32)
    proj_w = first[:, PACK : PACK + width]
    query_w = first[:, PACK + width :]

    padded = jnp.concatenate([left_rim[:, 13:], inputs], axis=1).astype(jnp.float32)
    mixed_conv, conv_back = jax.vjp(partial(conv_mix, row_count=rows), padded, taps)
    mixed_low = mixed_conv.astype(jnp.bfloat16).reshape(count, width)
    resid_in = inputs.astype(jnp.float32).reshape(count, width)
    hidden_one = resid_in + mat_dot(mixed_low, proj_w)
    normed_one, norm_one_back = jax.vjp(norm_rows, hidden_one, gain_first)
    normed_low = normed_one.astype(jnp.bfloat16)

    queries = mat_dot(normed_low, query_w).astype(jnp.bfloat16)
    far, diag = bias_tables(table, rows)
    info = jnp.concatenate([lengths, lax.axis_index("seq")[None].astype(jnp.int32)])
    (outer_w, down_w), normed_all, key_value, begun = gather_rows(
        info,
        far,
        diag,
        normed_low.reshape(seqs, rows, width),
        queries,
        second,
        [outer_plane, down_plane],
        ["xc", "xc"],
        sizes,
        2,
    )
    outer_w = outer_w.reshape(width, -1)
    down_w = down_w.reshape(hidden, -1)
    out_w = outer_w[:, :width]
    wide_w = outer_w[:, width:]
    normed_all = normed_all.reshape(seqs * length, width)
    rest = attend(info, far, diag, queries, key_value, rows, length, 1)

    grad_low = cotangent.reshape(count, width)
    if own % 16 == 0:
        layer_out, d_hidden_two, d_out_w, scaled, d_gain_two, wide_pieces, down_half = feed_forward(
            hidden_one,
            grad_low,
            outer_w,
            down_w,
            gain_second[None],
            (begun[0], rest[0]),
            (begun[2], rest[2]),
            sizes,
            4,
        )
        d_gain_two = d_gain_two[0]
    else:
        attended = jnp.concatenate([begun[0], rest[0]], axis=0)
        inverse = jnp.concatenate([begun[2], rest[2]], axis=0)
        hidden_two = hidden_one + mat_dot(attended, out_w)
        normed_two, norm_two_back = jax.vjp(norm_rows, hidden_two, gain_second)
        normed_two_low = normed_two.astype(jnp.bfloat16)
        both_pre = mat_dot(normed_two_low, wide_w)
        inner_act, inner_back = jax.vjp(gated, both_pre[:, :hidden], both_pre[:, hidden:])
        inner_low = inner_act.astype(jnp.bfloat16)
        layer_out = (hidden_two + mat_dot(inner_low, down_w)).astype(jnp.bfloat16)

        d_down_w = outer_sum(inner_low, grad_low).astype(jnp.bfloat16)
        d_gate, d_up = inner_back(back_dot(grad_low, down_w))
        d_both = jnp.concatenate([d_gate.astype(jnp.bfloat16), d_up.astype(jnp.bfloat16)], axis=1)
        d_wide_w = outer_sum(normed_two_low, d_both).astype(jnp.bfloat16)
        d_hidden_part, d_gain_two = norm_two_back(back_dot(d_both, wide_w))
        d_hidden_two = grad_low.astype(jnp.float32) + d_hidden_part
        d_attn_low = d_hidden_two.astype(jnp.bfloat16)
        d_out_w = outer_sum(attended, d_attn_low).astype(jnp.bfloat16)
        d_attended = back_dot(d_attn_low, out_w).astype(jnp.bfloat16)
        scaled = (d_attended.astype(jnp.float32) * inverse).astype(jnp.bfloat16)
        wide_pieces, down_half = halve_cores([d_wide_w, d_down_w], [True, False], sizes, 4)
    scaled, wide_pieces, down_half, d_out_w, layer_out = lax.optimization_barrier(
        (scaled, wide_pieces, down_half, d_out_w, layer_out)
    )
    wide_others = from_others(wide_pieces, sizes)
    early = seqs - 1
    assert early == 1
    dq_before, dkv_before, near_before = attend_back(
        info, far, diag, queries, scaled, begun[1], key_value, begun[3], rows, length, early
    )
    dq_before, dkv_before, near_before, wide_others = lax.optimization_barrier(
        (dq_before, dkv_before, near_before, wide_others)
    )
    d_normed_one, dq_last, near, (g_gate, g_up), (g_down,), last, joined = back_rows(
        info,
        far,
        diag,
        queries,
        scaled,
        rest[1],
        key_value,
        rest[3],
        dkv_before,
        normed_all,
        normed_low,
        second,
        dq_before,
        d_out_w,
        [[wide_pieces[0]] + wide_others, down_half],
        ["Zy", "xs"],
        [(hidden, hidden), None],
        sizes,
        rows,
        5,
    )
    d_table = bias_grad(near_before + near, rows).reshape(heads * NB)
    d_queries = jnp.concatenate([dq_before, dq_last], axis=0)
    if joined:
        inner, inner_order = last, "s"
    else:
        d_key_value = jnp.concatenate([dkv_before, last[None]], axis=0).reshape(seqs * length, 2 * width)
        d_second_w = outer_sum(normed_all, d_key_value).astype(jnp.bfloat16)
        d_query_w = outer_sum(normed_low, d_queries).astype(jnp.bfloat16)
        inner, inner_order = jnp.concatenate([d_query_w, d_out_w, d_second_w], axis=1), "cxs"
    d_normed_one = d_normed_one.reshape(count, width)
    d_normed_one = d_normed_one + back_dot(d_queries, query_w)
    d_first_part, d_gain_one = norm_one_back(d_normed_one)
    d_hidden_one = d_hidden_two + d_first_part
    d_mix_low = d_hidden_one.astype(jnp.bfloat16)
    d_proj_w = outer_sum(mixed_low, d_mix_low).astype(jnp.bfloat16)
    d_mixed = back_dot(d_mix_low, proj_w).reshape(seqs, rows, width)
    d_padded, d_taps = conv_back(d_mixed)
    d_inputs = d_hidden_one.reshape(seqs, rows, width) + d_padded[:, 3:, :]
    d_small = jnp.concatenate(
        [
            d_taps.T,
            d_gain_one[None],
            d_gain_two[None],
            jnp.pad(d_table.reshape(devices, own_bias), ((0, 0), (0, own - own_bias))).reshape(1, width),
            jnp.zeros((16 - TAPS - 3, width), jnp.float32),
        ],
        axis=0,
    )
    d_last = jnp.concatenate([d_proj_w, jnp.pad(d_small.T, ((0, 0), (0, PACK - 16))).astype(jnp.bfloat16)], axis=1)
    (g_proj, g_small), (g_query, g_out, g_second), spill = reduce_all(
        [d_last, inner],
        ["cxs", inner_order],
        sizes,
        6,
        spill=d_padded[:, :8, :],
        splits=[(width, PACK), (width, width, 2 * width)],
    )
    assert pair == PACK
    done = finish(
        layer_out,
        d_inputs,
        spill,
        g_small,
        g_proj,
        g_query,
        g_out,
        g_second,
        g_gate,
        g_up,
        g_down.reshape(w_down.shape),
    )
    layer_out, input_grad, g_taps, g_proj, g_query, g_key, g_value, g_out, g_gate, g_up, g_down = done
    return (
        layer_out.reshape(seqs, rows, width),
        input_grad,
        g_taps,
        g_small[:, TAPS],
        g_proj,
        g_query,
        g_key,
        g_value,
        g_out,
        g_small[:, TAPS + 1],
        g_gate,
        g_up,
        g_down,
        g_small[:own_bias, TAPS + 2],
    )


def solution(mesh):
    in_specs = (
        P("batch", "seq", None),
        P("batch"),
        P(("batch", "seq"), None),
        P(("batch", "seq")),
        P(("batch", "seq"), None),
        P(("batch", "seq"), None),
        P(("batch", "seq"), None),
        P(("batch", "seq"), None),
        P(("batch", "seq"), None),
        P(("batch", "seq")),
        P(("batch", "seq"), None),
        P(("batch", "seq"), None),
        P(("batch", "seq"), None),
        P(("batch", "seq")),
        P("batch", "seq", None),
    )
    out_specs = (
        P("batch", "seq", None),
        P("batch", "seq", None),
        P(("batch", "seq"), None),
        P(("batch", "seq")),
        P(("batch", "seq"), None),
        P(("batch", "seq"), None),
        P(("batch", "seq"), None),
        P(("batch", "seq"), None),
        P(("batch", "seq"), None),
        P(("batch", "seq")),
        P(("batch", "seq"), None),
        P(("batch", "seq"), None),
        P(("batch", "seq"), None),
        P(("batch", "seq")),
    )
    return jax.shard_map(
        on_device, mesh=mesh, in_specs=in_specs, out_specs=out_specs, check_vma=False
    )
```

```python
import functools
from functools import partial

import jax
import jax.numpy as jnp
import numpy as np
from jax import lax
from jax.experimental import pallas as pl
from jax.experimental.pallas import tpu as pltpu
from jax.sharding import PartitionSpec as P

NB = 32
EPSILON = 1e-06
LIMITS = (12, 16, 23, 32, 46, 64, 91)
WINDOWS = ((2, 0), (3, 2), (4, 5))
TAPS = 9
PACK = 128
SPAN = 8

def mat_dot(lhs_array, rhs_array):
    return jnp.dot(lhs_array, rhs_array, preferred_element_type=jnp.float32)


def outer_sum(lhs_array, rhs_array):
    return lax.dot_general(
        lhs_array, rhs_array, (((0,), (0,)), ((), ())), preferred_element_type=jnp.float32
    )


def back_dot(grad_rows, weight):
    return lax.dot_general(
        grad_rows, weight, (((1,), (1,)), ((), ())), preferred_element_type=jnp.float32
    )


def bucket_of(relative):
    distance = jnp.abs(relative)
    larger = jnp.full(relative.shape, 8, jnp.int32)
    for threshold in LIMITS:
        larger = larger + (distance >= threshold).astype(jnp.int32)
    inside = jnp.where(distance < 8, distance, larger)
    return inside + 16 * (relative > 0).astype(jnp.int32)


def norm_rows(hidden, gain_row):
    return (
        hidden * lax.rsqrt(jnp.mean(hidden * hidden, axis=-1, keepdims=True) + EPSILON) * gain_row
    )


def gated(gate_pre, up_pre):
    return jax.nn.gelu(gate_pre, approximate=True) * up_pre


def conv_mix(padded, taps, row_count):
    summed = jnp.zeros(padded.shape[:-2] + (row_count, padded.shape[-1]), jnp.float32)
    for window_len, offset in WINDOWS:
        conv_sum = jnp.zeros_like(summed)
        for tap_index in range(window_len):
            shifted = lax.slice_in_dim(
                padded, 3 - tap_index, 3 - tap_index + row_count, axis=padded.ndim - 2
            )
            conv_sum = conv_sum + taps[:, offset + tap_index] * shifted
        summed = summed + jax.nn.gelu(conv_sum, approximate=True)
    return summed


def near_offsets(rows):
    lane = np.arange(2 * rows)
    lane = np.where(lane < rows, lane, lane - 2 * rows)
    return rows * (np.arange(3)[:, None, None] - 1) + np.arange(8)[None, :, None] - lane[None, None, :]


def bias_tables(table, rows):
    heads = table.shape[0]
    buckets = bucket_of(jnp.asarray(near_offsets(rows)[:, 0, :], jnp.int32)).reshape(-1)
    onehot = (buckets[None, :] == jnp.arange(NB, dtype=jnp.int32)[:, None]).astype(jnp.float32)
    diag = jnp.dot(table, onehot, precision=lax.Precision.HIGHEST)
    far = jnp.stack([table[:, NB // 2 - 1], table[:, NB - 1]], axis=1)
    return far, diag.reshape(heads // 2, 6, 2 * rows)


def bias_grad(near, rows):
    near = near.reshape(near.shape[0] * 2, 5, 8, 2 * rows)
    buckets = bucket_of(jnp.asarray(near_offsets(rows), jnp.int32))
    hit = buckets[None] == jnp.arange(NB, dtype=jnp.int32)[:, None, None, None]
    grad = jnp.sum(jnp.where(hit[None], near[:, None, 1:4], 0.0), axis=(2, 3, 4))
    left = jnp.sum(near[:, 0], axis=(1, 2))
    right = jnp.sum(near[:, 4], axis=(1, 2))
    return grad.at[:, NB // 2 - 1].add(left).at[:, NB - 1].add(right)


def nt_dot(a, b):
    return lax.dot_general(a, b, (((1,), (1,)), ((), ())), preferred_element_type=jnp.float32)


def tn_dot(a, b):
    return lax.dot_general(a, b, (((0,), (0,)), ((), ())), preferred_element_type=jnp.float32)


def nn_dot(a, b):
    return lax.dot_general(a, b, (((1,), (0,)), ((), ())), preferred_element_type=jnp.float32)


def fill_bias(rows, far_ref, diag_ref, bias_ref, pair):
    for a in range(2):
        bias_ref[a, 0] = jnp.full((rows, rows), far_ref[2 * pair + a, 0], jnp.float32)
        bias_ref[a, 4] = jnp.full((rows, rows), far_ref[2 * pair + a, 1], jnp.float32)
        for c in range(3):
            base = jnp.broadcast_to(diag_ref[0, 3 * a + c : 3 * a + c + 1, :], (rows, 2 * rows))
            bias_ref[a, 1 + c] = pltpu.roll(base, 0, 1, stride=1, stride_axis=0)[:, :rows]


def head_halves(block):
    lane = lax.broadcasted_iota(jnp.int32, block.shape, 1)
    zero = jnp.zeros_like(block)
    half = block.shape[1] // 2
    return jnp.where(lane < half, block, zero), jnp.where(lane < half, zero, block)


def attend_pair(rows, length, first, q, keys, values, spans, bias_ref, s_ref, acc_ref):
    halves = head_halves(q)
    wide = q.shape[1]
    half = wide // 2
    key_row = lax.broadcasted_iota(jnp.int32, (rows, rows), 0)
    lane = lax.broadcasted_iota(jnp.int32, (SPAN * rows, wide), 1)

    def scores(i, peaks):
        kc = i * SPAN
        k = keys(pl.ds(kc * rows, SPAN * rows))
        new = list(peaks)
        for a in range(2):
            full = nt_dot(k, halves[a])
            for u in range(SPAN):
                slot = jnp.clip(kc + u - first + 2, 0, 4)
                valid = key_row < length - (kc + u) * rows
                s = full[u * rows : (u + 1) * rows] + bias_ref[a, slot]
                s = jnp.where(valid, s, -1e9)
                s_ref[a, pl.ds((kc + u) * rows, rows), :] = s
                new[a] = jnp.maximum(new[a], jnp.max(s.reshape(rows // 8, 8, rows), axis=0))
        return tuple(new)

    def weigh(i, carry):
        here = pl.ds(i * SPAN * rows, SPAN * rows)
        v = values(here)
        ones = jnp.ones_like(v)
        for a, v_one in enumerate((jnp.where(lane < half, v, ones), jnp.where(lane < half, ones, v))):
            e = jnp.exp(s_ref[a, here, :] - tops[a])
            acc_ref[a] += tn_dot(v_one, e.astype(jnp.bfloat16))
        return carry

    low = jnp.full((8, rows), -jnp.inf, jnp.float32)
    peaks = scores(0, (low, low)) if spans == 1 else lax.fori_loop(0, spans, scores, (low, low))
    tops = [jnp.max(p, axis=0, keepdims=True) for p in peaks]
    acc_ref[...] = jnp.zeros_like(acc_ref)
    if spans == 1:
        weigh(0, 0)
    else:
        lax.fori_loop(0, spans, weigh, 0)
    inv = jnp.concatenate([1.0 / acc_ref[0, half:], 1.0 / acc_ref[1, :half]], axis=0)
    out = jnp.concatenate([acc_ref[0, :half], acc_ref[1, half:]], axis=0) * inv
    return out.T, inv.T, tops


def attend_kernel(rows, skip, info_ref, far_ref, diag_ref, q_ref, k_ref, v_ref, *refs):
    o_ref, full_ref, inv_ref, peak_ref, bias_ref, s_ref, acc_ref = refs
    pair, b = pl.program_id(0), pl.program_id(1)

    @pl.when(b == 0)
    def _():
        fill_bias(rows, far_ref, diag_ref, bias_ref, pair)

    out, inv, tops = attend_pair(
        rows,
        info_ref[b + skip],
        info_ref[info_ref.shape[0] - 1],
        q_ref[...],
        lambda here: k_ref[0, here, :],
        lambda here: v_ref[0, here, :],
        k_ref.shape[1] // (SPAN * rows),
        bias_ref,
        s_ref,
        acc_ref,
    )
    o_ref[...] = out.astype(o_ref.dtype)
    full_ref[...] = out
    inv_ref[...] = inv
    for a in range(2):
        peak_ref[0, 0, a : a + 1, :] = tops[a]


def attention_cost(q, kv, products):
    flops = products * 8 * q.shape[0] * kv.shape[1] * q.shape[1]
    return pl.CostEstimate(
        flops=flops, bytes_accessed=2 * (q.size + kv.size) * products, transcendentals=8 * q.shape[0] * kv.shape[1]
    )


def attention_shapes(seqs, rows, width, pairs):
    shape = (seqs * rows, width)
    return [
        jax.ShapeDtypeStruct(shape, jnp.bfloat16),
        jax.ShapeDtypeStruct(shape, jnp.float32),
        jax.ShapeDtypeStruct(shape, jnp.float32),
        jax.ShapeDtypeStruct((seqs, pairs, 2, rows), jnp.float32),
    ]


def attend(info, far, diag, q, kv, rows, length, skip):
    heads = far.shape[0]
    seqs = kv.shape[0]
    wide = 2 * (q.shape[1] // heads)
    pairs = heads // 2
    smem = pl.BlockSpec(memory_space=pltpu.SMEM)
    return pl.pallas_call(
        functools.partial(attend_kernel, rows, skip),
        grid=(pairs, seqs - skip),
        in_specs=[
            smem,
            smem,
            pl.BlockSpec((1, 6, 2 * rows), lambda p, b: (p, 0, 0)),
            pl.BlockSpec((rows, wide), lambda p, b: (b + skip, p)),
            pl.BlockSpec((1, length, wide), lambda p, b: (b + skip, 0, 2 * p)),
            pl.BlockSpec((1, length, wide), lambda p, b: (b + skip, 0, 2 * p + 1)),
        ],
        out_specs=[pl.BlockSpec((rows, wide), lambda p, b: (b, p))] * 3
        + [pl.BlockSpec((1, 1, 2, rows), lambda p, b: (b, p, 0, 0))],
        out_shape=attention_shapes(seqs - skip, rows, q.shape[1], pairs),
        scratch_shapes=[
            pltpu.VMEM((2, 5, rows, rows), jnp.float32),
            pltpu.VMEM((2, length, rows), jnp.float32),
            pltpu.VMEM((2, wide, rows), jnp.float32),
        ],
        compiler_params=pltpu.CompilerParams(vmem_limit_bytes=48 << 20),
        cost_estimate=attention_cost(q, kv, 1),
        name="attend",
    )(info, far, diag, q, kv, kv)


def back_pair(rows, length, first, q, g, full, key_value, peak, bias_ref, sum_ref, acc_ref, write):
    q_half, g_half = head_halves(q), head_halves(g)
    wide = q.shape[1]
    half = wide // 2
    key_row = lax.broadcasted_iota(jnp.int32, (rows, rows), 0)
    acc_ref[...] = jnp.zeros_like(acc_ref)
    along = (g.astype(jnp.float32) * full).T
    delta = [jnp.sum(along[a * half : (a + 1) * half], axis=0, keepdims=True) for a in range(2)]
    keys, spans = key_value

    def step(i, carry):
        kc = i * SPAN
        here = pl.ds(kc * rows, SPAN * rows)
        k, v = keys(here)
        dk = dv = None
        for a in range(2):
            s = nt_dot(k, q_half[a])
            dp = nt_dot(v, g_half[a])
            es, dss = [], []
            for u in range(SPAN):
                part = slice(u * rows, (u + 1) * rows)
                slot = jnp.clip(kc + u - first + 2, 0, 4)
                valid = key_row < length - (kc + u) * rows
                e = jnp.exp(s[part] + bias_ref[a, slot] - peak[a])
                e_low = jnp.where(valid, e, 0.0).astype(jnp.bfloat16)
                ds = e_low.astype(jnp.float32) * (dp[part] - delta[a])
                sum_ref[a, slot] += ds
                es.append(e_low)
                dss.append(ds.astype(jnp.bfloat16))
            e_low, ds_low = jnp.concatenate(es, axis=0), jnp.concatenate(dss, axis=0)
            dv_a = nn_dot(e_low, g_half[a])
            dk_a = nn_dot(ds_low, q_half[a])
            dv = dv_a if dv is None else dv + dv_a
            dk = dk_a if dk is None else dk + dk_a
            acc_ref[a] += tn_dot(k, ds_low)
        write(here, dk.astype(jnp.bfloat16), dv.astype(jnp.bfloat16))
        return carry

    if spans == 1:
        step(0, 0)
    else:
        lax.fori_loop(0, spans, step, 0)
    return jnp.concatenate([acc_ref[0, :half], acc_ref[1, half:]], axis=0).T.astype(jnp.bfloat16)


def near_sums(rows, sum_ref, write):
    for a in range(2):
        for slot in range(5):
            total_sum = jnp.zeros((8, 2 * rows), jnp.float32)
            for g in range(rows // 8):
                part = jnp.concatenate(
                    [sum_ref[a, slot, 8 * g : 8 * g + 8, :], jnp.zeros((8, rows), jnp.float32)], axis=1
                )
                if g and 0 < slot < 4:
                    part = pltpu.roll(part, 2 * rows - 8 * g, 1)
                total_sum = total_sum + part
            write(a, slot, total_sum)


def attend_back_kernel(rows, info_ref, far_ref, diag_ref, q_ref, g_ref, full_ref, k_ref, v_ref, peak_ref,
                       dq_ref, dkv_ref, near_ref, bias_ref, sum_ref, acc_ref):
    pair, b = pl.program_id(0), pl.program_id(1)

    @pl.when(b == 0)
    def _():
        fill_bias(rows, far_ref, diag_ref, bias_ref, pair)
        sum_ref[...] = jnp.zeros_like(sum_ref)

    wide = q_ref.shape[1]

    def write(here, dk, dv):
        dkv_ref[0, here, :wide] = dk
        dkv_ref[0, here, wide:] = dv

    dq_ref[...] = back_pair(
        rows,
        info_ref[b],
        info_ref[info_ref.shape[0] - 1],
        q_ref[...],
        g_ref[...],
        full_ref[...],
        (lambda here: (k_ref[0, here, :], v_ref[0, here, :]), k_ref.shape[1] // (SPAN * rows)),
        [peak_ref[0, 0, a : a + 1, :] for a in range(2)],
        bias_ref,
        sum_ref,
        acc_ref,
        write,
    )

    @pl.when(b == pl.num_programs(1) - 1)
    def _():
        def keep(a, slot, value):
            near_ref[0, a, slot] = value

        near_sums(rows, sum_ref, keep)


def attend_back(info, far, diag, q, g, full, kv, peak, rows, length, seqs):
    heads = far.shape[0]
    wide = 2 * (q.shape[1] // heads)
    pairs = heads // 2
    smem = pl.BlockSpec(memory_space=pltpu.SMEM)
    row_spec = pl.BlockSpec((rows, wide), lambda p, b: (b, p))
    return pl.pallas_call(
        functools.partial(attend_back_kernel, rows),
        grid=(pairs, seqs),
        in_specs=[
            smem,
            smem,
            pl.BlockSpec((1, 6, 2 * rows), lambda p, b: (p, 0, 0)),
            row_spec,
            row_spec,
            row_spec,
            pl.BlockSpec((1, length, wide), lambda p, b: (b, 0, 2 * p)),
            pl.BlockSpec((1, length, wide), lambda p, b: (b, 0, 2 * p + 1)),
            pl.BlockSpec((1, 1, 2, rows), lambda p, b: (b, p, 0, 0)),
        ],
        out_specs=[
            row_spec,
            pl.BlockSpec((1, length, 2 * wide), lambda p, b: (b, 0, p)),
            pl.BlockSpec((1, 2, 5, 8, 2 * rows), lambda p, b: (p, 0, 0, 0, 0)),
        ],
        out_shape=[
            jax.ShapeDtypeStruct((seqs * rows, q.shape[1]), jnp.bfloat16),
            jax.ShapeDtypeStruct((seqs,) + kv.shape[1:], jnp.bfloat16),
            jax.ShapeDtypeStruct((pairs, 2, 5, 8, 2 * rows), jnp.float32),
        ],
        scratch_shapes=[
            pltpu.VMEM((2, 5, rows, rows), jnp.float32),
            pltpu.VMEM((2, 5, rows, rows), jnp.float32),
            pltpu.VMEM((2, wide, rows), jnp.float32),
        ],
        compiler_params=pltpu.CompilerParams(vmem_limit_bytes=48 << 20),
        cost_estimate=attention_cost(q, kv, 3),
        name="attend_back",
    )(info, far, diag, q, g, full, kv, kv, peak)


SLOTS = ("x", "c", "z", "y")
MESH = pl.DeviceIdType.MESH


def layout_of(batch, seq):
    fast = 1 << ((seq.bit_length() - 1) // 2)
    return {"x": batch // 2, "c": 2, "z": seq // fast, "y": fast}


def tile_block(rows, cols):
    return (rows, cols) if rows % 16 == 0 else (rows * cols // 128, 128)


def place(sizes):
    b, s = lax.axis_index("batch"), lax.axis_index("seq")
    return {
        "x": lax.div(b, 2),
        "c": lax.rem(b, 2),
        "z": lax.div(s, sizes["y"]),
        "y": lax.rem(s, sizes["y"]),
    }


def device_at(sizes, me, dim, at):
    spot = dict(me)
    spot[dim] = at
    return (spot["x"] * 2 + spot["c"], spot["z"] * sizes["y"] + spot["y"])


def seq_peer(sizes, me, k):
    n = sizes["z"] * sizes["y"]
    return (me["x"] * 2 + me["c"], lax.rem(me["z"] * sizes["y"] + me["y"] + k, n))


def greet(sizes, me, dims):
    barrier = pltpu.get_barrier_semaphore()
    total = 0
    if "s" in dims:
        total = sizes["z"] * sizes["y"] - 1
        for k in range(1, total + 1):
            pl.semaphore_signal(barrier, inc=1, device_id=seq_peer(sizes, me, k), device_id_type=MESH)
        dims = [d for d in dims if d not in "szy"]
    for dim in dims:
        for k in range(1, sizes[dim]):
            peer = device_at(sizes, me, dim, lax.rem(me[dim] + k, sizes[dim]))
            pl.semaphore_signal(barrier, inc=1, device_id=peer, device_id_type=MESH)
            total += 1
    pl.semaphore_wait(barrier, total)


class Sems:
    def __init__(self, send, recv):
        self.send, self.recv, self.used = send, recv, 0

    def take(self, count):
        first = self.used
        self.used += count
        assert self.used <= self.send.shape[0]
        return first

    def copy(self, src, dst, index, device):
        return pltpu.make_async_remote_copy(
            src_ref=src, dst_ref=dst, send_sem=self.send.at[index], recv_sem=self.recv.at[index],
            device_id=device, device_id_type=MESH,
        )


def run_together(tasks, plan=()):
    tasks = list(tasks)
    over_already = set()
    for i in plan:
        if i not in over_already:
            try:
                next(tasks[i])
            except StopIteration:
                over_already.add(i)
    tasks = [t for i, t in enumerate(tasks) if i not in over_already]
    while tasks:
        left = []
        for task in tasks:
            try:
                next(task)
                left.append(task)
            except StopIteration:
                pass
        tasks = left


def gather_task(sizes, me, src, out, local_sem, sems, order):
    before = [] if isinstance(src, list) else list(SLOTS[len(SLOTS) - (len(src.shape) - 2) :])
    dims = [d for d in SLOTS if d in order.lower() or d in before]
    mine = out.at[tuple(me[d] for d in dims if d not in before)]
    if isinstance(src, list):
        first = 0
        owns = []
        for i, (ref, lo, hi) in enumerate(src):
            owns.append(
                pltpu.make_async_copy(ref.at[:, lo:hi], mine.at[:, first : first + hi - lo], local_sem.at[i])
            )
            first += hi - lo
    else:
        owns = [pltpu.make_async_copy(src, mine, local_sem.at[0])]
    for own in owns:
        own.start()
    for own in owns:
        own.wait()
    done = before
    sent = []
    for dim in order:
        direct, dim = dim.isupper(), dim.lower()
        n, at = sizes[dim], me[dim]

        def region(origin):
            spots = []
            for d in dims:
                spots.append(slice(None) if d in done else (origin if d == dim else me[d]))
            return out.at[tuple(spots)]

        if n == 2:
            base = sems.take(1)
            other = 1 - at
            send = sems.copy(region(at), region(at), base, device_at(sizes, me, dim, other))
            send.start()
            yield
            sems.copy(region(other), region(other), base, device_at(sizes, me, dim, other)).wait_recv()
            sent.append((None, send))
        elif direct:
            base = sems.take(n - 1)
            for k in range(1, n):
                peer = device_at(sizes, me, dim, lax.rem(at + k, n))
                send = sems.copy(region(at), region(at), base + k - 1, peer)
                send.start()
                sent.append((None, send))
            yield
            for k in range(1, n):
                origin = lax.rem(at + n - k, n)
                sems.copy(region(origin), region(origin), base + k - 1, device_at(sizes, me, dim, origin)).wait_recv()
        else:
            for t in range(n - 1):
                base = sems.take(2)
                to_right = (at + 1 < n) & (at - t >= 0)
                to_left = (at >= 1) & (at + t < n)
                from_left = (at >= 1) & (at - 1 - t >= 0)
                from_right = (at + 1 < n) & (at + 1 + t < n)
                right = sems.copy(region(at - t), region(at - t), base, device_at(sizes, me, dim, at + 1))
                left = sems.copy(region(at + t), region(at + t), base + 1, device_at(sizes, me, dim, at - 1))
                pl.when(to_right)(right.start)
                pl.when(to_left)(left.start)
                sent += [(to_right, right), (to_left, left)]
                yield
                got = sems.copy(region(at - 1 - t), region(at - 1 - t), base, device_at(sizes, me, dim, at - 1))
                pl.when(from_left)(got.wait_recv)
                got = sems.copy(region(at + 1 + t), region(at + 1 + t), base + 1, device_at(sizes, me, dim, at + 1))
                pl.when(from_right)(got.wait_recv)
        done.append(dim)
    for cond, send in sent:
        if cond is None:
            send.wait_send()
        else:
            pl.when(cond)(send.wait_send)


def spread_task(sizes, me, src, out, sems):
    z, y, n, fast = me["z"], me["y"], sizes["z"], sizes["y"]
    fan = sems.take((fast - 1) * n)
    base = sems.take(2 * (n - 1))

    def fan_copy(k, origin, owner, to):
        spot = out.at[origin, owner]
        return sems.copy(spot, spot, fan + (k - 1) * n + origin, device_at(sizes, me, "y", to))

    def fan_out(origin):
        for k in range(1, fast):
            fan_copy(k, origin, y, lax.rem(y + k, fast)).start()

    def along(origin, index, to):
        spot = out.at[origin, y]
        return sems.copy(spot, spot, base + index, device_at(sizes, me, "z", to))

    moves = []
    for t in range(n - 1):
        moves.append(
            (
                (along(z - t, 2 * t, z + 1), (z + 1 < n) & (z - t >= 0)),
                (along(z + t, 2 * t + 1, z - 1), (z >= 1) & (z + t < n)),
                (along(z - 1 - t, 2 * t, z - 1), (z >= 1) & (z - 1 - t >= 0), z - 1 - t),
                (along(z + 1 + t, 2 * t + 1, z + 1), (z + 1 < n) & (z + 1 + t < n), z + 1 + t),
            )
        )
    fans = [fan_copy(k, origin, y, lax.rem(y + k, fast)) for k in range(1, fast) for origin in range(n)]

    def begin(t):
        for send, cond in moves[t][:2]:
            pl.when(cond)(send.start)

    def chains():
        out[z, y] = src[...]
        begin(0)
        fan_out(z)
        yield
        for t in range(n - 1):
            for got, cond, origin in moves[t][2:]:
                pl.when(cond)(got.wait_recv)
            if t + 1 < n - 1:
                begin(t + 1)
            for got, cond, origin in moves[t][2:]:
                pl.when(cond)(partial(fan_out, origin))
            yield
        for send in fans:
            send.wait_send()
        for move in moves:
            for send, cond in move[:2]:
                pl.when(cond)(send.wait_send)

    def across_y(use):
        def step(i, carry):
            far = lax.div(i + 1, 2)
            origin = jnp.where(lax.rem(i, 2) == 1, z - far, z + far)

            @pl.when((origin >= 0) & (origin < n))
            def _():
                for k in range(1, fast):
                    owner = lax.rem(y + fast - k, fast)
                    fan_copy(k, origin, owner, owner).wait_recv()
                    use(origin, owner)

            return carry

        lax.fori_loop(0, 2 * n - 1, step, 0)

    return chains(), across_y


def shift_task(sizes, me, src, out, sems, step):
    n = sizes["z"] * sizes["y"]
    s = me["z"] * sizes["y"] + me["y"]
    base = sems.take(1)
    send = sems.copy(src, out, base, seq_peer(sizes, me, step % n))
    has_to = (s < n - 1) if step > 0 else (s > 0)
    has_from = (s > 0) if step > 0 else (s < n - 1)
    pl.when(has_to)(send.start)
    yield
    pl.when(has_from)(send.wait_recv)

    @pl.when(jnp.logical_not(has_from))
    def _():
        out[...] = jnp.zeros_like(out)

    yield
    pl.when(has_to)(send.wait_send)


def stage_count(sizes, order):
    return sum(1 if sizes[d] == 2 else 2 * (sizes[d] - 1) for d in order.lower())


def gather_kernel(sizes, orders, cuts, has_rim, *refs):
    count = len(orders)
    arrays = sum(1 if cut is None else len(cut) for cut in cuts)
    ins, outs = list(refs[: arrays + has_rim]), refs[arrays + has_rim : arrays + has_rim + count + has_rim]
    local_sem, send_sem, recv_sem = refs[arrays + count + 2 * has_rim :]
    me = place(sizes)
    used = [d for d in SLOTS if any(d in o.lower() for o in orders)]
    greet(sizes, me, used + ["s"] * has_rim)
    sems = Sems(send_sem, recv_sem)
    tasks = []
    for i in range(count):
        src = ins.pop(0) if cuts[i] is None else [(ins.pop(0), lo, hi) for lo, hi in cuts[i]]
        tasks.append(gather_task(sizes, me, src, outs[i], local_sem.at[i], sems, orders[i]))
    if has_rim:
        edge = ins[0].at[:, ins[0].shape[1] - outs[-1].shape[1] :, :]
        tasks.append(shift_task(sizes, me, edge, outs[-1], sems, 1))
    run_together(tasks)


def gather_shapes(shards, orders, sizes):
    ins, shapes = [], []
    cuts = []
    for shard, order in zip(shards, orders):
        if isinstance(shard, list) and shard[0][0].shape[0] % 16 == 0:
            whole = tuple(sizes[d] for d in SLOTS if d in order.lower())
            block = (shard[0][0].shape[0], sum(hi - lo for _, lo, hi in shard))
            shapes.append(jax.ShapeDtypeStruct(whole + block, shard[0][0].dtype))
            ins += [piece for piece, _, _ in shard]
            cuts.append([(lo, hi) for _, lo, hi in shard])
            continue
        if isinstance(shard, list):
            shard = jnp.concatenate([piece[:, lo:hi] for piece, lo, hi in shard], axis=1)
        ins.append(shard if shard.ndim > 2 else shard.reshape(tile_block(*shard.shape)))
        before = SLOTS[len(SLOTS) - (ins[-1].ndim - 2) :]
        whole = tuple(sizes[d] for d in SLOTS if d in order.lower() or d in before)
        shapes.append(jax.ShapeDtypeStruct(whole + ins[-1].shape[-2:], shard.dtype))
        cuts.append(None)
    return ins, shapes, sum(stage_count(sizes, o) for o in orders), cuts


def gather_all(shards, orders, sizes, collective_id, rim=None, name="gather"):
    ins, shapes, total, cuts = gather_shapes(shards, orders, sizes)
    out_specs = [pl.BlockSpec(memory_space=pl.ANY)] * len(shapes)
    in_specs = [pl.BlockSpec(memory_space=pltpu.VMEM)] * len(ins)
    if rim is not None:
        ins.append(rim)
        in_specs.append(pl.BlockSpec(memory_space=pl.ANY))
        shapes.append(jax.ShapeDtypeStruct((rim.shape[0], 16, rim.shape[2]), rim.dtype))
        out_specs.append(pl.BlockSpec(memory_space=pltpu.VMEM))
        total += 1
    return pl.pallas_call(
        functools.partial(gather_kernel, sizes, orders, cuts, int(rim is not None)),
        in_specs=in_specs,
        out_specs=out_specs,
        out_shape=shapes,
        scratch_shapes=[
            pltpu.SemaphoreType.DMA((len(orders), len(ins))),
            pltpu.SemaphoreType.DMA((total,)),
            pltpu.SemaphoreType.DMA((total,)),
        ],
        compiler_params=pltpu.CompilerParams(collective_id=collective_id, has_side_effects=True),
        name=name,
    )(*ins)


def gather_rows_kernel(sizes, rows, orders, *refs):
    count = len(orders)
    info_ref, far_ref, diag_ref, rows_ref, q_ref, second_ref = refs[:6]
    planes, refs = refs[6 : 6 + count], refs[6 + count :]
    gathered, refs = refs[:count], refs[count:]
    normed_out, kv_out, o_ref, full_ref, inv_ref, peak_ref = refs[:6]
    rows_buf, kv_buf, bias_ref, s_ref, acc_ref, local_sem, out_sem, send_sem, recv_sem = refs[6:]
    me = place(sizes)
    greet(sizes, me, SLOTS)
    sems = Sems(send_sem, recv_sem)
    first = me["z"] * sizes["y"] + me["y"]
    seqs, n = rows_ref.shape[0], sizes["z"]
    length = kv_buf.shape[1]
    pairs = diag_ref.shape[0]
    wide = q_ref.shape[1] // pairs
    weights = []
    for i in range(count):
        weights.append(gather_task(sizes, me, planes[i], gathered[i], local_sem.at[i], sems, orders[i]))
        next(weights[-1])
    pieces = [spread_task(sizes, me, rows_ref.at[p], rows_buf.at[p], sems) for p in range(seqs)]
    begun, rest = pieces[0][0], [p[0] for p in pieces[1:]]
    for _ in range(n):
        next(begun)
    for task in rest:
        next(task)

    def project(p):
        def block(z, y):
            at = pl.ds(pl.multiple_of((z * sizes["y"] + y) * rows, rows), rows)
            kv_buf[p, at, :] = nn_dot(rows_buf[p, z, y], second_ref[...]).astype(jnp.bfloat16)

        def column(z, carry):
            block(z, me["y"])
            return carry

        lax.fori_loop(0, n, column, 0)
        pieces[p][1](block)
        copies = [
            pltpu.make_async_copy(rows_buf.at[p], normed_out.at[p], out_sem.at[p, 0]),
            pltpu.make_async_copy(kv_buf.at[p], kv_out.at[p], out_sem.at[p, 1]),
        ]
        for copy in copies:
            copy.start()
        return copies

    copies = project(0)
    size = info_ref[0]

    def one_pair(p, carry):
        fill_bias(rows, far_ref, diag_ref.at[pl.ds(p, 1)], bias_ref, p)
        lanes = pl.ds(pl.multiple_of(p * wide, wide), wide)
        k_lanes = pl.ds(pl.multiple_of(2 * p * wide, wide), wide)
        v_lanes = pl.ds(pl.multiple_of((2 * p + 1) * wide, wide), wide)
        out, inv, tops = attend_pair(
            rows,
            size,
            first,
            q_ref[:rows, lanes],
            lambda here: kv_buf[0, here, k_lanes],
            lambda here: kv_buf[0, here, v_lanes],
            length // (SPAN * rows),
            bias_ref,
            s_ref,
            acc_ref,
        )
        o_ref[:, lanes] = out.astype(o_ref.dtype)
        full_ref[:, lanes] = out
        inv_ref[:, lanes] = inv
        for a in range(2):
            peak_ref[0, p, a : a + 1, :] = tops[a]
        for i in range(min(pairs, n - 1)):

            @pl.when(p == i)
            def _():
                for task in rest:
                    next(task)

        return carry

    lax.fori_loop(0, pairs, one_pair, 0)
    for _ in range(n - 1 - min(pairs, n - 1)):
        for task in rest:
            next(task)
    for task in weights:
        next(task, None)
    for p in range(1, seqs):
        copies += project(p)
    run_together(weights + [begun] + rest)
    for copy in copies:
        copy.wait()


def gather_rows(info, far, diag, normed, queries, second, planes, orders, sizes, collective_id):
    seqs, rows, width = normed.shape
    n, fast = sizes["z"], sizes["y"]
    length = rows * n * fast
    pairs = far.shape[0] // 2
    ins, shapes, total, _ = gather_shapes(planes, orders, sizes)
    total += seqs * ((fast - 1) * n + 2 * (n - 1))
    bf16, f32 = jnp.bfloat16, jnp.float32
    smem, vmem = pl.BlockSpec(memory_space=pltpu.SMEM), pl.BlockSpec(memory_space=pltpu.VMEM)
    anywhere = pl.BlockSpec(memory_space=pl.ANY)
    count = len(ins)
    outs = pl.pallas_call(
        functools.partial(gather_rows_kernel, sizes, rows, orders),
        in_specs=[smem, smem] + [vmem] * (4 + count),
        out_specs=[anywhere] * (count + 2) + [vmem] * 4,
        out_shape=shapes
        + [
            jax.ShapeDtypeStruct((seqs, n, fast, rows, width), bf16),
            jax.ShapeDtypeStruct((seqs, length, 2 * width), bf16),
        ]
        + attention_shapes(1, rows, width, pairs),
        scratch_shapes=[
            pltpu.VMEM((seqs, n, fast, rows, width), bf16),
            pltpu.VMEM((seqs, length, 2 * width), bf16),
            pltpu.VMEM((2, 5, rows, rows), f32),
            pltpu.VMEM((2, length, rows), f32),
            pltpu.VMEM((2, width // pairs, rows), f32),
            pltpu.SemaphoreType.DMA((count, 1)),
            pltpu.SemaphoreType.DMA((seqs, 2)),
            pltpu.SemaphoreType.DMA((total,)),
            pltpu.SemaphoreType.DMA((total,)),
        ],
        compiler_params=pltpu.CompilerParams(
            collective_id=collective_id, has_side_effects=True, vmem_limit_bytes=60 << 20
        ),
        name="gather_rows",
    )(info, far, diag, normed, queries, second, *ins)
    return outs[:count], outs[count], outs[count + 1], outs[count + 2 :]


def over(extents, body):
    total = 1
    for e in extents:
        total *= e
    if total == 1:
        body((0,) * len(extents))
        return

    def step(i, carry):
        spots = []
        for e in reversed(extents):
            spots.append(lax.rem(i, e))
            i = lax.div(i, e)
        body(tuple(reversed(spots)))
        return carry

    lax.fori_loop(0, total, step, 0)


def add_into(dst, src_of, extents):
    def body(spots):
        here = spots + (slice(None), slice(None))
        dst[here] = (dst[here].astype(jnp.float32) + src_of(spots).astype(jnp.float32)).astype(dst.dtype)

    over(extents, body)


def add_pair(out, first, second_of, extents):
    def body(spots):
        here = spots + (slice(None), slice(None))
        out[here] = (first[here].astype(jnp.float32) + second_of(spots).astype(jnp.float32)).astype(out.dtype)

    over(extents, body)


def reduce_task(sizes, me, src, out, bufs, sems, order, dims):
    remaining = list(dims)
    current = src
    stages = []
    for stage, dim in enumerate(order):
        last = stage == len(order) - 1
        if dim == "s":
            n, s = sizes["z"] * sizes["y"], me["z"] * sizes["y"] + me["y"]
            base = sems.take(n)
            sends, recvs = [], []
            for k in range(1, n):
                to = lax.rem(s + k, n)
                spot = current.at[lax.div(to, sizes["y"]), lax.rem(to, sizes["y"])]
                sends.append(sems.copy(spot, bufs[stage].at[k], base + k, seq_peer(sizes, me, k)))
                recvs.append(sems.copy(bufs[stage].at[k], bufs[stage].at[k], base + k, seq_peer(sizes, me, k)))
            stages.append((dim, n, current, bufs[stage], sends, recvs, None, None, None))
            continue
        direct, dim = dim.isupper(), dim.lower()
        n, at = sizes[dim], me[dim]
        spot = remaining.index(dim)
        remaining.remove(dim)
        extents = [sizes[d] for d in remaining]

        def block(j, source=current, spot=spot):
            return source.at[(slice(None),) * spot + (j,)]

        def values(j, source=current, spot=spot):
            return lambda spots: source[spots[:spot] + (j,) + spots[spot:] + (slice(None), slice(None))]

        if direct:
            base = sems.take(n)
            moves = []
            for k in range(1, n):
                to, origin = lax.rem(at + k, n), lax.rem(at + n - k, n)
                buf = bufs[stage].at[k]
                send = sems.copy(block(to), buf, base + k, device_at(sizes, me, dim, to))
                moves.append((send, sems.copy(buf, buf, base + k, device_at(sizes, me, dim, origin))))
            result = out if last else bufs[stage].at[0]
            stages.append(("direct", n, result, bufs[stage], moves, at, values, extents, last))
            current = result
        elif n == 2:
            send = sems.copy(block(1 - at), bufs[stage], sems.take(1), device_at(sizes, me, dim, 1 - at))
            stages.append((dim, n, None, bufs[stage], [send], at, values, extents, last))
            current = bufs[stage]
        else:
            chains = bufs[stage][0]
            result = out if last else bufs[stage][1]
            base = sems.take(2 * n)
            moves = []
            for slot in range(n - 1):
                for side in range(2):
                    lead = at if side == 0 else n - 1 - at
                    j = lax.rem((n - 1 - slot + at) if side == 0 else (slot + 1 + at + n), n)
                    buf = chains.at[side, j]
                    to = device_at(sizes, me, dim, at + 1 if side == 0 else at - 1)
                    index = base + side * n + j
                    plain, summed = sems.copy(block(j), buf, index, to), sems.copy(buf, buf, index, to)
                    moves.append((plain, summed, buf, j, lead == 0, (lead > 0) & (lead <= slot), lead <= slot))
            ends = []
            for side in range(2):
                buf = chains.at[side, at]
                ends.append(sems.copy(buf, buf, base + side * n + at, device_at(sizes, me, dim, at)))
            conds = (at > 0, at < n - 1)
            stages.append((dim, n, result, chains, moves, at, values, extents, (ends, conds)))
            current = result

    for dim, n, source, buf, moves, at, values, extents, last in stages:
        if dim == "s":
            for send in moves:
                send.start()
            yield
            total = source[me["z"], me["y"]].astype(jnp.float32)
            for k in range(1, n):
                at[k - 1].wait_recv()
                total = total + buf[k].astype(jnp.float32)
            out[...] = total
        elif dim == "direct":
            for send, _ in moves:
                send.start()
            yield
            for _, got in moves:
                got.wait_recv()

            def add_all(spots):
                here = spots + (slice(None), slice(None))
                total = values(at)(spots).astype(jnp.float32)
                for k in range(1, n):
                    total = total + buf[(k,) + here].astype(jnp.float32)
                source[here] = total.astype(source.dtype)

            over(extents, add_all)
        elif n == 2:
            moves[0].start()
            yield
            moves[0].wait_recv()
            if last:
                add_pair(out, buf, values(at), extents)
            else:
                add_into(buf, values(at), extents)
        else:
            for slot in range(n - 1):
                for plain, summed, target, j, is_first, is_later, _ in moves[2 * slot : 2 * slot + 2]:

                    def pass_on(summed=summed, target=target, j=j):
                        summed.wait_recv()
                        add_into(target, values(j), extents)
                        summed.start()

                    pl.when(is_first)(plain.start)
                    pl.when(is_later)(pass_on)
                yield

            def start(spots):
                here = spots + (slice(None), slice(None))
                source[here] = values(at)(spots).astype(source.dtype)

            over(extents, start)
            ends, conds = last
            for side in range(2):

                def finish(side=side):
                    ends[side].wait_recv()
                    add_into(source, lambda spots: buf[(side, at) + spots + (slice(None), slice(None))], extents)

                pl.when(conds[side])(finish)
    for dim, n, _, _, moves, _, _, _, _ in stages:
        for move in moves:
            if dim == "direct":
                move[0].wait_send()
            elif dim == "s" or n == 2:
                move.wait_send()
            else:
                pl.when(move[-1])(move[1].wait_send)


class Split:
    def __init__(self, parts):
        self.parts = parts
        self.dtype = parts[0].dtype

    def __setitem__(self, here, value):
        first = 0
        for part in self.parts:
            last = first + part.shape[-1]
            part[here] = value[:, first:last]
            first = last

    def __getitem__(self, here):
        return jnp.concatenate([part[here] for part in self.parts], axis=1)


def stage_buffers(sizes, block, dtype, dims, order):
    scratch, counts, left, total = [], [], list(dims), 0
    for dim in order:
        counts.append(1)
        if dim == "s":
            left = []
            n = sizes["z"] * sizes["y"]
            scratch.append(pltpu.VMEM((n,) + block, dtype))
            total += n
            continue
        left.remove(dim.lower())
        shape = tuple(sizes[d] for d in left) + block
        n = sizes[dim.lower()]
        if dim.isupper():
            scratch.append(pltpu.VMEM((n,) + shape, dtype))
            total += n
        elif n == 2:
            scratch.append(pltpu.VMEM(shape, dtype))
            total += 1
        else:
            scratch.append(pltpu.VMEM((2, n) + shape, dtype))
            total += 2 * n
            if dim != order[-1]:
                scratch.append(pltpu.VMEM(shape, dtype))
                counts[-1] = 2
    return scratch, counts, total, left


def stage_refs(sizes, order, counts, bufs):
    stages = []
    for dim, size in zip(order, counts):
        taken = [bufs.pop(0) for _ in range(size)]
        stages.append(taken[0] if dim == "s" or dim.isupper() or sizes[dim] == 2 else taken)
    return stages


def reduce_kernel(sizes, orders, dims, counts, splits, spill, *refs):
    count = len(orders)
    total = count + spill
    ends = sum(splits) + spill
    ins, outs = refs[:total], list(refs[total : total + ends])
    send_sem, recv_sem = refs[-2:]
    bufs = list(refs[total + ends : -2])
    me = place(sizes)
    used = [d for d in SLOTS if any(d in o.lower() for o in orders)]
    greet(sizes, me, used + ["s"] * (spill or any("s" in o for o in orders)))
    sems = Sems(send_sem, recv_sem)
    tasks = []
    for i in range(count):
        stages = stage_refs(sizes, orders[i], counts[i], bufs)
        parts = [outs.pop(0) for _ in range(splits[i])]
        out = parts[0] if len(parts) == 1 else Split(parts)
        tasks.append(reduce_task(sizes, me, ins[i], out, stages, sems, orders[i], dims[i]))
    if spill:
        tasks.insert(0, shift_task(sizes, me, ins[-1], outs.pop(0), sems, -1))
    run_together(tasks)


def cut_shapes(block, left, widths, sizes, dtype):
    if left or widths is None or sum(widths) != block[1]:
        shape = tuple(sizes[d] for d in left) + block
        return [jax.ShapeDtypeStruct(shape, dtype if left else jnp.float32)], widths
    return [jax.ShapeDtypeStruct((block[0], w), jnp.float32) for w in widths], None


def cut_columns(parts, widths):
    if widths is None:
        return parts
    full = parts[0].reshape(-1, sum(widths))
    edges = np.cumsum([0] + list(widths))
    return [full[:, int(lo) : int(hi)] for lo, hi in zip(edges[:-1], edges[1:])]


def reduce_all(grads, orders, sizes, collective_id, spill=None, splits=None, name="reduce"):
    ins, scratch, shapes, counts, all_dims, cuts, later = [], [], [], [], [], [], []
    splits = splits or [None] * len(grads)
    total = 0
    devices = sizes["x"] * sizes["c"] * sizes["z"] * sizes["y"]
    for grad, order, widths in zip(grads, orders, splits):
        dims = SLOTS[-(grad.ndim - 2) :] if grad.ndim > 2 else SLOTS
        if grad.ndim == 2:
            whole = tuple(sizes[d] for d in SLOTS)
            grad = grad.reshape(whole + tile_block(grad.shape[0] // devices, grad.shape[1]))
        block = grad.shape[-2:]
        ins.append(grad)
        all_dims.append(dims)
        more, taken, needed, left = stage_buffers(sizes, block, grad.dtype, dims, order)
        scratch += more
        total += needed
        counts.append(taken)
        ends, widths = cut_shapes(block, left, widths, sizes, grad.dtype)
        shapes += ends
        cuts.append(len(ends))
        later.append(widths)
    if spill is not None:
        ins.append(spill)
        shapes.append(jax.ShapeDtypeStruct(spill.shape, spill.dtype))
        total += 1
    outs = pl.pallas_call(
        functools.partial(reduce_kernel, sizes, orders, all_dims, counts, cuts, int(spill is not None)),
        in_specs=[pl.BlockSpec(memory_space=pltpu.VMEM)] * len(ins),
        out_specs=[pl.BlockSpec(memory_space=pltpu.VMEM)] * len(shapes),
        out_shape=shapes,
        scratch_shapes=scratch + [pltpu.SemaphoreType.DMA((total,)), pltpu.SemaphoreType.DMA((total,))],
        compiler_params=pltpu.CompilerParams(
            collective_id=collective_id, has_side_effects=True, vmem_limit_bytes=56 << 20
        ),
        name=name,
    )(*ins)
    outs = list(outs)
    results = []
    for cut, widths in zip(cuts, later):
        results.append(cut_columns([outs.pop(0) for _ in range(cut)], widths))
    return results + outs


def collect_task(sizes, me, src, out, ybuf, chain, sems, produce):
    z, y, n, fast = me["z"], me["y"], sizes["z"], sizes["y"]
    fan = sems.take((fast - 1) * n)
    base = sems.take(2 * n)

    def fan_copy(k, j):
        to = lax.rem(y + k, fast)
        index = fan + (k - 1) * n + j
        return sems.copy(src.at[j, to], ybuf.at[k - 1, j], index, device_at(sizes, me, "y", to))

    def spread(i, carry):
        far = n - 1 - lax.div(i, 2)
        j = jnp.where(lax.rem(i, 2) == 0, z + far, z - far)

        @pl.when((j >= 0) & (j < n))
        def _():
            produce(j)
            for k in range(1, fast):
                fan_copy(k, j).start()

        return carry

    def chain_copy(side, j, to, plain=False):
        buf = chain.at[side, j]
        return sems.copy(ybuf.at[0, j] if plain else buf, buf, base + side * n + j, device_at(sizes, me, "z", to))

    slots = []
    for slot in range(n - 1):
        for side in range(2):
            lead = z if side == 0 else n - 1 - z
            j = lax.rem((n - 1 - slot + z) if side == 0 else (slot + 1 + z + n), n)
            to = z + 1 if side == 0 else z - 1
            ends = (chain_copy(side, j, to, True), chain_copy(side, j, to))
            slots.append((side, j, ends, lead == 0, (lead > 0) & (lead <= slot), lead <= slot))
    fans = [fan_copy(k, j) for j in range(n) for k in range(1, fast)]
    lax.fori_loop(0, 2 * n - 1, spread, 0)
    yield

    def merge(j):
        for k in range(1, fast):
            fan_copy(k, j).wait_recv()
        value = src[j, y].astype(jnp.float32)
        for k in range(1, fast):
            value = value + ybuf[k - 1, j].astype(jnp.float32)
        return value

    for slot in range(n - 1):
        for side, j, (plain, summed), is_first, is_later, _ in slots[2 * slot : 2 * slot + 2]:

            def begin(plain=plain, j=j):
                ybuf[0, j] = merge(j).astype(ybuf.dtype)
                plain.start()

            def pass_on(summed=summed, side=side, j=j):
                value = merge(j)
                summed.wait_recv()
                chain[side, j] = (chain[side, j].astype(jnp.float32) + value).astype(chain.dtype)
                summed.start()

            pl.when(is_first)(begin)
            pl.when(is_later)(pass_on)
        yield
    out[...] = merge(z)

    def finish(side):
        chain_copy(side, z, z).wait_recv()
        out[...] += chain[side, z].astype(jnp.float32)

    pl.when(z > 0)(partial(finish, 0))
    pl.when(z < n - 1)(partial(finish, 1))
    for fan_end in fans:
        fan_end.wait_send()
    for _, _, (_, summed), _, _, active in slots:
        pl.when(active)(summed.wait_send)


def halve_kernel(sizes, apart, *refs):
    n, count = sizes["x"], len(apart)
    refs = list(refs)
    ins = [refs.pop(0) for _ in range(count)]
    outs = [[refs.pop(0) for _ in range(n)] if alone else refs.pop(0) for alone in apart]
    bufs = [refs.pop(0) for _ in range(count)]
    send_sem, recv_sem = refs
    me = place(sizes)
    greet(sizes, me, ("c",))
    sems = Sems(send_sem, recv_sem)
    c = me["c"]
    peer = device_at(sizes, me, "c", 1 - c)
    sends = {}
    for k in range(n - 1, -1, -1):
        for i, alone in enumerate(apart):
            at = lax.rem(me["x"] + k, n) if alone else k
            sends[k, i] = sems.copy(ins[i].at[at, 1 - c], bufs[i].at[k], sems.take(1), peer)
            sends[k, i].start()
    for k in range(n - 1, -1, -1):
        for i, alone in enumerate(apart):
            at = lax.rem(me["x"] + k, n) if alone else k
            sends[k, i].wait_recv()
            src = ins[i]

            def own(spots, src=src, at=at):
                return src[(at, c) + spots + (slice(None), slice(None))]

            add_pair(outs[i][k] if alone else outs[i].at[k], bufs[i].at[k], own, src.shape[2:-2])
    for send in sends.values():
        send.wait_send()


def halve_cores(grads, apart, sizes, collective_id, name="halve"):
    n = sizes["x"]
    whole = tuple(sizes[d] for d in SLOTS)
    devices = whole[0] * whole[1] * whole[2] * whole[3]
    ins = [g.reshape(whole + tile_block(g.shape[0] // devices, g.shape[1])) for g in grads]
    halves = [g.shape[:1] + g.shape[2:] for g in ins]
    shapes = []
    for h, g, alone in zip(halves, ins, apart):
        shapes += [jax.ShapeDtypeStruct(h[1:], g.dtype)] * n if alone else [jax.ShapeDtypeStruct(h, g.dtype)]
    total = n * len(ins)
    outs = pl.pallas_call(
        functools.partial(halve_kernel, sizes, apart),
        in_specs=[pl.BlockSpec(memory_space=pltpu.VMEM)] * len(ins),
        out_specs=[pl.BlockSpec(memory_space=pltpu.VMEM)] * len(shapes),
        out_shape=shapes,
        scratch_shapes=[pltpu.VMEM(h, g.dtype) for h, g in zip(halves, ins)]
        + [pltpu.SemaphoreType.DMA((total,)), pltpu.SemaphoreType.DMA((total,))],
        compiler_params=pltpu.CompilerParams(
            collective_id=collective_id, has_side_effects=True, vmem_limit_bytes=56 << 20
        ),
        name=name,
    )(*ins)
    outs = list(outs)
    return [[outs.pop(0) for _ in range(n)] if alone else outs.pop(0) for alone in apart]


def feed_forward_kernel(sizes, *refs):
    n = sizes["x"]
    hidden_ref, cot_ref, outer_ref, down_ref, gain_ref = refs[:5]
    att_parts, inv_parts, refs = refs[5:7], refs[7:9], refs[9:]
    layer_ref, d_hidden_ref, d_out_ref, scaled_ref, d_gain_ref = refs[:5]
    wide_outs, down_out = refs[5 : 5 + n], refs[5 + n]
    d_wide, d_down, wide_buf, down_buf, two_ref, low_ref, d_normed, att_ref, send_sem, recv_sem = refs[6 + n :]
    cut = att_parts[0].shape[0]
    att_ref[:cut] = att_parts[0][...]
    att_ref[cut:] = att_parts[1][...]
    me = place(sizes)
    greet(sizes, me, ("c",))
    sems = Sems(send_sem, recv_sem)
    c = me["c"]
    peer = device_at(sizes, me, "c", 1 - c)
    width = hidden_ref.shape[1]
    parts = 2 * n
    units = down_ref.shape[0] // parts
    two_ref[...] = hidden_ref[...] + nn_dot(att_ref[...], outer_ref[:, :width])
    gain = gain_ref[...]

    def scale():
        return lax.rsqrt(jnp.mean(two_ref[...] * two_ref[...], axis=1, keepdims=True) + EPSILON)

    low_ref[...] = (two_ref[...] * scale() * gain).astype(jnp.bfloat16)
    d_normed[...] = jnp.zeros_like(d_normed)
    d_hidden_ref[...] = two_ref[...]

    def down_copy(x):
        return sems.copy(d_down.at[x, 1 - c], down_buf.at[x], x, peer)

    def part(i, carry):
        gate_at = pl.ds(pl.multiple_of(i * units, units), units)
        up_at = pl.ds(pl.multiple_of((parts + i) * units, units), units)
        gate_w = outer_ref[:, pl.ds(pl.multiple_of(width + i * units, units), units)]
        up_w = outer_ref[:, pl.ds(pl.multiple_of(width + (parts + i) * units, units), units)]
        down_w = down_ref[gate_at, :]
        low, cot = low_ref[...], cot_ref[...]
        gate, up = nn_dot(low, gate_w), nn_dot(low, up_w)
        square = gate * gate
        bend = jnp.tanh(0.7978845608 * gate * (1.0 + 0.044715 * square))
        half = 0.5 * (1.0 + bend)
        act = gate * half
        slope = half + gate * (0.5 * (1.0 - bend * bend)) * (0.7978845608 * (1.0 + 3.0 * 0.044715 * square))
        inner = (act * up).astype(jnp.bfloat16)
        d_hidden_ref[...] += nn_dot(inner, down_w)
        d_inner = nt_dot(cot, down_w)
        d_gate = (d_inner * up * slope).astype(jnp.bfloat16)
        d_up = (d_inner * act).astype(jnp.bfloat16)
        d_down[lax.div(i, 2), lax.rem(i, 2)] = (
            tn_dot(inner, cot).astype(jnp.bfloat16).reshape(d_down.shape[2:])
        )
        pl.when(lax.rem(i, 2) != c)(lambda: down_copy(lax.div(i, 2)).start())
        block = d_wide.shape[:-1] + (units,)
        d_wide[..., gate_at] = tn_dot(low, d_gate).astype(jnp.bfloat16).reshape(block)
        d_wide[..., up_at] = tn_dot(low, d_up).astype(jnp.bfloat16).reshape(block)
        d_normed[...] += nt_dot(d_gate, gate_w) + nt_dot(d_up, up_w)
        return carry

    lax.fori_loop(0, parts, part, 0)
    sends = [down_copy(x) for x in range(n)]
    for x in range(n):
        send = sems.copy(d_wide.at[x, 1 - c], wide_buf.at[x], n + x, peer)
        send.start()
        sends.append(send)
    layer_ref[...] = d_hidden_ref[...].astype(jnp.bfloat16)
    two, s2 = two_ref[...], scale()
    pulled = gain * d_normed[...]
    d_gain_ref[...] = jnp.sum(d_normed[...] * two * s2, axis=0, keepdims=True)
    drift = jnp.mean(two * pulled, axis=1, keepdims=True)
    d_two = cot_ref[...].astype(jnp.float32) + s2 * pulled - two * (s2 * s2 * s2 * drift)
    d_hidden_ref[...] = d_two
    d_low = d_two.astype(jnp.bfloat16)
    d_out_ref[...] = tn_dot(att_ref[...], d_low).astype(jnp.bfloat16)
    d_att = nt_dot(d_low, outer_ref[:, :width]).astype(jnp.bfloat16)
    scaled_ref[:cut] = (d_att[:cut].astype(jnp.float32) * inv_parts[0][...]).astype(jnp.bfloat16)
    scaled_ref[cut:] = (d_att[cut:].astype(jnp.float32) * inv_parts[1][...]).astype(jnp.bfloat16)
    for send in sends:
        send.wait_recv()
    for x in range(n):
        add_pair(down_out.at[x], down_buf.at[x], lambda at, x=x: d_down[(x, c) + at], d_down.shape[2:-2])
        at_x = lax.rem(me["x"] + x, n)
        add_pair(wide_outs[x], wide_buf.at[at_x], lambda at, at_x=at_x: d_wide[(at_x, c) + at], d_wide.shape[2:-2])
    for send in sends:
        send.wait_send()


def feed_forward(hidden_one, cotangent, outer_w, down_w, gain, attended, inverse, sizes, collective_id):
    n = sizes["x"]
    whole = tuple(sizes[d] for d in SLOTS)
    devices = whole[0] * whole[1] * whole[2] * whole[3]
    count, width = hidden_one.shape
    hidden = down_w.shape[0]
    bf16, f32 = jnp.bfloat16, jnp.float32
    wide_block = (width // devices, 2 * hidden)
    down_block = (hidden // devices, width)
    plane = whole[2:]
    vmem = pl.BlockSpec(memory_space=pltpu.VMEM)
    outs = pl.pallas_call(
        functools.partial(feed_forward_kernel, sizes),
        in_specs=[vmem] * 9,
        out_specs=[vmem] * (6 + n),
        out_shape=[
            jax.ShapeDtypeStruct((count, width), bf16),
            jax.ShapeDtypeStruct((count, width), f32),
            jax.ShapeDtypeStruct((width, width), bf16),
            jax.ShapeDtypeStruct((count, width), bf16),
            jax.ShapeDtypeStruct((1, width), f32),
        ]
        + [jax.ShapeDtypeStruct(plane + wide_block, bf16)] * n
        + [jax.ShapeDtypeStruct((n,) + plane + down_block, bf16)],
        scratch_shapes=[
            pltpu.VMEM(whole + wide_block, bf16),
            pltpu.VMEM(whole + down_block, bf16),
            pltpu.VMEM((n,) + plane + wide_block, bf16),
            pltpu.VMEM((n,) + plane + down_block, bf16),
            pltpu.VMEM((count, width), f32),
            pltpu.VMEM((count, width), bf16),
            pltpu.VMEM((count, width), f32),
            pltpu.VMEM((count, width), bf16),
            pltpu.SemaphoreType.DMA((2 * n,)),
            pltpu.SemaphoreType.DMA((2 * n,)),
        ],
        compiler_params=pltpu.CompilerParams(
            collective_id=collective_id, has_side_effects=True, vmem_limit_bytes=60 << 20
        ),
        name="feed_forward",
    )(hidden_one, cotangent, outer_w, down_w, gain, *attended, *inverse)
    return list(outs[:5]) + [list(outs[5 : 5 + n]), outs[5 + n]]


def from_others(pieces, sizes):
    n = sizes["x"]
    got = []
    for k in range(1, n):
        pairs = [(((x + k) % n) * 2 + c, x * 2 + c) for x in range(n) for c in range(2)]
        got.append(lax.ppermute(pieces[n - k], "batch", pairs))
    return got


def back_rows_kernel(sizes, rows, tasks_info, inner, *refs):
    refs = list(refs)

    def take(count):
        taken = refs[:count]
        del refs[:count]
        return taken

    info_ref, far_ref, diag_ref, q_ref, g_ref, full_ref, peak_ref, kv_ref, dkv_ref, normed_ref, second_ref, near_before = take(12)
    if inner:
        own_ref, dq_before_ref, d_out_ref = take(3)
    grads = [take(info[4]) for info in tasks_info]
    d_normed_ref, dq_ref, near_ref = take(3)
    outs = [take(info[3]) for info in tasks_info]
    last_ref = take(1)[0]
    if inner:
        inner_ref = take(1)[0]
        inner_counts = inner
        d_last_ref = take(1)[0]
    else:
        d_last_ref = last_ref
    kv_buf, chunk_ref, normed_buf, d_rows_ref, ybuf, chain, bias_ref, sum_ref, acc_ref, total_ref = take(10)
    kv_sem, chunk_sem, normed_sem, send_sem, recv_sem = refs[-5:]
    bufs = refs[:-5]
    me = place(sizes)
    first = me["z"] * sizes["y"] + me["y"]
    seqs, length, _ = kv_ref.shape
    n = sizes["z"]
    step = length // n
    last = seqs - 1
    width = q_ref.shape[1]
    pairs = diag_ref.shape[0]
    wide = width // pairs
    fetch = pltpu.make_async_copy(kv_ref.at[last], kv_buf, kv_sem)
    fetch.start()
    greet(sizes, me, SLOTS + ("s",))
    sems = Sems(send_sem, recv_sem)
    ffn = []
    for (order, dims, counts, _, many), grad, out in zip(tasks_info, grads, outs):
        src = grad[0]
        if many > 1:
            src = bufs.pop(0)

            def total(spots, src=src, grad=grad):
                here = spots + (slice(None), slice(None))
                value = grad[0][here].astype(jnp.float32)
                for more in grad[1:]:
                    value = value + more[here].astype(jnp.float32)
                src[here] = value.astype(src.dtype)

            over(src.shape[:-2], total)
        stages = stage_refs(sizes, order, counts, bufs)
        ffn.append(reduce_task(sizes, me, src, out[0] if len(out) == 1 else Split(out), stages, sems, order, dims))
        next(ffn[-1])
    wide_task, down_task = ffn

    def rows_of(p):
        def produce(j):
            here = pl.ds(pl.multiple_of(j * step, step), step)
            if p < last:
                copy = pltpu.make_async_copy(dkv_ref.at[p, here], chunk_ref.at[0], chunk_sem.at[0])
                copy.start()
                copy.wait()
                block = chunk_ref[0]
            else:
                block = d_last_ref[here, :]
            block = nt_dot(block, second_ref[...]).astype(jnp.bfloat16)
            d_rows_ref[p, j] = block.reshape(d_rows_ref.shape[2:])

        return collect_task(
            sizes, me, d_rows_ref.at[p], d_normed_ref.at[p], ybuf.at[p], chain.at[p], sems, produce
        )

    before = [rows_of(p) for p in range(last)]
    for task in before:
        next(task)
    fetch.wait()
    size = info_ref[last]

    def one_pair(p, carry):
        fill_bias(rows, far_ref, diag_ref.at[pl.ds(p, 1)], bias_ref, p)
        sum_ref[...] = jnp.zeros_like(sum_ref)
        lanes = pl.ds(pl.multiple_of(p * wide, wide), wide)
        tail = slice(last * rows, seqs * rows)
        k_lanes = pl.ds(pl.multiple_of(2 * p * wide, wide), wide)
        v_lanes = pl.ds(pl.multiple_of((2 * p + 1) * wide, wide), wide)

        def write(here, dk, dv):
            d_last_ref[here, k_lanes] = dk
            d_last_ref[here, v_lanes] = dv

        dq_ref[:, lanes] = back_pair(
            rows,
            size,
            first,
            q_ref[tail, lanes],
            g_ref[tail, lanes],
            full_ref[:, lanes],
            (lambda here: (kv_buf[here, k_lanes], kv_buf[here, v_lanes]), length // (SPAN * rows)),
            [peak_ref[0, p, a : a + 1, :] for a in range(2)],
            bias_ref,
            sum_ref,
            acc_ref,
            write,
        )

        def keep(a, slot, value):
            near_ref[p, a, slot] = value + near_before[p, a, slot]

        near_sums(rows, sum_ref, keep)
        for i in range(min(pairs, n - 1)):

            @pl.when(p == i)
            def _():
                for task in before:
                    next(task, None)

        @pl.when(p == pairs - 1)
        def _():
            next(wide_task)
            next(down_task)

        return carry

    lax.fori_loop(0, pairs, one_pair, 0)
    after = rows_of(last)
    next(after)
    tasks = ffn + before + [after]
    if inner:
        steps = seqs * n
        early = last * n

        def at_step(i):
            return pl.ds(pl.multiple_of(i * step, step), step)

        def normed_copy(i):
            slot = lax.rem(i, 2)
            return pltpu.make_async_copy(normed_ref.at[at_step(i)], normed_buf.at[slot], normed_sem.at[slot])

        def early_copy(i):
            slot = lax.rem(i, 2)
            src = dkv_ref.at[lax.div(i, n), at_step(lax.rem(i, n))]
            return pltpu.make_async_copy(src, chunk_ref.at[slot], chunk_sem.at[slot])

        normed_copy(0).start()
        early_copy(0).start()
        total_ref[...] = jnp.zeros_like(total_ref)

        plan = [[], before, [], [wide_task], [after], [], [after]]

        def weigh(i, carry):
            pl.when(i + 1 < steps)(lambda: normed_copy(i + 1).start())
            pl.when(i + 1 < early)(lambda: early_copy(i + 1).start())
            normed_copy(i).wait()
            slot = lax.rem(i, 2)

            @pl.when(i < early)
            def _():
                early_copy(i).wait()
                total_ref[...] += tn_dot(normed_buf[slot], chunk_ref[slot])

            @pl.when(i >= early)
            def _():
                total_ref[...] += tn_dot(normed_buf[slot], d_last_ref[at_step(i - early), :])

            for k, tasks_now in enumerate(plan):

                @pl.when(i == k)
                def _():
                    for task in tasks_now:
                        next(task, None)

            return carry

        lax.fori_loop(0, steps, weigh, 0)
        block = inner_ref.shape[:-1]
        d_query = tn_dot(own_ref[last * rows :], dq_ref[...])
        if last:
            d_query = d_query + tn_dot(own_ref[: last * rows], dq_before_ref[...])
        inner_ref[..., :width] = d_query.astype(jnp.bfloat16).reshape(block + (width,))
        inner_ref[..., width : 2 * width] = d_out_ref[...]
        inner_ref[..., 2 * width :] = total_ref[...].astype(jnp.bfloat16).reshape(block + (2 * width,))
        stages = stage_refs(sizes, "cx", inner_counts, bufs)
        tasks.insert(0, reduce_task(sizes, me, inner_ref, last_ref, stages, sems, "cx", SLOTS))
    run_together(tasks)


def back_rows(info, far, diag, q, g, full, kv, peak, dkv, normed_all, normed_own, second, near_before, dq_before, d_out, grads,
              orders, splits, sizes, rows, collective_id, name="back_rows"):
    seqs, length, double = kv.shape
    width = q.shape[1]
    last = seqs - 1
    pairs = far.shape[0] // 2
    n, fast = sizes["z"], sizes["y"]
    step = length // n
    smem, vmem = pl.BlockSpec(memory_space=pltpu.SMEM), pl.BlockSpec(memory_space=pltpu.VMEM)
    anywhere = pl.BlockSpec(memory_space=pl.ANY)
    bf16, f32 = jnp.bfloat16, jnp.float32
    ins = [info, far, diag, q, g, full, peak, kv, dkv, normed_all, second, near_before]
    in_specs = [smem, smem] + [vmem] * 5 + [anywhere] * 3 + [vmem] * 2
    devices = sizes["x"] * sizes["c"] * n * fast
    own_block = (width // devices, 4 * width)
    inner = None
    scratch, total = [], 0
    if own_block[0] % 16 == 0:
        whole = tuple(sizes[d] for d in SLOTS)
        more, inner, needed, left = stage_buffers(sizes, own_block, bf16, SLOTS, "cx")
        inner_more = more
        total += needed
        ins += [normed_own, dq_before, d_out.reshape(whole + (own_block[0], width))]
        in_specs += [vmem] * 3
        last_shape = jax.ShapeDtypeStruct(tuple(sizes[d] for d in left) + own_block, bf16)
    else:
        last_shape = jax.ShapeDtypeStruct((length, double), bf16)
    tasks_info, shapes, later = [], [], []
    for grad, order, widths in zip(grads, orders, splits):
        many = isinstance(grad, list)
        given = grad if many else [grad]
        block = given[0].shape[-2:]
        dims = ("z", "y") if many else ("x", "z", "y")
        more, counts, needed, left = stage_buffers(sizes, block, given[0].dtype, dims, order)
        if len(given) > 1:
            more = [pltpu.VMEM(given[0].shape, given[0].dtype)] + more
        scratch += more
        total += needed
        ends, widths = cut_shapes(block, left, widths, sizes, given[0].dtype)
        shapes += ends
        later.append(widths)
        tasks_info.append((order, dims, counts, len(ends), len(given)))
        ins += given
        in_specs += [vmem] * len(given)
    head_shapes = [
        jax.ShapeDtypeStruct((seqs, rows, width), f32),
        jax.ShapeDtypeStruct((rows, width), bf16),
        jax.ShapeDtypeStruct((pairs, 2, 5, 8, 2 * rows), f32),
    ]
    own_scratch = []
    if inner:
        own_scratch = [pltpu.VMEM(whole + own_block, bf16), pltpu.VMEM((length, double), bf16)]
        scratch = scratch + inner_more
    block = (seqs, n, fast, rows, width)
    own_scratch += [
        pltpu.VMEM((length, double), bf16),
        pltpu.VMEM((2, step, double), bf16),
        pltpu.VMEM((2, step, width), bf16),
        pltpu.VMEM(block, bf16),
        pltpu.VMEM((seqs, fast - 1, n, rows, width), bf16),
        pltpu.VMEM((seqs, 2, n, rows, width), bf16),
        pltpu.VMEM((2, 5, rows, rows), f32),
        pltpu.VMEM((2, 5, rows, rows), f32),
        pltpu.VMEM((2, width // pairs, rows), f32),
        pltpu.VMEM((width, double), f32) if inner else pltpu.VMEM((8, 128), f32),
    ]
    total += seqs * ((fast - 1) * n + 2 * n)
    outs = pl.pallas_call(
        functools.partial(back_rows_kernel, sizes, rows, tasks_info, inner),
        in_specs=in_specs,
        out_specs=[vmem] * (len(shapes) + 4),
        out_shape=head_shapes + shapes + [last_shape],
        scratch_shapes=own_scratch
        + scratch
        + [
            pltpu.SemaphoreType.DMA,
            pltpu.SemaphoreType.DMA((2,)),
            pltpu.SemaphoreType.DMA((2,)),
            pltpu.SemaphoreType.DMA((total,)),
            pltpu.SemaphoreType.DMA((total,)),
        ],
        compiler_params=pltpu.CompilerParams(
            collective_id=collective_id, has_side_effects=True, vmem_limit_bytes=62 << 20
        ),
        name=name,
    )(*ins)
    outs = list(outs)
    heads = [outs.pop(0) for _ in range(3)]
    results = []
    for (_, _, _, cut, _), widths in zip(tasks_info, later):
        results.append(cut_columns([outs.pop(0) for _ in range(cut)], widths))
    return heads + results + [outs[0], inner is not None]


def finish_kernel(refs_in, *refs):
    layer, d_inputs, spill, small, proj, query, out, second, gate, up, down = refs[:refs_in]
    (o_layer, o_input, o_taps, o_proj, o_query, o_key, o_value, o_out, o_gate, o_up, o_down) = refs[refs_in:]
    o_layer[...] = layer[...]
    rows = d_inputs.shape[1]
    edge = lax.broadcasted_iota(jnp.int32, spill.shape[1:], 0)
    for b in range(d_inputs.shape[0]):
        o_input[b] = d_inputs[b].astype(o_input.dtype)
        late = jnp.where(edge >= 5, pltpu.roll(spill[b], 5, 0), 0.0)
        tail = d_inputs[b, rows - 16 :, :]
        late = jnp.concatenate([jnp.zeros_like(late), late], axis=0)
        o_input[b, rows - 16 :, :] = (tail + late).astype(o_input.dtype)
    o_taps[...] = small[:, :TAPS]
    for source, target in ((proj, o_proj), (query, o_query), (out, o_out), (gate, o_gate), (up, o_up), (down, o_down)):
        target[...] = source[...]
    pair = PACK
    for p in range(second.shape[1] // (2 * pair)):
        o_key[:, p * pair : (p + 1) * pair] = second[:, 2 * p * pair : (2 * p + 1) * pair]
        o_value[:, p * pair : (p + 1) * pair] = second[:, (2 * p + 1) * pair : (2 * p + 2) * pair]


def finish(*ins):
    layer, d_inputs, _, small, proj, query, out, second, gate, up, down = ins
    like = lambda x: jax.ShapeDtypeStruct(x.shape, x.dtype)
    vmem = pl.BlockSpec(memory_space=pltpu.VMEM)
    return pl.pallas_call(
        functools.partial(finish_kernel, len(ins)),
        in_specs=[vmem] * len(ins),
        out_specs=[vmem] * 11,
        out_shape=[
            like(layer),
            jax.ShapeDtypeStruct(d_inputs.shape, jnp.bfloat16),
            jax.ShapeDtypeStruct((small.shape[0], TAPS), jnp.float32),
            like(proj),
            like(query),
            like(proj),
            like(proj),
            like(out),
            like(gate),
            like(up),
            like(down),
        ],
        compiler_params=pltpu.CompilerParams(vmem_limit_bytes=32 << 20),
        name="finish",
    )(*ins)


def on_device(
    inputs,
    lengths,
    conv_taps,
    gain_attn,
    w_proj,
    w_query,
    w_key,
    w_value,
    w_out,
    gain_ffn,
    w_gate,
    w_up,
    w_down,
    rel_bias,
    cotangent,
):
    batch, seq = lax.axis_size("batch"), lax.axis_size("seq")
    sizes = layout_of(batch, seq)
    devices = batch * seq
    seqs, rows, width = inputs.shape
    length = rows * seq
    count = seqs * rows
    own = w_proj.shape[0]
    own_bias = rel_bias.shape[0]
    heads = own_bias * devices // NB
    hidden = w_gate.shape[1]

    small = jnp.concatenate(
        [
            conv_taps,
            gain_attn[:, None],
            gain_ffn[:, None],
            jnp.pad(rel_bias, (0, own - own_bias))[:, None],
            jnp.zeros((own, PACK - TAPS - 3), jnp.bfloat16),
        ],
        axis=1,
    )
    pairs = heads // 2
    pair = width // pairs
    key_value_w = []
    for p in range(pairs):
        key_value_w += [(w_key, p * pair, (p + 1) * pair), (w_value, p * pair, (p + 1) * pair)]
    first, second, outer_plane, down_plane, left_rim = gather_all(
        [
            [(small, 0, PACK), (w_proj, 0, width), (w_query, 0, width)],
            key_value_w,
            [(w_out, 0, width), (w_gate, 0, hidden), (w_up, 0, hidden)],
            w_down,
        ],
        ["Zyxc", "Zxyc", "zy", "yz"],
        sizes,
        1,
        rim=inputs,
        name="gather_first",
    )
    first = first.reshape(width, -1)
    second = second.reshape(width, -1)
    taps = first[:, :TAPS].astype(jnp.float32)
    gain_first = first[:, TAPS].astype(jnp.float32)
    gain_second = first[:, TAPS + 1].astype(jnp.float32)
    table = first[:, TAPS + 2].reshape(devices, own)[:, :own_bias].reshape(heads, NB).astype(jnp.float32)
    proj_w = first[:, PACK : PACK + width]
    query_w = first[:, PACK + width :]

    padded = jnp.concatenate([left_rim[:, 13:], inputs], axis=1).astype(jnp.float32)
    mixed_conv, conv_back = jax.vjp(partial(conv_mix, row_count=rows), padded, taps)
    mixed_low = mixed_conv.astype(jnp.bfloat16).reshape(count, width)
    resid_in = inputs.astype(jnp.float32).reshape(count, width)
    hidden_one = resid_in + mat_dot(mixed_low, proj_w)
    normed_one, norm_one_back = jax.vjp(norm_rows, hidden_one, gain_first)
    normed_low = normed_one.astype(jnp.bfloat16)

    queries = mat_dot(normed_low, query_w).astype(jnp.bfloat16)
    far, diag = bias_tables(table, rows)
    info = jnp.concatenate([lengths, lax.axis_index("seq")[None].astype(jnp.int32)])
    (outer_w, down_w), normed_all, key_value, begun = gather_rows(
        info,
        far,
        diag,
        normed_low.reshape(seqs, rows, width),
        queries,
        second,
        [outer_plane, down_plane],
        ["xc", "xc"],
        sizes,
        2,
    )
    outer_w = outer_w.reshape(width, -1)
    down_w = down_w.reshape(hidden, -1)
    out_w = outer_w[:, :width]
    wide_w = outer_w[:, width:]
    normed_all = normed_all.reshape(seqs * length, width)
    rest = attend(info, far, diag, queries, key_value, rows, length, 1)

    grad_low = cotangent.reshape(count, width)
    if own % 16 == 0:
        layer_out, d_hidden_two, d_out_w, scaled, d_gain_two, wide_pieces, down_half = feed_forward(
            hidden_one,
            grad_low,
            outer_w,
            down_w,
            gain_second[None],
            (begun[0], rest[0]),
            (begun[2], rest[2]),
            sizes,
            4,
        )
        d_gain_two = d_gain_two[0]
    else:
        attended = jnp.concatenate([begun[0], rest[0]], axis=0)
        inverse = jnp.concatenate([begun[2], rest[2]], axis=0)
        hidden_two = hidden_one + mat_dot(attended, out_w)
        normed_two, norm_two_back = jax.vjp(norm_rows, hidden_two, gain_second)
        normed_two_low = normed_two.astype(jnp.bfloat16)
        both_pre = mat_dot(normed_two_low, wide_w)
        inner_act, inner_back = jax.vjp(gated, both_pre[:, :hidden], both_pre[:, hidden:])
        inner_low = inner_act.astype(jnp.bfloat16)
        layer_out = (hidden_two + mat_dot(inner_low, down_w)).astype(jnp.bfloat16)

        d_down_w = outer_sum(inner_low, grad_low).astype(jnp.bfloat16)
        d_gate, d_up = inner_back(back_dot(grad_low, down_w))
        d_both = jnp.concatenate([d_gate.astype(jnp.bfloat16), d_up.astype(jnp.bfloat16)], axis=1)
        d_wide_w = outer_sum(normed_two_low, d_both).astype(jnp.bfloat16)
        d_hidden_part, d_gain_two = norm_two_back(back_dot(d_both, wide_w))
        d_hidden_two = grad_low.astype(jnp.float32) + d_hidden_part
        d_attn_low = d_hidden_two.astype(jnp.bfloat16)
        d_out_w = outer_sum(attended, d_attn_low).astype(jnp.bfloat16)
        d_attended = back_dot(d_attn_low, out_w).astype(jnp.bfloat16)
        scaled = (d_attended.astype(jnp.float32) * inverse).astype(jnp.bfloat16)
        wide_pieces, down_half = halve_cores([d_wide_w, d_down_w], [True, False], sizes, 4)
    scaled, wide_pieces, down_half, d_out_w, layer_out = lax.optimization_barrier(
        (scaled, wide_pieces, down_half, d_out_w, layer_out)
    )
    wide_others = from_others(wide_pieces, sizes)
    early = seqs - 1
    assert early == 1
    dq_before, dkv_before, near_before = attend_back(
        info, far, diag, queries, scaled, begun[1], key_value, begun[3], rows, length, early
    )
    dq_before, dkv_before, near_before, wide_others = lax.optimization_barrier(
        (dq_before, dkv_before, near_before, wide_others)
    )
    d_normed_one, dq_last, near, (g_gate, g_up), (g_down,), last, joined = back_rows(
        info,
        far,
        diag,
        queries,
        scaled,
        rest[1],
        key_value,
        rest[3],
        dkv_before,
        normed_all,
        normed_low,
        second,
        near_before,
        dq_before,
        d_out_w,
        [[wide_pieces[0]] + wide_others, down_half],
        ["Zy", "xs"],
        [(hidden, hidden), None],
        sizes,
        rows,
        5,
    )
    d_table = bias_grad(near, rows).reshape(heads * NB)
    d_queries = jnp.concatenate([dq_before, dq_last], axis=0)
    if joined:
        inner, inner_order = last, "s"
    else:
        d_key_value = jnp.concatenate([dkv_before, last[None]], axis=0).reshape(seqs * length, 2 * width)
        d_second_w = outer_sum(normed_all, d_key_value).astype(jnp.bfloat16)
        d_query_w = outer_sum(normed_low, d_queries).astype(jnp.bfloat16)
        inner, inner_order = jnp.concatenate([d_query_w, d_out_w, d_second_w], axis=1), "cxs"
    d_normed_one = d_normed_one.reshape(count, width)
    d_normed_one = d_normed_one + back_dot(d_queries, query_w)
    d_first_part, d_gain_one = norm_one_back(d_normed_one)
    d_hidden_one = d_hidden_two + d_first_part
    d_mix_low = d_hidden_one.astype(jnp.bfloat16)
    d_proj_w = outer_sum(mixed_low, d_mix_low).astype(jnp.bfloat16)
    d_mixed = back_dot(d_mix_low, proj_w).reshape(seqs, rows, width)
    d_padded, d_taps = conv_back(d_mixed)
    d_inputs = d_hidden_one.reshape(seqs, rows, width) + d_padded[:, 3:, :]
    d_small = jnp.concatenate(
        [
            d_taps.T,
            d_gain_one[None],
            d_gain_two[None],
            jnp.pad(d_table.reshape(devices, own_bias), ((0, 0), (0, own - own_bias))).reshape(1, width),
            jnp.zeros((16 - TAPS - 3, width), jnp.float32),
        ],
        axis=0,
    )
    d_last = jnp.concatenate([d_proj_w, jnp.pad(d_small.T, ((0, 0), (0, PACK - 16))).astype(jnp.bfloat16)], axis=1)
    (g_proj, g_small), (g_query, g_out, g_second), spill = reduce_all(
        [d_last, inner],
        ["cxs", inner_order],
        sizes,
        6,
        spill=d_padded[:, :8, :],
        splits=[(width, PACK), (width, width, 2 * width)],
    )
    assert pair == PACK
    done = finish(
        layer_out,
        d_inputs,
        spill,
        g_small,
        g_proj,
        g_query,
        g_out,
        g_second,
        g_gate,
        g_up,
        g_down.reshape(w_down.shape),
    )
    layer_out, input_grad, g_taps, g_proj, g_query, g_key, g_value, g_out, g_gate, g_up, g_down = done
    return (
        layer_out.reshape(seqs, rows, width),
        input_grad,
        g_taps,
        g_small[:, TAPS],
        g_proj,
        g_query,
        g_key,
        g_value,
        g_out,
        g_small[:, TAPS + 1],
        g_gate,
        g_up,
        g_down,
        g_small[:own_bias, TAPS + 2],
    )


def solution(mesh):
    in_specs = (
        P("batch", "seq", None),
        P("batch"),
        P(("batch", "seq"), None),
        P(("batch", "seq")),
        P(("batch", "seq"), None),
        P(("batch", "seq"), None),
        P(("batch", "seq"), None),
        P(("batch", "seq"), None),
        P(("batch", "seq"), None),
        P(("batch", "seq")),
        P(("batch", "seq"), None),
        P(("batch", "seq"), None),
        P(("batch", "seq"), None),
        P(("batch", "seq")),
        P("batch", "seq", None),
    )
    out_specs = (
        P("batch", "seq", None),
        P("batch", "seq", None),
        P(("batch", "seq"), None),
        P(("batch", "seq")),
        P(("batch", "seq"), None),
        P(("batch", "seq"), None),
        P(("batch", "seq"), None),
        P(("batch", "seq"), None),
        P(("batch", "seq"), None),
        P(("batch", "seq")),
        P(("batch", "seq"), None),
        P(("batch", "seq"), None),
        P(("batch", "seq"), None),
        P(("batch", "seq")),
    )
    return jax.shard_map(
        on_device, mesh=mesh, in_specs=in_specs, out_specs=out_specs, check_vma=False
    )
```
